32 devices in a mesh: dp: 2 (over y), ctx: 4 (over x, core), tp: 4 (over z).
Axes of the slice: x: 2, y: 2, z: 4, core: 2. Of those that a mesh axis runs over, the one named last changes fastest.
Arguments:
- hidden: bfloat16 [8, 1024, 2048], P('dp', 'ctx', 'tp'), may hold values from -6 to 6
- cotangent: bfloat16 [8, 1024, 2048], P('dp', 'ctx', 'tp'), may hold values from -6 to 6
- segments: int32 [8, 1024], P('dp', 'ctx'), may hold values from 0 to 17, as said below
- positions: int32 [8, 1024], P('dp', 'ctx'), may hold values from 0 to 1023, as said below
- w_query: bfloat16 [2048, 2048], P(('dp', 'ctx'), 'tp')
- w_key: bfloat16 [2048, 2048], P(('dp', 'ctx'), 'tp')
- w_value: bfloat16 [2048, 2048], P(('dp', 'ctx'), 'tp'), may hold values from -0.125 to 0.125
- w_out: bfloat16 [2048, 2048], P('tp', ('dp', 'ctx'))
- w_gate: bfloat16 [2048, 8192], P(('dp', 'ctx'), 'tp'), may hold values from -0.125 to 0.125
- w_up: bfloat16 [2048, 8192], P(('dp', 'ctx'), 'tp'), may hold values from -0.125 to 0.125
- w_down: bfloat16 [8192, 2048], P('tp', ('dp', 'ctx'))
- q_gain: float32 [2048], P('tp'), may hold values from 1 to 1.8
- k_gain: float32 [2048], P('tp'), may hold values from 1 to 1.8
- attn_gain: float32 [2048], P('tp'), may hold values from 0.5 to 1.5
- mlp_gain: float32 [2048], P('tp'), may hold values from 0.5 to 1.5
Outputs:
- out_hidden: bfloat16 [8, 1024, 2048], P('dp', 'ctx', 'tp')
- grad_hidden: bfloat16 [8, 1024, 2048], P('dp', 'ctx', 'tp')
- grad_w_query: float32 [2048, 2048], P(('dp', 'ctx'), 'tp')
- grad_w_key: float32 [2048, 2048], P(('dp', 'ctx'), 'tp')
- grad_w_value: float32 [2048, 2048], P(('dp', 'ctx'), 'tp')
- grad_w_out: float32 [2048, 2048], P('tp', ('dp', 'ctx'))
- grad_w_gate: float32 [2048, 8192], P(('dp', 'ctx'), 'tp')
- grad_w_up: float32 [2048, 8192], P(('dp', 'ctx'), 'tp')
- grad_w_down: float32 [8192, 2048], P('tp', ('dp', 'ctx'))
- grad_q_gain: float32 [2048], P('tp')
- grad_k_gain: float32 [2048], P('tp')
- grad_attn_gain: float32 [2048], P('tp')
- grad_mlp_gain: float32 [2048], P('tp')
The draws below stay inside these ranges and needn't reach their ends.
Inputs may be any that keep to these rules, and one draw needn't show every extreme that they name: `segments`: in each sequence segment numbers start at 0 and never fall; each step of one numbers the next document; every document that the sequence's end does not cut has at least 60 tokens. `positions`: each token's position counts from 0 at the first token of its document.
All inputs are finite; a program needn't handle non-finite values.
Results may differ from the reference program's by a relative error of at most 0.025.
Values may be sent and summed in bfloat16 or wider, within the bound.
A program may use at most 256 MiB of HBM per device.

```python
import math
from functools import partial
import jax
import jax.numpy as jnp
from jax import lax

D = 2048
HEADS = 16
HEAD_DIM = 128
FF = 8192
MIN_DOC = 60
SEQ_LEN = 1024
SEQS = 8


def ramp_weight(key, rows, cols, fan_in, rising):
    along = jnp.arange(cols, dtype=jnp.float32) / (cols - 1)
    if not rising:
        along = 1.0 - along
    base = jax.random.normal(key, (rows, cols), jnp.float32)
    lower, upper = (0.6, 1.3)
    amplitude = lower * (upper / lower) ** along
    return base * amplitude[None, :] * fan_in ** (-0.5)


def draw_w_query(key, part):
    return ramp_weight(jax.random.fold_in(key, 101), D, D, D, True).astype(jnp.bfloat16)


def draw_w_key(key, part):
    return ramp_weight(jax.random.fold_in(key, 102), D, D, D, False).astype(jnp.bfloat16)


def draw_w_out(key, part):
    return ramp_weight(jax.random.fold_in(key, 103), D, D, D, True).astype(jnp.bfloat16)


def draw_w_down(key, part):
    return ramp_weight(jax.random.fold_in(key, 104), FF, D, FF, True).astype(jnp.bfloat16)


def doc_layout(key):
    inner = jax.random.fold_in(key, 11)
    slots = SEQ_LEN // MIN_DOC + 1
    lengths = jax.random.randint(inner, (SEQS, slots), MIN_DOC, SEQ_LEN + 1, dtype=jnp.int32)
    lengths = lengths.at[0, 0].set(SEQ_LEN)
    lengths = lengths.at[1].set(MIN_DOC)
    ends = jnp.cumsum(lengths, axis=1).astype(jnp.int32)
    places = jnp.arange(SEQ_LEN, dtype=jnp.int32)
    segment = jnp.sum((ends[:, None, :] <= places[None, :, None]).astype(jnp.int32), axis=2).astype(jnp.int32)
    starts = (ends - lengths).astype(jnp.int32)
    first = jnp.take_along_axis(starts, segment, axis=1)
    return (segment, (places[None, :] - first).astype(jnp.int32))


def draw_segments(key, part):
    return doc_layout(key)[0]


def draw_positions(key, part):
    return doc_layout(key)[1]


def shard_levels(stream_key, extent, pieces, least, high):
    loudness = 1.0
    for position, blocks in pieces:
        draws = jax.random.uniform(jax.random.fold_in(jax.random.fold_in(stream_key, 6), position), (blocks,), jnp.float32, least / len(pieces), high / len(pieces))
        loudness = loudness * jnp.repeat(jnp.exp(draws), extent[position] // blocks).reshape((-1,) + (1,) * (len(extent) - 1 - position))
    return loudness


def scatter_about(stream_key, dims, scale, reach, cuts=(), held_as=jnp.bfloat16):
    drawn = jax.random.normal(stream_key, dims, jnp.float32) * scale
    if len(cuts) > 0:
        drawn = shard_levels(stream_key, dims, cuts, -0.22, 0.18) * drawn
    return jnp.clip(drawn, min=-reach, max=reach).astype(held_as)


def setup_inputs(seed: int = 0) -> dict:
    splits = jax.random.split(jax.random.key(seed), 16)
    hidden = scatter_about(splits[0], (SEQS, SEQ_LEN, D), 1.0, 6.0, ((0, 2), (1, 4), (2, 4)))
    cotangent = scatter_about(splits[1], (SEQS, SEQ_LEN, D), 1.0, 6.0, ((0, 2), (1, 4), (2, 4)))
    segments = draw_segments(jax.random.fold_in(splits[15], 71), 0)
    positions = draw_positions(jax.random.fold_in(splits[15], 71), 0)
    w_query = draw_w_query(jax.random.fold_in(splits[15], 71), 0)
    w_key = draw_w_key(jax.random.fold_in(splits[15], 71), 0)
    w_value = scatter_about(splits[6], (D, D), D ** -0.5, 0.125, ((0, 8), (1, 4)))
    w_out = draw_w_out(jax.random.fold_in(splits[15], 71), 0)
    w_gate = scatter_about(splits[8], (D, FF), D ** -0.5, 0.125, ((0, 8), (1, 4)))
    w_up = scatter_about(splits[9], (D, FF), D ** -0.5, 0.125, ((0, 8), (1, 4)))
    w_down = draw_w_down(jax.random.fold_in(splits[15], 71), 0)
    q_gain = jnp.clip(1.0 + 0.79999995 * jax.random.uniform(splits[11], (D,), jnp.float32) ** shard_levels(splits[11], (D,), ((0, 4),), -0.2, 0.2), 1.0, 1.8)
    k_gain = jnp.clip(1.0 + 0.79999995 * jax.random.uniform(splits[12], (D,), jnp.float32) ** shard_levels(splits[12], (D,), ((0, 4),), -0.2, 0.2), 1.0, 1.8)
    attn_gain = jnp.clip(1.0 + 0.1 * jax.random.normal(splits[13], (D,), jnp.float32), 0.5, 1.5)
    mlp_gain = jnp.clip(1.0 + 0.1 * jax.random.normal(splits[14], (D,), jnp.float32), 0.5, 1.5)
    return {"hidden": hidden, "cotangent": cotangent, "segments": segments, "positions": positions, "w_query": w_query, "w_key": w_key, "w_value": w_value, "w_out": w_out, "w_gate": w_gate, "w_up": w_up, "w_down": w_down, "q_gain": q_gain, "k_gain": k_gain, "attn_gain": attn_gain, "mlp_gain": mlp_gain}


EPS = 1e-06
THETA = 500000.0
NEG = -1e+30
HIGH = lax.Precision.HIGHEST

@jax.custom_vjp
def low(v):
    return lax.optimization_barrier(v.astype(jnp.bfloat16)).astype(jnp.float32)

@jax.custom_vjp
def low_back(v):
    return v

def low_keep(v):
    return (low(v), None)

def low_pass(kept, grad):
    return (grad,)

def back_keep(v):
    return (v, None)

def back_low(kept, grad):
    return (low(grad),)
low.defvjp(low_keep, low_pass)
low_back.defvjp(back_keep, back_low)

def matmul(left, right):
    return jnp.einsum('gld,de->gle', left, right, precision=HIGH)

def rms_norm(value, gain):
    return value * lax.rsqrt(lax.optimization_barrier(jnp.mean(value * value, axis=-1, keepdims=True)) + EPS) * gain

def rotary(positions, depth):
    half = depth // 2
    freqs = THETA ** (-(jnp.arange(half, dtype=jnp.float32) * 2.0) / depth)
    angles = positions.astype(jnp.float32)[..., None] * freqs
    return (jnp.cos(angles)[..., None, :], jnp.sin(angles)[..., None, :])

def turn(value, cosine, sine):
    half = value.shape[-1] // 2
    first = value[..., :half]
    second = value[..., half:]
    return jnp.concatenate([first * cosine - second * sine, second * cosine + first * sine], axis=-1)

def head_attention(parts, segment):
    query, key, values = parts
    length = query.shape[1]
    logits = low_back(jnp.einsum('gqd,gkd->gqk', query, key, precision=HIGH) * (1.0 / math.sqrt(HEAD_DIM)))
    places = jnp.arange(length, dtype=jnp.int32)
    causal = places[:, None] >= places[None, :]
    allowed = jnp.logical_and(segment[:, :, None] == segment[:, None, :], causal[None])
    probs = jax.nn.softmax(jnp.where(allowed, logits, NEG), axis=-1)
    return jnp.einsum('gqk,gkd->gqd', low(probs), values, precision=HIGH)

def forward(hidden, w_query, w_key, w_value, w_out, w_gate, w_up, w_down, q_gain, k_gain, attn_gain, mlp_gain, segment, positions):
    groups, length, width = hidden.shape

    def by_heads(value):
        return value.reshape(groups, length, HEADS, HEAD_DIM).transpose(2, 0, 1, 3)
    query_raw = low_back(matmul(hidden, w_query))
    key_raw = low_back(matmul(hidden, w_key))
    values = low(low_back(matmul(hidden, w_value)))
    cosine, sine = rotary(positions, HEAD_DIM)
    query = low(turn(rms_norm(query_raw, q_gain).reshape(groups, length, HEADS, HEAD_DIM), cosine, sine))
    key = low(turn(rms_norm(key_raw, k_gain).reshape(groups, length, HEADS, HEAD_DIM), cosine, sine))
    attend = jax.checkpoint(partial(head_attention, segment=segment))
    heads_out = lax.map(attend, (query.transpose(2, 0, 1, 3), key.transpose(2, 0, 1, 3), by_heads(values)))
    heads_b = low(low_back(heads_out.transpose(1, 2, 0, 3).reshape(groups, length, width)))
    branch_attn = low_back(matmul(heads_b, w_out))
    resid = hidden + rms_norm(branch_attn, attn_gain)
    resid_b = low(resid)
    gate = low_back(matmul(resid_b, w_gate))
    up_val = low_back(matmul(resid_b, w_up))
    act = low(jax.nn.silu(gate) * up_val)
    branch_mlp = low_back(matmul(act, w_down))
    return resid + rms_norm(branch_mlp, mlp_gain)

def reference(hidden, cotangent, segments, positions, w_query, w_key, w_value, w_out, w_gate, w_up, w_down, q_gain, k_gain, attn_gain, mlp_gain):
    params = tuple((tensor.astype(jnp.float32) for tensor in (w_query, w_key, w_value, w_out, w_gate, w_up, w_down, q_gain, k_gain, attn_gain, mlp_gain)))
    group = math.gcd(SEQS, max(1, 4096 // SEQ_LEN))
    count = SEQS // group

    def grouped(value):
        return value.reshape((count, group) + value.shape[1:])

    def step(carry, item):
        block, grad_block, segment, places = item

        def apply(inputs, *weights):
            return forward(inputs, *weights, segment, places)
        result, pullback = jax.vjp(apply, block.astype(jnp.float32), *params)
        grads = pullback(grad_block.astype(jnp.float32))
        carry = tuple((left + right for left, right in zip(carry, grads[1:])))
        return (carry, (result.astype(jnp.bfloat16), grads[0].astype(jnp.bfloat16)))
    start = tuple((jnp.zeros(tensor.shape, jnp.float32) for tensor in params))
    totals, (outputs, input_grads) = lax.scan(step, start, (grouped(hidden), grouped(cotangent), grouped(segments), grouped(positions)))
    return (outputs.reshape(hidden.shape), input_grads.reshape(hidden.shape), totals[0], totals[1], totals[2], totals[3], totals[4], totals[5], totals[6], totals[7], totals[8], totals[9], totals[10])
```

```python
import functools
import math

import jax
import jax.numpy as jnp
from jax import lax
from jax.experimental import pallas as pl
from jax.experimental.pallas import tpu as pltpu
from jax.sharding import PartitionSpec as P

D = 2048
HEAD_DIM = 128
EPS = 1e-06
THETA = 500000.0
NEG = -1e30
BF = jnp.bfloat16
F32 = jnp.float32
MESH = pl.DeviceIdType.MESH
HBM = pl.BlockSpec(memory_space=pltpu.HBM)


class Sems:
    def __init__(self):
        self.count = 0
        self.ref = None

    def take(self, number):
        first = self.count
        self.count += number
        return first

    def at(self, index):
        return self.ref.at[index]


def when(cond, body):
    if cond is None:
        body()
    else:
        pl.when(cond)(body)


def both(a, b):
    if a is None:
        return b
    if b is None:
        return a
    return jnp.logical_and(a, b)


class Place:
    def __init__(self, tp_size):
        self.n = tp_size
        self.tp = lax.axis_index("tp")
        self.dp = lax.axis_index("dp")
        self.ctx = lax.axis_index("ctx")
        self.slot = self.dp * 4 + self.ctx


class Task:
    inputs = ()
    outputs = ()
    scratch = ()
    sems = 0
    axes = ()

    def emit(self, place, ins, outs, scr, sem):
        raise NotImplementedError


def remote(src, dst, sem, send, recv, device):
    return pltpu.make_async_remote_copy(
        src_ref=src, dst_ref=dst, send_sem=sem.at(send), recv_sem=sem.at(recv), device_id=device, device_id_type=MESH
    )


class LineGather(Task):
    axes = ("tp",)

    def __init__(self, array, n, pieces=2):
        self.n, self.pieces = n, pieces
        rows, width = array.shape
        self.rows, self.width = rows, width
        self.inputs = (array,)
        self.outputs = (jax.ShapeDtypeStruct((rows, n * width), array.dtype),)
        self.scratch = ()
        self.sems = 1 + 4 * (n - 1) * pieces
        self.unit = rows * width * 2 * 2 / 88e3

    def emit(self, place, ins, outs, scr, sem):
        n, pieces, width = self.n, self.pieces, self.width
        step = self.rows // pieces
        src, out = ins[0], outs[0]
        me = place.tp

        def spot(chunk, piece):
            return out.at[pl.ds(piece * step, step), pl.ds(pl.multiple_of(chunk * width, width), width)]

        own = pltpu.make_async_copy(src, out.at[:, pl.ds(pl.multiple_of(me * width, width), width)], sem.at(0))
        own.start()
        sends = []
        for s in range(n):
            for piece in range(pieces):
                for way in (0, 1):
                    have = None if s == 0 else (me >= s if way == 0 else me + s < n)
                    edge = me < n - 1 if way == 0 else me > 0
                    chunk = me - s if way == 0 else me + s
                    index = 1 + 2 * (((s * 2 + way) * pieces) + piece)
                    if s > 0:
                        prev = 1 + 2 * ((((s - 1) * 2 + way) * pieces) + piece)
                        got = remote(spot(chunk, piece), spot(chunk, piece), sem, prev, prev + 1, {"tp": me})
                        when(have, got.wait_recv)
                    if s < n - 1:
                        origin = src.at[pl.ds(piece * step, step)] if s == 0 else spot(chunk, piece)
                        to = me + 1 if way == 0 else me - 1
                        copy = remote(origin, spot(chunk, piece), sem, index, index + 1, {"tp": to})
                        cond = both(have, edge)
                        when(cond, copy.start)
                        sends.append((cond, copy))
                yield (s + (piece + 1) / pieces) * self.unit * 1.33
        for cond, copy in sends:
            when(cond, copy.wait_send)
        own.wait()


class LineScatter(Task):
    axes = ("tp",)

    def __init__(self, array, n, pieces=2):
        self.n, self.pieces = n, pieces
        rows, wide = array.shape
        width = wide // n
        self.rows, self.width = rows, width
        self.inputs = (array,)
        self.outputs = (jax.ShapeDtypeStruct((rows, width), F32),)
        self.scratch = (
            pltpu.VMEM((n, rows, width), BF),
            pltpu.VMEM((2, n - 1, rows, width), BF),
            pltpu.VMEM((rows, width), F32),
        )
        self.sems = n + 4 * (n - 1) * pieces + 1
        self.unit = rows * width * 2 * 2 / 88e3

    def emit(self, place, ins, outs, scr, sem):
        n, pieces, width = self.n, self.pieces, self.width
        step = self.rows // pieces
        src, out = ins[0], outs[0]
        mine, came, total = scr
        me = place.tp
        loads = []
        for c in range(n):
            load = pltpu.make_async_copy(src.at[:, pl.ds(c * width, width)], mine.at[c], sem.at(c))
            load.start()
            loads.append(load)
        for load in loads:
            load.wait()
        sends = []
        tile = min(64, step)

        def add_into(c, way, k, piece):
            @pl.loop(0, step // tile)
            def _(i):
                rows = pl.ds(pl.multiple_of(piece * step + i * tile, tile), tile)
                mine[c, rows] = (mine[c, rows].astype(F32) + came[way, k, rows].astype(F32)).astype(BF)

        for k in range(n - 1):
            for piece in range(pieces):
                rows = pl.ds(piece * step, step)
                for way in (0, 1):
                    index = n + 2 * (((k * 2 + way) * pieces) + piece)
                    dest = n - 1 - k if way == 0 else k
                    sending = me < dest if way == 0 else me > dest
                    inner = me > 0 if way == 0 else me < n - 1
                    to = me + 1 if way == 0 else me - 1
                    copy = remote(mine.at[dest, rows], came.at[way, k, rows], sem, index, index + 1, {"tp": to})

                    def take(copy=copy, dest=dest, way=way, k=k, piece=piece):
                        copy.wait_recv()
                        add_into(dest, way, k, piece)

                    when(both(sending, inner), take)
                    when(sending, copy.start)
                    sends.append((sending, copy))
                yield (k + 1.2 + piece / pieces) * self.unit * 1.33
        for piece in range(pieces):
            rows = pl.ds(piece * step, step)
            for way in (0, 1):
                inner = me > 0 if way == 0 else me < n - 1
                k = n - 1 - me if way == 0 else me
                base = n + 2 * ((k * 2 + way) * pieces + piece)
                got = pltpu.make_async_remote_copy(
                    src_ref=came.at[way, k, rows],
                    dst_ref=came.at[way, k, rows],
                    send_sem=sem.at(base),
                    recv_sem=sem.at(base + 1),
                    device_id={"tp": me},
                    device_id_type=MESH,
                )
                when(inner, got.wait_recv)

            @pl.loop(0, step // tile)
            def _(i):
                part = pl.ds(pl.multiple_of(piece * step + i * tile, tile), tile)
                total[part] = mine[me, part].astype(F32)

            for way in (0, 1):
                inner = me > 0 if way == 0 else me < n - 1
                k = n - 1 - me if way == 0 else me

                def fold(way=way, k=k):
                    @pl.loop(0, step // tile)
                    def _(i):
                        part = pl.ds(pl.multiple_of(piece * step + i * tile, tile), tile)
                        total[part] = total[part] + came[way, k, part].astype(F32)

                when(inner, fold)
        last = pltpu.make_async_copy(total, out, sem.at(self.sems - 1))
        last.start()
        for cond, copy in sends:
            when(cond, copy.wait_send)
        last.wait()


class PlaneGather(Task):
    def __init__(self, array, dim, with_dp, rank=0.0):
        self.dim, self.with_dp, self.rank = dim, with_dp, rank
        self.inputs = (array,)
        shape = list(array.shape)
        self.size = shape[dim]
        self.rows = shape[0]
        self.blocks = 8 if with_dp else 4
        shape[dim] *= self.blocks
        self.outputs = (jax.ShapeDtypeStruct(tuple(shape), array.dtype),)
        self.axes = ("ctx", "dp") if with_dp else ("ctx",)
        self.sems = 1 + 2 * (3 + 2 + 2 + 2 + 2)
        self.unit = math.prod(array.shape) * 2 * 2 / 88e3

    def emit(self, place, ins, outs, scr, sem):
        src, out = ins[0], outs[0]
        dp, ctx = place.dp, place.ctx
        half = self.rows // 2

        def spot(d, c, part=None):
            block = d * 4 + c if self.with_dp else c
            where = pl.ds(pl.multiple_of(block * self.size, self.size), self.size)
            if self.dim == 1:
                if part is None:
                    return out.at[:, where]
                return out.at[pl.ds(part * half, half), where]
            if part is None:
                return out.at[where]
            return out.at[pl.ds(pl.multiple_of(block * self.size + part * half, half), half)]

        xdev, ydev, cdev = {"ctx": ctx ^ 2}, {"dp": dp ^ 1}, {"ctx": ctx ^ 1}
        mine = spot(dp, ctx)
        own = pltpu.make_async_copy(src, mine, sem.at(0))
        own.start()
        sends = []

        def send(index, origin, target, device):
            copy = remote(origin, target, sem, 1 + 2 * index, 2 + 2 * index, device)
            copy.start()
            sends.append(copy)

        def got(index, target):
            remote(target, target, sem, 1 + 2 * index, 2 + 2 * index, cdev).wait_recv()

        send(0, src, mine, xdev)
        if self.with_dp:
            send(1, src, mine, ydev)
        send(2, src, mine, cdev)
        yield self.rank + self.unit * 1.0
        from_x = spot(dp, ctx ^ 2)
        got(0, from_x)
        if self.with_dp:
            send(3, spot(dp, ctx ^ 2, 0), spot(dp, ctx ^ 2, 0), ydev)
        send(5, from_x, from_x, cdev)
        if self.with_dp:
            from_y = spot(dp ^ 1, ctx)
            got(1, from_y)
            send(4, spot(dp ^ 1, ctx, 1), spot(dp ^ 1, ctx, 1), xdev)
            send(6, from_y, from_y, cdev)
            yield self.rank + self.unit * 1.5
            for part in (0, 1):
                diagonal = spot(dp ^ 1, ctx ^ 2, part)
                got(3 + part, diagonal)
                send(7 + part, diagonal, diagonal, cdev)
        yield self.rank + self.unit * 1.6
        got(2, spot(dp, ctx ^ 1))
        got(5, spot(dp, ctx ^ 3))
        if self.with_dp:
            got(6, spot(dp ^ 1, ctx ^ 1))
            for part in (0, 1):
                got(7 + part, spot(dp ^ 1, ctx ^ 3, part))
        for copy in sends:
            copy.wait_send()
        own.wait()


class PlaneScatter(Task):
    def __init__(self, array, dim, with_dp, rank=0.0):
        self.dim, self.with_dp, self.rank = dim, with_dp, rank
        self.inputs = (array,)
        shape = list(array.shape)
        self.blocks = 8 if with_dp else 4
        shape[dim] //= self.blocks
        self.size = shape[dim]
        self.rows, self.width = shape
        self.outputs = (jax.ShapeDtypeStruct(tuple(shape), F32),)
        self.axes = ("ctx", "dp") if with_dp else ("ctx",)
        chips = self.blocks // 2
        self.chips = chips
        block = (self.rows, self.width)
        self.scratch = (
            pltpu.VMEM((chips,) + block, BF),
            pltpu.VMEM((chips,) + block, BF),
            pltpu.VMEM((2,) + block, BF),
            pltpu.VMEM((self.rows, self.width), BF),
            pltpu.VMEM(block, F32),
        )
        self.sems = 2 * chips + chips + 1 + 2 * 6
        self.unit = self.rows * self.width * 2 * 2 / 88e3

    def emit(self, place, ins, outs, scr, sem):
        src, out = ins[0], outs[0]
        mine, came, chip_in, diag_in, total = scr
        dp, ctx = place.dp, place.ctx
        core = ctx & 1
        chips = self.chips
        half = self.rows // 2
        tile = min(32, half)
        xdev, ydev, cdev = {"ctx": ctx ^ 2}, {"dp": dp ^ 1}, {"ctx": ctx ^ 1}

        def place_of(q):
            x = (ctx >> 1) ^ (q & 1)
            d = dp ^ (q >> 1)
            return d, x

        def spot(q, c):
            d, x = place_of(q)
            block = d * 4 + x * 2 + c if self.with_dp else x * 2 + c
            where = pl.ds(pl.multiple_of(block * self.size, self.size), self.size)
            return src.at[:, where] if self.dim == 1 else src.at[where]

        order = (3, 1, 2, 0) if self.with_dp else (1, 0)
        sends = []
        loads = {}
        for q in order:
            copy = remote(spot(q, core ^ 1), came.at[q], sem, 2 * q, 2 * q + 1, cdev)
            copy.start()
            sends.append(copy)
            load = pltpu.make_async_copy(spot(q, core), mine.at[q], sem.at(2 * chips + q))
            load.start()
            loads[q] = (load, copy)
        base = 3 * chips + 1

        def hop(index, origin, target, device):
            copy = remote(origin, target, sem, base + 2 * index, base + 2 * index + 1, device)
            copy.start()
            sends.append(copy)
            return copy

        def got(index, target):
            remote(target, target, sem, base + 2 * index, base + 2 * index + 1, cdev).wait_recv()

        def add(into, other, first, count):
            @pl.loop(0, count // tile)
            def _(i):
                part = pl.ds(pl.multiple_of(first + i * tile, tile), tile)
                into[part] = (into[part].astype(F32) + other[part].astype(F32)).astype(BF)

        top, low = pl.ds(0, half), pl.ds(half, half)
        yield self.rank + 4.0
        for q in order:
            load, copy = loads[q]
            load.wait()
            copy.wait_recv()
            add(mine.at[q], came.at[q], 0, self.rows)
            if q == 3:
                hop(0, mine.at[3, top], diag_in.at[top], xdev)
                hop(1, mine.at[3, low], diag_in.at[low], ydev)
            if q == 1 and self.with_dp:
                hop(2, mine.at[1, top], chip_in.at[0, top], xdev)
            if q == 1 and not self.with_dp:
                hop(2, mine.at[1], chip_in.at[0], xdev)
            if q == 2:
                hop(3, mine.at[2, low], chip_in.at[1, low], ydev)
        if self.with_dp:
            yield self.rank + 4.0 + self.unit * 0.7
            got(0, diag_in.at[top])
            add(mine.at[2], diag_in, 0, half)
            hop(4, mine.at[2, top], chip_in.at[1, top], ydev)
            got(1, diag_in.at[low])
            add(mine.at[1], diag_in, half, half)
            hop(5, mine.at[1, low], chip_in.at[0, low], xdev)
        yield self.rank + 4.0 + self.unit * 1.6
        if self.with_dp:
            got(2, chip_in.at[0, top])
            got(5, chip_in.at[0, low])
            got(3, chip_in.at[1, low])
            got(4, chip_in.at[1, top])
        else:
            got(2, chip_in.at[0])

        @pl.loop(0, self.rows // tile)
        def _(i):
            part = pl.ds(pl.multiple_of(i * tile, tile), tile)
            value = mine[0, part].astype(F32) + chip_in[0, part].astype(F32)
            if self.with_dp:
                value = value + chip_in[1, part].astype(F32)
            total[part] = value

        last = pltpu.make_async_copy(total, out, sem.at(3 * chips))
        last.start()
        for copy in sends:
            copy.wait_send()
        last.wait()


def run_tasks(name, ident, tp_size, tasks):
    sems = Sems()
    firsts = [sems.take(task.sems) for task in tasks]
    inputs = [a for task in tasks for a in task.inputs]
    outputs = [o for task in tasks for o in task.outputs]
    scratch = [s for task in tasks for s in task.scratch]
    axes = set(a for task in tasks for a in task.axes)

    def kernel(*refs):
        place = Place(tp_size)
        ins, rest = list(refs[: len(inputs)]), list(refs[len(inputs) :])
        outs, rest = rest[: len(outputs)], rest[len(outputs) :]
        scr, sem_ref = rest[: len(scratch)], rest[len(scratch)]
        barrier = pltpu.get_barrier_semaphore()

        def greet(device):
            pl.semaphore_signal(barrier, inc=1, device_id=device, device_id_type=MESH)

        fixed = 0
        if "ctx" in axes:
            greet({"ctx": place.ctx ^ 1})
            greet({"ctx": place.ctx ^ 2})
            fixed += 2
        if "dp" in axes:
            greet({"dp": place.dp ^ 1})
            fixed += 1
        if "tp" in axes:
            up, down = place.tp < tp_size - 1, place.tp > 0
            when(up, lambda: greet({"tp": place.tp + 1}))
            when(down, lambda: greet({"tp": place.tp - 1}))
        peers = jnp.int32(fixed)
        if "tp" in axes:
            peers = peers + up.astype(jnp.int32) + down.astype(jnp.int32)
        pl.semaphore_wait(barrier, peers)

        class View:
            def __init__(self, first):
                self.first = first

            def at(self, index):
                return sem_ref.at[self.first + index]

        running = []
        for task, first in zip(tasks, firsts):
            a, ins = ins[: len(task.inputs)], ins[len(task.inputs) :]
            b, outs = outs[: len(task.outputs)], outs[len(task.outputs) :]
            c, scr = scr[: len(task.scratch)], scr[len(task.scratch) :]
            running.append([-1.0, task.emit(place, a, b, c, View(first))])
        while running:
            entry = min(running, key=lambda item: item[0])
            try:
                entry[0] = next(entry[1])
            except StopIteration:
                running.remove(entry)

    result = pl.pallas_call(
        kernel,
        out_shape=tuple(outputs),
        in_specs=[HBM] * len(inputs),
        out_specs=tuple([HBM] * len(outputs)),
        scratch_shapes=list(scratch) + [pltpu.SemaphoreType.DMA((sems.count,))],
        compiler_params=pltpu.CompilerParams(
            collective_id=ident, has_side_effects=True, vmem_limit_bytes=56 * 1024 * 1024
        ),
        name=name,
    )(*inputs)
    return result


def general_row_total(value):
    return lax.psum(value, "tp")


def general_widen(value):
    return lax.all_gather(value, "tp", axis=1, tiled=True)


def general_narrow(value):
    return lax.psum_scatter(
        value.astype(jnp.bfloat16), "tp", scatter_dimension=1, tiled=True
    ).astype(jnp.float32)


def general_contract_last(left, right):
    return lax.dot_general(
        left, right, (((1,), (1,)), ((), ())), preferred_element_type=jnp.float32
    )


def general_contract_first(left, right):
    return lax.dot_general(
        left, right, (((0,), (0,)), ((), ())), preferred_element_type=jnp.float32
    )


def general_rotary(positions, depth):
    half = depth // 2
    freqs = THETA ** (-(jnp.arange(half, dtype=jnp.float32) * 2.0) / depth)
    angles = positions.astype(jnp.float32)[..., None] * freqs
    return (jnp.cos(angles)[..., None, :], jnp.sin(angles)[..., None, :])


def general_turn(value, cosine, sine):
    half = value.shape[-1] // 2
    first = value[..., :half]
    second = value[..., half:]
    return jnp.concatenate(
        [first * cosine - second * sine, second * cosine + first * sine], axis=-1
    )


def general_turn_back(grad, cosine, sine):
    half = grad.shape[-1] // 2
    first = grad[..., :half]
    second = grad[..., half:]
    return jnp.concatenate(
        [first * cosine + second * sine, second * cosine - first * sine], axis=-1
    )


def general_norm_grad(scaled, value, factor, inner):
    return factor[:, None] * scaled - value * (factor**3 * inner / D)[:, None]


def general(
    hidden,
    cotangent,
    segments,
    positions,
    w_query,
    w_key,
    w_value,
    w_out,
    w_gate,
    w_up,
    w_down,
    q_gain,
    k_gain,
    attn_gain,
    mlp_gain,
):
    local_seqs, slice_len, local_width = hidden.shape
    per_batch = local_seqs // 2
    rows = per_batch * slice_len
    heads_here = q_gain.shape[0] // HEAD_DIM
    scale = 1.0 / math.sqrt(HEAD_DIM)
    query_index = lax.axis_index("ctx") * slice_len + jnp.arange(slice_len, dtype=jnp.int32)
    outputs = []
    input_grads = []
    weight_grads = None
    q_gain_grad = jnp.zeros(q_gain.shape, jnp.float32)
    k_gain_grad = jnp.zeros(k_gain.shape, jnp.float32)
    attn_gain_grad = jnp.zeros(attn_gain.shape, jnp.float32)
    mlp_gain_grad = jnp.zeros(mlp_gain.shape, jnp.float32)
    for batch in range(2):
        lower = batch * per_batch
        tokens_in = hidden[lower : lower + per_batch].reshape(rows, local_width)
        seg_here = segments[lower : lower + per_batch]
        pos_here = positions[lower : lower + per_batch].reshape(rows)
        gathered = (
            lax.all_gather(w_query, ("dp", "ctx"), axis=0, tiled=True),
            lax.all_gather(w_key, ("dp", "ctx"), axis=0, tiled=True),
            lax.all_gather(w_value, ("dp", "ctx"), axis=0, tiled=True),
            lax.all_gather(w_out, ("dp", "ctx"), axis=1, tiled=True),
            lax.all_gather(w_gate, ("dp", "ctx"), axis=0, tiled=True),
            lax.all_gather(w_up, ("dp", "ctx"), axis=0, tiled=True),
            lax.all_gather(w_down, ("dp", "ctx"), axis=1, tiled=True),
        )
        query_full, key_full, value_full, out_full, gate_full, up_full, down_full = gathered
        if weight_grads is None:
            weight_grads = tuple((jnp.zeros(tensor.shape, jnp.float32) for tensor in gathered))
        wide_in = general_widen(tokens_in)
        query_raw = jnp.dot(wide_in, query_full, preferred_element_type=jnp.float32)
        key_raw = jnp.dot(wide_in, key_full, preferred_element_type=jnp.float32)
        value_raw = jnp.dot(wide_in, value_full, preferred_element_type=jnp.float32)
        query_sq, key_sq = general_row_total(
            (jnp.sum(query_raw * query_raw, axis=1), jnp.sum(key_raw * key_raw, axis=1))
        )
        query_scale = lax.rsqrt(query_sq / D + EPS)
        key_scale = lax.rsqrt(key_sq / D + EPS)
        cosine, sine = general_rotary(pos_here, HEAD_DIM)
        query_rot = general_turn(
            (query_raw * query_scale[:, None] * q_gain).reshape(rows, heads_here, HEAD_DIM),
            cosine,
            sine,
        )
        key_rot = general_turn(
            (key_raw * key_scale[:, None] * k_gain).reshape(rows, heads_here, HEAD_DIM),
            cosine,
            sine,
        )
        query_b = query_rot.astype(jnp.bfloat16).reshape(per_batch, slice_len, heads_here, HEAD_DIM)
        key_b = key_rot.astype(jnp.bfloat16).reshape(per_batch, slice_len, heads_here * HEAD_DIM)
        value_b = value_raw.astype(jnp.bfloat16).reshape(
            per_batch, slice_len, heads_here * HEAD_DIM
        )

        def allowed_pairs(seg_piece, count):
            key_index = jnp.arange(count, dtype=jnp.int32)
            causal = query_index[:, None] >= key_index[None, :]
            same = seg_here[:, None, :, None] == seg_piece[:, None, None, :]
            return jnp.logical_and(same, causal[None, None])

        start_peak = jnp.full((per_batch, heads_here, slice_len), NEG, jnp.float32)
        peak = start_peak
        key_piece = lax.all_gather(key_b, "ctx", axis=1, tiled=True)
        value_piece = lax.all_gather(value_b, "ctx", axis=1, tiled=True)
        attend_seg_piece = lax.all_gather(seg_here, "ctx", axis=1, tiled=True)
        attend_count = key_piece.shape[1]
        key_four = key_piece.reshape(per_batch, attend_count, heads_here, HEAD_DIM)
        value_four = value_piece.reshape(per_batch, attend_count, heads_here, HEAD_DIM)
        allowed = allowed_pairs(attend_seg_piece, attend_count)
        logits = scale * jnp.einsum(
            "sqhd,skhd->shqk", query_b, key_four, preferred_element_type=jnp.float32
        )
        logits = jnp.where(allowed, logits, NEG)
        fresh = jnp.maximum(peak, jnp.max(logits, axis=-1))
        weights = jnp.where(allowed, jnp.exp(logits - fresh[..., None]), 0.0)
        total = jnp.sum(weights, axis=-1)
        accum = jnp.einsum(
            "shqk,skhd->shqd",
            weights.astype(jnp.bfloat16),
            value_four,
            preferred_element_type=jnp.float32,
        )
        peak, total, accum = (fresh, total, accum)
        logsum = peak + jnp.log(total)
        out_heads = (
            (accum / total[..., None]).transpose(0, 2, 1, 3).reshape(rows, heads_here * HEAD_DIM)
        )
        out_b = out_heads.astype(jnp.bfloat16)
        attn_raw = general_narrow(jnp.dot(out_b, out_full, preferred_element_type=jnp.float32))
        attn_scale = lax.rsqrt(general_row_total(jnp.sum(attn_raw * attn_raw, axis=1)) / D + EPS)
        resid = tokens_in.astype(jnp.float32) + attn_raw * attn_scale[:, None] * attn_gain
        wide_mid = general_widen(resid.astype(jnp.bfloat16))
        gate = jnp.dot(wide_mid, gate_full, preferred_element_type=jnp.float32)
        up_val = jnp.dot(wide_mid, up_full, preferred_element_type=jnp.float32)
        sigma = jax.nn.sigmoid(gate)
        swish = gate * sigma
        act_b = (swish * up_val).astype(jnp.bfloat16)
        mlp_raw = general_narrow(jnp.dot(act_b, down_full, preferred_element_type=jnp.float32))
        mlp_scale = lax.rsqrt(general_row_total(jnp.sum(mlp_raw * mlp_raw, axis=1)) / D + EPS)
        result = resid + mlp_raw * mlp_scale[:, None] * mlp_gain
        outputs.append(result.astype(jnp.bfloat16).reshape(per_batch, slice_len, local_width))
        again = (
            lax.all_gather(w_query, ("dp", "ctx"), axis=0, tiled=True),
            lax.all_gather(w_key, ("dp", "ctx"), axis=0, tiled=True),
            lax.all_gather(w_value, ("dp", "ctx"), axis=0, tiled=True),
            lax.all_gather(w_out, ("dp", "ctx"), axis=1, tiled=True),
            lax.all_gather(w_gate, ("dp", "ctx"), axis=0, tiled=True),
            lax.all_gather(w_up, ("dp", "ctx"), axis=0, tiled=True),
            lax.all_gather(w_down, ("dp", "ctx"), axis=1, tiled=True),
        )
        query_back, key_back, value_back, out_back, gate_back, up_back, down_back = again
        grad_out = (
            cotangent[lower : lower + per_batch].reshape(rows, local_width).astype(jnp.float32)
        )
        mlp_gain_grad = mlp_gain_grad + jnp.sum(grad_out * mlp_raw * mlp_scale[:, None], axis=0)
        scaled = grad_out * mlp_gain
        grad_mlp = general_norm_grad(
            scaled, mlp_raw, mlp_scale, general_row_total(jnp.sum(scaled * mlp_raw, axis=1))
        )
        wide_grad_mlp = general_widen(grad_mlp.astype(jnp.bfloat16))
        grad_act = general_contract_last(wide_grad_mlp, down_back)
        grad_gate = (grad_act * up_val * sigma * (1.0 + gate * (1.0 - sigma))).astype(jnp.bfloat16)
        grad_up = (grad_act * swish).astype(jnp.bfloat16)
        grad_resid = grad_out + general_narrow(
            general_contract_last(grad_gate, gate_back) + general_contract_last(grad_up, up_back)
        )
        attn_gain_grad = attn_gain_grad + jnp.sum(
            grad_resid * attn_raw * attn_scale[:, None], axis=0
        )
        scaled = grad_resid * attn_gain
        grad_attn = general_norm_grad(
            scaled, attn_raw, attn_scale, general_row_total(jnp.sum(scaled * attn_raw, axis=1))
        )
        wide_grad_attn = general_widen(grad_attn.astype(jnp.bfloat16))
        grad_heads = general_contract_last(wide_grad_attn, out_back).astype(jnp.bfloat16)
        dout_four = grad_heads.reshape(per_batch, slice_len, heads_here, HEAD_DIM)
        delta = jnp.sum(
            (grad_heads.astype(jnp.float32) * out_heads).reshape(
                per_batch, slice_len, heads_here, HEAD_DIM
            ),
            axis=-1,
        ).transpose(0, 2, 1)

        def attend_back(piece):
            key_piece, value_piece, seg_piece = piece
            count = key_piece.shape[1]
            key_four = key_piece.reshape(per_batch, count, heads_here, HEAD_DIM)
            value_four = value_piece.reshape(per_batch, count, heads_here, HEAD_DIM)
            allowed = allowed_pairs(seg_piece, count)
            logits = scale * jnp.einsum(
                "sqhd,skhd->shqk", query_b, key_four, preferred_element_type=jnp.float32
            )
            probs = jnp.where(allowed, jnp.exp(logits - logsum[..., None]), 0.0)
            grad_probs = jnp.einsum(
                "sqhd,skhd->shqk", dout_four, value_four, preferred_element_type=jnp.float32
            )
            grad_logits = (probs * (grad_probs - delta[..., None])).astype(jnp.bfloat16)
            grad_query = scale * jnp.einsum(
                "shqk,skhd->sqhd", grad_logits, key_four, preferred_element_type=jnp.float32
            )
            key_grad = scale * jnp.einsum(
                "shqk,sqhd->skhd", grad_logits, query_b, preferred_element_type=jnp.float32
            )
            value_grad = jnp.einsum(
                "shqk,sqhd->skhd",
                probs.astype(jnp.bfloat16),
                dout_four,
                preferred_element_type=jnp.float32,
            )
            grad_keys = key_grad.reshape(per_batch, count, heads_here * HEAD_DIM)
            grad_values = value_grad.reshape(per_batch, count, heads_here * HEAD_DIM)
            return (grad_query, grad_keys, grad_values)

        grad_query, grad_keys, grad_values = attend_back(
            (
                lax.all_gather(key_b, "ctx", axis=1, tiled=True),
                lax.all_gather(value_b, "ctx", axis=1, tiled=True),
                lax.all_gather(seg_here, "ctx", axis=1, tiled=True),
            )
        )
        key_grad_mine, value_grad_mine = (
            lax.psum_scatter(
                grad_keys.astype(jnp.bfloat16), "ctx", scatter_dimension=1, tiled=True
            ).astype(jnp.float32),
            lax.psum_scatter(
                grad_values.astype(jnp.bfloat16), "ctx", scatter_dimension=1, tiled=True
            ).astype(jnp.float32),
        )
        grad_qnorm = general_turn_back(
            grad_query.reshape(rows, heads_here, HEAD_DIM), cosine, sine
        ).reshape(rows, heads_here * HEAD_DIM)
        grad_knorm = general_turn_back(
            key_grad_mine.reshape(rows, heads_here, HEAD_DIM), cosine, sine
        ).reshape(rows, heads_here * HEAD_DIM)
        q_gain_grad = q_gain_grad + jnp.sum(grad_qnorm * query_raw * query_scale[:, None], axis=0)
        k_gain_grad = k_gain_grad + jnp.sum(grad_knorm * key_raw * key_scale[:, None], axis=0)
        q_scaled = grad_qnorm * q_gain
        k_scaled = grad_knorm * k_gain
        q_inner, k_inner = general_row_total(
            (jnp.sum(q_scaled * query_raw, axis=1), jnp.sum(k_scaled * key_raw, axis=1))
        )
        grad_query_raw = general_norm_grad(q_scaled, query_raw, query_scale, q_inner).astype(jnp.bfloat16)
        grad_key_raw = general_norm_grad(k_scaled, key_raw, key_scale, k_inner).astype(jnp.bfloat16)
        grad_value_raw = value_grad_mine.reshape(rows, heads_here * HEAD_DIM).astype(jnp.bfloat16)
        back_terms = (
            general_contract_last(grad_query_raw, query_back)
            + general_contract_last(grad_key_raw, key_back)
            + general_contract_last(grad_value_raw, value_back)
        )
        grad_in = grad_resid + general_narrow(back_terms)
        input_grads.append(grad_in.astype(jnp.bfloat16).reshape(per_batch, slice_len, local_width))
        fresh_grads = (
            general_contract_first(wide_in, grad_query_raw),
            general_contract_first(wide_in, grad_key_raw),
            general_contract_first(wide_in, grad_value_raw),
            general_contract_first(out_b, wide_grad_attn),
            general_contract_first(wide_mid, grad_gate),
            general_contract_first(wide_mid, grad_up),
            general_contract_first(act_b, wide_grad_mlp),
        )
        weight_grads = tuple((left + right for left, right in zip(weight_grads, fresh_grads)))
    finals = (
        lax.psum_scatter(
            weight_grads[0].astype(jnp.bfloat16), ("dp", "ctx"), scatter_dimension=0, tiled=True
        ).astype(jnp.float32),
        lax.psum_scatter(
            weight_grads[1].astype(jnp.bfloat16), ("dp", "ctx"), scatter_dimension=0, tiled=True
        ).astype(jnp.float32),
        lax.psum_scatter(
            weight_grads[2].astype(jnp.bfloat16), ("dp", "ctx"), scatter_dimension=0, tiled=True
        ).astype(jnp.float32),
        lax.psum_scatter(
            weight_grads[3].astype(jnp.bfloat16), ("dp", "ctx"), scatter_dimension=1, tiled=True
        ).astype(jnp.float32),
        lax.psum_scatter(
            weight_grads[4].astype(jnp.bfloat16), ("dp", "ctx"), scatter_dimension=0, tiled=True
        ).astype(jnp.float32),
        lax.psum_scatter(
            weight_grads[5].astype(jnp.bfloat16), ("dp", "ctx"), scatter_dimension=0, tiled=True
        ).astype(jnp.float32),
        lax.psum_scatter(
            weight_grads[6].astype(jnp.bfloat16), ("dp", "ctx"), scatter_dimension=1, tiled=True
        ).astype(jnp.float32),
    )
    gains = lax.psum((q_gain_grad, k_gain_grad, attn_gain_grad, mlp_gain_grad), ("dp", "ctx"))
    return (
        jnp.concatenate(outputs, axis=0),
        jnp.concatenate(input_grads, axis=0),
        finals[0],
        finals[1],
        finals[2],
        finals[3],
        finals[4],
        finals[5],
        finals[6],
        gains[0],
        gains[1],
        gains[2],
        gains[3],
    )


def contract_last(left, right):
    return lax.dot_general(left, right, (((1,), (1,)), ((), ())), preferred_element_type=F32)


def contract_first(left, right):
    return lax.dot_general(left, right, (((0,), (0,)), ((), ())), preferred_element_type=F32)


def mm(left, right):
    return jnp.dot(left, right, preferred_element_type=F32)


def rotary(positions, depth):
    half = depth // 2
    freqs = THETA ** (-(jnp.arange(half, dtype=F32) * 2.0) / depth)
    angles = positions.astype(F32)[..., None] * freqs
    return (jnp.cos(angles)[..., None, :], jnp.sin(angles)[..., None, :])


def turn(value, cosine, sine):
    half = value.shape[-1] // 2
    first, second = value[..., :half], value[..., half:]
    return jnp.concatenate([first * cosine - second * sine, second * cosine + first * sine], axis=-1)


def turn_back(grad, cosine, sine):
    return turn(grad, cosine, -sine)


def norm_grad(scaled, value, factor, inner):
    return factor[:, None] * scaled - value * (factor**3 * inner / D)[:, None]


def totals(*values):
    return lax.psum(values, "tp")


def planned(
    hidden, cotangent, segments, positions, w_query, w_key, w_value, w_out, w_gate, w_up, w_down,
    q_gain, k_gain, attn_gain, mlp_gain,
):
    n = lax.axis_size("tp")
    seqs, slice_len, width = hidden.shape
    per = seqs // 2
    rows = per * slice_len
    heads = width // HEAD_DIM
    ctx_size = 4
    scale = 1.0 / math.sqrt(HEAD_DIM)
    query_index = lax.axis_index("ctx") * slice_len + jnp.arange(slice_len, dtype=jnp.int32)
    x_in = [hidden[b * per : (b + 1) * per].reshape(rows, width) for b in (0, 1)]
    cot = [cotangent[b * per : (b + 1) * per].reshape(rows, width).astype(F32) for b in (0, 1)]
    segs = [segments[b * per : (b + 1) * per] for b in (0, 1)]
    seg_all = lax.all_gather(segments, "ctx", axis=0, tiled=False)
    angles = [rotary(positions[b * per : (b + 1) * per].reshape(rows), HEAD_DIM) for b in (0, 1)]
    key_index = jnp.arange(ctx_size * slice_len, dtype=jnp.int32).reshape(ctx_size, slice_len)
    st = [dict(), dict()]

    def allowed(b):
        seg_keys = seg_all[:, b * per : (b + 1) * per]
        causal = query_index[:, None, None] >= key_index[None]
        same = segs[b][:, None, :, None, None] == seg_keys.transpose(1, 0, 2)[:, None, None]
        return jnp.logical_and(same, causal[None, None])

    def qkv(b, wide):
        s = st[b]
        s["wide"] = wide
        s["q_raw"], s["k_raw"] = mm(wide, wq), mm(wide, wk)
        value = mm(wide, wv)
        q_sq, k_sq = totals(jnp.sum(s["q_raw"] ** 2, axis=1), jnp.sum(s["k_raw"] ** 2, axis=1))
        s["q_s"], s["k_s"] = lax.rsqrt(q_sq / D + EPS), lax.rsqrt(k_sq / D + EPS)
        cosine, sine = angles[b]
        turned = lambda raw, f, gain: turn((raw * f[:, None] * gain).reshape(rows, heads, HEAD_DIM), cosine, sine)
        s["q"] = turned(s["q_raw"], s["q_s"], q_gain).astype(BF).reshape(per, slice_len, heads, HEAD_DIM)
        key = turned(s["k_raw"], s["k_s"], k_gain).astype(BF).reshape(rows, width)
        return jnp.concatenate([key, value.astype(BF)], axis=1)

    def attend(b, kv):
        s = st[b]
        kv = kv.reshape(ctx_size, per, slice_len, 2, heads, HEAD_DIM)
        s["k"], s["v"] = kv[:, :, :, 0], kv[:, :, :, 1]
        ok = allowed(b)
        logits = scale * jnp.einsum("sqhd,cskhd->shqck", s["q"], s["k"], preferred_element_type=F32)
        logits = jnp.where(ok, logits, NEG)
        peak = jnp.max(logits, axis=(-1, -2))
        weights = jnp.where(ok, jnp.exp(logits - peak[..., None, None]), 0.0)
        total = jnp.sum(weights, axis=(-1, -2))
        acc = jnp.einsum("shqck,cskhd->shqd", weights.astype(BF), s["v"], preferred_element_type=F32)
        s["logsum"] = peak + jnp.log(total)
        s["heads"] = (acc / total[..., None]).transpose(0, 2, 1, 3).reshape(rows, width)
        s["heads_b"] = s["heads"].astype(BF)
        return mm(s["heads_b"], wo).astype(BF)

    def after_attn(b, raw):
        s = st[b]
        s["attn"] = raw
        (sq,) = totals(jnp.sum(raw * raw, axis=1))
        s["attn_s"] = lax.rsqrt(sq / D + EPS)
        s["resid"] = x_in[b].astype(F32) + raw * s["attn_s"][:, None] * attn_gain
        return s["resid"].astype(BF)

    def mlp(b, wide):
        s = st[b]
        s["mid"] = wide
        s["gate"], s["up"] = mm(wide, wg), mm(wide, wu)
        s["act"] = (s["gate"] * jax.nn.sigmoid(s["gate"]) * s["up"]).astype(BF)
        return mm(s["act"], wd).astype(BF)

    def after_mlp(b, raw):
        s = st[b]
        scaled = cot[b] * mlp_gain
        sq, inner = totals(jnp.sum(raw * raw, axis=1), jnp.sum(scaled * raw, axis=1))
        factor = lax.rsqrt(sq / D + EPS)
        s["out"] = (s["resid"] + raw * factor[:, None] * mlp_gain).astype(BF)
        s["g_mlp_gain"] = jnp.sum(cot[b] * raw * factor[:, None], axis=0)
        return norm_grad(scaled, raw, factor, inner).astype(BF)

    def mlp_back(b, wide):
        s = st[b]
        s["g_mlp"] = wide
        g_act = contract_last(wide, wd)
        sigma = jax.nn.sigmoid(s["gate"])
        s["g_gate"] = (g_act * s["up"] * sigma * (1.0 + s["gate"] * (1.0 - sigma))).astype(BF)
        s["g_up"] = (g_act * s["gate"] * sigma).astype(BF)
        return (contract_last(s["g_gate"], wg) + contract_last(s["g_up"], wu)).astype(BF)

    def after_resid(b, raw):
        s = st[b]
        s["g_resid"] = cot[b] + raw
        scaled = s["g_resid"] * attn_gain
        (inner,) = totals(jnp.sum(scaled * s["attn"], axis=1))
        s["g_attn_gain"] = jnp.sum(s["g_resid"] * s["attn"] * s["attn_s"][:, None], axis=0)
        return norm_grad(scaled, s["attn"], s["attn_s"], inner).astype(BF)

    def attn_back(b, wide):
        s = st[b]
        s["g_attn"] = wide
        g_heads = contract_last(wide, wo).astype(BF)
        g_four = g_heads.reshape(per, slice_len, heads, HEAD_DIM)
        delta = jnp.sum((g_heads.astype(F32) * s["heads"]).reshape(per, slice_len, heads, HEAD_DIM), axis=-1)
        delta = delta.transpose(0, 2, 1)
        logits = scale * jnp.einsum("sqhd,cskhd->shqck", s["q"], s["k"], preferred_element_type=F32)
        probs = jnp.where(allowed(b), jnp.exp(logits - s["logsum"][..., None, None]), 0.0)
        g_probs = jnp.einsum("sqhd,cskhd->shqck", g_four, s["v"], preferred_element_type=F32)
        g_logits = (probs * (g_probs - delta[..., None, None])).astype(BF)
        s["g_q"] = scale * jnp.einsum("shqck,cskhd->sqhd", g_logits, s["k"], preferred_element_type=F32)
        g_k = scale * jnp.einsum("shqck,sqhd->cskhd", g_logits, s["q"], preferred_element_type=F32)
        g_v = jnp.einsum("shqck,sqhd->cskhd", probs.astype(BF), g_four, preferred_element_type=F32)
        shape = (ctx_size * rows, width)
        return jnp.concatenate([g_k.astype(BF).reshape(shape), g_v.astype(BF).reshape(shape)], axis=1)

    def qkv_back(b, g_kv):
        s = st[b]
        cosine, sine = angles[b]
        back = lambda g: turn_back(g.reshape(rows, heads, HEAD_DIM), cosine, sine).reshape(rows, width)
        g_qn, g_kn = back(s["g_q"]), back(g_kv[:, :width])
        s["g_q_gain"] = jnp.sum(g_qn * s["q_raw"] * s["q_s"][:, None], axis=0)
        s["g_k_gain"] = jnp.sum(g_kn * s["k_raw"] * s["k_s"][:, None], axis=0)
        q_in, k_in = totals(jnp.sum(g_qn * q_gain * s["q_raw"], axis=1), jnp.sum(g_kn * k_gain * s["k_raw"], axis=1))
        s["g_qr"] = norm_grad(g_qn * q_gain, s["q_raw"], s["q_s"], q_in).astype(BF)
        s["g_kr"] = norm_grad(g_kn * k_gain, s["k_raw"], s["k_s"], k_in).astype(BF)
        s["g_vr"] = g_kv[:, width:].astype(BF)
        return (contract_last(s["g_qr"], wq) + contract_last(s["g_kr"], wk) + contract_last(s["g_vr"], wv)).astype(BF)

    def weight_grad(left, right):
        return (contract_first(st[0][left], st[0][right]) + contract_first(st[1][left], st[1][right])).astype(BF)

    def final(b, raw):
        return (st[b]["g_resid"] + raw).astype(BF)

    gather = lambda a: LineGather(a, n)
    scatter = lambda a: LineScatter(a, n)
    wide0, wq, wk, wv = run_tasks(
        "slot0", 0, n, [gather(x_in[0]), PlaneGather(w_query, 0, True), PlaneGather(w_key, 0, True, 4.0), PlaneGather(w_value, 0, True, 8.0)]
    )
    kv0 = qkv(0, wide0)
    wide1, kvs0, wo = run_tasks("slot1", 1, n, [gather(x_in[1]), PlaneGather(kv0, 0, False), PlaneGather(w_out, 1, True, 9.0)])
    kv1 = qkv(1, wide1)
    part0 = attend(0, kvs0)
    raw0, kvs1, wg = run_tasks("slot2", 2, n, [scatter(part0), PlaneGather(kv1, 0, False), PlaneGather(w_gate, 0, True, 9.0)])
    part1 = attend(1, kvs1)
    mid0, raw1, wu, wd = run_tasks(
        "slot3", 3, n, [gather(after_attn(0, raw0)), scatter(part1), PlaneGather(w_up, 0, True), PlaneGather(w_down, 1, True, 18.0)]
    )
    part0 = mlp(0, mid0)
    raw0, mid1 = run_tasks("slot4", 4, n, [scatter(part0), gather(after_attn(1, raw1))])
    part1 = mlp(1, mid1)
    wide0, raw1 = run_tasks("slot5", 5, n, [gather(after_mlp(0, raw0)), scatter(part1)])
    part0 = mlp_back(0, wide0)
    raw0, wide1 = run_tasks("slot6", 6, n, [scatter(part0), gather(after_mlp(1, raw1))])
    part1 = mlp_back(1, wide1)
    d_down = weight_grad("act", "g_mlp")
    wide0, raw1, g_down = run_tasks(
        "slot7", 7, n, [gather(after_resid(0, raw0)), scatter(part1), PlaneScatter(d_down, 1, True)]
    )
    kv0 = attn_back(0, wide0)
    d_gate = weight_grad("mid", "g_gate")
    wide1, kvs0, g_gate = run_tasks(
        "slot8", 8, n, [gather(after_resid(1, raw1)), PlaneScatter(kv0, 0, False), PlaneScatter(d_gate, 0, True)]
    )
    part0 = qkv_back(0, kvs0)
    kv1 = attn_back(1, wide1)
    d_up = weight_grad("mid", "g_up")
    raw0, kvs1, g_up = run_tasks("slot9", 9, n, [scatter(part0), PlaneScatter(kv1, 0, False), PlaneScatter(d_up, 0, True)])
    part1 = qkv_back(1, kvs1)
    d_out = weight_grad("heads_b", "g_attn")
    d_q, d_k, d_v = weight_grad("wide", "g_qr"), weight_grad("wide", "g_kr"), weight_grad("wide", "g_vr")
    raw1, g_out, g_q, g_k, g_v = run_tasks(
        "slot10", 10, n,
        [scatter(part1), PlaneScatter(d_out, 1, True), PlaneScatter(d_q, 0, True), PlaneScatter(d_k, 0, True), PlaneScatter(d_v, 0, True)],
    )
    gains = lax.psum(tuple(st[0][g] + st[1][g] for g in ("g_q_gain", "g_k_gain", "g_attn_gain", "g_mlp_gain")), ("dp", "ctx"))
    shape = (per, slice_len, width)
    return (
        jnp.concatenate([st[0]["out"].reshape(shape), st[1]["out"].reshape(shape)], axis=0),
        jnp.concatenate([final(0, raw0).reshape(shape), final(1, raw1).reshape(shape)], axis=0),
        g_q, g_k, g_v, g_out, g_gate, g_up, g_down, *gains,
    )


def solution(mesh):
    rows, cols = P(("dp", "ctx"), "tp"), P("tp", ("dp", "ctx"))
    act, gain = P("dp", "ctx", "tp"), P("tp")
    size = dict(mesh.shape)
    body = planned if (size["dp"], size["ctx"]) == (2, 4) else general
    return jax.shard_map(
        body,
        mesh=mesh,
        in_specs=(act, act, P("dp", "ctx"), P("dp", "ctx"), rows, rows, rows, cols, rows, rows, cols, gain, gain, gain, gain),
        out_specs=(act, act, rows, rows, rows, cols, rows, rows, cols, gain, gain, gain, gain),
        check_vma=False,
    )
```

```python
import functools
import math

import jax
import jax.numpy as jnp
from jax import lax
from jax.experimental import pallas as pl
from jax.experimental.pallas import tpu as pltpu
from jax.sharding import PartitionSpec as P

D = 2048
HEAD_DIM = 128
EPS = 1e-06
THETA = 500000.0
NEG = -1e30
BF = jnp.bfloat16
F32 = jnp.float32
MESH = pl.DeviceIdType.MESH
HBM = pl.BlockSpec(memory_space=pltpu.HBM)


class Place:
    def __init__(self, tp_size):
        self.n = tp_size
        self.tp = lax.axis_index("tp")
        self.dp = lax.axis_index("dp")
        self.ctx = lax.axis_index("ctx")
        self.slot = self.dp * 4 + self.ctx


class Task:
    inputs = ()
    outputs = ()
    scratch = ()
    sems = 0
    axes = ()
    after = None
    done = None

    def emit(self, place, ins, outs, scr, sem):
        raise NotImplementedError


def remote(src, dst, sem, send, recv, device):
    return pltpu.make_async_remote_copy(
        src_ref=src, dst_ref=dst, send_sem=sem.at(send), recv_sem=sem.at(recv), device_id=device, device_id_type=MESH
    )


class PlaneGather(Task):
    def __init__(self, array, dim, with_dp, rank=0.0, lean=False, after=None, done=None):
        self.dim, self.with_dp, self.rank, self.lean = dim, with_dp, rank, lean
        self.after, self.done = after, done
        self.inputs = (array,)
        shape = list(array.shape)
        self.size = shape[dim]
        self.rows = shape[0]
        self.blocks = 8 if with_dp else 4
        shape[dim] *= self.blocks
        self.outputs = (jax.ShapeDtypeStruct(tuple(shape), array.dtype),)
        self.axes = ("ctx", "dp") if with_dp else ("ctx",)
        self.sems = 1 + 2 * (3 + 2 + 2 + 2 + 2)
        self.unit = math.prod(array.shape) * 2 * 2 / 88e3

    def emit(self, place, ins, outs, scr, sem):
        src, out = ins[0], outs[0]
        dp, ctx = place.dp, place.ctx
        half = self.rows // 2

        def spot(d, c, part=None):
            block = d * 4 + c if self.with_dp else c
            where = pl.ds(pl.multiple_of(block * self.size, self.size), self.size)
            if self.dim == 1:
                if part is None:
                    return out.at[:, where]
                return out.at[pl.ds(part * half, half), where]
            if part is None:
                return out.at[where]
            return out.at[pl.ds(pl.multiple_of(block * self.size + part * half, half), half)]

        xdev, ydev, cdev = {"ctx": ctx ^ 2}, {"dp": dp ^ 1}, {"ctx": ctx ^ 1}
        mine = spot(dp, ctx)
        own = pltpu.make_async_copy(src, mine, sem.at(0))
        own.start()
        sends = []

        def send(index, origin, target, device):
            copy = remote(origin, target, sem, 1 + 2 * index, 2 + 2 * index, device)
            copy.start()
            sends.append(copy)

        def got(index, target):
            remote(target, target, sem, 1 + 2 * index, 2 + 2 * index, cdev).wait_recv()

        send(0, src, mine, xdev)
        if self.with_dp:
            send(1, src, mine, ydev)
        send(2, src, mine, cdev)
        yield self.rank + self.unit * 1.0
        from_x = spot(dp, ctx ^ 2)
        got(0, from_x)
        if self.with_dp and self.lean:
            send(3, from_x, from_x, ydev)
        elif self.with_dp:
            send(3, spot(dp, ctx ^ 2, 0), spot(dp, ctx ^ 2, 0), ydev)
        send(5, from_x, from_x, cdev)
        if self.with_dp:
            from_y = spot(dp ^ 1, ctx)
            got(1, from_y)
            parts = (None,) if self.lean else (0, 1)
            if not self.lean:
                send(4, spot(dp ^ 1, ctx, 1), spot(dp ^ 1, ctx, 1), xdev)
            send(6, from_y, from_y, cdev)
            yield self.rank + self.unit * (2.0 if self.lean else 1.5)
            for k, part in enumerate(parts):
                diagonal = spot(dp ^ 1, ctx ^ 2, part)
                got(3 + k, diagonal)
                send(7 + k, diagonal, diagonal, cdev)
        yield self.rank + self.unit * (2.1 if self.lean else 1.6)
        got(2, spot(dp, ctx ^ 1))
        got(5, spot(dp, ctx ^ 3))
        if self.with_dp:
            got(6, spot(dp ^ 1, ctx ^ 1))
            for k, part in enumerate(parts):
                got(7 + k, spot(dp ^ 1, ctx ^ 3, part))
        for copy in sends:
            copy.wait_send()
        own.wait()


class PlaneScatter(Task):
    def __init__(self, array, dim, with_dp, rank=0.0, lean=False, after=None, done=None):
        self.dim, self.with_dp, self.rank, self.lean = dim, with_dp, rank, lean
        self.after, self.done = after, done
        self.inputs = (array,)
        shape = list(array.shape)
        self.blocks = 8 if with_dp else 4
        shape[dim] //= self.blocks
        self.size = shape[dim]
        self.rows, self.width = shape
        self.outputs = (jax.ShapeDtypeStruct(tuple(shape), F32),)
        self.axes = ("ctx", "dp") if with_dp else ("ctx",)
        chips = self.blocks // 2
        self.chips = chips
        block = (self.rows, self.width)
        self.scratch = (
            pltpu.VMEM((chips,) + block, BF),
            pltpu.VMEM((chips,) + block, BF),
            pltpu.VMEM((2,) + block, BF),
            pltpu.VMEM((self.rows, self.width), BF),
            pltpu.VMEM(block, F32),
        )
        self.sems = 2 * chips + chips + 1 + 2 * 6
        self.unit = self.rows * self.width * 2 * 2 / 88e3

    def emit(self, place, ins, outs, scr, sem):
        src, out = ins[0], outs[0]
        mine, came, chip_in, diag_in, total = scr
        dp, ctx = place.dp, place.ctx
        core = ctx & 1
        chips = self.chips
        half = self.rows // 2
        tile = min(32, half)
        xdev, ydev, cdev = {"ctx": ctx ^ 2}, {"dp": dp ^ 1}, {"ctx": ctx ^ 1}

        def place_of(q):
            x = (ctx >> 1) ^ (q & 1)
            d = dp ^ (q >> 1)
            return d, x

        def spot(q, c):
            d, x = place_of(q)
            block = d * 4 + x * 2 + c if self.with_dp else x * 2 + c
            where = pl.ds(pl.multiple_of(block * self.size, self.size), self.size)
            return src.at[:, where] if self.dim == 1 else src.at[where]

        order = (3, 1, 2, 0) if self.with_dp else (1, 0)
        sends = []
        loads = {}
        for q in order:
            copy = remote(spot(q, core ^ 1), came.at[q], sem, 2 * q, 2 * q + 1, cdev)
            copy.start()
            sends.append(copy)
            load = pltpu.make_async_copy(spot(q, core), mine.at[q], sem.at(2 * chips + q))
            load.start()
            loads[q] = (load, copy)
        base = 3 * chips + 1

        def hop(index, origin, target, device):
            copy = remote(origin, target, sem, base + 2 * index, base + 2 * index + 1, device)
            copy.start()
            sends.append(copy)
            return copy

        def got(index, target):
            remote(target, target, sem, base + 2 * index, base + 2 * index + 1, cdev).wait_recv()

        def add(into, other, first, count):
            @pl.loop(0, count // tile)
            def _(i):
                part = pl.ds(pl.multiple_of(first + i * tile, tile), tile)
                into[part] = (into[part].astype(F32) + other[part].astype(F32)).astype(BF)

        top, low = pl.ds(0, half), pl.ds(half, half)
        yield self.rank + 4.0
        for q in order:
            load, copy = loads[q]
            load.wait()
            copy.wait_recv()
            add(mine.at[q], came.at[q], 0, self.rows)
            if q == 3 and self.lean:
                hop(1, mine.at[3], diag_in, ydev)
            elif q == 3:
                hop(0, mine.at[3, top], diag_in.at[top], xdev)
                hop(1, mine.at[3, low], diag_in.at[low], ydev)
            if q == 1 and self.with_dp and not self.lean:
                hop(2, mine.at[1, top], chip_in.at[0, top], xdev)
            if q == 1 and not self.with_dp:
                hop(2, mine.at[1], chip_in.at[0], xdev)
            if q == 2 and self.lean:
                hop(3, mine.at[2], chip_in.at[1], ydev)
            elif q == 2:
                hop(3, mine.at[2, low], chip_in.at[1, low], ydev)
        if self.lean:
            yield self.rank + 4.0 + self.unit * 1.2
            got(1, diag_in)
            add(mine.at[1], diag_in, 0, self.rows)
            hop(5, mine.at[1], chip_in.at[0], xdev)
        elif self.with_dp:
            yield self.rank + 4.0 + self.unit * 0.7
            got(0, diag_in.at[top])
            add(mine.at[2], diag_in, 0, half)
            hop(4, mine.at[2, top], chip_in.at[1, top], ydev)
            got(1, diag_in.at[low])
            add(mine.at[1], diag_in, half, half)
            hop(5, mine.at[1, low], chip_in.at[0, low], xdev)
        yield self.rank + 4.0 + self.unit * (2.2 if self.lean else 1.6)
        if self.lean:
            got(5, chip_in.at[0])
            got(3, chip_in.at[1])
        elif self.with_dp:
            got(2, chip_in.at[0, top])
            got(5, chip_in.at[0, low])
            got(3, chip_in.at[1, low])
            got(4, chip_in.at[1, top])
        else:
            got(2, chip_in.at[0])

        @pl.loop(0, self.rows // tile)
        def _(i):
            part = pl.ds(pl.multiple_of(i * tile, tile), tile)
            value = mine[0, part].astype(F32) + chip_in[0, part].astype(F32)
            if self.with_dp:
                value = value + chip_in[1, part].astype(F32)
            total[part] = value

        last = pltpu.make_async_copy(total, out, sem.at(3 * chips))
        last.start()
        for copy in sends:
            copy.wait_send()
        last.wait()


class Handle:
    ref = None
    sem = None
    waited = False
    lazy = False
    value = None

    def __init__(self, shape=None, dtype=None):
        self.shape, self.dtype = shape, dtype


class Slot:
    def __init__(self, name, ident):
        self.name, self.ident = name, ident
        self.inputs, self.outputs, self.scratch = [], [], []
        self.sem_count = 0
        self.tasks = []
        self.axes = set()
        self.early = []
        self.loads, self.stores = [], []
        self.flags = {}
        self.now = 0.0

    def sems(self, number):
        first = self.sem_count
        self.sem_count += number
        return first

    def hbm_in(self, array):
        if isinstance(array, Handle):
            return array
        handle = Handle(array.shape, array.dtype)
        self.inputs.append((array, handle))
        return handle

    def hbm_out(self, shape, dtype):
        handle = Handle(shape, dtype)
        self.outputs.append((jax.ShapeDtypeStruct(shape, dtype), handle))
        return handle

    def vmem(self, shape, dtype):
        handle = Handle(shape, dtype)
        self.scratch.append((pltpu.VMEM(shape, dtype), handle))
        return handle

    def load(self, array):
        handle = self.vmem(array.shape, array.dtype)
        handle.source = self.hbm_in(array)
        handle.sem = self.sems(1)
        self.loads.append(handle)
        return handle

    def store(self, shape, dtype):
        handle = self.vmem(shape, dtype)
        handle.target = self.hbm_out(shape, dtype)
        handle.sem = self.sems(1)
        self.stores.append(handle)
        return handle

    def late(self, array):
        handle = self.vmem(array.shape, array.dtype)
        handle.source = self.hbm_in(array)
        handle.sem = self.sems(1)
        handle.lazy = True
        self.loads.append(handle)
        return handle

    def fetch(self, *handles):
        for handle in handles:
            pltpu.make_async_copy(handle.source.ref, handle.ref, self.sem(handle.sem)).start()

    def need(self, *handles):
        for handle in handles:
            if not handle.waited:
                handle.waited = True
                pltpu.make_async_copy(handle.source.ref, handle.ref, self.sem(handle.sem)).wait()

    def flush(self, *handles):
        for handle in handles:
            pltpu.make_async_copy(handle.ref, handle.target.ref, self.sem(handle.sem)).start()

    def sem(self, index):
        return self.sem_ref.at[index]

    def at(self, index):
        return self.sem_ref.at[index]

    def add(self, body):
        self.tasks.append(body)

    def mark(self, flag):
        self.flags[flag] = True

    def mark_early(self, flag):
        self.early.append(flag)

    def kernel(self, *refs):
        refs = list(refs)
        for group in (self.inputs, self.outputs, self.scratch):
            for _, handle in group:
                handle.ref = refs.pop(0)
        self.sem_ref = refs.pop(0)
        self.flags, self.now = {flag: True for flag in self.early}, 0.0
        for handle in self.loads:
            handle.waited = False
            if not handle.lazy:
                pltpu.make_async_copy(handle.source.ref, handle.ref, self.sem(handle.sem)).start()
        self.place = place = Place(4)
        barrier = pltpu.get_barrier_semaphore()
        peers = []
        if "ctx" in self.axes:
            peers += [{"ctx": place.ctx ^ 1}, {"ctx": place.ctx ^ 2}]
        if "dp" in self.axes:
            peers += [{"dp": place.dp ^ 1}]
        if "tp" in self.axes:
            peers += [{"tp": place.tp ^ k} for k in (1, 2, 3)]
        for device in peers:
            pl.semaphore_signal(barrier, inc=1, device_id=device, device_id_type=MESH)
        pl.semaphore_wait(barrier, len(peers))
        running = [[("at", 0.0), task()] for task in self.tasks]
        while running:
            ready = None
            for entry in running:
                kind, value = entry[0]
                if (kind == "at" and value <= self.now) or (kind == "flag" and value in self.flags):
                    ready = entry
                    break
            if ready is None:
                times = [entry[0][1] for entry in running if entry[0][0] == "at"]
                self.now = min(times)
                continue
            try:
                got = next(ready[1])
            except StopIteration:
                running.remove(ready)
                continue
            if got[0] == "did":
                self.now += got[1]
                got = ("at", self.now)
            ready[0] = got
        for handle in self.stores:
            pltpu.make_async_copy(handle.ref, handle.target.ref, self.sem(handle.sem)).wait()

    def run(self):
        values = pl.pallas_call(
            self.kernel,
            out_shape=tuple(o for o, _ in self.outputs),
            in_specs=[HBM] * len(self.inputs),
            out_specs=tuple([HBM] * len(self.outputs)),
            scratch_shapes=[s for s, _ in self.scratch] + [pltpu.SemaphoreType.DMA((self.sem_count,))],
            compiler_params=pltpu.CompilerParams(
                collective_id=self.ident, has_side_effects=True, vmem_limit_bytes=62 * 1024 * 1024
            ),
            name=self.name,
        )(*[a for a, _ in self.inputs])
        for (_, handle), value in zip(self.outputs, values):
            handle.value = value


def attach(slot, task):
    ins = [slot.hbm_in(a) for a in task.inputs]
    outs = [slot.hbm_out(o.shape, o.dtype) for o in task.outputs]
    scr = []
    for s in task.scratch:
        handle = Handle()
        slot.scratch.append((s, handle))
        scr.append(handle)
    first = slot.sems(task.sems)
    slot.axes |= set(task.axes)

    class View:
        def at(self, index):
            return slot.sem_ref.at[first + index]

    def body():
        if task.after is not None:
            yield ("flag", task.after)
            task.rank = slot.now
        for t in task.emit(slot.place, [h.ref for h in ins], [h.ref for h in outs], [h.ref for h in scr], View()):
            yield ("at", t)
        if task.done is not None:
            slot.mark(task.done)

    slot.add(body)
    return outs


def any_of(me, values):
    values = sorted(values)
    cond = me == values[0]
    for v in values[1:]:
        cond = jnp.logical_or(cond, me == v)
    return cond


def pick(me, table):
    items = sorted(table.items())
    out = jnp.int32(items[0][1])
    for key, value in items[1:]:
        out = jnp.where(me == key, jnp.int32(value), out)
    return out


PAIR = {0: ["A0", "R3", "R2", "R1"], 1: ["A1", "A0", "R3", "R2"], 2: ["A2", "A1", "A0", "R3"]}
ONLY_A = {0: ["A0", "", ""], 1: ["A1", "A0", ""], 2: ["A2", "A1", "A0"]}
ONLY_R = {0: ["R3", "R2", "R1"], 1: ["", "R3", "R2"], 2: ["", "", "R3"]}


class Line:
    def __init__(self, slot, rows, width, gather=None, scatter=False, pieces=2, keep=True):
        self.slot, self.rows, self.width, self.pieces = slot, rows, width, pieces
        self.gather, self.scatter = gather is not None, scatter
        slot.axes.add("tp")
        right = PAIR if self.gather and scatter else (ONLY_A if self.gather else ONLY_R)
        flip = lambda m: m if not m else m[0] + str(3 - int(m[1]))
        self.tables = (right, {3 - d: [flip(m) for m in row] for d, row in right.items()})
        self.steps = len(right[0])
        self.keep = keep
        if self.gather:
            self.source = slot.hbm_in(gather)
            self.wide = slot.vmem((4, rows, width), BF)
            self.own_sem = slot.sems(1)
            if keep:
                self.out = slot.hbm_out((rows, 4 * width), BF)
                self.out_sem = slot.sems(4)
        if scatter:
            self.mine = slot.vmem((4, rows, width), BF)
            self.came = slot.vmem((2, self.steps, rows, width), BF)
        self.base = slot.sems(4 * self.steps * pieces)
        self.unit = rows * width * 4 / 88e3
        slot.add(self.body)

    def chunk(self, k):
        me = self.slot.place.tp
        return (me, pick(me, {0: 1, 1: 2, 2: 1, 3: 2}), pick(me, {0: 2, 1: 0, 2: 3, 3: 1}), pick(me, {0: 3, 1: 3, 2: 0, 3: 0}))[k]

    def index(self, way, t, p):
        return self.base + 2 * ((way * self.steps + t) * self.pieces + p)

    def part(self, p):
        step = self.rows // self.pieces
        return pl.ds(p * step, step)

    def sends(self, t, p):
        me = self.slot.place.tp
        rows = self.part(p)
        for way in (0, 1):
            for kind in "AR":
                table = {d: int(row[t][1]) for d, row in self.tables[way].items() if row[t][:1] == kind}
                if not table:
                    continue
                block = pick(me, table)
                if kind == "A":
                    target = self.wide.ref.at[block, rows]
                    origin = self.source.ref.at[rows] if t == 0 else target
                else:
                    target = self.came.ref.at[way, t, rows]
                    origin = self.mine.ref.at[block, rows]
                index = self.index(way, t, p)
                to = me + 1 if way == 0 else me - 1
                yield kind, any_of(me, table), remote(origin, target, self.slot, index, index + 1, {"tp": to})

    def arrivals(self, t, p):
        me = self.slot.place.tp
        rows = self.part(p)
        step = self.rows // self.pieces
        tile = 64
        for way in (0, 1):
            off = 1 if way == 0 else -1
            froms = {d + off: row[t] for d, row in self.tables[way].items() if row[t]}
            sample = self.wide.ref.at[0, rows] if self.gather else self.came.ref.at[0, 0, rows]
            index = self.index(way, t, p)
            pl.when(any_of(me, froms))(remote(sample, sample, self.slot, index, index + 1, {"tp": me}).wait_recv)
            adds = {d: int(m[1]) for d, m in froms.items() if m[0] == "R" and int(m[1]) != d}
            if adds:
                block = pick(me, adds)
                mine, came = self.mine.ref, self.came.ref

                @pl.when(any_of(me, adds))
                def _():
                    @pl.loop(0, step // tile)
                    def _(i):
                        part = pl.ds(pl.multiple_of(p * step + i * tile, tile), tile)
                        mine[block, part] = (mine[block, part].astype(F32) + came[way, t, part].astype(F32)).astype(BF)

    def body(self):
        slot = self.slot
        me = slot.place.tp
        if self.gather:
            own = pltpu.make_async_copy(self.source.ref, self.wide.ref.at[me], slot.sem(self.own_sem))
            own.start()
        start = 0.0
        for t in range(self.steps):
            for p in range(self.pieces):
                if t > 0:
                    yield ("at", start + (t - 1 + (p + 1) / self.pieces) * self.unit + 0.5)
                    self.arrivals(t - 1, p)
                    if p == self.pieces - 1 and self.gather and t <= 3:
                        slot.mark("chunk%d" % t)
                messages = list(self.sends(t, p))
                for kind, cond, copy in messages:
                    if kind == "A":
                        pl.when(cond)(copy.start)
                if any(kind == "R" for kind, _, _ in messages):
                    first = t == (1 if self.gather else 0)
                    if p == 0:
                        for c in ((3, 0) if first else (2, 1)):
                            yield ("flag", "part%d" % c)
                        start = max(start, slot.now - t * self.unit)
                    for kind, cond, copy in messages:
                        if kind == "R":
                            pl.when(cond)(copy.start)
                if t == 0 and p == 0 and self.gather:
                    yield ("at", 1.0)
                    own.wait()
                    slot.mark("chunk0")
        for p in range(self.pieces):
            yield ("at", start + (self.steps - 1 + (p + 1) / self.pieces) * self.unit + 0.5)
            self.arrivals(self.steps - 1, p)
        if self.gather and self.steps == 3:
            slot.mark("chunk3")
        if self.scatter:
            slot.mark("reduced")
        outs = []
        if self.gather and self.keep:
            for c in range(4):
                where = self.out.ref.at[:, pl.ds(c * self.width, self.width)]
                outs.append(pltpu.make_async_copy(self.wide.ref.at[c], where, slot.sem(self.out_sem + c)))
                outs[-1].start()
        yield ("at", start + self.steps * self.unit + 1.0)
        for t in range(self.steps):
            for p in range(self.pieces):
                for _, cond, copy in self.sends(t, p):
                    pl.when(cond)(copy.wait_send)
        for copy in outs:
            copy.wait()

    def total(self, part):
        me = self.slot.place.tp
        last = self.steps - 1
        left = jnp.where(me > 0, self.came.ref[0, last, part].astype(F32), 0.0)
        right = jnp.where(me < 3, self.came.ref[1, last, part].astype(F32), 0.0)
        return self.mine.ref[me, part].astype(F32) + left + right


def tiled(count, tile, body):
    @pl.loop(0, count // tile)
    def _(i):
        body(pl.ds(pl.multiple_of(i * tile, tile), tile))


class Weights:
    def __init__(self, slot, arrays, shape, order, where):
        self.slot, self.order, self.where = slot, order, where
        self.arrays = [slot.hbm_in(a) for a in arrays]
        self.buffer = slot.vmem((2, len(arrays)) + shape, BF)
        self.base = slot.sems(2 * len(arrays))
        self.step = 0

    def copies(self, step):
        block = self.order[step] if not callable(self.order) else self.order(step)
        for j, array in enumerate(self.arrays):
            yield pltpu.make_async_copy(
                self.where(array.ref, block),
                self.buffer.ref.at[step % 2, j],
                self.slot.sem(self.base + 2 * j + step % 2),
            )

    def start(self, step):
        for copy in self.copies(step):
            copy.start()

    def take(self, step):
        for copy in self.copies(step):
            copy.wait()
        return [self.buffer.ref.at[step % 2, j] for j in range(len(self.arrays))]


def row_block(ref, c):
    return ref.at[pl.ds(pl.multiple_of(c * 512, 512), 512)]


def col_block(ref, c):
    return ref.at[:, pl.ds(pl.multiple_of(c * 512, 512), 512)]


def consume(slot, line, arrays, shape, where, last, multiply, cost, flag):
    weights = Weights(slot, arrays, shape, line.chunk, where)

    def body():
        weights.start(0)
        for k in range(4):
            if k < 3:
                weights.start(k + 1)
            yield ("flag", "chunk%d" % k)
            blocks = weights.take(k)
            chunk = line.chunk(k)
            for j, block in enumerate(blocks):
                multiply(k == 0, line.wide.ref.at[chunk], block, j)
                yield ("did", cost)
        yield from last()
        slot.mark(flag)

    slot.add(body)


def dot_nn(left, right):
    return jnp.dot(left, right, preferred_element_type=F32)


def dot_nt(left, right):
    return lax.dot_general(left, right, (((1,), (1,)), ((), ())), preferred_element_type=F32)


def produce(slot, line, lefts, arrays, shape, where, dot, cost):
    order = (3, 0, 2, 1)
    weights = Weights(slot, arrays, shape, order, where)

    def body():
        weights.start(0)
        slot.need(*lefts)
        for k, c in enumerate(order):
            if k < 3:
                weights.start(k + 1)
            blocks = weights.take(k)
            value = None
            for left, block in zip(lefts, blocks):
                term = dot(left.ref[...], block[...])
                value = term if value is None else value + term
            line.mine.ref[c] = value.astype(BF)
            yield ("did", cost)
            slot.mark("part%d" % c)

    slot.add(body)


class RowTotals:
    def __init__(self, slot, rows):
        self.slot, self.rows = slot, rows
        self.stat = slot.vmem((rows, 128), F32)
        self.send = slot.vmem((8, rows), F32)
        self.came = slot.vmem((3, 8, rows), F32)
        self.total = slot.vmem((rows, 128), F32)
        self.base = slot.sems(6)

    def put(self, part, *columns):
        lane = lax.broadcasted_iota(jnp.int32, (columns[0].shape[0], 128), 1)
        value = jnp.zeros((columns[0].shape[0], 128), F32)
        for k, column in enumerate(columns):
            value = jnp.where(lane == k, column, value)
        self.stat.ref[part] = value

    def exchange(self):
        slot, me = self.slot, self.slot.place.tp
        send = self.send.ref
        send[...] = jnp.transpose(self.stat.ref[...])[0:8]
        copies = []
        for k in (1, 2, 3):
            copies.append(
                remote(send, self.came.ref.at[k - 1], slot, self.base + 2 * (k - 1), self.base + 2 * (k - 1) + 1, {"tp": me ^ k})
            )
            copies[-1].start()
        yield ("at", slot.now + 2.5)
        for copy in copies:
            copy.wait()
        total = send[...] + self.came.ref[0] + self.came.ref[1] + self.came.ref[2]
        wide = jnp.concatenate([total, jnp.zeros((120, self.rows), F32)], axis=0)
        self.total.ref[...] = jnp.transpose(wide)

    def column(self, part, k):
        return self.total.ref[part, k : k + 1]


def attn_finish(slot, line, rows, width, x, gain):
    x, gain = slot.load(x), slot.load(gain.reshape(1, width))
    raw, resid = slot.store((rows, width), F32), slot.store((rows, width), F32)
    resid_b, factor = slot.store((rows, width), BF), slot.store((rows, 128), F32)
    totals = RowTotals(slot, rows)

    def body():
        yield ("flag", "reduced")

        def first(part):
            value = line.total(part)
            raw.ref[part] = value
            totals.put(part, jnp.sum(value * value, axis=1, keepdims=True))

        tiled(rows, 32, first)
        slot.need(x, gain)
        slot.flush(raw)
        yield from totals.exchange()

        def second(part):
            scale = lax.rsqrt(totals.column(part, 0) / D + EPS)
            value = x.ref[part].astype(F32) + raw.ref[part] * scale * gain.ref[...]
            resid.ref[part] = value
            resid_b.ref[part] = value.astype(BF)
            factor.ref[part] = jnp.broadcast_to(scale, (32, 128))

        tiled(rows, 32, second)
        slot.flush(resid_b, resid, factor)

    slot.add(body)
    return [raw.target, resid.target, resid_b.target, factor.target]


def mlp_finish(slot, line, rows, width, resid, cot, gain):
    resid, cot, gain = slot.load(resid), slot.load(cot), slot.load(gain.reshape(1, width))
    raw = slot.vmem((rows, width), F32)
    out, grad = slot.store((rows, width), BF), slot.store((rows, width), BF)
    gain_grad = slot.store((8, width), F32)
    totals = RowTotals(slot, rows)

    def body():
        yield ("flag", "reduced")
        slot.need(resid, cot, gain)

        def first(part):
            value = line.total(part)
            raw.ref[part] = value
            scaled = cot.ref[part].astype(F32) * gain.ref[...]
            totals.put(part, jnp.sum(value * value, axis=1, keepdims=True), jnp.sum(scaled * value, axis=1, keepdims=True))

        tiled(rows, 32, first)
        gain_grad.ref[...] = jnp.zeros((8, width), F32)
        yield from totals.exchange()

        def second(part):
            scale = lax.rsqrt(totals.column(part, 0) / D + EPS)
            inner = totals.column(part, 1)
            value = raw.ref[part]
            given = cot.ref[part].astype(F32)
            normed = value * scale
            grad.ref[part] = (scale * (given * gain.ref[...]) - value * (scale * scale * scale * inner / D)).astype(BF)
            out.ref[part] = (resid.ref[part] + normed * gain.ref[...]).astype(BF)
            terms = given * normed
            for i in range(4):
                gain_grad.ref[...] += terms[8 * i : 8 * i + 8]

        tiled(rows, 32, second)
        slot.flush(grad, out, gain_grad)

    slot.add(body)
    return [out.target, grad.target, gain_grad.target]


def resid_finish(slot, line, rows, width, cot, attn, factor, gain):
    cot, attn, factor, gain = slot.load(cot), slot.load(attn), slot.load(factor), slot.load(gain.reshape(1, width))
    resid, grad = slot.store((rows, width), F32), slot.store((rows, width), BF)
    gain_grad = slot.store((8, width), F32)
    totals = RowTotals(slot, rows)

    def body():
        yield ("flag", "reduced")
        slot.need(cot, attn, factor, gain)

        def first(part):
            value = line.total(part) + cot.ref[part].astype(F32)
            resid.ref[part] = value
            totals.put(part, jnp.sum(value * gain.ref[...] * attn.ref[part], axis=1, keepdims=True))

        tiled(rows, 32, first)
        gain_grad.ref[...] = jnp.zeros((8, width), F32)
        slot.flush(resid)
        yield from totals.exchange()

        def second(part):
            scale = factor.ref[part, 0:1]
            inner = totals.column(part, 0)
            value, given = attn.ref[part], resid.ref[part]
            grad.ref[part] = (scale * (given * gain.ref[...]) - value * (scale * scale * scale * inner / D)).astype(BF)
            terms = given * value * scale
            for i in range(4):
                gain_grad.ref[...] += terms[8 * i : 8 * i + 8]

        tiled(rows, 32, second)
        slot.flush(grad, gain_grad)

    slot.add(body)
    return [resid.target, grad.target, gain_grad.target]


def last_finish(slot, line, rows, width, resid):
    resid = slot.load(resid)
    out = slot.store((rows, width), BF)

    def body():
        yield ("flag", "reduced")
        slot.need(resid)

        def first(part):
            out.ref[part] = (line.total(part) + resid.ref[part]).astype(BF)

        tiled(rows, 32, first)
        slot.flush(out)

    slot.add(body)
    return [out.target]


def given_partial(slot, line, array):
    source = slot.hbm_in(array)
    base = slot.sems(4)

    def body():
        copies = {}
        for c in (3, 0, 2, 1):
            copies[c] = pltpu.make_async_copy(
                source.ref.at[:, pl.ds(c * line.width, line.width)], line.mine.ref.at[c], slot.sem(base + c)
            )
            copies[c].start()
        yield ("at", 1.0)
        for c in (3, 0, 2, 1):
            copies[c].wait()
            slot.mark("part%d" % c)

    slot.add(body)


def gate_up(slot, line, rows, w_gate, w_up):
    ff = w_gate.shape[1]
    acc = slot.vmem((2, rows, ff), F32)
    gate, up, act = (slot.store((rows, ff), BF) for _ in range(3))

    def multiply(first, left, block, j):
        @pl.loop(0, ff // 1024)
        def _(i):
            cols = pl.ds(pl.multiple_of(i * 1024, 1024), 1024)
            value = dot_nn(left[...], block[:, cols])
            acc.ref[j, :, cols] = value if first else acc.ref[j, :, cols] + value

    def last():
        half = rows // 2
        for h in (0, 1):

            @pl.loop(0, half // 16)
            def _(i):
                part = pl.ds(pl.multiple_of(h * half + i * 16, 16), 16)
                g, u = acc.ref[0, part], acc.ref[1, part]
                gate.ref[part] = g.astype(BF)
                up.ref[part] = u.astype(BF)
                act.ref[part] = (g * jax.nn.sigmoid(g) * u).astype(BF)

            yield ("did", 2.0)
        slot.flush(act, gate, up)

    consume(slot, line, (w_gate, w_up), (512, ff), row_block, last, multiply, 2.2, "mlp")
    return [gate.target, up.target, act.target]


def act_back(slot, line, rows, w_down, gate, up):
    ff = w_down.shape[0]
    acc = slot.vmem((rows, ff), F32)
    gate, up = slot.load(gate), slot.load(up)
    g_gate, g_up = slot.store((rows, ff), BF), slot.store((rows, ff), BF)

    def multiply(first, left, block, j):
        @pl.loop(0, ff // 1024)
        def _(i):
            cols = pl.ds(pl.multiple_of(i * 1024, 1024), 1024)
            value = dot_nt(left[...], block[cols])
            acc.ref[:, cols] = value if first else acc.ref[:, cols] + value

    def last():
        slot.need(gate, up)
        half = rows // 2
        for h in (0, 1):

            @pl.loop(0, half // 16)
            def _(i):
                part = pl.ds(pl.multiple_of(h * half + i * 16, 16), 16)
                grad, g, u = acc.ref[part], gate.ref[part].astype(F32), up.ref[part].astype(F32)
                sigma = jax.nn.sigmoid(g)
                g_gate.ref[part] = (grad * u * sigma * (1.0 + g * (1.0 - sigma))).astype(BF)
                g_up.ref[part] = (grad * g * sigma).astype(BF)

            yield ("did", 2.5)
        slot.flush(g_gate, g_up)

    consume(slot, line, (w_down,), (ff, 512), col_block, last, multiply, 2.4, "back")
    return [g_gate.target, g_up.target]


def half_turn(value):
    return pltpu.roll(value, HEAD_DIM // 2, axis=1)


def tables(slot, positions, freqs, sign):
    count = positions.shape[0]
    positions, freqs, sign = slot.load(positions), slot.load(freqs), slot.load(sign)
    cosine, sine = slot.store((count, HEAD_DIM), F32), slot.store((count, HEAD_DIM), F32)

    def body():
        slot.need(positions, freqs, sign)

        def first(part):
            angle = positions.ref[part].astype(F32) * freqs.ref[...]
            cosine.ref[part] = jnp.cos(angle)
            sine.ref[part] = jnp.sin(angle) * sign.ref[...]

        tiled(count, 32, first)
        slot.flush(cosine, sine)
        yield ("did", 6.0)
        slot.mark("tables")

    slot.add(body)
    return cosine, sine


def head_cols(h):
    return pl.ds(h * HEAD_DIM, HEAD_DIM)


def project(slot, line, rows, width, weights, flags, gains, cosine, sine, first_row):
    stages = [slot.late(w) for w in weights]
    gains = [slot.load(g.reshape(1, width)) for g in gains]
    raws = [slot.store((rows, width), F32) for _ in (0, 1)]
    query, kv = slot.store((rows, width), BF), slot.store((rows, 2 * width), BF)
    factor = slot.store((rows, 128), F32)
    totals = RowTotals(slot, rows)
    half = rows // 2

    def body():
        for j in range(3):
            if flags is not None:
                yield ("flag", flags[j])
            slot.fetch(stages[j])
        yield ("flag", "chunk3")
        wide = line.wide.ref
        for j in range(3):
            slot.need(stages[j])
            weight = stages[j].ref

            @pl.loop(0, 2)
            def _(i):
                part = pl.ds(pl.multiple_of(i * half, half), half)
                value = dot_nn(wide[0, part], weight[0:width])
                for c in (1, 2, 3):
                    value = value + dot_nn(wide[c, part], weight[c * width : (c + 1) * width])
                if j < 2:
                    raws[j].ref[part] = value
                else:
                    kv.ref[part, width : 2 * width] = value.astype(BF)

            yield ("did", 2.0)

        def first(part):
            q, k = raws[0].ref[part], raws[1].ref[part]
            totals.put(part, jnp.sum(q * q, axis=1, keepdims=True), jnp.sum(k * k, axis=1, keepdims=True))

        tiled(rows, 32, first)
        slot.flush(*raws)
        yield from totals.exchange()
        yield ("flag", "tables")
        slot.need(*gains)
        slot.need(*[t for t in (cosine, sine) if hasattr(t, "source")])

        def second(part, trig):
            lane = lax.broadcasted_iota(jnp.int32, (32, 128), 1)
            scales = [lax.rsqrt(totals.column(part, j) / D + EPS) for j in (0, 1)]
            factor.ref[part] = jnp.where(lane == 0, scales[0], scales[1])
            co, si = cosine.ref[trig], sine.ref[trig]
            for j, target in ((0, query), (1, kv)):
                for h in range(width // HEAD_DIM):
                    value = raws[j].ref[part, head_cols(h)] * scales[j] * gains[j].ref[:, head_cols(h)]
                    target.ref[part, head_cols(h)] = (value * co + half_turn(value) * si).astype(BF)

        @pl.loop(0, rows // 32)
        def _(i):
            second(pl.ds(pl.multiple_of(i * 32, 32), 32), pl.ds(pl.multiple_of(first_row + i * 32, 32), 32))

        slot.flush(kv, query, factor)

    slot.add(body)
    return [raws[0].target, raws[1].target, query.target, kv.target, factor.target]


class Mask:
    def __init__(self, slot, seg_all, seg_cols, first, count):
        self.slot, self.first, self.count = slot, first, count
        self.keys, self.mine = slot.load(seg_all), slot.load(seg_cols)
        self.mask = slot.vmem((count, 4 * count), F32)

    def fill(self, s):
        self.slot.need(self.keys, self.mine)
        count = self.count
        ctx = self.slot.place.ctx
        mine = self.mine.ref[(self.first + s) * count : (self.first + s + 1) * count, 0:1]
        for c in range(4):
            keys = self.keys.ref[8 * c + self.first + s : 8 * c + self.first + s + 1, :]
            row = ctx * count + lax.broadcasted_iota(jnp.int32, (count, count), 0)
            col = c * count + lax.broadcasted_iota(jnp.int32, (count, count), 1)
            fine = jnp.logical_and(mine == keys, row >= col)
            self.mask.ref[:, c * count : (c + 1) * count] = jnp.where(fine, 0.0, NEG)


def attend(slot, flag, kv, query, mask, rows, width):
    kv, query = slot.late(kv), slot.load(query)
    count = mask.count
    heads, heads_b = slot.store((rows, width), F32), slot.store((rows, width), BF)
    logsum = slot.store((rows, 128), F32)
    logits = slot.vmem((count, 4 * count), F32)
    scale = 1.0 / math.sqrt(HEAD_DIM)

    def body():
        yield ("flag", flag)
        slot.fetch(kv)
        mask.fill(0)
        yield ("did", 1.5)
        slot.need(kv, query)
        logsum.ref[...] = jnp.zeros((rows, 128), F32)
        for s in range(rows // count):
            mine = pl.ds(s * count, count)
            if s:
                mask.fill(s)

            @pl.loop(0, width // HEAD_DIM)
            def _(h):
                cols = pl.ds(pl.multiple_of(h * HEAD_DIM, HEAD_DIM), HEAD_DIM)
                vcols = pl.ds(pl.multiple_of(width + h * HEAD_DIM, HEAD_DIM), HEAD_DIM)
                q = query.ref[mine, cols]
                peak = jnp.full((count, 1), NEG, F32)
                for c in range(4):
                    keys = kv.ref[pl.ds(c * rows + s * count, count), cols]
                    block = pl.ds(c * count, count)
                    value = dot_nt(q, keys) * scale + mask.mask.ref[:, block]
                    logits.ref[:, block] = value
                    peak = jnp.maximum(peak, jnp.max(value, axis=1, keepdims=True))
                total = jnp.zeros((count, 1), F32)
                acc = jnp.zeros((count, HEAD_DIM), F32)
                for c in range(4):
                    vals = kv.ref[pl.ds(c * rows + s * count, count), vcols]
                    weight = jnp.exp(logits.ref[:, pl.ds(c * count, count)] - peak)
                    total = total + jnp.sum(weight, axis=1, keepdims=True)
                    acc = acc + dot_nn(weight.astype(BF), vals)
                out = acc / total
                heads.ref[mine, cols] = out
                heads_b.ref[mine, cols] = out.astype(BF)
                lane = lax.broadcasted_iota(jnp.int32, (count, 128), 1)
                logsum.ref[mine] = jnp.where(lane == h, peak + jnp.log(total), logsum.ref[mine])

            yield ("did", 4.0)
        slot.flush(heads_b, heads, logsum)

    slot.add(body)
    return [heads.target, heads_b.target, logsum.target]


def attend_back(slot, line, kv, query, heads, logsum, mask, rows, width, w_out):
    kv, query, heads, logsum = slot.load(kv), slot.load(query), slot.load(heads), slot.load(logsum)
    count = mask.count
    acc = slot.vmem((rows, width), F32)
    grad = slot.vmem((rows, width), BF)
    g_query, g_kv = slot.store((rows, width), F32), slot.store((4 * rows, 2 * width), BF)
    scale = 1.0 / math.sqrt(HEAD_DIM)

    def multiply(first, left, block, j):
        value = dot_nt(left[...], block[...])
        acc.ref[...] = value if first else acc.ref[...] + value

    def last():
        grad.ref[...] = acc.ref[...].astype(BF)
        slot.need(kv, query, heads, logsum)
        for s in range(rows // count):
            mine = pl.ds(s * count, count)
            mask.fill(s)
            yield ("did", 1.0)

            @pl.loop(0, width // HEAD_DIM)
            def _(h):
                cols = pl.ds(pl.multiple_of(h * HEAD_DIM, HEAD_DIM), HEAD_DIM)
                vcols = pl.ds(pl.multiple_of(width + h * HEAD_DIM, HEAD_DIM), HEAD_DIM)
                q, g = query.ref[mine, cols], grad.ref[mine, cols]
                delta = jnp.sum(g.astype(F32) * heads.ref[mine, cols], axis=1, keepdims=True)
                lane = lax.broadcasted_iota(jnp.int32, (count, 128), 1)
                logs = jnp.sum(jnp.where(lane == h, logsum.ref[mine], 0.0), axis=1, keepdims=True)
                total = jnp.zeros((count, HEAD_DIM), F32)
                for c in range(4):
                    there = pl.ds(c * rows + s * count, count)
                    keys, vals = kv.ref[there, cols], kv.ref[there, vcols]
                    value = dot_nt(q, keys) * scale + mask.mask.ref[:, pl.ds(c * count, count)]
                    probs = jnp.exp(value - logs)
                    slopes = (probs * (dot_nt(g, vals) - delta)).astype(BF)
                    total = total + dot_nn(slopes, keys)
                    g_kv.ref[there, cols] = (dot_tn(slopes, q) * scale).astype(BF)
                    g_kv.ref[there, vcols] = dot_tn(probs.astype(BF), g).astype(BF)
                g_query.ref[mine, cols] = total * scale

            yield ("did", 8.0)
        slot.flush(g_kv, g_query)

    consume(slot, line, (w_out,), (width, width), col_block, last, multiply, 0.6, "heads")
    return [g_query.target, g_kv.target]


def dot_tn(left, right):
    return lax.dot_general(left, right, (((0,), (0,)), ((), ())), preferred_element_type=F32)


def project_back(slot, flag, g_query, g_kv, raws, factor, gains, cosine, sine, first_row, rows, width):
    g_kv = slot.late(g_kv)
    g_query, factor = slot.load(g_query), slot.load(factor)
    raws = [slot.load(r) for r in raws]
    gains = [slot.load(g.reshape(1, width)) for g in gains]
    cosine, sine = slot.load(cosine), slot.load(sine)
    outs = [slot.store((rows, width), BF) for _ in range(3)]
    gain_grads = [slot.store((8, width), F32) for _ in range(2)]
    totals = RowTotals(slot, rows)

    def body():
        yield ("flag", flag)
        slot.fetch(g_kv)
        yield ("at", slot.now + 1.0)
        slot.need(g_kv, g_query, factor, cosine, sine, *raws, *gains)
        for g in gain_grads:
            g.ref[...] = jnp.zeros((8, width), F32)

        @pl.loop(0, rows // 32)
        def _(i):
            part = pl.ds(pl.multiple_of(i * 32, 32), 32)
            trig = pl.ds(pl.multiple_of(first_row + i * 32, 32), 32)
            co, si = cosine.ref[trig], sine.ref[trig]
            sums = []
            for j, source in ((0, g_query), (1, g_kv)):
                scale = factor.ref[part, j : j + 1]
                total = jnp.zeros((32, 1), F32)
                for h in range(width // HEAD_DIM):
                    cols = head_cols(h)
                    value = source.ref[part, cols]
                    value = value * co - half_turn(value) * si
                    source.ref[part, cols] = value
                    raw = raws[j].ref[part, cols]
                    total = total + jnp.sum(value * gains[j].ref[:, cols] * raw, axis=1, keepdims=True)
                    terms = value * raw * scale
                    for r in range(4):
                        gain_grads[j].ref[:, cols] += terms[8 * r : 8 * r + 8]
                sums.append(total)
            totals.put(part, *sums)

        slot.flush(*gain_grads)
        yield ("did", 3.0)
        yield from totals.exchange()

        def second(part):
            for j, source in ((0, g_query), (1, g_kv)):
                scale = factor.ref[part, j : j + 1]
                inner = totals.column(part, j)
                value = source.ref[part, 0:width] * gains[j].ref[...]
                outs[j].ref[part] = (scale * value - raws[j].ref[part] * (scale * scale * scale * inner / D)).astype(BF)
            outs[2].ref[part] = g_kv.ref[part, width : 2 * width].astype(BF)

        tiled(rows, 32, second)
        slot.flush(*outs)

    slot.add(body)
    return [h.target for h in outs + gain_grads]


def general_row_total(value):
    return lax.psum(value, "tp")


def general_widen(value):
    return lax.all_gather(value, "tp", axis=1, tiled=True)


def general_narrow(value):
    return lax.psum_scatter(
        value.astype(jnp.bfloat16), "tp", scatter_dimension=1, tiled=True
    ).astype(jnp.float32)


def general_contract_last(left, right):
    return lax.dot_general(
        left, right, (((1,), (1,)), ((), ())), preferred_element_type=jnp.float32
    )


def general_contract_first(left, right):
    return lax.dot_general(
        left, right, (((0,), (0,)), ((), ())), preferred_element_type=jnp.float32
    )


def general_rotary(positions, depth):
    half = depth // 2
    freqs = THETA ** (-(jnp.arange(half, dtype=jnp.float32) * 2.0) / depth)
    angles = positions.astype(jnp.float32)[..., None] * freqs
    return (jnp.cos(angles)[..., None, :], jnp.sin(angles)[..., None, :])


def general_turn(value, cosine, sine):
    half = value.shape[-1] // 2
    first = value[..., :half]
    second = value[..., half:]
    return jnp.concatenate(
        [first * cosine - second * sine, second * cosine + first * sine], axis=-1
    )


def general_turn_back(grad, cosine, sine):
    half = grad.shape[-1] // 2
    first = grad[..., :half]
    second = grad[..., half:]
    return jnp.concatenate(
        [first * cosine + second * sine, second * cosine - first * sine], axis=-1
    )


def general_norm_grad(scaled, value, factor, inner):
    return factor[:, None] * scaled - value * (factor**3 * inner / D)[:, None]


def general(
    hidden,
    cotangent,
    segments,
    positions,
    w_query,
    w_key,
    w_value,
    w_out,
    w_gate,
    w_up,
    w_down,
    q_gain,
    k_gain,
    attn_gain,
    mlp_gain,
):
    local_seqs, slice_len, local_width = hidden.shape
    per_batch = local_seqs // 2
    rows = per_batch * slice_len
    heads_here = q_gain.shape[0] // HEAD_DIM
    scale = 1.0 / math.sqrt(HEAD_DIM)
    query_index = lax.axis_index("ctx") * slice_len + jnp.arange(slice_len, dtype=jnp.int32)
    outputs = []
    input_grads = []
    weight_grads = None
    q_gain_grad = jnp.zeros(q_gain.shape, jnp.float32)
    k_gain_grad = jnp.zeros(k_gain.shape, jnp.float32)
    attn_gain_grad = jnp.zeros(attn_gain.shape, jnp.float32)
    mlp_gain_grad = jnp.zeros(mlp_gain.shape, jnp.float32)
    for batch in range(2):
        lower = batch * per_batch
        tokens_in = hidden[lower : lower + per_batch].reshape(rows, local_width)
        seg_here = segments[lower : lower + per_batch]
        pos_here = positions[lower : lower + per_batch].reshape(rows)
        gathered = (
            lax.all_gather(w_query, ("dp", "ctx"), axis=0, tiled=True),
            lax.all_gather(w_key, ("dp", "ctx"), axis=0, tiled=True),
            lax.all_gather(w_value, ("dp", "ctx"), axis=0, tiled=True),
            lax.all_gather(w_out, ("dp", "ctx"), axis=1, tiled=True),
            lax.all_gather(w_gate, ("dp", "ctx"), axis=0, tiled=True),
            lax.all_gather(w_up, ("dp", "ctx"), axis=0, tiled=True),
            lax.all_gather(w_down, ("dp", "ctx"), axis=1, tiled=True),
        )
        query_full, key_full, value_full, out_full, gate_full, up_full, down_full = gathered
        if weight_grads is None:
            weight_grads = tuple((jnp.zeros(tensor.shape, jnp.float32) for tensor in gathered))
        wide_in = general_widen(tokens_in)
        query_raw = jnp.dot(wide_in, query_full, preferred_element_type=jnp.float32)
        key_raw = jnp.dot(wide_in, key_full, preferred_element_type=jnp.float32)
        value_raw = jnp.dot(wide_in, value_full, preferred_element_type=jnp.float32)
        query_sq, key_sq = general_row_total(
            (jnp.sum(query_raw * query_raw, axis=1), jnp.sum(key_raw * key_raw, axis=1))
        )
        query_scale = lax.rsqrt(query_sq / D + EPS)
        key_scale = lax.rsqrt(key_sq / D + EPS)
        cosine, sine = general_rotary(pos_here, HEAD_DIM)
        query_rot = general_turn(
            (query_raw * query_scale[:, None] * q_gain).reshape(rows, heads_here, HEAD_DIM),
            cosine,
            sine,
        )
        key_rot = general_turn(
            (key_raw * key_scale[:, None] * k_gain).reshape(rows, heads_here, HEAD_DIM),
            cosine,
            sine,
        )
        query_b = query_rot.astype(jnp.bfloat16).reshape(per_batch, slice_len, heads_here, HEAD_DIM)
        key_b = key_rot.astype(jnp.bfloat16).reshape(per_batch, slice_len, heads_here * HEAD_DIM)
        value_b = value_raw.astype(jnp.bfloat16).reshape(
            per_batch, slice_len, heads_here * HEAD_DIM
        )

        def allowed_pairs(seg_piece, count):
            key_index = jnp.arange(count, dtype=jnp.int32)
            causal = query_index[:, None] >= key_index[None, :]
            same = seg_here[:, None, :, None] == seg_piece[:, None, None, :]
            return jnp.logical_and(same, causal[None, None])

        start_peak = jnp.full((per_batch, heads_here, slice_len), NEG, jnp.float32)
        peak = start_peak
        key_piece = lax.all_gather(key_b, "ctx", axis=1, tiled=True)
        value_piece = lax.all_gather(value_b, "ctx", axis=1, tiled=True)
        attend_seg_piece = lax.all_gather(seg_here, "ctx", axis=1, tiled=True)
        attend_count = key_piece.shape[1]
        key_four = key_piece.reshape(per_batch, attend_count, heads_here, HEAD_DIM)
        value_four = value_piece.reshape(per_batch, attend_count, heads_here, HEAD_DIM)
        allowed = allowed_pairs(attend_seg_piece, attend_count)
        logits = scale * jnp.einsum(
            "sqhd,skhd->shqk", query_b, key_four, preferred_element_type=jnp.float32
        )
        logits = jnp.where(allowed, logits, NEG)
        fresh = jnp.maximum(peak, jnp.max(logits, axis=-1))
        weights = jnp.where(allowed, jnp.exp(logits - fresh[..., None]), 0.0)
        total = jnp.sum(weights, axis=-1)
        accum = jnp.einsum(
            "shqk,skhd->shqd",
            weights.astype(jnp.bfloat16),
            value_four,
            preferred_element_type=jnp.float32,
        )
        peak, total, accum = (fresh, total, accum)
        logsum = peak + jnp.log(total)
        out_heads = (
            (accum / total[..., None]).transpose(0, 2, 1, 3).reshape(rows, heads_here * HEAD_DIM)
        )
        out_b = out_heads.astype(jnp.bfloat16)
        attn_raw = general_narrow(jnp.dot(out_b, out_full, preferred_element_type=jnp.float32))
        attn_scale = lax.rsqrt(general_row_total(jnp.sum(attn_raw * attn_raw, axis=1)) / D + EPS)
        resid = tokens_in.astype(jnp.float32) + attn_raw * attn_scale[:, None] * attn_gain
        wide_mid = general_widen(resid.astype(jnp.bfloat16))
        gate = jnp.dot(wide_mid, gate_full, preferred_element_type=jnp.float32)
        up_val = jnp.dot(wide_mid, up_full, preferred_element_type=jnp.float32)
        sigma = jax.nn.sigmoid(gate)
        swish = gate * sigma
        act_b = (swish * up_val).astype(jnp.bfloat16)
        mlp_raw = general_narrow(jnp.dot(act_b, down_full, preferred_element_type=jnp.float32))
        mlp_scale = lax.rsqrt(general_row_total(jnp.sum(mlp_raw * mlp_raw, axis=1)) / D + EPS)
        result = resid + mlp_raw * mlp_scale[:, None] * mlp_gain
        outputs.append(result.astype(jnp.bfloat16).reshape(per_batch, slice_len, local_width))
        again = (
            lax.all_gather(w_query, ("dp", "ctx"), axis=0, tiled=True),
            lax.all_gather(w_key, ("dp", "ctx"), axis=0, tiled=True),
            lax.all_gather(w_value, ("dp", "ctx"), axis=0, tiled=True),
            lax.all_gather(w_out, ("dp", "ctx"), axis=1, tiled=True),
            lax.all_gather(w_gate, ("dp", "ctx"), axis=0, tiled=True),
            lax.all_gather(w_up, ("dp", "ctx"), axis=0, tiled=True),
            lax.all_gather(w_down, ("dp", "ctx"), axis=1, tiled=True),
        )
        query_back, key_back, value_back, out_back, gate_back, up_back, down_back = again
        grad_out = (
            cotangent[lower : lower + per_batch].reshape(rows, local_width).astype(jnp.float32)
        )
        mlp_gain_grad = mlp_gain_grad + jnp.sum(grad_out * mlp_raw * mlp_scale[:, None], axis=0)
        scaled = grad_out * mlp_gain
        grad_mlp = general_norm_grad(
            scaled, mlp_raw, mlp_scale, general_row_total(jnp.sum(scaled * mlp_raw, axis=1))
        )
        wide_grad_mlp = general_widen(grad_mlp.astype(jnp.bfloat16))
        grad_act = general_contract_last(wide_grad_mlp, down_back)
        grad_gate = (grad_act * up_val * sigma * (1.0 + gate * (1.0 - sigma))).astype(jnp.bfloat16)
        grad_up = (grad_act * swish).astype(jnp.bfloat16)
        grad_resid = grad_out + general_narrow(
            general_contract_last(grad_gate, gate_back) + general_contract_last(grad_up, up_back)
        )
        attn_gain_grad = attn_gain_grad + jnp.sum(
            grad_resid * attn_raw * attn_scale[:, None], axis=0
        )
        scaled = grad_resid * attn_gain
        grad_attn = general_norm_grad(
            scaled, attn_raw, attn_scale, general_row_total(jnp.sum(scaled * attn_raw, axis=1))
        )
        wide_grad_attn = general_widen(grad_attn.astype(jnp.bfloat16))
        grad_heads = general_contract_last(wide_grad_attn, out_back).astype(jnp.bfloat16)
        dout_four = grad_heads.reshape(per_batch, slice_len, heads_here, HEAD_DIM)
        delta = jnp.sum(
            (grad_heads.astype(jnp.float32) * out_heads).reshape(
                per_batch, slice_len, heads_here, HEAD_DIM
            ),
            axis=-1,
        ).transpose(0, 2, 1)

        def attend_back(piece):
            key_piece, value_piece, seg_piece = piece
            count = key_piece.shape[1]
            key_four = key_piece.reshape(per_batch, count, heads_here, HEAD_DIM)
            value_four = value_piece.reshape(per_batch, count, heads_here, HEAD_DIM)
            allowed = allowed_pairs(seg_piece, count)
            logits = scale * jnp.einsum(
                "sqhd,skhd->shqk", query_b, key_four, preferred_element_type=jnp.float32
            )
            probs = jnp.where(allowed, jnp.exp(logits - logsum[..., None]), 0.0)
            grad_probs = jnp.einsum(
                "sqhd,skhd->shqk", dout_four, value_four, preferred_element_type=jnp.float32
            )
            grad_logits = (probs * (grad_probs - delta[..., None])).astype(jnp.bfloat16)
            grad_query = scale * jnp.einsum(
                "shqk,skhd->sqhd", grad_logits, key_four, preferred_element_type=jnp.float32
            )
            key_grad = scale * jnp.einsum(
                "shqk,sqhd->skhd", grad_logits, query_b, preferred_element_type=jnp.float32
            )
            value_grad = jnp.einsum(
                "shqk,sqhd->skhd",
                probs.astype(jnp.bfloat16),
                dout_four,
                preferred_element_type=jnp.float32,
            )
            grad_keys = key_grad.reshape(per_batch, count, heads_here * HEAD_DIM)
            grad_values = value_grad.reshape(per_batch, count, heads_here * HEAD_DIM)
            return (grad_query, grad_keys, grad_values)

        grad_query, grad_keys, grad_values = attend_back(
            (
                lax.all_gather(key_b, "ctx", axis=1, tiled=True),
                lax.all_gather(value_b, "ctx", axis=1, tiled=True),
                lax.all_gather(seg_here, "ctx", axis=1, tiled=True),
            )
        )
        key_grad_mine, value_grad_mine = (
            lax.psum_scatter(
                grad_keys.astype(jnp.bfloat16), "ctx", scatter_dimension=1, tiled=True
            ).astype(jnp.float32),
            lax.psum_scatter(
                grad_values.astype(jnp.bfloat16), "ctx", scatter_dimension=1, tiled=True
            ).astype(jnp.float32),
        )
        grad_qnorm = general_turn_back(
            grad_query.reshape(rows, heads_here, HEAD_DIM), cosine, sine
        ).reshape(rows, heads_here * HEAD_DIM)
        grad_knorm = general_turn_back(
            key_grad_mine.reshape(rows, heads_here, HEAD_DIM), cosine, sine
        ).reshape(rows, heads_here * HEAD_DIM)
        q_gain_grad = q_gain_grad + jnp.sum(grad_qnorm * query_raw * query_scale[:, None], axis=0)
        k_gain_grad = k_gain_grad + jnp.sum(grad_knorm * key_raw * key_scale[:, None], axis=0)
        q_scaled = grad_qnorm * q_gain
        k_scaled = grad_knorm * k_gain
        q_inner, k_inner = general_row_total(
            (jnp.sum(q_scaled * query_raw, axis=1), jnp.sum(k_scaled * key_raw, axis=1))
        )
        grad_query_raw = general_norm_grad(q_scaled, query_raw, query_scale, q_inner).astype(jnp.bfloat16)
        grad_key_raw = general_norm_grad(k_scaled, key_raw, key_scale, k_inner).astype(jnp.bfloat16)
        grad_value_raw = value_grad_mine.reshape(rows, heads_here * HEAD_DIM).astype(jnp.bfloat16)
        back_terms = (
            general_contract_last(grad_query_raw, query_back)
            + general_contract_last(grad_key_raw, key_back)
            + general_contract_last(grad_value_raw, value_back)
        )
        grad_in = grad_resid + general_narrow(back_terms)
        input_grads.append(grad_in.astype(jnp.bfloat16).reshape(per_batch, slice_len, local_width))
        fresh_grads = (
            general_contract_first(wide_in, grad_query_raw),
            general_contract_first(wide_in, grad_key_raw),
            general_contract_first(wide_in, grad_value_raw),
            general_contract_first(out_b, wide_grad_attn),
            general_contract_first(wide_mid, grad_gate),
            general_contract_first(wide_mid, grad_up),
            general_contract_first(act_b, wide_grad_mlp),
        )
        weight_grads = tuple((left + right for left, right in zip(weight_grads, fresh_grads)))
    finals = (
        lax.psum_scatter(
            weight_grads[0].astype(jnp.bfloat16), ("dp", "ctx"), scatter_dimension=0, tiled=True
        ).astype(jnp.float32),
        lax.psum_scatter(
            weight_grads[1].astype(jnp.bfloat16), ("dp", "ctx"), scatter_dimension=0, tiled=True
        ).astype(jnp.float32),
        lax.psum_scatter(
            weight_grads[2].astype(jnp.bfloat16), ("dp", "ctx"), scatter_dimension=0, tiled=True
        ).astype(jnp.float32),
        lax.psum_scatter(
            weight_grads[3].astype(jnp.bfloat16), ("dp", "ctx"), scatter_dimension=1, tiled=True
        ).astype(jnp.float32),
        lax.psum_scatter(
            weight_grads[4].astype(jnp.bfloat16), ("dp", "ctx"), scatter_dimension=0, tiled=True
        ).astype(jnp.float32),
        lax.psum_scatter(
            weight_grads[5].astype(jnp.bfloat16), ("dp", "ctx"), scatter_dimension=0, tiled=True
        ).astype(jnp.float32),
        lax.psum_scatter(
            weight_grads[6].astype(jnp.bfloat16), ("dp", "ctx"), scatter_dimension=1, tiled=True
        ).astype(jnp.float32),
    )
    gains = lax.psum((q_gain_grad, k_gain_grad, attn_gain_grad, mlp_gain_grad), ("dp", "ctx"))
    return (
        jnp.concatenate(outputs, axis=0),
        jnp.concatenate(input_grads, axis=0),
        finals[0],
        finals[1],
        finals[2],
        finals[3],
        finals[4],
        finals[5],
        finals[6],
        gains[0],
        gains[1],
        gains[2],
        gains[3],
    )


def weight_grad(left, right):
    value = dot_tn(left[0], right[0]) + dot_tn(left[1], right[1])
    return value.astype(BF)


class Batch:
    pass


def planned(
    hidden, cotangent, segments, positions, w_query, w_key, w_value, w_out, w_gate, w_up, w_down,
    q_gain, k_gain, attn_gain, mlp_gain,
):
    seqs, count, width = hidden.shape
    per = seqs // 2
    rows = per * count
    ff = w_gate.shape[1]
    batches = (Batch(), Batch())
    one, two = batches
    for b, batch in enumerate(batches):
        batch.x = hidden[b * per : (b + 1) * per].reshape(rows, width)
        batch.cot = cotangent[b * per : (b + 1) * per].reshape(rows, width)
    seg_cols = jnp.broadcast_to(segments.reshape(seqs * count, 1), (seqs * count, 128))
    pos_cols = jnp.broadcast_to(positions.reshape(seqs * count, 1), (seqs * count, 128))
    half = HEAD_DIM // 2
    freqs = THETA ** (-(jnp.arange(half, dtype=F32) * 2.0) / HEAD_DIM)
    freqs = jnp.concatenate([freqs, freqs]).reshape(1, HEAD_DIM)
    sign = jnp.concatenate([-jnp.ones(half, F32), jnp.ones(half, F32)]).reshape(1, HEAD_DIM)
    seg_pad = jnp.concatenate([segments, jnp.zeros((8 - seqs, count), segments.dtype)], axis=0)
    norms = (q_gain, k_gain)

    s = Slot("slot0", 0)
    line = Line(s, rows, width, gather=one.x)
    full = [attach(s, PlaneGather(w, 0, True, 4.0 * i, done="w%d" % i))[0] for i, w in enumerate((w_query, w_key, w_value))]
    w_out_h = attach(s, PlaneGather(w_out, 1, True, 12.0))[0]
    seg_h = attach(s, PlaneGather(seg_pad, 0, False, 2.0))[0]
    cosine, sine = tables(s, pos_cols, freqs, sign)
    made = project(s, line, rows, width, full, ("w0", "w1", "w2"), norms, cosine, sine, 0)
    s.run()
    wq, wk, wv = (h.value for h in full)
    wo, seg_all, cosine, sine = w_out_h.value, seg_h.value, cosine.target.value, sine.target.value
    one.q_raw, one.k_raw, one.q, one.kv, one.qk_factor = (h.value for h in made)
    one.wide = line.out.value

    s = Slot("slot1", 1)
    line = Line(s, rows, width, gather=two.x)
    kvs = attach(s, PlaneGather(one.kv, 0, False, done="kv"))[0]
    w_gate_h = attach(s, PlaneGather(w_gate, 0, True, 9.0, lean=True))[0]
    s.mark_early("tables")
    made = project(s, line, rows, width, (wq, wk, wv), None, norms, s.load(cosine), s.load(sine), rows)
    mask = Mask(s, seg_all, seg_cols, 0, count)
    felt = attend(s, "kv", kvs, one.q, mask, rows, width)
    s.run()
    wg, one.kvs = w_gate_h.value, kvs.value
    two.q_raw, two.k_raw, two.q, two.kv, two.qk_factor = (h.value for h in made)
    one.heads, one.heads_b, one.logsum = (h.value for h in felt)
    two.wide = line.out.value

    s = Slot("slot2", 2)
    line = Line(s, rows, width, scatter=True)
    kvs = attach(s, PlaneGather(two.kv, 0, False, done="kv"))[0]
    w_up_h = attach(s, PlaneGather(w_up, 0, True, 9.0, lean=True))[0]
    ends = attn_finish(s, line, rows, width, one.x, attn_gain)
    produce(s, line, [s.load(one.heads_b)], [wo], (width, width), col_block, dot_nn, 0.6)
    mask = Mask(s, seg_all, seg_cols, per, count)
    felt = attend(s, "kv", kvs, two.q, mask, rows, width)
    s.run()
    wu, two.kvs = w_up_h.value, kvs.value
    one.attn, one.resid, one.resid_b, one.factor = (h.value for h in ends)
    two.heads, two.heads_b, two.logsum = (h.value for h in felt)

    s = Slot("slot3", 3)
    line = Line(s, rows, width, gather=one.resid_b, scatter=True)
    w_down_h = attach(s, PlaneGather(w_down, 1, True))[0]
    ends = attn_finish(s, line, rows, width, two.x, attn_gain)
    produce(s, line, [s.load(two.heads_b)], [wo], (width, width), col_block, dot_nn, 0.6)
    inner = gate_up(s, line, rows, wg, wu)
    s.run()
    wd, one.mid = w_down_h.value, line.out.value
    two.attn, two.resid, two.resid_b, two.factor = (h.value for h in ends)
    one.gate, one.up, one.act = (h.value for h in inner)

    s = Slot("slot4", 4)
    line = Line(s, rows, width, gather=two.resid_b, scatter=True)
    ends = mlp_finish(s, line, rows, width, one.resid, one.cot, mlp_gain)
    produce(s, line, [s.load(one.act)], [wd], (ff, 512), col_block, dot_nn, 1.8)
    inner = gate_up(s, line, rows, wg, wu)
    s.run()
    two.mid = line.out.value
    one.out, one.g_mlp_b, one.g_mlp_gain = (h.value for h in ends)
    two.gate, two.up, two.act = (h.value for h in inner)

    s = Slot("slot5", 5)
    line = Line(s, rows, width, gather=one.g_mlp_b, scatter=True)
    ends = mlp_finish(s, line, rows, width, two.resid, two.cot, mlp_gain)
    produce(s, line, [s.load(two.act)], [wd], (ff, 512), col_block, dot_nn, 1.8)
    inner = act_back(s, line, rows, wd, one.gate, one.up)
    s.run()
    one.g_mlp = line.out.value
    two.out, two.g_mlp_b, two.g_mlp_gain = (h.value for h in ends)
    one.g_gate, one.g_up = (h.value for h in inner)

    s = Slot("slot6", 6)
    line = Line(s, rows, width, gather=two.g_mlp_b, scatter=True)
    ends = resid_finish(s, line, rows, width, one.cot, one.attn, one.factor, attn_gain)
    produce(s, line, [s.load(one.g_gate), s.load(one.g_up)], [wg, wu], (512, ff), row_block, dot_nt, 3.6)
    inner = act_back(s, line, rows, wd, two.gate, two.up)
    s.run()
    two.g_mlp = line.out.value
    one.g_resid, one.g_attn_b, one.g_attn_gain = (h.value for h in ends)
    two.g_gate, two.g_up = (h.value for h in inner)

    d_down = weight_grad((one.act, two.act), (one.g_mlp, two.g_mlp))
    s = Slot("slot7", 7)
    line = Line(s, rows, width, gather=one.g_attn_b, scatter=True)
    g_down = attach(s, PlaneScatter(d_down, 1, True))[0]
    ends = resid_finish(s, line, rows, width, two.cot, two.attn, two.factor, attn_gain)
    produce(s, line, [s.load(two.g_gate), s.load(two.g_up)], [wg, wu], (512, ff), row_block, dot_nt, 3.6)
    mask = Mask(s, seg_all, seg_cols, 0, count)
    back = attend_back(s, line, one.kvs, one.q, one.heads, one.logsum, mask, rows, width, wo)
    s.run()
    one.g_attn = line.out.value
    two.g_resid, two.g_attn_b, two.g_attn_gain = (h.value for h in ends)
    one.g_q, one.g_kv = (h.value for h in back)

    d_gate = weight_grad((one.mid, two.mid), (one.g_gate, two.g_gate))
    s = Slot("slot8", 8)
    line = Line(s, rows, width, gather=two.g_attn_b)
    g_kv = attach(s, PlaneScatter(one.g_kv, 0, False, done="kv"))[0]
    g_gate = attach(s, PlaneScatter(d_gate, 0, True, lean=True))[0]
    raws = project_back(s, "kv", one.g_q, g_kv, (one.q_raw, one.k_raw), one.qk_factor, norms, cosine, sine, 0, rows, width)
    mask = Mask(s, seg_all, seg_cols, per, count)
    back = attend_back(s, line, two.kvs, two.q, two.heads, two.logsum, mask, rows, width, wo)
    s.run()
    two.g_attn = line.out.value
    one.g_qr, one.g_kr, one.g_vr, one.g_q_gain, one.g_k_gain = (h.value for h in raws)
    two.g_q, two.g_kv = (h.value for h in back)

    d_up = weight_grad((one.mid, two.mid), (one.g_up, two.g_up))
    s = Slot("slot9", 9)
    line = Line(s, rows, width, scatter=True)
    g_kv = attach(s, PlaneScatter(two.g_kv, 0, False, done="kv"))[0]
    g_up = attach(s, PlaneScatter(d_up, 0, True, lean=True))[0]
    fin_one = last_finish(s, line, rows, width, one.g_resid)[0]
    produce(s, line, [s.load(g) for g in (one.g_qr, one.g_kr, one.g_vr)], [wq, wk, wv], (512, width), row_block, dot_nt, 1.6)
    raws = project_back(s, "kv", two.g_q, g_kv, (two.q_raw, two.k_raw), two.qk_factor, norms, cosine, sine, rows, rows, width)
    s.run()
    two.g_qr, two.g_kr, two.g_vr, two.g_q_gain, two.g_k_gain = (h.value for h in raws)

    wides = (one.wide, two.wide)
    grads = [
        weight_grad(wides, (one.g_qr, two.g_qr)),
        weight_grad(wides, (one.g_kr, two.g_kr)),
        weight_grad(wides, (one.g_vr, two.g_vr)),
        weight_grad((one.heads_b, two.heads_b), (one.g_attn, two.g_attn)),
    ]
    s = Slot("slot10", 10)
    line = Line(s, rows, width, scatter=True)
    planes = [attach(s, PlaneScatter(g, i // 3, True))[0] for i, g in enumerate(grads)]
    fin_two = last_finish(s, line, rows, width, two.g_resid)[0]
    produce(s, line, [s.load(g) for g in (two.g_qr, two.g_kr, two.g_vr)], [wq, wk, wv], (512, width), row_block, dot_nt, 1.6)
    s.run()
    g_q, g_k, g_v, g_out = (h.value for h in planes)
    gains = (
        one.g_q_gain + two.g_q_gain,
        one.g_k_gain + two.g_k_gain,
        one.g_attn_gain + two.g_attn_gain,
        one.g_mlp_gain + two.g_mlp_gain,
    )
    gains = lax.psum(tuple(jnp.sum(g, axis=0) for g in gains), ("dp", "ctx"))
    shape = (per, count, width)
    return (
        jnp.concatenate([one.out.reshape(shape), two.out.reshape(shape)], axis=0),
        jnp.concatenate([fin_one.value.reshape(shape), fin_two.value.reshape(shape)], axis=0),
        g_q, g_k, g_v, g_out, g_gate.value, g_up.value, g_down.value, *gains,
    )


def solution(mesh):
    rows, cols = P(("dp", "ctx"), "tp"), P("tp", ("dp", "ctx"))
    act, gain = P("dp", "ctx", "tp"), P("tp")
    size = dict(mesh.shape)
    body = planned if (size["dp"], size["ctx"], size["tp"]) == (2, 4, 4) else general
    return jax.shard_map(
        body,
        mesh=mesh,
        in_specs=(act, act, P("dp", "ctx"), P("dp", "ctx"), rows, rows, rows, cols, rows, rows, cols, gain, gain, gain, gain),
        out_specs=(act, act, rows, rows, rows, cols, rows, rows, cols, gain, gain, gain, gain),
        check_vma=False,
    )
```

```python
import functools
import math

import jax
import jax.numpy as jnp
from jax import lax
from jax.experimental import pallas as pl
from jax.experimental.pallas import tpu as pltpu
from jax.sharding import PartitionSpec as P

D = 2048
HEAD_DIM = 128
EPS = 1e-06
THETA = 500000.0
NEG = -1e30
BF = jnp.bfloat16
F32 = jnp.float32
MESH = pl.DeviceIdType.MESH
HBM = pl.BlockSpec(memory_space=pltpu.HBM)


class Place:
    def __init__(self, tp_size):
        self.n = tp_size
        self.tp = lax.axis_index("tp")
        self.dp = lax.axis_index("dp")
        self.ctx = lax.axis_index("ctx")
        self.slot = self.dp * 4 + self.ctx


def remote(src, dst, sem, send, recv, device):
    return pltpu.make_async_remote_copy(
        src_ref=src, dst_ref=dst, send_sem=sem.at(send), recv_sem=sem.at(recv), device_id=device, device_id_type=MESH
    )


class Step:
    def __init__(self, job, name, link, time, deps, rank, issue=None, arrive=None):
        self.job, self.name, self.link, self.time, self.deps, self.rank = job, name, link, time, deps, rank
        self.issue, self.arrive = issue, arrive


class Plane:
    def __init__(self, slot):
        self.slot = slot
        self.jobs = []
        slot.plane = self
        slot.axes.add("ctx")

    def gather(self, array, dim, with_dp, pieces=1, start=0.0, after=None, done=None, cols=None):
        return self.append(Gather(self.slot, array, dim, with_dp, pieces, start, after, done, cols))

    def scatter(self, array, dim, with_dp, pieces=1, start=0.0, after=None, done=None, out=None):
        return self.append(Scatter(self.slot, array, dim, with_dp, pieces, start, after, done, out))

    def append(self, job):
        job.number = len(self.jobs)
        self.jobs.append(job)
        if job.with_dp:
            self.slot.axes.add("dp")
        self.slot.add(lambda: job.body(self), True)
        return job.out

    def plan(self):
        load = [0.0, 0.0]
        for job in self.jobs:
            load[0] += job.unit * job.pieces
            load[1] += job.unit * job.pieces if job.with_dp else 0.0
        steps = []
        for job in self.jobs:
            for p in range(job.pieces):
                via = 0 if load[0] < load[1] else 1
                if job.with_dp:
                    load[via] += job.unit
                steps += job.steps(p, via)
        times, free, actions = {}, [0.0, 0.0], []
        begun = [0.0, 0.0]
        pending = list(steps)
        while pending:
            best = None
            for step in pending:
                if any((step.job, d) not in times for d in step.deps):
                    continue
                ready = max([step.job.start] + [times[step.job, d] for d in step.deps])
                when_free = ready if step.link is None else max(ready, free[step.link])
                key = (when_free, step.job.number, step.rank)
                if best is None or key < best[0]:
                    best = (key, step, ready, when_free)
            _, step, ready, begin = best
            pending.remove(step)
            end = begin + step.time
            if step.link is not None:
                issue_at = max(ready, begun[step.link])
                begun[step.link], free[step.link] = begin, end
                actions.append((issue_at, 1, len(actions), step.job, step.issue))
            arrive_at = end + (0.7 if step.link is not None else 0.0)
            actions.append((arrive_at, 0, len(actions), step.job, step.arrive))
            times[step.job, step.name] = arrive_at
        actions.sort(key=lambda a: a[:3])
        self.actions = actions
        self.end = max(a[0] for a in actions)


class Job:
    def body(self, plane):
        slot = self.slot
        if not plane.planned:
            plane.plan()
            plane.planned = True
        if self.after is not None:
            yield ("flag", self.after)
        shift = max(0.0, slot.now - self.start) if self.after is not None else 0.0
        yield ("at", self.start)
        self.begin()
        for time, _, _, job, emit in plane.actions:
            if job is self:
                yield ("at", time + shift)
                emit()
        yield ("at", slot.now + 1.0)
        self.finish()
        if self.done is not None:
            slot.mark(self.done)

    def send(self, index, origin, target, device):
        copy = remote(origin, target, self.slot, self.base + 2 * index, self.base + 2 * index + 1, device)
        copy.start()
        self.sent.append(copy)

    def got(self, index, target):
        remote(target, target, self.slot, self.base + 2 * index, self.base + 2 * index + 1, self.cdev).wait_recv()

    def coordinates(self):
        self.dp, self.ctx = self.slot.place.dp, self.slot.place.ctx
        self.xdev, self.ydev, self.cdev = {"ctx": self.ctx ^ 2}, {"dp": self.dp ^ 1}, {"ctx": self.ctx ^ 1}
        self.sent = []


class Gather(Job):
    def __init__(self, slot, array, dim, with_dp, pieces, start, after, done, cols):
        self.slot, self.dim, self.with_dp, self.pieces = slot, dim, with_dp, pieces
        self.start, self.after, self.done = start, after, done
        self.handle = slot.hbm_in(array)
        shape = list(array.shape)
        self.cols = pl.ds(0, shape[1]) if cols is None else pl.ds(*cols)
        if cols is not None:
            shape[1] = cols[1]
        self.size, self.rows = shape[dim], shape[0]
        self.unit = math.prod(shape) * 2 / 43e3 / pieces
        shape[dim] *= 8 if with_dp else 4
        self.out = slot.hbm_out(tuple(shape), array.dtype)
        self.own = slot.sems(1)
        self.base = slot.sems(2 * pieces * 7)

    def spot(self, d, c, p):
        out = self.out.ref
        block = d * 4 + c if self.with_dp else c
        step = self.rows // self.pieces
        if self.dim == 1:
            return out.at[pl.ds(p * step, step), pl.ds(pl.multiple_of(block * self.size, self.size), self.size)]
        return out.at[pl.ds(pl.multiple_of(block * self.size + p * step, step), step)]

    def begin(self):
        self.coordinates()
        self.source = src = self.handle.ref.at[:, self.cols]
        step = self.rows // self.pieces
        for p in range(self.pieces):
            part = pl.ds(p * step, step)
            self.send(7 * p, src.at[part], self.spot(self.dp, self.ctx, p), self.cdev)
        if self.dim == 1:
            mine = self.out.ref.at[:, pl.ds(pl.multiple_of((self.dp * 4 + self.ctx) * self.size, self.size), self.size)]
        else:
            block = self.dp * 4 + self.ctx if self.with_dp else self.ctx
            mine = self.out.ref.at[pl.ds(pl.multiple_of(block * self.size, self.size), self.size)]
        self.kept = pltpu.make_async_copy(src, mine, self.slot.sem(self.own))
        self.kept.start()

    def steps(self, p, via):
        def direct(k, device):
            def issue():
                step = self.rows // self.pieces
                part = pl.ds(p * step, step)
                self.send(7 * p + 1 + k, self.source.at[part], self.spot(self.dp, self.ctx, p), device())

            return issue

        def forward(k, place):
            def arrive():
                here = self.spot(*place(), p)
                self.got(7 * p + 1 + k, here)
                self.send(7 * p + 4 + k, here, here, self.cdev)

            return arrive

        from_x = lambda: (self.dp, self.ctx ^ 2)
        from_y = lambda: (self.dp ^ 1, self.ctx)
        corner = lambda: (self.dp ^ 1, self.ctx ^ 2)
        xdev, ydev = (lambda: self.xdev), (lambda: self.ydev)
        out = [Step(self, (p, 0), 0, self.unit, [], 2 * p, direct(0, xdev), forward(0, from_x))]
        if self.with_dp:
            out.append(Step(self, (p, 1), 1, self.unit, [], 2 * p, direct(1, ydev), forward(1, from_y)))

            def hop():
                here = self.spot(*(from_y() if via == 0 else from_x()), p)
                self.send(7 * p + 3, here, here, self.xdev if via == 0 else self.ydev)

            out.append(Step(self, (p, 2), via, self.unit, [(p, 1 - via)], 2 * p + 1, hop, forward(2, corner)))
        return out

    def finish(self):
        for p in range(self.pieces):
            self.got(7 * p, self.spot(self.dp, self.ctx ^ 1, p))
            self.got(7 * p + 4, self.spot(self.dp, self.ctx ^ 3, p))
            if self.with_dp:
                self.got(7 * p + 5, self.spot(self.dp ^ 1, self.ctx ^ 1, p))
                self.got(7 * p + 6, self.spot(self.dp ^ 1, self.ctx ^ 3, p))
        for copy in self.sent:
            copy.wait_send()
        self.kept.wait()


class Scatter(Job):
    def __init__(self, slot, array, dim, with_dp, pieces, start, after, done, out):
        self.slot, self.dim, self.with_dp, self.pieces = slot, dim, with_dp, pieces
        self.start, self.after, self.done = start, after, done
        self.source = slot.hbm_in(array)
        shape = list(array.shape)
        self.chips = chips = 4 if with_dp else 2
        shape[dim] //= 2 * chips
        self.size = shape[dim]
        self.rows, self.width = shape
        self.unit = math.prod(shape) * 2 / 43e3 / pieces
        if out is None:
            self.out, self.where = slot.hbm_out(tuple(shape), F32), None
        else:
            self.out, self.where = out
        block = tuple(shape)
        self.mine, self.came = slot.vmem((chips,) + block, BF), slot.vmem((chips,) + block, BF)
        self.chip_in = slot.vmem((chips // 2,) + block, BF)
        self.diag = slot.vmem(block, BF) if with_dp else None
        self.total = slot.vmem(block, F32)
        self.loads = slot.sems(chips * pieces)
        self.outs = slot.sems(pieces)
        self.base = slot.sems(2 * pieces * (chips + 3))

    def spot(self, q, c, p):
        x = (self.ctx >> 1) ^ (q & 1)
        d = self.dp ^ (q >> 1)
        block = d * 4 + x * 2 + c if self.with_dp else x * 2 + c
        step = self.rows // self.pieces
        if self.dim == 1:
            return self.source.ref.at[pl.ds(p * step, step), pl.ds(pl.multiple_of(block * self.size, self.size), self.size)]
        return self.source.ref.at[pl.ds(pl.multiple_of(block * self.size + p * step, step), step)]

    def part(self, p):
        step = self.rows // self.pieces
        return pl.ds(p * step, step)

    def load(self, q, p):
        core = self.ctx & 1
        return pltpu.make_async_copy(
            self.spot(q, core, p), self.mine.ref.at[q, self.part(p)], self.slot.sem(self.loads + q * self.pieces + p)
        )

    def begin(self):
        self.coordinates()
        core = self.ctx & 1
        self.order = (3, 1, 2, 0) if self.with_dp else (1, 0)
        self.per = self.chips + 3
        for p in range(self.pieces):
            for q in self.order:
                self.send(self.per * p + q, self.spot(q, core ^ 1, p), self.came.ref.at[q, self.part(p)], self.cdev)
                self.load(q, p).start()

    def add(self, into, other, p):
        step = self.rows // self.pieces
        tile = min(32, step)

        @pl.loop(0, step // tile)
        def _(i):
            part = pl.ds(pl.multiple_of(p * step + i * tile, tile), tile)
            into[part] = (into[part].astype(F32) + other[part].astype(F32)).astype(BF)

    def steps(self, p, via):
        mine, came = self.mine, self.came

        def cores():
            for q in self.order:
                self.load(q, p).wait()
                self.got(self.per * p + q, came.ref.at[q, self.part(p)])
                self.add(mine.ref.at[q], came.ref.at[q], p)

        def out(k, q, target, device):
            def issue():
                self.send(self.per * p + self.chips + k, mine.ref.at[q, self.part(p)], target(), device())

            return issue

        xdev, ydev = (lambda: self.xdev), (lambda: self.ydev)
        into = lambda j: (lambda: self.chip_in.ref.at[j, self.part(p)])
        done = {}

        def last(k, j):
            def arrive():
                self.got(self.per * p + self.chips + k, self.chip_in.ref.at[j, self.part(p)])
                done[j] = True
                if len(done) == self.chips // 2:
                    done.clear()
                    self.close(p)

            return arrive

        steps = [Step(self, (p, "c"), None, 2.0 + self.unit * 0.5, [], 3 * p, None, cores)]
        if not self.with_dp:
            steps.append(Step(self, (p, 0), 0, self.unit, [(p, "c")], 3 * p + 1, out(0, 1, into(0), xdev), last(0, 0)))
            return steps
        corner = lambda: self.diag.ref.at[self.part(p)]

        def fold():
            self.got(self.per * p + self.chips + 2, corner())
            self.add(mine.ref.at[2 if via == 0 else 1], self.diag.ref, p)

        steps.append(
            Step(self, (p, 2), via, self.unit, [(p, "c")], 3 * p, out(2, 3, corner, xdev if via == 0 else ydev), fold)
        )
        for k, device in ((0, xdev), (1, ydev)):
            deps = [(p, "c")] if k == via else [(p, 2)]
            steps.append(Step(self, (p, k), k, self.unit, deps, 3 * p + 1, out(k, 1 + k, into(k), device), last(k, k)))
        return steps

    def result(self, p):
        target = self.out.ref
        step = self.rows // self.pieces
        if self.where is None:
            target = target.at[pl.ds(p * step, step)]
        else:
            row, col = self.where
            target = target.at[pl.ds(row + p * step, step), pl.ds(col, self.width)]
        return pltpu.make_async_copy(self.total.ref.at[self.part(p)], target, self.slot.sem(self.outs + p))

    def close(self, p):
        step = self.rows // self.pieces
        tile = min(32, step)
        mine, chip_in, total = self.mine.ref, self.chip_in.ref, self.total.ref

        @pl.loop(0, step // tile)
        def _(i):
            part = pl.ds(pl.multiple_of(p * step + i * tile, tile), tile)
            value = mine[0, part].astype(F32) + chip_in[0, part].astype(F32)
            if self.with_dp:
                value = value + chip_in[1, part].astype(F32)
            total[part] = value

        self.result(p).start()

    def finish(self):
        for copy in self.sent:
            copy.wait_send()
        for p in range(self.pieces):
            self.result(p).wait()


class Handle:
    ref = None
    sem = None
    waited = False
    lazy = False
    value = None

    def __init__(self, shape=None, dtype=None):
        self.shape, self.dtype = shape, dtype


class Slot:
    def __init__(self, name, ident):
        self.name, self.ident = name, ident
        self.inputs, self.outputs, self.scratch = [], [], []
        self.sem_count = 0
        self.tasks = []
        self.axes = set()
        self.early = []
        self.plane = None
        self.loads, self.stores = [], []
        self.flags = {}
        self.now = 0.0

    def sems(self, number):
        first = self.sem_count
        self.sem_count += number
        return first

    def hbm_in(self, array):
        if isinstance(array, Handle):
            return array
        handle = Handle(array.shape, array.dtype)
        self.inputs.append((array, handle))
        return handle

    def hbm_out(self, shape, dtype):
        handle = Handle(shape, dtype)
        self.outputs.append((jax.ShapeDtypeStruct(shape, dtype), handle))
        return handle

    def vmem(self, shape, dtype):
        handle = Handle(shape, dtype)
        self.scratch.append((pltpu.VMEM(shape, dtype), handle))
        return handle

    def load(self, array):
        handle = self.vmem(array.shape, array.dtype)
        handle.source = self.hbm_in(array)
        handle.sem = self.sems(1)
        self.loads.append(handle)
        return handle

    def store(self, shape, dtype):
        handle = self.vmem(shape, dtype)
        handle.target = self.hbm_out(shape, dtype)
        handle.sem = self.sems(1)
        self.stores.append(handle)
        return handle

    def late(self, array):
        handle = self.vmem(array.shape, array.dtype)
        handle.source = self.hbm_in(array)
        handle.sem = self.sems(1)
        handle.lazy = True
        self.loads.append(handle)
        return handle

    def fetch(self, *handles):
        for handle in handles:
            pltpu.make_async_copy(handle.source.ref, handle.ref, self.sem(handle.sem)).start()

    def need(self, *handles):
        for handle in handles:
            if not handle.waited:
                handle.waited = True
                pltpu.make_async_copy(handle.source.ref, handle.ref, self.sem(handle.sem)).wait()

    def flush(self, *handles):
        for handle in handles:
            pltpu.make_async_copy(handle.ref, handle.target.ref, self.sem(handle.sem)).start()

    def sem(self, index):
        return self.sem_ref.at[index]

    def at(self, index):
        return self.sem_ref.at[index]

    def add(self, body, transfers=False):
        self.tasks.append((body, transfers))

    def mark(self, flag):
        self.flags[flag] = True

    def mark_early(self, flag):
        self.early.append(flag)

    def kernel(self, *refs):
        refs = list(refs)
        for group in (self.inputs, self.outputs, self.scratch):
            for _, handle in group:
                handle.ref = refs.pop(0)
        self.sem_ref = refs.pop(0)
        self.flags, self.now = {flag: True for flag in self.early}, 0.0
        for handle in self.loads:
            handle.waited = False
            if not handle.lazy:
                pltpu.make_async_copy(handle.source.ref, handle.ref, self.sem(handle.sem)).start()
        self.place = place = Place(4)
        barrier = pltpu.get_barrier_semaphore()
        peers = []
        if "ctx" in self.axes:
            peers += [{"ctx": place.ctx ^ 1}, {"ctx": place.ctx ^ 2}]
        if "dp" in self.axes:
            peers += [{"dp": place.dp ^ 1}]
        if "tp" in self.axes:
            peers += [{"tp": place.tp ^ k} for k in (1, 2, 3)]
        for device in peers:
            pl.semaphore_signal(barrier, inc=1, device_id=device, device_id_type=MESH)
        pl.semaphore_wait(barrier, len(peers))
        if self.plane is not None:
            self.plane.planned = False
        running = [[("at", 0.0), task(), 0 if transfers else 1, i] for i, (task, transfers) in enumerate(self.tasks)]
        while running:
            ready = None
            for entry in running:
                kind, value = entry[0]
                if (kind == "at" and value <= self.now) or (kind == "flag" and value in self.flags):
                    key = (entry[2], value if kind == "at" and entry[2] == 0 else 0.0, entry[3])
                    if ready is None or key < ready[0]:
                        ready = (key, entry)
            if ready is None:
                self.now = min(entry[0][1] for entry in running if entry[0][0] == "at")
                continue
            entry = ready[1]
            try:
                got = next(entry[1])
            except StopIteration:
                running.remove(entry)
                continue
            if got[0] == "did":
                self.now += got[1]
                got = ("at", self.now)
            entry[0] = got
        for handle in self.stores:
            pltpu.make_async_copy(handle.ref, handle.target.ref, self.sem(handle.sem)).wait()

    def run(self):
        values = pl.pallas_call(
            self.kernel,
            out_shape=tuple(o for o, _ in self.outputs),
            in_specs=[HBM] * len(self.inputs),
            out_specs=tuple([HBM] * len(self.outputs)),
            scratch_shapes=[s for s, _ in self.scratch] + [pltpu.SemaphoreType.DMA((self.sem_count,))],
            compiler_params=pltpu.CompilerParams(
                collective_id=self.ident, has_side_effects=True, vmem_limit_bytes=62 * 1024 * 1024
            ),
            name=self.name,
        )(*[a for a, _ in self.inputs])
        for (_, handle), value in zip(self.outputs, values):
            handle.value = value


def any_of(me, values):
    values = sorted(values)
    cond = me == values[0]
    for v in values[1:]:
        cond = jnp.logical_or(cond, me == v)
    return cond


def pick(me, table):
    items = sorted(table.items())
    out = jnp.int32(items[0][1])
    for key, value in items[1:]:
        out = jnp.where(me == key, jnp.int32(value), out)
    return out


PAIR = {0: ["A0", "R3", "R2", "R1"], 1: ["A1", "A0", "R3", "R2"], 2: ["A2", "A1", "A0", "R3"]}
ONLY_A = {0: ["A0", "", ""], 1: ["A1", "A0", ""], 2: ["A2", "A1", "A0"]}
ONLY_R = {0: ["R3", "R2", "R1"], 1: ["", "R3", "R2"], 2: ["", "", "R3"]}


class Line:
    def __init__(self, slot, rows, width, gather=None, scatter=False, pieces=2, keep=True):
        self.slot, self.rows, self.width, self.pieces = slot, rows, width, pieces
        self.gather, self.scatter = gather is not None, scatter
        slot.axes.add("tp")
        right = PAIR if self.gather and scatter else (ONLY_A if self.gather else ONLY_R)
        flip = lambda m: m if not m else m[0] + str(3 - int(m[1]))
        self.tables = (right, {3 - d: [flip(m) for m in row] for d, row in right.items()})
        self.steps = len(right[0])
        self.keep = keep
        if self.gather:
            self.source = slot.hbm_in(gather)
            self.wide = slot.vmem((4, rows, width), BF)
            self.own_sem = slot.sems(1)
            if keep:
                self.out = slot.hbm_out((rows, 4 * width), BF)
                self.out_sem = slot.sems(4)
        if scatter:
            self.mine = slot.vmem((4, rows, width), BF)
            self.skip = self.steps - 3
            self.came = slot.vmem((2, 3, rows, width), BF)
        self.base = slot.sems(4 * self.steps * pieces)
        self.unit = rows * width * 4 / 88e3
        slot.add(self.body, True)

    def chunk(self, k):
        me = self.slot.place.tp
        return (me, pick(me, {0: 1, 1: 2, 2: 1, 3: 2}), pick(me, {0: 2, 1: 0, 2: 3, 3: 1}), pick(me, {0: 3, 1: 3, 2: 0, 3: 0}))[k]

    def index(self, way, t, p):
        return self.base + 2 * ((way * self.steps + t) * self.pieces + p)

    def part(self, p):
        step = self.rows // self.pieces
        return pl.ds(p * step, step)

    def sends(self, t, p):
        me = self.slot.place.tp
        rows = self.part(p)
        for way in (0, 1):
            for kind in "AR":
                table = {d: int(row[t][1]) for d, row in self.tables[way].items() if row[t][:1] == kind}
                if not table:
                    continue
                block = pick(me, table)
                if kind == "A":
                    target = self.wide.ref.at[block, rows]
                    origin = self.source.ref.at[rows] if t == 0 else target
                else:
                    target = self.came.ref.at[way, t - self.skip, rows]
                    origin = self.mine.ref.at[block, rows]
                index = self.index(way, t, p)
                to = me + 1 if way == 0 else me - 1
                yield kind, any_of(me, table), remote(origin, target, self.slot, index, index + 1, {"tp": to})

    def arrivals(self, t, p):
        me = self.slot.place.tp
        rows = self.part(p)
        step = self.rows // self.pieces
        tile = 64
        for way in (0, 1):
            off = 1 if way == 0 else -1
            froms = {d + off: row[t] for d, row in self.tables[way].items() if row[t]}
            sample = self.wide.ref.at[0, rows] if self.gather else self.came.ref.at[0, 0, rows]
            index = self.index(way, t, p)
            pl.when(any_of(me, froms))(remote(sample, sample, self.slot, index, index + 1, {"tp": me}).wait_recv)
            adds = {d: int(m[1]) for d, m in froms.items() if m[0] == "R" and int(m[1]) != d}
            if adds:
                block = pick(me, adds)
                mine, came = self.mine.ref, self.came.ref

                @pl.when(any_of(me, adds))
                def _():
                    @pl.loop(0, step // tile)
                    def _(i):
                        part = pl.ds(pl.multiple_of(p * step + i * tile, tile), tile)
                        mine[block, part] = (mine[block, part].astype(F32) + came[way, t - self.skip, part].astype(F32)).astype(BF)

    def body(self):
        slot = self.slot
        me = slot.place.tp
        if self.gather:
            own = pltpu.make_async_copy(self.source.ref, self.wide.ref.at[me], slot.sem(self.own_sem))
            own.start()
        start = 0.0
        for t in range(self.steps):
            for p in range(self.pieces):
                if t > 0:
                    yield ("at", start + (t - 1 + (p + 1) / self.pieces) * self.unit + 0.5)
                    self.arrivals(t - 1, p)
                    if p == self.pieces - 1 and self.gather and t <= 3:
                        slot.mark("chunk%d" % t)
                messages = list(self.sends(t, p))
                for kind, cond, copy in messages:
                    if kind == "A":
                        pl.when(cond)(copy.start)
                if any(kind == "R" for kind, _, _ in messages):
                    first = t == (1 if self.gather else 0)
                    if p == 0:
                        for c in ((3, 0) if first else (2, 1)):
                            yield ("flag", "part%d" % c)
                        start = max(start, slot.now - t * self.unit)
                    for kind, cond, copy in messages:
                        if kind == "R":
                            pl.when(cond)(copy.start)
                if t == 0 and p == 0 and self.gather:
                    yield ("at", 1.0)
                    own.wait()
                    slot.mark("chunk0")
        for p in range(self.pieces):
            yield ("at", start + (self.steps - 1 + (p + 1) / self.pieces) * self.unit + 0.5)
            self.arrivals(self.steps - 1, p)
        if self.gather and self.steps == 3:
            slot.mark("chunk3")
        if self.scatter:
            slot.mark("reduced")
        outs = []
        if self.gather and self.keep:
            for c in range(4):
                where = self.out.ref.at[:, pl.ds(c * self.width, self.width)]
                outs.append(pltpu.make_async_copy(self.wide.ref.at[c], where, slot.sem(self.out_sem + c)))
                outs[-1].start()
        yield ("at", start + self.steps * self.unit + 1.0)
        for t in range(self.steps):
            for p in range(self.pieces):
                for _, cond, copy in self.sends(t, p):
                    pl.when(cond)(copy.wait_send)
        for copy in outs:
            copy.wait()

    def total(self, part):
        me = self.slot.place.tp
        last = 2
        left = jnp.where(me > 0, self.came.ref[0, last, part].astype(F32), 0.0)
        right = jnp.where(me < 3, self.came.ref[1, last, part].astype(F32), 0.0)
        return self.mine.ref[me, part].astype(F32) + left + right


def tiled(count, tile, body):
    @pl.loop(0, count // tile)
    def _(i):
        body(pl.ds(pl.multiple_of(i * tile, tile), tile))


class Weights:
    def __init__(self, slot, arrays, shape, order, where):
        self.slot, self.order, self.where = slot, order, where
        self.arrays = [slot.hbm_in(a) for a in arrays]
        self.buffer = slot.vmem((2, len(arrays)) + shape, BF)
        self.base = slot.sems(2 * len(arrays))
        self.step = 0

    def copies(self, step):
        block = self.order[step] if not callable(self.order) else self.order(step)
        for j, array in enumerate(self.arrays):
            yield pltpu.make_async_copy(
                self.where(array.ref, block),
                self.buffer.ref.at[step % 2, j],
                self.slot.sem(self.base + 2 * j + step % 2),
            )

    def start(self, step):
        for copy in self.copies(step):
            copy.start()

    def take(self, step):
        for copy in self.copies(step):
            copy.wait()
        return [self.buffer.ref.at[step % 2, j] for j in range(len(self.arrays))]


def row_block(ref, c):
    return ref.at[pl.ds(pl.multiple_of(c * 512, 512), 512)]


def col_block(ref, c):
    return ref.at[:, pl.ds(pl.multiple_of(c * 512, 512), 512)]


def consume(slot, line, arrays, shape, where, last, multiply, cost, flag):
    weights = Weights(slot, arrays, shape, line.chunk, where)

    def body():
        weights.start(0)
        for k in range(4):
            if k < 3:
                weights.start(k + 1)
            yield ("flag", "chunk%d" % k)
            blocks = weights.take(k)
            chunk = line.chunk(k)
            for j, block in enumerate(blocks):
                multiply(k == 0, line.wide.ref.at[chunk], block, j)
                yield ("did", cost)
        yield from last()
        slot.mark(flag)

    slot.add(body)


def dot_nn(left, right):
    return jnp.dot(left, right, preferred_element_type=F32)


def dot_nt(left, right):
    return lax.dot_general(left, right, (((1,), (1,)), ((), ())), preferred_element_type=F32)


def produce(slot, line, lefts, arrays, shape, where, dot, cost):
    order = (3, 0, 2, 1)
    weights = Weights(slot, arrays, shape, order, where)
    each = len(arrays) // len(lefts)

    def body():
        weights.start(0)
        slot.need(*lefts)
        for k, c in enumerate(order):
            if k < 3:
                weights.start(k + 1)
            blocks = weights.take(k)
            value = None
            for j, block in enumerate(blocks):
                left = lefts[j // each].ref
                wide = left.shape[1] // each
                term = dot(left[:, pl.ds((j % each) * wide, wide)], block[...])
                value = term if value is None else value + term
            line.mine.ref[c] = value.astype(BF)
            yield ("did", cost)
            slot.mark("part%d" % c)

    slot.add(body)


def weight_grad(slot, lefts, rights, out, where, flags, cost):
    buffer = slot.vmem(out[1], BF)
    base = slot.sems(1)

    def body():
        slot.need(*lefts, *rights)
        tall, wide = out[1]
        for k, (rows, cols) in enumerate(where):
            target = buffer.ref

            @pl.loop(0, (tall // 512) * (wide // 512))
            def _(i):
                r, c = (i, 0) if wide == 512 else (0, i)
                row = pl.ds(pl.multiple_of(rows + r * 512, 512), 512)
                col = pl.ds(pl.multiple_of(cols + c * 512, 512), 512)
                value = dot_tn(lefts[0].ref[:, row], rights[0].ref[:, col])
                value = value + dot_tn(lefts[1].ref[:, row], rights[1].ref[:, col])
                here = (pl.ds(pl.multiple_of(r * 512, 512), 512), pl.ds(pl.multiple_of(c * 512, 512), 512))
                target[here] = value.astype(BF)

            copy = pltpu.make_async_copy(target, out[0][k].ref, slot.sem(base))
            copy.start()
            yield ("did", cost)
            copy.wait()
            slot.mark(flags[k])

    slot.add(body)


class RowTotals:
    def __init__(self, slot, rows):
        self.slot, self.rows = slot, rows
        self.stat = slot.vmem((rows, 128), F32)
        self.send = slot.vmem((8, rows), F32)
        self.came = slot.vmem((3, 8, rows), F32)
        self.total = slot.vmem((rows, 128), F32)
        self.base = slot.sems(6)

    def put(self, part, *columns):
        lane = lax.broadcasted_iota(jnp.int32, (columns[0].shape[0], 128), 1)
        value = jnp.zeros((columns[0].shape[0], 128), F32)
        for k, column in enumerate(columns):
            value = jnp.where(lane == k, column, value)
        self.stat.ref[part] = value

    def exchange(self):
        slot, me = self.slot, self.slot.place.tp
        send = self.send.ref
        send[...] = jnp.transpose(self.stat.ref[...])[0:8]
        copies = []
        for k in (1, 2, 3):
            copies.append(
                remote(send, self.came.ref.at[k - 1], slot, self.base + 2 * (k - 1), self.base + 2 * (k - 1) + 1, {"tp": me ^ k})
            )
            copies[-1].start()
        yield ("at", slot.now + 2.5)
        for copy in copies:
            copy.wait()
        total = send[...] + self.came.ref[0] + self.came.ref[1] + self.came.ref[2]
        wide = jnp.concatenate([total, jnp.zeros((120, self.rows), F32)], axis=0)
        self.total.ref[...] = jnp.transpose(wide)

    def column(self, part, k):
        return self.total.ref[part, k : k + 1]


def attn_finish(slot, line, rows, width, x, gain):
    x, gain = slot.load(x), slot.load(gain.reshape(1, width))
    raw, resid = slot.store((rows, width), F32), slot.store((rows, width), F32)
    resid_b, factor = slot.store((rows, width), BF), slot.store((rows, 128), F32)
    totals = RowTotals(slot, rows)

    def body():
        yield ("flag", "reduced")

        def first(part):
            value = line.total(part)
            raw.ref[part] = value
            totals.put(part, jnp.sum(value * value, axis=1, keepdims=True))

        tiled(rows, 32, first)
        slot.need(x, gain)
        slot.flush(raw)
        yield from totals.exchange()

        def second(part):
            scale = lax.rsqrt(totals.column(part, 0) / D + EPS)
            value = x.ref[part].astype(F32) + raw.ref[part] * scale * gain.ref[...]
            resid.ref[part] = value
            resid_b.ref[part] = value.astype(BF)
            factor.ref[part] = jnp.broadcast_to(scale, (32, 128))

        tiled(rows, 32, second)
        slot.flush(resid_b, resid, factor)

    slot.add(body)
    return [raw.target, resid.target, resid_b.target, factor.target]


def mlp_finish(slot, line, rows, width, resid, cot, gain):
    resid, cot, gain = slot.load(resid), slot.load(cot), slot.load(gain.reshape(1, width))
    raw = slot.vmem((rows, width), F32)
    out, grad = slot.store((rows, width), BF), slot.store((rows, width), BF)
    gain_grad = slot.store((8, width), F32)
    totals = RowTotals(slot, rows)

    def body():
        yield ("flag", "reduced")
        slot.need(resid, cot, gain)

        def first(part):
            value = line.total(part)
            raw.ref[part] = value
            scaled = cot.ref[part].astype(F32) * gain.ref[...]
            totals.put(part, jnp.sum(value * value, axis=1, keepdims=True), jnp.sum(scaled * value, axis=1, keepdims=True))

        tiled(rows, 32, first)
        gain_grad.ref[...] = jnp.zeros((8, width), F32)
        yield from totals.exchange()

        def second(part):
            scale = lax.rsqrt(totals.column(part, 0) / D + EPS)
            inner = totals.column(part, 1)
            value = raw.ref[part]
            given = cot.ref[part].astype(F32)
            normed = value * scale
            grad.ref[part] = (scale * (given * gain.ref[...]) - value * (scale * scale * scale * inner / D)).astype(BF)
            out.ref[part] = (resid.ref[part] + normed * gain.ref[...]).astype(BF)
            terms = given * normed
            for i in range(4):
                gain_grad.ref[...] += terms[8 * i : 8 * i + 8]

        tiled(rows, 32, second)
        slot.flush(grad, out, gain_grad)

    slot.add(body)
    return [out.target, grad.target, gain_grad.target]


def resid_finish(slot, line, rows, width, cot, attn, factor, gain):
    cot, attn, factor, gain = slot.load(cot), slot.load(attn), slot.load(factor), slot.load(gain.reshape(1, width))
    resid, grad = slot.store((rows, width), F32), slot.store((rows, width), BF)
    gain_grad = slot.store((8, width), F32)
    totals = RowTotals(slot, rows)

    def body():
        yield ("flag", "reduced")
        slot.need(cot, attn, factor, gain)

        def first(part):
            value = line.total(part) + cot.ref[part].astype(F32)
            resid.ref[part] = value
            totals.put(part, jnp.sum(value * gain.ref[...] * attn.ref[part], axis=1, keepdims=True))

        tiled(rows, 32, first)
        gain_grad.ref[...] = jnp.zeros((8, width), F32)
        slot.flush(resid)
        yield from totals.exchange()

        def second(part):
            scale = factor.ref[part, 0:1]
            inner = totals.column(part, 0)
            value, given = attn.ref[part], resid.ref[part]
            grad.ref[part] = (scale * (given * gain.ref[...]) - value * (scale * scale * scale * inner / D)).astype(BF)
            terms = given * value * scale
            for i in range(4):
                gain_grad.ref[...] += terms[8 * i : 8 * i + 8]

        tiled(rows, 32, second)
        slot.flush(grad, gain_grad)

    slot.add(body)
    return [resid.target, grad.target, gain_grad.target]


def last_finish(slot, line, rows, width, resid):
    resid = slot.load(resid)
    out = slot.store((rows, width), BF)

    def body():
        yield ("flag", "reduced")
        slot.need(resid)

        def first(part):
            out.ref[part] = (line.total(part) + resid.ref[part]).astype(BF)

        tiled(rows, 32, first)
        slot.flush(out)

    slot.add(body)
    return [out.target]


def given_partial(slot, line, array):
    source = slot.hbm_in(array)
    base = slot.sems(4)

    def body():
        copies = {}
        for c in (3, 0, 2, 1):
            copies[c] = pltpu.make_async_copy(
                source.ref.at[:, pl.ds(c * line.width, line.width)], line.mine.ref.at[c], slot.sem(base + c)
            )
            copies[c].start()
        yield ("at", 1.0)
        for c in (3, 0, 2, 1):
            copies[c].wait()
            slot.mark("part%d" % c)

    slot.add(body)


def gate_up(slot, line, rows, w_gate, w_up):
    parts, wide = len(w_gate), w_gate[0].shape[1]
    ff = parts * wide
    acc = slot.vmem((2, rows, ff), F32)
    gate, up, act = (slot.store((rows, ff), BF) for _ in range(3))

    def multiply(first, left, block, j):
        cols = pl.ds((j % parts) * wide, wide)
        value = dot_nn(left[...], block[...])
        acc.ref[j // parts, :, cols] = value if first else acc.ref[j // parts, :, cols] + value

    def last():
        half = rows // 2
        for h in (0, 1):

            @pl.loop(0, half // 16)
            def _(i):
                part = pl.ds(pl.multiple_of(h * half + i * 16, 16), 16)
                g, u = acc.ref[0, part], acc.ref[1, part]
                gate.ref[part] = g.astype(BF)
                up.ref[part] = u.astype(BF)
                act.ref[part] = (g * jax.nn.sigmoid(g) * u).astype(BF)

            yield ("did", 2.0)
        slot.flush(act, gate, up)

    consume(slot, line, tuple(w_gate) + tuple(w_up), (512, wide), row_block, last, multiply, 0.6, "mlp")
    return [gate.target, up.target, act.target]


def act_back(slot, line, rows, w_down, gate, up):
    ff = w_down.shape[0]
    acc = slot.vmem((rows, ff), F32)
    gate, up = slot.load(gate), slot.load(up)
    g_gate, g_up = slot.store((rows, ff), BF), slot.store((rows, ff), BF)

    def multiply(first, left, block, j):
        @pl.loop(0, ff // 1024)
        def _(i):
            cols = pl.ds(pl.multiple_of(i * 1024, 1024), 1024)
            value = dot_nt(left[...], block[cols])
            acc.ref[:, cols] = value if first else acc.ref[:, cols] + value

    def last():
        slot.need(gate, up)
        half = rows // 2
        for h in (0, 1):

            @pl.loop(0, half // 16)
            def _(i):
                part = pl.ds(pl.multiple_of(h * half + i * 16, 16), 16)
                grad, g, u = acc.ref[part], gate.ref[part].astype(F32), up.ref[part].astype(F32)
                sigma = jax.nn.sigmoid(g)
                g_gate.ref[part] = (grad * u * sigma * (1.0 + g * (1.0 - sigma))).astype(BF)
                g_up.ref[part] = (grad * g * sigma).astype(BF)

            yield ("did", 2.5)
        slot.flush(g_gate, g_up)

    consume(slot, line, (w_down,), (ff, 512), col_block, last, multiply, 2.4, "back")
    return [g_gate.target, g_up.target]


def half_turn(value):
    return pltpu.roll(value, HEAD_DIM // 2, axis=1)


def tables(slot, positions, freqs, sign):
    count = positions.shape[0]
    positions, freqs, sign = slot.load(positions), slot.load(freqs), slot.load(sign)
    cosine, sine = slot.store((count, HEAD_DIM), F32), slot.store((count, HEAD_DIM), F32)

    def body():
        slot.need(positions, freqs, sign)

        def first(part):
            angle = positions.ref[part].astype(F32) * freqs.ref[...]
            cosine.ref[part] = jnp.cos(angle)
            sine.ref[part] = jnp.sin(angle) * sign.ref[...]

        tiled(count, 32, first)
        slot.flush(cosine, sine)
        yield ("did", 6.0)
        slot.mark("tables")

    slot.add(body)
    return cosine, sine


def head_cols(h):
    return pl.ds(h * HEAD_DIM, HEAD_DIM)


def project(slot, line, rows, width, weights, flags, gains, cosine, sine, first_row):
    stages = [slot.late(w) for w in weights]
    gains = [slot.load(g.reshape(1, width)) for g in gains]
    raws = [slot.store((rows, width), F32) for _ in (0, 1)]
    query, kv = slot.store((rows, width), BF), slot.store((rows, 2 * width), BF)
    factor = slot.store((rows, 128), F32)
    totals = RowTotals(slot, rows)
    half = rows // 2

    def body():
        for j in range(3):
            if flags is not None:
                yield ("flag", flags[j])
            slot.fetch(stages[j])
        yield ("flag", "chunk3")
        wide = line.wide.ref
        for j in range(3):
            slot.need(stages[j])
            weight = stages[j].ref

            @pl.loop(0, 2)
            def _(i):
                part = pl.ds(pl.multiple_of(i * half, half), half)
                value = dot_nn(wide[0, part], weight[0:width])
                for c in (1, 2, 3):
                    value = value + dot_nn(wide[c, part], weight[c * width : (c + 1) * width])
                if j < 2:
                    raws[j].ref[part] = value
                else:
                    kv.ref[part, width : 2 * width] = value.astype(BF)

            yield ("did", 2.0)

        def first(part):
            q, k = raws[0].ref[part], raws[1].ref[part]
            totals.put(part, jnp.sum(q * q, axis=1, keepdims=True), jnp.sum(k * k, axis=1, keepdims=True))

        tiled(rows, 32, first)
        slot.flush(*raws)
        yield from totals.exchange()
        yield ("flag", "tables")
        slot.need(*gains)
        slot.need(*[t for t in (cosine, sine) if hasattr(t, "source")])

        def second(part, trig):
            lane = lax.broadcasted_iota(jnp.int32, (32, 128), 1)
            scales = [lax.rsqrt(totals.column(part, j) / D + EPS) for j in (0, 1)]
            factor.ref[part] = jnp.where(lane == 0, scales[0], scales[1])
            co, si = cosine.ref[trig], sine.ref[trig]
            for j, target in ((0, query), (1, kv)):
                for h in range(width // HEAD_DIM):
                    value = raws[j].ref[part, head_cols(h)] * scales[j] * gains[j].ref[:, head_cols(h)]
                    target.ref[part, head_cols(h)] = (value * co + half_turn(value) * si).astype(BF)

        @pl.loop(0, rows // 32)
        def _(i):
            second(pl.ds(pl.multiple_of(i * 32, 32), 32), pl.ds(pl.multiple_of(first_row + i * 32, 32), 32))

        slot.flush(kv, query, factor)

    slot.add(body)
    return [raws[0].target, raws[1].target, query.target, kv.target, factor.target]


class Mask:
    def __init__(self, slot, seg_all, seg_cols, first, count):
        self.slot, self.first, self.count = slot, first, count
        self.keys, self.mine = slot.load(seg_all), slot.load(seg_cols)
        self.mask = slot.vmem((count, 4 * count), F32)

    def fill(self, s):
        self.slot.need(self.keys, self.mine)
        count = self.count
        ctx = self.slot.place.ctx
        mine = self.mine.ref[(self.first + s) * count : (self.first + s + 1) * count, 0:1]
        for c in range(4):
            keys = self.keys.ref[8 * c + self.first + s : 8 * c + self.first + s + 1, :]
            row = ctx * count + lax.broadcasted_iota(jnp.int32, (count, count), 0)
            col = c * count + lax.broadcasted_iota(jnp.int32, (count, count), 1)
            fine = jnp.logical_and(mine == keys, row >= col)
            self.mask.ref[:, c * count : (c + 1) * count] = jnp.where(fine, 0.0, NEG)


def attend(slot, flag, kv, query, mask, rows, width):
    kv, query = slot.late(kv), slot.load(query)
    count = mask.count
    heads, heads_b = slot.store((rows, width), F32), slot.store((rows, width), BF)
    logsum = slot.store((rows, 128), F32)
    logits = slot.vmem((count, 4 * count), F32)
    scale = 1.0 / math.sqrt(HEAD_DIM)

    def body():
        yield ("flag", flag)
        slot.fetch(kv)
        mask.fill(0)
        yield ("did", 1.5)
        slot.need(kv, query)
        logsum.ref[...] = jnp.zeros((rows, 128), F32)
        for s in range(rows // count):
            mine = pl.ds(s * count, count)
            if s:
                mask.fill(s)

            @pl.loop(0, width // HEAD_DIM)
            def _(h):
                cols = pl.ds(pl.multiple_of(h * HEAD_DIM, HEAD_DIM), HEAD_DIM)
                vcols = pl.ds(pl.multiple_of(width + h * HEAD_DIM, HEAD_DIM), HEAD_DIM)
                q = query.ref[mine, cols]
                peak = jnp.full((count, 1), NEG, F32)
                for c in range(4):
                    keys = kv.ref[pl.ds(c * rows + s * count, count), cols]
                    block = pl.ds(c * count, count)
                    value = dot_nt(q, keys) * scale + mask.mask.ref[:, block]
                    logits.ref[:, block] = value
                    peak = jnp.maximum(peak, jnp.max(value, axis=1, keepdims=True))
                total = jnp.zeros((count, 1), F32)
                acc = jnp.zeros((count, HEAD_DIM), F32)
                for c in range(4):
                    vals = kv.ref[pl.ds(c * rows + s * count, count), vcols]
                    weight = jnp.exp(logits.ref[:, pl.ds(c * count, count)] - peak)
                    total = total + jnp.sum(weight, axis=1, keepdims=True)
                    acc = acc + dot_nn(weight.astype(BF), vals)
                out = acc / total
                heads.ref[mine, cols] = out
                heads_b.ref[mine, cols] = out.astype(BF)
                lane = lax.broadcasted_iota(jnp.int32, (count, 128), 1)
                logsum.ref[mine] = jnp.where(lane == h, peak + jnp.log(total), logsum.ref[mine])

            yield ("did", 4.0)
        slot.flush(heads_b, heads, logsum)

    slot.add(body)
    return [heads.target, heads_b.target, logsum.target]


def attend_back(slot, line, kv, query, heads, logsum, mask, rows, width, w_out):
    kv, query, heads, logsum = slot.load(kv), slot.load(query), slot.load(heads), slot.load(logsum)
    count = mask.count
    grad = slot.vmem((rows, width), BF)
    g_query, g_kv = slot.store((rows, width), F32), slot.store((4 * rows, 2 * width), BF)
    acc = g_query
    scale = 1.0 / math.sqrt(HEAD_DIM)

    def multiply(first, left, block, j):
        value = dot_nt(left[...], block[...])
        acc.ref[...] = value if first else acc.ref[...] + value

    def last():
        grad.ref[...] = acc.ref[...].astype(BF)
        slot.need(kv, query, heads, logsum)
        for s in range(rows // count):
            mine = pl.ds(s * count, count)
            mask.fill(s)
            yield ("did", 1.0)

            @pl.loop(0, width // HEAD_DIM)
            def _(h):
                cols = pl.ds(pl.multiple_of(h * HEAD_DIM, HEAD_DIM), HEAD_DIM)
                vcols = pl.ds(pl.multiple_of(width + h * HEAD_DIM, HEAD_DIM), HEAD_DIM)
                q, g = query.ref[mine, cols], grad.ref[mine, cols]
                delta = jnp.sum(g.astype(F32) * heads.ref[mine, cols], axis=1, keepdims=True)
                lane = lax.broadcasted_iota(jnp.int32, (count, 128), 1)
                logs = jnp.sum(jnp.where(lane == h, logsum.ref[mine], 0.0), axis=1, keepdims=True)
                total = jnp.zeros((count, HEAD_DIM), F32)
                for c in range(4):
                    there = pl.ds(c * rows + s * count, count)
                    keys, vals = kv.ref[there, cols], kv.ref[there, vcols]
                    value = dot_nt(q, keys) * scale + mask.mask.ref[:, pl.ds(c * count, count)]
                    probs = jnp.exp(value - logs)
                    slopes = (probs * (dot_nt(g, vals) - delta)).astype(BF)
                    total = total + dot_nn(slopes, keys)
                    g_kv.ref[there, cols] = (dot_tn(slopes, q) * scale).astype(BF)
                    g_kv.ref[there, vcols] = dot_tn(probs.astype(BF), g).astype(BF)
                g_query.ref[mine, cols] = total * scale

            yield ("did", 8.0)
        slot.flush(g_kv, g_query)

    consume(slot, line, (w_out,), (width, width), col_block, last, multiply, 0.6, "heads")
    return [g_query.target, g_kv.target]


def dot_tn(left, right):
    return lax.dot_general(left, right, (((0,), (0,)), ((), ())), preferred_element_type=F32)


def project_back(slot, flag, g_query, g_kv, raws, factor, gains, cosine, sine, first_row, rows, width):
    g_kv = slot.late(g_kv)
    g_query, factor = slot.load(g_query), slot.load(factor)
    raws = [slot.load(r) for r in raws]
    gains = [slot.load(g.reshape(1, width)) for g in gains]
    cosine, sine = slot.load(cosine), slot.load(sine)
    outs = [slot.store((rows, width), BF) for _ in range(3)]
    gain_grads = [slot.store((8, width), F32) for _ in range(2)]
    totals = RowTotals(slot, rows)

    def body():
        yield ("flag", flag)
        slot.fetch(g_kv)
        yield ("at", slot.now + 1.0)
        slot.need(g_kv, g_query, factor, cosine, sine, *raws, *gains)
        for g in gain_grads:
            g.ref[...] = jnp.zeros((8, width), F32)

        @pl.loop(0, rows // 32)
        def _(i):
            part = pl.ds(pl.multiple_of(i * 32, 32), 32)
            trig = pl.ds(pl.multiple_of(first_row + i * 32, 32), 32)
            co, si = cosine.ref[trig], sine.ref[trig]
            sums = []
            for j, source in ((0, g_query), (1, g_kv)):
                scale = factor.ref[part, j : j + 1]
                total = jnp.zeros((32, 1), F32)
                for h in range(width // HEAD_DIM):
                    cols = head_cols(h)
                    value = source.ref[part, cols]
                    value = value * co - half_turn(value) * si
                    source.ref[part, cols] = value
                    raw = raws[j].ref[part, cols]
                    total = total + jnp.sum(value * gains[j].ref[:, cols] * raw, axis=1, keepdims=True)
                    terms = value * raw * scale
                    for r in range(4):
                        gain_grads[j].ref[:, cols] += terms[8 * r : 8 * r + 8]
                sums.append(total)
            totals.put(part, *sums)

        slot.flush(*gain_grads)
        yield ("did", 3.0)
        yield from totals.exchange()

        def second(part):
            for j, source in ((0, g_query), (1, g_kv)):
                scale = factor.ref[part, j : j + 1]
                inner = totals.column(part, j)
                value = source.ref[part, 0:width] * gains[j].ref[...]
                outs[j].ref[part] = (scale * value - raws[j].ref[part] * (scale * scale * scale * inner / D)).astype(BF)
            outs[2].ref[part] = g_kv.ref[part, width : 2 * width].astype(BF)

        tiled(rows, 32, second)
        slot.flush(*outs)

    slot.add(body)
    return [h.target for h in outs + gain_grads]


def gain_sums(slot, arrays):
    loads = [slot.load(a) for a in arrays]
    width = arrays[0].shape[1]
    mine = [slot.vmem((8, width), F32) for _ in range(3)]
    came = [slot.vmem((8, width), F32) for _ in range(3)]
    out = slot.store((8, width), F32)
    base = slot.sems(6)
    slot.axes |= {"ctx", "dp"}

    def body():
        place = slot.place
        yield ("at", 2.0)
        slot.need(*loads)
        rows = []
        for k in range(0, len(loads), 2):
            rows.append(jnp.sum(loads[k].ref[...] + loads[k + 1].ref[...], axis=0, keepdims=True))
        value = jnp.concatenate(rows + [jnp.zeros((8 - len(rows), width), F32)], axis=0)
        for k, device in enumerate(({"ctx": place.ctx ^ 1}, {"ctx": place.ctx ^ 2}, {"dp": place.dp ^ 1})):
            mine[k].ref[...] = value
            copy = remote(mine[k].ref, came[k].ref, slot, base + 2 * k, base + 2 * k + 1, device)
            copy.start()
            yield ("at", 9.0 + 4.0 * k)
            copy.wait()
            value = mine[k].ref[...] + came[k].ref[...]
        out.ref[...] = value
        slot.flush(out)

    slot.add(body, True)
    return out.target


def tall_grad(slot, plane, lefts, rights, out, starts, prefix):
    tall, wide = lefts[0].shape[1], rights[0].shape[1]
    lefts, rights = [slot.load(a) for a in lefts], [slot.load(a) for a in rights]
    count = wide // 512
    flags = [prefix + str(k) for k in range(count)]
    blocks = [slot.hbm_out((tall, 512), BF) for _ in range(count)]
    weight_grad(slot, lefts, rights, (blocks, (tall, 512)), [(0, 512 * k) for k in range(count)], flags, 4.5)
    for k in range(count):
        plane.scatter(blocks[k], 0, True, 1, starts[k], flags[k], None, (out, (0, 512 * k)))


def wide_grad(slot, plane, lefts, rights, out, starts, prefix):
    tall, wide = lefts[0].shape[1], rights[0].shape[1]
    lefts, rights = [slot.load(a) for a in lefts], [slot.load(a) for a in rights]
    count = tall // 512
    flags = [prefix + str(k) for k in range(count)]
    blocks = [slot.hbm_out((512, wide), BF) for _ in range(count)]
    weight_grad(slot, lefts, rights, (blocks, (512, wide)), [(512 * k, 0) for k in range(count)], flags, 4.5)
    for k in range(count):
        plane.scatter(blocks[k], 1, True, 1, starts[k], flags[k], None, (out, (512 * k, 0)))


def general_row_total(value):
    return lax.psum(value, "tp")


def general_widen(value):
    return lax.all_gather(value, "tp", axis=1, tiled=True)


def general_narrow(value):
    return lax.psum_scatter(
        value.astype(jnp.bfloat16), "tp", scatter_dimension=1, tiled=True
    ).astype(jnp.float32)


def general_contract_last(left, right):
    return lax.dot_general(
        left, right, (((1,), (1,)), ((), ())), preferred_element_type=jnp.float32
    )


def general_contract_first(left, right):
    return lax.dot_general(
        left, right, (((0,), (0,)), ((), ())), preferred_element_type=jnp.float32
    )


def general_rotary(positions, depth):
    half = depth // 2
    freqs = THETA ** (-(jnp.arange(half, dtype=jnp.float32) * 2.0) / depth)
    angles = positions.astype(jnp.float32)[..., None] * freqs
    return (jnp.cos(angles)[..., None, :], jnp.sin(angles)[..., None, :])


def general_turn(value, cosine, sine):
    half = value.shape[-1] // 2
    first = value[..., :half]
    second = value[..., half:]
    return jnp.concatenate(
        [first * cosine - second * sine, second * cosine + first * sine], axis=-1
    )


def general_turn_back(grad, cosine, sine):
    half = grad.shape[-1] // 2
    first = grad[..., :half]
    second = grad[..., half:]
    return jnp.concatenate(
        [first * cosine + second * sine, second * cosine - first * sine], axis=-1
    )


def general_norm_grad(scaled, value, factor, inner):
    return factor[:, None] * scaled - value * (factor**3 * inner / D)[:, None]


def general(
    hidden,
    cotangent,
    segments,
    positions,
    w_query,
    w_key,
    w_value,
    w_out,
    w_gate,
    w_up,
    w_down,
    q_gain,
    k_gain,
    attn_gain,
    mlp_gain,
):
    local_seqs, slice_len, local_width = hidden.shape
    per_batch = local_seqs // 2
    rows = per_batch * slice_len
    heads_here = q_gain.shape[0] // HEAD_DIM
    scale = 1.0 / math.sqrt(HEAD_DIM)
    query_index = lax.axis_index("ctx") * slice_len + jnp.arange(slice_len, dtype=jnp.int32)
    outputs = []
    input_grads = []
    weight_grads = None
    q_gain_grad = jnp.zeros(q_gain.shape, jnp.float32)
    k_gain_grad = jnp.zeros(k_gain.shape, jnp.float32)
    attn_gain_grad = jnp.zeros(attn_gain.shape, jnp.float32)
    mlp_gain_grad = jnp.zeros(mlp_gain.shape, jnp.float32)
    for batch in range(2):
        lower = batch * per_batch
        tokens_in = hidden[lower : lower + per_batch].reshape(rows, local_width)
        seg_here = segments[lower : lower + per_batch]
        pos_here = positions[lower : lower + per_batch].reshape(rows)
        gathered = (
            lax.all_gather(w_query, ("dp", "ctx"), axis=0, tiled=True),
            lax.all_gather(w_key, ("dp", "ctx"), axis=0, tiled=True),
            lax.all_gather(w_value, ("dp", "ctx"), axis=0, tiled=True),
            lax.all_gather(w_out, ("dp", "ctx"), axis=1, tiled=True),
            lax.all_gather(w_gate, ("dp", "ctx"), axis=0, tiled=True),
            lax.all_gather(w_up, ("dp", "ctx"), axis=0, tiled=True),
            lax.all_gather(w_down, ("dp", "ctx"), axis=1, tiled=True),
        )
        query_full, key_full, value_full, out_full, gate_full, up_full, down_full = gathered
        if weight_grads is None:
            weight_grads = tuple((jnp.zeros(tensor.shape, jnp.float32) for tensor in gathered))
        wide_in = general_widen(tokens_in)
        query_raw = jnp.dot(wide_in, query_full, preferred_element_type=jnp.float32)
        key_raw = jnp.dot(wide_in, key_full, preferred_element_type=jnp.float32)
        value_raw = jnp.dot(wide_in, value_full, preferred_element_type=jnp.float32)
        query_sq, key_sq = general_row_total(
            (jnp.sum(query_raw * query_raw, axis=1), jnp.sum(key_raw * key_raw, axis=1))
        )
        query_scale = lax.rsqrt(query_sq / D + EPS)
        key_scale = lax.rsqrt(key_sq / D + EPS)
        cosine, sine = general_rotary(pos_here, HEAD_DIM)
        query_rot = general_turn(
            (query_raw * query_scale[:, None] * q_gain).reshape(rows, heads_here, HEAD_DIM),
            cosine,
            sine,
        )
        key_rot = general_turn(
            (key_raw * key_scale[:, None] * k_gain).reshape(rows, heads_here, HEAD_DIM),
            cosine,
            sine,
        )
        query_b = query_rot.astype(jnp.bfloat16).reshape(per_batch, slice_len, heads_here, HEAD_DIM)
        key_b = key_rot.astype(jnp.bfloat16).reshape(per_batch, slice_len, heads_here * HEAD_DIM)
        value_b = value_raw.astype(jnp.bfloat16).reshape(
            per_batch, slice_len, heads_here * HEAD_DIM
        )

        def allowed_pairs(seg_piece, count):
            key_index = jnp.arange(count, dtype=jnp.int32)
            causal = query_index[:, None] >= key_index[None, :]
            same = seg_here[:, None, :, None] == seg_piece[:, None, None, :]
            return jnp.logical_and(same, causal[None, None])

        start_peak = jnp.full((per_batch, heads_here, slice_len), NEG, jnp.float32)
        peak = start_peak
        key_piece = lax.all_gather(key_b, "ctx", axis=1, tiled=True)
        value_piece = lax.all_gather(value_b, "ctx", axis=1, tiled=True)
        attend_seg_piece = lax.all_gather(seg_here, "ctx", axis=1, tiled=True)
        attend_count = key_piece.shape[1]
        key_four = key_piece.reshape(per_batch, attend_count, heads_here, HEAD_DIM)
        value_four = value_piece.reshape(per_batch, attend_count, heads_here, HEAD_DIM)
        allowed = allowed_pairs(attend_seg_piece, attend_count)
        logits = scale * jnp.einsum(
            "sqhd,skhd->shqk", query_b, key_four, preferred_element_type=jnp.float32
        )
        logits = jnp.where(allowed, logits, NEG)
        fresh = jnp.maximum(peak, jnp.max(logits, axis=-1))
        weights = jnp.where(allowed, jnp.exp(logits - fresh[..., None]), 0.0)
        total = jnp.sum(weights, axis=-1)
        accum = jnp.einsum(
            "shqk,skhd->shqd",
            weights.astype(jnp.bfloat16),
            value_four,
            preferred_element_type=jnp.float32,
        )
        peak, total, accum = (fresh, total, accum)
        logsum = peak + jnp.log(total)
        out_heads = (
            (accum / total[..., None]).transpose(0, 2, 1, 3).reshape(rows, heads_here * HEAD_DIM)
        )
        out_b = out_heads.astype(jnp.bfloat16)
        attn_raw = general_narrow(jnp.dot(out_b, out_full, preferred_element_type=jnp.float32))
        attn_scale = lax.rsqrt(general_row_total(jnp.sum(attn_raw * attn_raw, axis=1)) / D + EPS)
        resid = tokens_in.astype(jnp.float32) + attn_raw * attn_scale[:, None] * attn_gain
        wide_mid = general_widen(resid.astype(jnp.bfloat16))
        gate = jnp.dot(wide_mid, gate_full, preferred_element_type=jnp.float32)
        up_val = jnp.dot(wide_mid, up_full, preferred_element_type=jnp.float32)
        sigma = jax.nn.sigmoid(gate)
        swish = gate * sigma
        act_b = (swish * up_val).astype(jnp.bfloat16)
        mlp_raw = general_narrow(jnp.dot(act_b, down_full, preferred_element_type=jnp.float32))
        mlp_scale = lax.rsqrt(general_row_total(jnp.sum(mlp_raw * mlp_raw, axis=1)) / D + EPS)
        result = resid + mlp_raw * mlp_scale[:, None] * mlp_gain
        outputs.append(result.astype(jnp.bfloat16).reshape(per_batch, slice_len, local_width))
        again = (
            lax.all_gather(w_query, ("dp", "ctx"), axis=0, tiled=True),
            lax.all_gather(w_key, ("dp", "ctx"), axis=0, tiled=True),
            lax.all_gather(w_value, ("dp", "ctx"), axis=0, tiled=True),
            lax.all_gather(w_out, ("dp", "ctx"), axis=1, tiled=True),
            lax.all_gather(w_gate, ("dp", "ctx"), axis=0, tiled=True),
            lax.all_gather(w_up, ("dp", "ctx"), axis=0, tiled=True),
            lax.all_gather(w_down, ("dp", "ctx"), axis=1, tiled=True),
        )
        query_back, key_back, value_back, out_back, gate_back, up_back, down_back = again
        grad_out = (
            cotangent[lower : lower + per_batch].reshape(rows, local_width).astype(jnp.float32)
        )
        mlp_gain_grad = mlp_gain_grad + jnp.sum(grad_out * mlp_raw * mlp_scale[:, None], axis=0)
        scaled = grad_out * mlp_gain
        grad_mlp = general_norm_grad(
            scaled, mlp_raw, mlp_scale, general_row_total(jnp.sum(scaled * mlp_raw, axis=1))
        )
        wide_grad_mlp = general_widen(grad_mlp.astype(jnp.bfloat16))
        grad_act = general_contract_last(wide_grad_mlp, down_back)
        grad_gate = (grad_act * up_val * sigma * (1.0 + gate * (1.0 - sigma))).astype(jnp.bfloat16)
        grad_up = (grad_act * swish).astype(jnp.bfloat16)
        grad_resid = grad_out + general_narrow(
            general_contract_last(grad_gate, gate_back) + general_contract_last(grad_up, up_back)
        )
        attn_gain_grad = attn_gain_grad + jnp.sum(
            grad_resid * attn_raw * attn_scale[:, None], axis=0
        )
        scaled = grad_resid * attn_gain
        grad_attn = general_norm_grad(
            scaled, attn_raw, attn_scale, general_row_total(jnp.sum(scaled * attn_raw, axis=1))
        )
        wide_grad_attn = general_widen(grad_attn.astype(jnp.bfloat16))
        grad_heads = general_contract_last(wide_grad_attn, out_back).astype(jnp.bfloat16)
        dout_four = grad_heads.reshape(per_batch, slice_len, heads_here, HEAD_DIM)
        delta = jnp.sum(
            (grad_heads.astype(jnp.float32) * out_heads).reshape(
                per_batch, slice_len, heads_here, HEAD_DIM
            ),
            axis=-1,
        ).transpose(0, 2, 1)

        def attend_back(piece):
            key_piece, value_piece, seg_piece = piece
            count = key_piece.shape[1]
            key_four = key_piece.reshape(per_batch, count, heads_here, HEAD_DIM)
            value_four = value_piece.reshape(per_batch, count, heads_here, HEAD_DIM)
            allowed = allowed_pairs(seg_piece, count)
            logits = scale * jnp.einsum(
                "sqhd,skhd->shqk", query_b, key_four, preferred_element_type=jnp.float32
            )
            probs = jnp.where(allowed, jnp.exp(logits - logsum[..., None]), 0.0)
            grad_probs = jnp.einsum(
                "sqhd,skhd->shqk", dout_four, value_four, preferred_element_type=jnp.float32
            )
            grad_logits = (probs * (grad_probs - delta[..., None])).astype(jnp.bfloat16)
            grad_query = scale * jnp.einsum(
                "shqk,skhd->sqhd", grad_logits, key_four, preferred_element_type=jnp.float32
            )
            key_grad = scale * jnp.einsum(
                "shqk,sqhd->skhd", grad_logits, query_b, preferred_element_type=jnp.float32
            )
            value_grad = jnp.einsum(
                "shqk,sqhd->skhd",
                probs.astype(jnp.bfloat16),
                dout_four,
                preferred_element_type=jnp.float32,
            )
            grad_keys = key_grad.reshape(per_batch, count, heads_here * HEAD_DIM)
            grad_values = value_grad.reshape(per_batch, count, heads_here * HEAD_DIM)
            return (grad_query, grad_keys, grad_values)

        grad_query, grad_keys, grad_values = attend_back(
            (
                lax.all_gather(key_b, "ctx", axis=1, tiled=True),
                lax.all_gather(value_b, "ctx", axis=1, tiled=True),
                lax.all_gather(seg_here, "ctx", axis=1, tiled=True),
            )
        )
        key_grad_mine, value_grad_mine = (
            lax.psum_scatter(
                grad_keys.astype(jnp.bfloat16), "ctx", scatter_dimension=1, tiled=True
            ).astype(jnp.float32),
            lax.psum_scatter(
                grad_values.astype(jnp.bfloat16), "ctx", scatter_dimension=1, tiled=True
            ).astype(jnp.float32),
        )
        grad_qnorm = general_turn_back(
            grad_query.reshape(rows, heads_here, HEAD_DIM), cosine, sine
        ).reshape(rows, heads_here * HEAD_DIM)
        grad_knorm = general_turn_back(
            key_grad_mine.reshape(rows, heads_here, HEAD_DIM), cosine, sine
        ).reshape(rows, heads_here * HEAD_DIM)
        q_gain_grad = q_gain_grad + jnp.sum(grad_qnorm * query_raw * query_scale[:, None], axis=0)
        k_gain_grad = k_gain_grad + jnp.sum(grad_knorm * key_raw * key_scale[:, None], axis=0)
        q_scaled = grad_qnorm * q_gain
        k_scaled = grad_knorm * k_gain
        q_inner, k_inner = general_row_total(
            (jnp.sum(q_scaled * query_raw, axis=1), jnp.sum(k_scaled * key_raw, axis=1))
        )
        grad_query_raw = general_norm_grad(q_scaled, query_raw, query_scale, q_inner).astype(jnp.bfloat16)
        grad_key_raw = general_norm_grad(k_scaled, key_raw, key_scale, k_inner).astype(jnp.bfloat16)
        grad_value_raw = value_grad_mine.reshape(rows, heads_here * HEAD_DIM).astype(jnp.bfloat16)
        back_terms = (
            general_contract_last(grad_query_raw, query_back)
            + general_contract_last(grad_key_raw, key_back)
            + general_contract_last(grad_value_raw, value_back)
        )
        grad_in = grad_resid + general_narrow(back_terms)
        input_grads.append(grad_in.astype(jnp.bfloat16).reshape(per_batch, slice_len, local_width))
        fresh_grads = (
            general_contract_first(wide_in, grad_query_raw),
            general_contract_first(wide_in, grad_key_raw),
            general_contract_first(wide_in, grad_value_raw),
            general_contract_first(out_b, wide_grad_attn),
            general_contract_first(wide_mid, grad_gate),
            general_contract_first(wide_mid, grad_up),
            general_contract_first(act_b, wide_grad_mlp),
        )
        weight_grads = tuple((left + right for left, right in zip(weight_grads, fresh_grads)))
    finals = (
        lax.psum_scatter(
            weight_grads[0].astype(jnp.bfloat16), ("dp", "ctx"), scatter_dimension=0, tiled=True
        ).astype(jnp.float32),
        lax.psum_scatter(
            weight_grads[1].astype(jnp.bfloat16), ("dp", "ctx"), scatter_dimension=0, tiled=True
        ).astype(jnp.float32),
        lax.psum_scatter(
            weight_grads[2].astype(jnp.bfloat16), ("dp", "ctx"), scatter_dimension=0, tiled=True
        ).astype(jnp.float32),
        lax.psum_scatter(
            weight_grads[3].astype(jnp.bfloat16), ("dp", "ctx"), scatter_dimension=1, tiled=True
        ).astype(jnp.float32),
        lax.psum_scatter(
            weight_grads[4].astype(jnp.bfloat16), ("dp", "ctx"), scatter_dimension=0, tiled=True
        ).astype(jnp.float32),
        lax.psum_scatter(
            weight_grads[5].astype(jnp.bfloat16), ("dp", "ctx"), scatter_dimension=0, tiled=True
        ).astype(jnp.float32),
        lax.psum_scatter(
            weight_grads[6].astype(jnp.bfloat16), ("dp", "ctx"), scatter_dimension=1, tiled=True
        ).astype(jnp.float32),
    )
    gains = lax.psum((q_gain_grad, k_gain_grad, attn_gain_grad, mlp_gain_grad), ("dp", "ctx"))
    return (
        jnp.concatenate(outputs, axis=0),
        jnp.concatenate(input_grads, axis=0),
        finals[0],
        finals[1],
        finals[2],
        finals[3],
        finals[4],
        finals[5],
        finals[6],
        gains[0],
        gains[1],
        gains[2],
        gains[3],
    )


class Batch:
    pass


def planned(
    hidden, cotangent, segments, positions, w_query, w_key, w_value, w_out, w_gate, w_up, w_down,
    q_gain, k_gain, attn_gain, mlp_gain,
):
    seqs, count, width = hidden.shape
    per = seqs // 2
    rows = per * count
    ff = w_gate.shape[1]
    batches = (Batch(), Batch())
    one, two = batches
    for b, batch in enumerate(batches):
        batch.x = hidden[b * per : (b + 1) * per].reshape(rows, width)
        batch.cot = cotangent[b * per : (b + 1) * per].reshape(rows, width)
    seg_cols = jnp.broadcast_to(segments.reshape(seqs * count, 1), (seqs * count, 128))
    pos_cols = jnp.broadcast_to(positions.reshape(seqs * count, 1), (seqs * count, 128))
    half = HEAD_DIM // 2
    freqs = THETA ** (-(jnp.arange(half, dtype=F32) * 2.0) / HEAD_DIM)
    freqs = jnp.concatenate([freqs, freqs]).reshape(1, HEAD_DIM)
    sign = jnp.concatenate([-jnp.ones(half, F32), jnp.ones(half, F32)]).reshape(1, HEAD_DIM)
    seg_pad = jnp.concatenate([segments, jnp.zeros((8 - seqs, count), segments.dtype)], axis=0)
    norms = (q_gain, k_gain)

    quarters = [(512 * k, 512) for k in range(ff // 512)]
    wg, wu = [], []

    s = Slot("slot0", 0)
    line = Line(s, rows, width, gather=one.x)
    plane = Plane(s)
    seg_h = plane.gather(seg_pad, 0, False)
    full = [plane.gather(w, 0, True, done="w%d" % i) for i, w in enumerate((w_query, w_key, w_value))]
    w_out_h = plane.gather(w_out, 1, True)
    some = [plane.gather(w_gate, 0, True, cols=c) for c in quarters[:2]]
    cosine, sine = tables(s, pos_cols, freqs, sign)
    made = project(s, line, rows, width, full, ("w0", "w1", "w2"), norms, cosine, sine, 0)
    s.run()
    wq, wk, wv = (h.value for h in full)
    wg += [h.value for h in some]
    wo, seg_all, cosine, sine = w_out_h.value, seg_h.value, cosine.target.value, sine.target.value
    one.q_raw, one.k_raw, one.q, one.kv, one.qk_factor = (h.value for h in made)
    one.wide = line.out.value

    s = Slot("slot1", 1)
    line = Line(s, rows, width, gather=two.x)
    plane = Plane(s)
    kvs = plane.gather(one.kv, 0, False, 4, done="kv")
    some = [plane.gather(w_gate, 0, True, cols=c) for c in quarters[2:]]
    more = plane.gather(w_up, 0, True, cols=quarters[0])
    s.mark_early("tables")
    mask = Mask(s, seg_all, seg_cols, 0, count)
    felt = attend(s, "kv", kvs, one.q, mask, rows, width)
    made = project(s, line, rows, width, (wq, wk, wv), None, norms, s.load(cosine), s.load(sine), rows)
    s.run()
    wg += [h.value for h in some]
    wu.append(more.value)
    one.kvs = kvs.value
    two.q_raw, two.k_raw, two.q, two.kv, two.qk_factor = (h.value for h in made)
    one.heads, one.heads_b, one.logsum = (h.value for h in felt)
    two.wide = line.out.value

    s = Slot("slot2", 2)
    line = Line(s, rows, width, scatter=True)
    plane = Plane(s)
    kvs = plane.gather(two.kv, 0, False, 4, done="kv")
    some = [plane.gather(w_up, 0, True, cols=c) for c in quarters[1:]]
    ends = attn_finish(s, line, rows, width, one.x, attn_gain)
    produce(s, line, [s.load(one.heads_b)], [wo], (width, width), col_block, dot_nn, 0.6)
    mask = Mask(s, seg_all, seg_cols, per, count)
    felt = attend(s, "kv", kvs, two.q, mask, rows, width)
    s.run()
    wu += [h.value for h in some]
    two.kvs = kvs.value
    one.attn, one.resid, one.resid_b, one.factor = (h.value for h in ends)
    two.heads, two.heads_b, two.logsum = (h.value for h in felt)

    s = Slot("slot3", 3)
    line = Line(s, rows, width, gather=one.resid_b, scatter=True)
    w_down_h = Plane(s).gather(w_down, 1, True, 4)
    ends = attn_finish(s, line, rows, width, two.x, attn_gain)
    produce(s, line, [s.load(two.heads_b)], [wo], (width, width), col_block, dot_nn, 0.6)
    inner = gate_up(s, line, rows, wg, wu)
    s.run()
    wd, one.mid = w_down_h.value, line.out.value
    two.attn, two.resid, two.resid_b, two.factor = (h.value for h in ends)
    one.gate, one.up, one.act = (h.value for h in inner)

    s = Slot("slot4", 4)
    line = Line(s, rows, width, gather=two.resid_b, scatter=True)
    ends = mlp_finish(s, line, rows, width, one.resid, one.cot, mlp_gain)
    produce(s, line, [s.load(one.act)], [wd], (ff, 512), col_block, dot_nn, 1.8)
    inner = gate_up(s, line, rows, wg, wu)
    s.run()
    two.mid = line.out.value
    one.out, one.g_mlp_b, one.g_mlp_gain = (h.value for h in ends)
    two.gate, two.up, two.act = (h.value for h in inner)

    s = Slot("slot5", 5)
    line = Line(s, rows, width, gather=one.g_mlp_b, scatter=True)
    ends = mlp_finish(s, line, rows, width, two.resid, two.cot, mlp_gain)
    produce(s, line, [s.load(two.act)], [wd], (ff, 512), col_block, dot_nn, 1.8)
    inner = act_back(s, line, rows, wd, one.gate, one.up)
    s.run()
    one.g_mlp = line.out.value
    two.out, two.g_mlp_b, two.g_mlp_gain = (h.value for h in ends)
    one.g_gate, one.g_up = (h.value for h in inner)

    s = Slot("slot6", 6)
    line = Line(s, rows, width, gather=two.g_mlp_b, scatter=True)
    ends = resid_finish(s, line, rows, width, one.cot, one.attn, one.factor, attn_gain)
    produce(s, line, [s.load(one.g_gate), s.load(one.g_up)], wg + wu, (512, 512), row_block, dot_nt, 4.4)
    inner = act_back(s, line, rows, wd, two.gate, two.up)
    s.run()
    two.g_mlp = line.out.value
    one.g_resid, one.g_attn_b, one.g_attn_gain = (h.value for h in ends)
    two.g_gate, two.g_up = (h.value for h in inner)

    s = Slot("slot7", 7)
    line = Line(s, rows, width, gather=one.g_attn_b, scatter=True)
    plane = Plane(s)
    g_down = s.hbm_out(w_down.shape, F32)
    ends = resid_finish(s, line, rows, width, two.cot, two.attn, two.factor, attn_gain)
    produce(s, line, [s.load(two.g_gate), s.load(two.g_up)], wg + wu, (512, 512), row_block, dot_nt, 4.4)
    mask = Mask(s, seg_all, seg_cols, 0, count)
    back = attend_back(s, line, one.kvs, one.q, one.heads, one.logsum, mask, rows, width, wo)
    wide_grad(s, plane, (one.act, two.act), (one.g_mlp, two.g_mlp), g_down, (22.0, 27.0, 31.0, 36.0), "d")
    s.run()
    one.g_attn = line.out.value
    two.g_resid, two.g_attn_b, two.g_attn_gain = (h.value for h in ends)
    one.g_q, one.g_kv = (h.value for h in back)

    s = Slot("slot8", 8)
    line = Line(s, rows, width, gather=two.g_attn_b)
    plane = Plane(s)
    g_kv = plane.scatter(one.g_kv, 0, False, 4, done="kv")
    g_gate = s.hbm_out(w_gate.shape, F32)
    raws = project_back(s, "kv", one.g_q, g_kv, (one.q_raw, one.k_raw), one.qk_factor, norms, cosine, sine, 0, rows, width)
    mask = Mask(s, seg_all, seg_cols, per, count)
    back = attend_back(s, line, two.kvs, two.q, two.heads, two.logsum, mask, rows, width, wo)
    tall_grad(s, plane, (one.mid, two.mid), (one.g_gate, two.g_gate), g_gate, (8.0, 13.0, 18.0, 22.0), "g")
    s.run()
    two.g_attn = line.out.value
    one.g_qr, one.g_kr, one.g_vr, one.g_q_gain, one.g_k_gain = (h.value for h in raws)
    two.g_q, two.g_kv = (h.value for h in back)

    s = Slot("slot9", 9)
    line = Line(s, rows, width, scatter=True)
    plane = Plane(s)
    g_kv = plane.scatter(two.g_kv, 0, False, 4, done="kv")
    g_up = s.hbm_out(w_up.shape, F32)
    fin_one = last_finish(s, line, rows, width, one.g_resid)[0]
    produce(s, line, [s.load(g) for g in (one.g_qr, one.g_kr, one.g_vr)], [wq, wk, wv], (512, width), row_block, dot_nt, 1.6)
    raws = project_back(s, "kv", two.g_q, g_kv, (two.q_raw, two.k_raw), two.qk_factor, norms, cosine, sine, rows, rows, width)
    tall_grad(s, plane, (one.mid, two.mid), (one.g_up, two.g_up), g_up, (13.0, 18.0, 22.0, 27.0), "u")
    s.run()
    two.g_qr, two.g_kr, two.g_vr, two.g_q_gain, two.g_k_gain = (h.value for h in raws)

    s = Slot("slot10", 10)
    line = Line(s, rows, width, scatter=True)
    plane = Plane(s)
    fin_two = last_finish(s, line, rows, width, two.g_resid)[0]
    produce(s, line, [s.load(g) for g in (two.g_qr, two.g_kr, two.g_vr)], [wq, wk, wv], (512, width), row_block, dot_nt, 1.6)
    sums = gain_sums(
        s,
        (one.g_q_gain, two.g_q_gain, one.g_k_gain, two.g_k_gain)
        + (one.g_attn_gain, two.g_attn_gain, one.g_mlp_gain, two.g_mlp_gain),
    )
    wides = (one.wide, two.wide)
    g_q, g_k, g_v = (s.hbm_out(w_query.shape, F32) for _ in range(3))
    g_out = s.hbm_out(w_out.shape, F32)
    tall_grad(s, plane, wides, (one.g_qr, two.g_qr), g_q, (13.0,), "q")
    tall_grad(s, plane, wides, (one.g_kr, two.g_kr), g_k, (18.0,), "k")
    tall_grad(s, plane, wides, (one.g_vr, two.g_vr), g_v, (22.0,), "v")
    wide_grad(s, plane, (one.heads_b, two.heads_b), (one.g_attn, two.g_attn), g_out, (27.0,), "o")
    s.run()
    gains = [sums.value[k] for k in range(4)]
    shape = (per, count, width)
    return (
        jnp.concatenate([one.out.reshape(shape), two.out.reshape(shape)], axis=0),
        jnp.concatenate([fin_one.value.reshape(shape), fin_two.value.reshape(shape)], axis=0),
        *(g.value for g in (g_q, g_k, g_v, g_out, g_gate, g_up, g_down)),
        *gains,
    )


def solution(mesh):
    rows, cols = P(("dp", "ctx"), "tp"), P("tp", ("dp", "ctx"))
    act, gain = P("dp", "ctx", "tp"), P("tp")
    size = dict(mesh.shape)
    body = planned if (size["dp"], size["ctx"], size["tp"]) == (2, 4, 4) else general
    return jax.shard_map(
        body,
        mesh=mesh,
        in_specs=(act, act, P("dp", "ctx"), P("dp", "ctx"), rows, rows, rows, cols, rows, rows, cols, gain, gain, gain, gain),
        out_specs=(act, act, rows, rows, rows, cols, rows, rows, cols, gain, gain, gain, gain),
        check_vma=False,
    )
```

```python
import functools
import math

import jax
import jax.numpy as jnp
from jax import lax
from jax.experimental import pallas as pl
from jax.experimental.pallas import tpu as pltpu
from jax.sharding import PartitionSpec as P

D = 2048
HEAD_DIM = 128
EPS = 1e-06
THETA = 500000.0
NEG = -1e30
BF = jnp.bfloat16
F32 = jnp.float32
MESH = pl.DeviceIdType.MESH
HBM = pl.BlockSpec(memory_space=pltpu.HBM)


class Place:
    def __init__(self, tp_size):
        self.n = tp_size
        self.tp = lax.axis_index("tp")
        self.dp = lax.axis_index("dp")
        self.ctx = lax.axis_index("ctx")
        self.slot = self.dp * 4 + self.ctx


def remote(src, dst, sem, send, recv, device):
    return pltpu.make_async_remote_copy(
        src_ref=src, dst_ref=dst, send_sem=sem.at(send), recv_sem=sem.at(recv), device_id=device, device_id_type=MESH
    )


class Step:
    def __init__(self, job, name, link, time, deps, rank, issue=None, arrive=None):
        self.job, self.name, self.link, self.time, self.deps, self.rank = job, name, link, time, deps, rank
        self.issue, self.arrive = issue, arrive


class Plane:
    def __init__(self, slot):
        self.slot = slot
        self.jobs = []
        slot.plane = self
        slot.axes.add("ctx")

    def gather(self, array, dim, with_dp, pieces=1, start=0.0, after=None, done=None, cols=None):
        return self.append(Gather(self.slot, array, dim, with_dp, pieces, start, after, done, cols))

    def scatter(self, array, dim, with_dp, pieces=1, start=0.0, after=None, done=None, out=None):
        return self.append(Scatter(self.slot, array, dim, with_dp, pieces, start, after, done, out))

    def append(self, job):
        job.number = len(self.jobs)
        self.jobs.append(job)
        if job.with_dp:
            self.slot.axes.add("dp")
        self.slot.add(lambda: job.body(self), True)
        return job.out

    def plan(self):
        pieces = [(job, p) for job in self.jobs for p in range(job.pieces)]
        choice, load = {}, [0.0, 0.0]
        for job, p in pieces:
            load[0] += job.unit
            load[1] += job.unit if job.with_dp else 0.0
        for job, p in pieces:
            via = 0 if load[0] < load[1] else 1
            choice[job, p] = via
            if job.with_dp:
                load[via] += job.unit
        best = self.lay(choice)
        for _ in range(2):
            for key in pieces:
                if key[0].with_dp:
                    trial = dict(choice)
                    trial[key] = 1 - trial[key]
                    result = self.lay(trial)
                    if result[0] < best[0] - 0.01:
                        choice, best = trial, result
        self.actions = best[1]

    def lay(self, choice):
        steps = [step for job in self.jobs for p in range(job.pieces) for step in job.steps(p, choice[job, p])]
        times, free, actions = {}, [0.0, 0.0], []
        pending = list(steps)
        while pending:
            best = None
            for step in pending:
                if any((step.job, d) not in times for d in step.deps):
                    continue
                ready = max([step.job.start] + [times[step.job, d] for d in step.deps])
                key = (ready, step.job.number, step.rank)
                if best is None or key < best[0]:
                    best = (key, step)
            (ready, _, _), step = best
            pending.remove(step)
            if step.link is None:
                arrive_at = ready + step.time
            else:
                begin = max(ready, free[step.link])
                free[step.link] = begin + step.time
                actions.append((ready, 1, len(actions), step.job, step.issue))
                arrive_at = begin + step.time + 0.7
            actions.append((arrive_at, 0, len(actions), step.job, step.arrive))
            times[step.job, step.name] = arrive_at
        actions.sort(key=lambda a: a[:3])
        return sum(times.values()) / len(times) / 10 + max(times.values()), actions


class Job:
    def body(self, plane):
        slot = self.slot
        if not plane.planned:
            plane.plan()
            plane.planned = True
        if self.after is not None:
            yield ("flag", self.after)
        shift = max(0.0, slot.now - self.start) if self.after is not None else 0.0
        yield ("at", self.start)
        self.begin()
        yield ("at", self.start + shift + 1.0)
        self.settle()
        for time, _, _, job, emit in plane.actions:
            if job is self:
                yield ("at", time + shift)
                emit()
        yield ("at", slot.now + 1.0)
        self.finish()
        if self.done is not None:
            slot.mark(self.done)

    def send(self, index, origin, target, device):
        copy = remote(origin, target, self.slot, self.base + 2 * index, self.base + 2 * index + 1, device)
        copy.start()
        self.sent.append(copy)

    def got(self, index, target):
        remote(target, target, self.slot, self.base + 2 * index, self.base + 2 * index + 1, self.cdev).wait_recv()

    def settle(self):
        pass

    def coordinates(self):
        self.dp, self.ctx = self.slot.place.dp, self.slot.place.ctx
        self.xdev, self.ydev, self.cdev = {"ctx": self.ctx ^ 2}, {"dp": self.dp ^ 1}, {"ctx": self.ctx ^ 1}
        self.sent = []


class Gather(Job):
    def __init__(self, slot, array, dim, with_dp, pieces, start, after, done, cols):
        self.slot, self.dim, self.with_dp, self.pieces = slot, dim, with_dp, pieces
        self.start, self.after, self.done = start, after, done
        self.handle = slot.hbm_in(array)
        shape = list(array.shape)
        self.cols = pl.ds(0, shape[1]) if cols is None else pl.ds(*cols)
        if cols is not None:
            shape[1] = cols[1]
        self.size, self.rows = shape[dim], shape[0]
        self.unit = math.prod(shape) * 2 / (slot.rates[1] * 1e3) / pieces
        self.hold = slot.vmem(tuple(shape), array.dtype)
        shape[dim] *= 8 if with_dp else 4
        self.out = slot.hbm_out(tuple(shape), array.dtype)
        self.own = slot.sems(2)
        self.base = slot.sems(2 * pieces * 7)

    def spot(self, d, c, p):
        out = self.out.ref
        block = d * 4 + c if self.with_dp else c
        step = self.rows // self.pieces
        if self.dim == 1:
            return out.at[pl.ds(p * step, step), pl.ds(pl.multiple_of(block * self.size, self.size), self.size)]
        return out.at[pl.ds(pl.multiple_of(block * self.size + p * step, step), step)]

    def begin(self):
        self.coordinates()
        self.source = src = self.handle.ref.at[:, self.cols]
        step = self.rows // self.pieces
        for p in range(self.pieces):
            part = pl.ds(p * step, step)
            self.send(7 * p, src.at[part], self.spot(self.dp, self.ctx, p), self.cdev)
        if self.dim == 1:
            mine = self.out.ref.at[:, pl.ds(pl.multiple_of((self.dp * 4 + self.ctx) * self.size, self.size), self.size)]
        else:
            block = self.dp * 4 + self.ctx if self.with_dp else self.ctx
            mine = self.out.ref.at[pl.ds(pl.multiple_of(block * self.size, self.size), self.size)]
        self.held = pltpu.make_async_copy(src, self.hold.ref, self.slot.sem(self.own))
        self.kept = pltpu.make_async_copy(self.hold.ref, mine, self.slot.sem(self.own + 1))
        self.held.start()

    def settle(self):
        self.held.wait()
        self.kept.start()

    def steps(self, p, via):
        def direct(k, device):
            def issue():
                step = self.rows // self.pieces
                part = pl.ds(p * step, step)
                self.send(7 * p + 1 + k, self.source.at[part], self.spot(self.dp, self.ctx, p), device())

            return issue

        def forward(k, place):
            def arrive():
                here = self.spot(*place(), p)
                self.got(7 * p + 1 + k, here)
                self.send(7 * p + 4 + k, here, here, self.cdev)

            return arrive

        from_x = lambda: (self.dp, self.ctx ^ 2)
        from_y = lambda: (self.dp ^ 1, self.ctx)
        corner = lambda: (self.dp ^ 1, self.ctx ^ 2)
        xdev, ydev = (lambda: self.xdev), (lambda: self.ydev)
        out = [Step(self, (p, 0), 0, self.unit, [], 2 * p, direct(0, xdev), forward(0, from_x))]
        if self.with_dp:
            out.append(Step(self, (p, 1), 1, self.unit, [], 2 * p, direct(1, ydev), forward(1, from_y)))

            def hop():
                here = self.spot(*(from_y() if via == 0 else from_x()), p)
                self.send(7 * p + 3, here, here, self.xdev if via == 0 else self.ydev)

            out.append(Step(self, (p, 2), via, self.unit, [(p, 1 - via)], 2 * p + 1, hop, forward(2, corner)))
        return out

    def finish(self):
        for p in range(self.pieces):
            self.got(7 * p, self.spot(self.dp, self.ctx ^ 1, p))
            self.got(7 * p + 4, self.spot(self.dp, self.ctx ^ 3, p))
            if self.with_dp:
                self.got(7 * p + 5, self.spot(self.dp ^ 1, self.ctx ^ 1, p))
                self.got(7 * p + 6, self.spot(self.dp ^ 1, self.ctx ^ 3, p))
        for copy in self.sent:
            copy.wait_send()
        self.kept.wait()


class Scatter(Job):
    def __init__(self, slot, array, dim, with_dp, pieces, start, after, done, out):
        self.slot, self.dim, self.with_dp, self.pieces = slot, dim, with_dp, pieces
        self.start, self.after, self.done = start, after, done
        self.source = slot.hbm_in(array)
        shape = list(array.shape)
        self.chips = chips = 4 if with_dp else 2
        shape[dim] //= 2 * chips
        self.size = shape[dim]
        self.rows, self.width = shape
        self.unit = math.prod(shape) * 2 / (slot.rates[1] * 1e3) / pieces
        if out is None:
            self.out, self.where = slot.hbm_out(tuple(shape), F32), None
        else:
            self.out, self.where = out
        block = tuple(shape)
        self.mine, self.came = slot.vmem((chips,) + block, BF), slot.vmem((chips,) + block, BF)
        self.chip_in = slot.vmem((chips // 2,) + block, BF)
        self.diag = slot.vmem(block, BF) if with_dp else None
        self.total = slot.vmem(block, F32)
        self.loads = slot.sems(chips * pieces)
        self.outs = slot.sems(pieces)
        self.base = slot.sems(2 * pieces * (chips + 3))

    def spot(self, q, c, p):
        x = (self.ctx >> 1) ^ (q & 1)
        d = self.dp ^ (q >> 1)
        block = d * 4 + x * 2 + c if self.with_dp else x * 2 + c
        step = self.rows // self.pieces
        if self.dim == 1:
            return self.source.ref.at[pl.ds(p * step, step), pl.ds(pl.multiple_of(block * self.size, self.size), self.size)]
        return self.source.ref.at[pl.ds(pl.multiple_of(block * self.size + p * step, step), step)]

    def part(self, p):
        step = self.rows // self.pieces
        return pl.ds(p * step, step)

    def load(self, q, p):
        core = self.ctx & 1
        return pltpu.make_async_copy(
            self.spot(q, core, p), self.mine.ref.at[q, self.part(p)], self.slot.sem(self.loads + q * self.pieces + p)
        )

    def begin(self):
        self.coordinates()
        core = self.ctx & 1
        self.order = (3, 1, 2, 0) if self.with_dp else (1, 0)
        self.per = self.chips + 3
        for p in range(self.pieces):
            for q in self.order:
                self.send(self.per * p + q, self.spot(q, core ^ 1, p), self.came.ref.at[q, self.part(p)], self.cdev)
                self.load(q, p).start()

    def add(self, into, other, p):
        step = self.rows // self.pieces
        tile = min(32, step)

        @pl.loop(0, step // tile)
        def _(i):
            part = pl.ds(pl.multiple_of(p * step + i * tile, tile), tile)
            into[part] = (into[part].astype(F32) + other[part].astype(F32)).astype(BF)

    def steps(self, p, via):
        mine, came = self.mine, self.came

        def cores():
            for q in self.order:
                self.load(q, p).wait()
                self.got(self.per * p + q, came.ref.at[q, self.part(p)])
                self.add(mine.ref.at[q], came.ref.at[q], p)

        def out(k, q, target, device):
            def issue():
                self.send(self.per * p + self.chips + k, mine.ref.at[q, self.part(p)], target(), device())

            return issue

        xdev, ydev = (lambda: self.xdev), (lambda: self.ydev)
        into = lambda j: (lambda: self.chip_in.ref.at[j, self.part(p)])
        done = {}

        def last(k, j):
            def arrive():
                self.got(self.per * p + self.chips + k, self.chip_in.ref.at[j, self.part(p)])
                done[j] = True
                if len(done) == self.chips // 2:
                    done.clear()
                    self.close(p)

            return arrive

        steps = [Step(self, (p, "c"), None, 2.0 + self.unit * 0.5, [], 3 * p, None, cores)]
        if not self.with_dp:
            steps.append(Step(self, (p, 0), 0, self.unit, [(p, "c")], 3 * p + 1, out(0, 1, into(0), xdev), last(0, 0)))
            return steps
        corner = lambda: self.diag.ref.at[self.part(p)]

        def fold():
            self.got(self.per * p + self.chips + 2, corner())
            self.add(mine.ref.at[2 if via == 0 else 1], self.diag.ref, p)

        steps.append(
            Step(self, (p, 2), via, self.unit, [(p, "c")], 3 * p, out(2, 3, corner, xdev if via == 0 else ydev), fold)
        )
        for k, device in ((0, xdev), (1, ydev)):
            deps = [(p, "c")] if k == via else [(p, 2)]
            steps.append(Step(self, (p, k), k, self.unit, deps, 3 * p + 1, out(k, 1 + k, into(k), device), last(k, k)))
        return steps

    def result(self, p):
        target = self.out.ref
        step = self.rows // self.pieces
        if self.where is None:
            target = target.at[pl.ds(p * step, step)]
        else:
            row, col = self.where
            target = target.at[pl.ds(row + p * step, step), pl.ds(col, self.width)]
        return pltpu.make_async_copy(self.total.ref.at[self.part(p)], target, self.slot.sem(self.outs + p))

    def close(self, p):
        step = self.rows // self.pieces
        tile = min(32, step)
        mine, chip_in, total = self.mine.ref, self.chip_in.ref, self.total.ref

        @pl.loop(0, step // tile)
        def _(i):
            part = pl.ds(pl.multiple_of(p * step + i * tile, tile), tile)
            value = mine[0, part].astype(F32) + chip_in[0, part].astype(F32)
            if self.with_dp:
                value = value + chip_in[1, part].astype(F32)
            total[part] = value

        self.result(p).start()

    def finish(self):
        for copy in self.sent:
            copy.wait_send()
        for p in range(self.pieces):
            self.result(p).wait()


class Handle:
    ref = None
    sem = None
    waited = False
    lazy = False
    halves = False
    value = None

    def __init__(self, shape=None, dtype=None):
        self.shape, self.dtype = shape, dtype


class Slot:
    def __init__(self, name, ident, line_rate=97.0, plane_rate=48.0):
        self.name, self.ident = name, ident
        self.rates = (line_rate, plane_rate)
        self.inputs, self.outputs, self.scratch = [], [], []
        self.sem_count = 0
        self.tasks = []
        self.axes = set()
        self.early = []
        self.prologue = []
        self.plane = None
        self.loads, self.stores = [], []
        self.flags = {}
        self.now = 0.0

    def sems(self, number):
        first = self.sem_count
        self.sem_count += number
        return first

    def hbm_in(self, array):
        if isinstance(array, Handle):
            return array
        handle = Handle(array.shape, array.dtype)
        self.inputs.append((array, handle))
        return handle

    def hbm_out(self, shape, dtype):
        handle = Handle(shape, dtype)
        self.outputs.append((jax.ShapeDtypeStruct(shape, dtype), handle))
        return handle

    def vmem(self, shape, dtype):
        handle = Handle(shape, dtype)
        self.scratch.append((pltpu.VMEM(shape, dtype), handle))
        return handle

    def load(self, array):
        handle = self.vmem(array.shape, array.dtype)
        handle.source = self.hbm_in(array)
        handle.sem = self.sems(1)
        self.loads.append(handle)
        return handle

    def store(self, shape, dtype):
        handle = self.vmem(shape, dtype)
        handle.target = self.hbm_out(shape, dtype)
        handle.sem = self.sems(2)
        self.stores.append(handle)
        return handle

    def late(self, array):
        handle = self.vmem(array.shape, array.dtype)
        handle.source = self.hbm_in(array)
        handle.sem = self.sems(1)
        handle.lazy = True
        self.loads.append(handle)
        return handle

    def fetch(self, *handles):
        for handle in handles:
            pltpu.make_async_copy(handle.source.ref, handle.ref, self.sem(handle.sem)).start()

    def need(self, *handles):
        for handle in handles:
            if not handle.waited:
                handle.waited = True
                pltpu.make_async_copy(handle.source.ref, handle.ref, self.sem(handle.sem)).wait()

    def flush(self, *handles):
        for handle in handles:
            pltpu.make_async_copy(handle.ref, handle.target.ref, self.sem(handle.sem)).start()

    def flush_half(self, h, *handles):
        for handle in handles:
            half = handle.shape[0] // 2
            part = pl.ds(h * half, half)
            handle.halves = True
            pltpu.make_async_copy(handle.ref.at[part], handle.target.ref.at[part], self.sem(handle.sem + h)).start()

    def sem(self, index):
        return self.sem_ref.at[index]

    def at(self, index):
        return self.sem_ref.at[index]

    def add(self, body, transfers=False):
        self.tasks.append((body, transfers))

    def mark(self, flag):
        self.flags[flag] = True

    def mark_early(self, flag):
        self.early.append(flag)

    def kernel(self, *refs):
        refs = list(refs)
        for group in (self.inputs, self.outputs, self.scratch):
            for _, handle in group:
                handle.ref = refs.pop(0)
        self.sem_ref = refs.pop(0)
        self.flags, self.now = {flag: True for flag in self.early}, 0.0
        for handle in self.loads:
            handle.waited = False
            if not handle.lazy:
                pltpu.make_async_copy(handle.source.ref, handle.ref, self.sem(handle.sem)).start()
        for begin in self.prologue:
            begin()
        self.place = place = Place(4)
        barrier = pltpu.get_barrier_semaphore()
        peers = []
        if "ctx" in self.axes:
            peers += [{"ctx": place.ctx ^ 1}, {"ctx": place.ctx ^ 2}]
        if "dp" in self.axes:
            peers += [{"dp": place.dp ^ 1}]
        if "tp" in self.axes:
            peers += [{"tp": place.tp ^ k} for k in (1, 2, 3)]
        for device in peers:
            pl.semaphore_signal(barrier, inc=1, device_id=device, device_id_type=MESH)
        pl.semaphore_wait(barrier, len(peers))
        if self.plane is not None:
            self.plane.planned = False
        running = [[("at", 0.0), task(), 0 if transfers else 1, i] for i, (task, transfers) in enumerate(self.tasks)]
        while running:
            ready = None
            for entry in running:
                kind, value = entry[0]
                if (kind == "at" and value <= self.now) or (kind == "flag" and value in self.flags):
                    key = (entry[2], value if kind == "at" and entry[2] == 0 else 0.0, entry[3])
                    if ready is None or key < ready[0]:
                        ready = (key, entry)
            if ready is None:
                self.now = min(entry[0][1] for entry in running if entry[0][0] == "at")
                continue
            entry = ready[1]
            try:
                got = next(entry[1])
            except StopIteration:
                running.remove(entry)
                continue
            if got[0] == "did":
                self.now += got[1]
                got = ("at", self.now)
            entry[0] = got
        for handle in self.stores:
            if not handle.halves:
                pltpu.make_async_copy(handle.ref, handle.target.ref, self.sem(handle.sem)).wait()
                continue
            half = handle.shape[0] // 2
            for h in (0, 1):
                part = pl.ds(h * half, half)
                pltpu.make_async_copy(handle.ref.at[part], handle.target.ref.at[part], self.sem(handle.sem + h)).wait()

    def run(self):
        values = pl.pallas_call(
            self.kernel,
            out_shape=tuple(o for o, _ in self.outputs),
            in_specs=[HBM] * len(self.inputs),
            out_specs=tuple([HBM] * len(self.outputs)),
            scratch_shapes=[s for s, _ in self.scratch] + [pltpu.SemaphoreType.DMA((self.sem_count,))],
            compiler_params=pltpu.CompilerParams(
                collective_id=self.ident, has_side_effects=True, vmem_limit_bytes=62 * 1024 * 1024
            ),
            name=self.name,
        )(*[a for a, _ in self.inputs])
        for (_, handle), value in zip(self.outputs, values):
            handle.value = value


def any_of(me, values):
    values = sorted(values)
    cond = me == values[0]
    for v in values[1:]:
        cond = jnp.logical_or(cond, me == v)
    return cond


def pick(me, table):
    items = sorted(table.items())
    out = jnp.int32(items[0][1])
    for key, value in items[1:]:
        out = jnp.where(me == key, jnp.int32(value), out)
    return out


PAIR = {0: ["A0", "R3", "R2", "R1"], 1: ["A1", "A0", "R3", "R2"], 2: ["A2", "A1", "A0", "R3"]}
ONLY_A = {0: ["A0", "", ""], 1: ["A1", "A0", ""], 2: ["A2", "A1", "A0"]}
ONLY_R = {0: ["R3", "R2", "R1"], 1: ["", "R3", "R2"], 2: ["", "", "R3"]}


class Line:
    def __init__(self, slot, rows, width, gather=None, scatter=False, pieces=2, keep=True):
        self.slot, self.rows, self.width, self.pieces = slot, rows, width, pieces
        self.gather, self.scatter = gather is not None, scatter
        slot.axes.add("tp")
        right = PAIR if self.gather and scatter else (ONLY_A if self.gather else ONLY_R)
        flip = lambda m: m if not m else m[0] + str(3 - int(m[1]))
        self.tables = (right, {3 - d: [flip(m) for m in row] for d, row in right.items()})
        self.steps = len(right[0])
        self.keep = keep
        if self.gather:
            self.source = slot.hbm_in(gather)
            self.wide = slot.vmem((4, rows, width), BF)
            self.own_sem = slot.sems(1)
            if keep:
                self.out = slot.hbm_out((rows, 4 * width), BF)
                self.out_sem = slot.sems(4)
        if scatter:
            self.mine = slot.vmem((4, rows, width), BF)
            self.skip = self.steps - 3
            self.came = slot.vmem((2, 3, rows, width), BF)
        self.base = slot.sems(4 * self.steps * pieces)
        self.unit = rows * width * 4 / (slot.rates[0] * 1e3)
        slot.add(self.body, True)

    def chunk(self, k):
        me = self.slot.place.tp
        return (me, pick(me, {0: 1, 1: 2, 2: 1, 3: 2}), pick(me, {0: 2, 1: 0, 2: 3, 3: 1}), pick(me, {0: 3, 1: 3, 2: 0, 3: 0}))[k]

    def index(self, way, t, p):
        return self.base + 2 * ((way * self.steps + t) * self.pieces + p)

    def part(self, p):
        step = self.rows // self.pieces
        return pl.ds(p * step, step)

    def sends(self, t, p):
        me = self.slot.place.tp
        rows = self.part(p)
        for way in (0, 1):
            for kind in "AR":
                table = {d: int(row[t][1]) for d, row in self.tables[way].items() if row[t][:1] == kind}
                if not table:
                    continue
                block = pick(me, table)
                if kind == "A":
                    target = self.wide.ref.at[block, rows]
                    origin = self.source.ref.at[rows] if t == 0 else target
                else:
                    target = self.came.ref.at[way, t - self.skip, rows]
                    origin = self.mine.ref.at[block, rows]
                index = self.index(way, t, p)
                to = me + 1 if way == 0 else me - 1
                yield kind, any_of(me, table), remote(origin, target, self.slot, index, index + 1, {"tp": to})

    def arrivals(self, t, p):
        me = self.slot.place.tp
        rows = self.part(p)
        step = self.rows // self.pieces
        tile = 64
        for way in (0, 1):
            off = 1 if way == 0 else -1
            froms = {d + off: row[t] for d, row in self.tables[way].items() if row[t]}
            sample = self.wide.ref.at[0, rows] if self.gather else self.came.ref.at[0, 0, rows]
            index = self.index(way, t, p)
            pl.when(any_of(me, froms))(remote(sample, sample, self.slot, index, index + 1, {"tp": me}).wait_recv)
            adds = {d: int(m[1]) for d, m in froms.items() if m[0] == "R" and int(m[1]) != d}
            if adds:
                block = pick(me, adds)
                mine, came = self.mine.ref, self.came.ref

                @pl.when(any_of(me, adds))
                def _():
                    @pl.loop(0, step // tile)
                    def _(i):
                        part = pl.ds(pl.multiple_of(p * step + i * tile, tile), tile)
                        mine[block, part] = (mine[block, part].astype(F32) + came[way, t - self.skip, part].astype(F32)).astype(BF)

    def body(self):
        slot = self.slot
        me = slot.place.tp
        if self.gather:
            own = pltpu.make_async_copy(self.source.ref, self.wide.ref.at[me], slot.sem(self.own_sem))
            own.start()
        start = 0.0
        for t in range(self.steps):
            for p in range(self.pieces):
                if t > 0:
                    yield ("at", start + (t - 1 + (p + 1) / self.pieces) * self.unit + 0.5)
                    self.arrivals(t - 1, p)
                    if p == self.pieces - 1 and self.gather and t <= 3:
                        slot.mark("chunk%d" % t)
                messages = list(self.sends(t, p))
                for kind, cond, copy in messages:
                    if kind == "A":
                        pl.when(cond)(copy.start)
                if any(kind == "R" for kind, _, _ in messages):
                    first = t == (1 if self.gather else 0)
                    if p == 0:
                        for c in ((3, 0) if first else (2, 1)):
                            yield ("flag", "part%d" % c)
                        start = max(start, slot.now - t * self.unit)
                    for kind, cond, copy in messages:
                        if kind == "R":
                            pl.when(cond)(copy.start)
                if t == 0 and p == 0 and self.gather:
                    yield ("at", 1.0)
                    own.wait()
                    slot.mark("chunk0")
        for p in range(self.pieces):
            yield ("at", start + (self.steps - 1 + (p + 1) / self.pieces) * self.unit + 0.5)
            self.arrivals(self.steps - 1, p)
            if self.scatter and (2 * p + 2) % self.pieces == 0:
                slot.mark("reduced%d" % (2 * (p + 1) // self.pieces - 1))
        if self.gather and self.steps == 3:
            slot.mark("chunk3")
        outs = []
        if self.gather and self.keep:
            for c in range(4):
                where = self.out.ref.at[:, pl.ds(c * self.width, self.width)]
                outs.append(pltpu.make_async_copy(self.wide.ref.at[c], where, slot.sem(self.out_sem + c)))
                outs[-1].start()
        yield ("at", start + self.steps * self.unit + 1.0)
        for t in range(self.steps):
            for p in range(self.pieces):
                for _, cond, copy in self.sends(t, p):
                    pl.when(cond)(copy.wait_send)
        for copy in outs:
            copy.wait()

    def total(self, part):
        me = self.slot.place.tp
        last = 2
        left = jnp.where(me > 0, self.came.ref[0, last, part].astype(F32), 0.0)
        right = jnp.where(me < 3, self.came.ref[1, last, part].astype(F32), 0.0)
        return self.mine.ref[me, part].astype(F32) + left + right


def tiled(count, tile, body):
    @pl.loop(0, count // tile)
    def _(i):
        body(pl.ds(pl.multiple_of(i * tile, tile), tile))


class Weights:
    def __init__(self, slot, groups, shape, order, where):
        self.slot, self.order, self.where = slot, order, where
        self.groups = [[slot.hbm_in(a) for a in group] for group in groups]
        self.wide = shape[1] // len(groups[0])
        self.buffer = slot.vmem((2, len(groups)) + shape, BF)
        self.base = slot.sems(2 * sum(len(g) for g in groups))

    def copies(self, step):
        block = self.order[step] if not callable(self.order) else self.order(step)
        index = self.base + step % 2
        for j, group in enumerate(self.groups):
            for k, array in enumerate(group):
                target = self.buffer.ref.at[step % 2, j]
                if len(group) > 1:
                    target = target.at[:, pl.ds(k * self.wide, self.wide)]
                yield pltpu.make_async_copy(self.where(array.ref, block), target, self.slot.sem(index))
                index += 2

    def start(self, step):
        for copy in self.copies(step):
            copy.start()

    def take(self, step):
        for copy in self.copies(step):
            copy.wait()
        return [self.buffer.ref.at[step % 2, j] for j in range(len(self.groups))]


def row_block(ref, c):
    return ref.at[pl.ds(pl.multiple_of(c * 512, 512), 512)]


def col_block(ref, c):
    return ref.at[:, pl.ds(pl.multiple_of(c * 512, 512), 512)]


def consume(slot, line, groups, shape, where, last, multiply, parts, cost):
    weights = Weights(slot, groups, shape, line.chunk, where)

    def body():
        weights.start(0)
        for k in range(4):
            if k < 3:
                weights.start(k + 1)
            yield ("flag", "chunk%d" % k)
            blocks = weights.take(k)
            chunk = line.chunk(k)
            for j, block in enumerate(blocks):
                for part in range(parts):
                    multiply(k == 0, line.wide.ref.at[chunk], block, j, part)
                    yield ("did", cost)
        yield from last()

    slot.add(body)


def dot_nn(left, right):
    return jnp.dot(left, right, preferred_element_type=F32)


def dot_nt(left, right):
    return lax.dot_general(left, right, (((1,), (1,)), ((), ())), preferred_element_type=F32)


def produce(slot, line, lefts, groups, shape, where, dot, cost, gate=None):
    order = (3, 0, 2, 1)
    weights = Weights(slot, groups, shape, order, where)

    def body():
        weights.start(0)
        if gate is not None:
            yield ("flag", gate)
        slot.need(*lefts)
        half = line.rows // 2
        for k, c in enumerate(order):
            if k < 3:
                weights.start(k + 1)
            blocks = weights.take(k)
            for h in (0, 1):
                part = pl.ds(h * half, half)
                value = None
                for left, block in zip(lefts, blocks):
                    term = dot(left.ref[part], block[...])
                    value = term if value is None else value + term
                line.mine.ref[c, part] = value.astype(BF)
                yield ("did", cost / 2)
            slot.mark("part%d" % c)

    slot.add(body)


def joined(slot, arrays):
    rows = arrays[0].shape[0]
    handle = slot.vmem((len(arrays) * rows, arrays[0].shape[1]), arrays[0].dtype)
    sources = [slot.hbm_in(a) for a in arrays]
    base = slot.sems(len(arrays))

    def copies():
        return [
            pltpu.make_async_copy(a.ref, handle.ref.at[pl.ds(b * rows, rows)], slot.sem(base + b)) for b, a in enumerate(sources)
        ]

    def begin():
        handle.waited = False
        for copy in copies():
            copy.start()

    def ready():
        if not handle.waited:
            handle.waited = True
            for copy in copies():
                copy.wait()

    slot.prologue.append(begin)
    handle.ready = ready
    return handle


def weight_grad(slot, left, right, out, where, flags, cost, gates):
    buffer = slot.vmem(out[1], BF)
    base = slot.sems(1)

    def body():
        yield ("at", 2.5)
        tall, wide = out[1]
        target = buffer.ref
        for k, (rows, cols) in enumerate(where):
            if gates is not None:
                yield ("flag", gates[k])
            left.ready()
            right.ready()
            for i in range((tall // 512) * (wide // 512)):
                r, c = (512 * i, 0) if wide == 512 else (0, 512 * i)
                value = dot_tn(left.ref[:, pl.ds(rows + r, 512)], right.ref[:, pl.ds(cols + c, 512)])
                target[pl.ds(r, 512), pl.ds(c, 512)] = value.astype(BF)
                yield ("did", cost / 4)
            copy = pltpu.make_async_copy(target, out[0][k].ref, slot.sem(base))
            copy.start()
            yield ("at", slot.now + 0.7)
            copy.wait()
            slot.mark(flags[k])

    slot.add(body)


class RowTotals:
    def __init__(self, slot, rows):
        self.slot, self.rows = slot, rows
        self.stat = slot.vmem((rows, 128), F32)
        self.send = slot.vmem((8, rows), F32)
        self.came = slot.vmem((3, 8, rows), F32)
        self.total = slot.vmem((rows, 128), F32)
        self.base = slot.sems(6)

    def put(self, part, *columns):
        lane = lax.broadcasted_iota(jnp.int32, (columns[0].shape[0], 128), 1)
        value = jnp.zeros((columns[0].shape[0], 128), F32)
        for k, column in enumerate(columns):
            value = jnp.where(lane == k, column, value)
        self.stat.ref[part] = value

    def exchange(self):
        slot, me = self.slot, self.slot.place.tp
        send = self.send.ref
        send[...] = jnp.transpose(self.stat.ref[...])[0:8]
        copies = []
        for k in (1, 2, 3):
            copies.append(
                remote(send, self.came.ref.at[k - 1], slot, self.base + 2 * (k - 1), self.base + 2 * (k - 1) + 1, {"tp": me ^ k})
            )
            copies[-1].start()
        yield ("at", slot.now + 2.5)
        for copy in copies:
            copy.wait()
        total = send[...] + self.came.ref[0] + self.came.ref[1] + self.came.ref[2]
        wide = jnp.concatenate([total, jnp.zeros((120, self.rows), F32)], axis=0)
        self.total.ref[...] = jnp.transpose(wide)

    def column(self, part, k):
        return self.total.ref[part, k : k + 1]


def finish(slot, line, rows, begin, first, second, flushed, ended, needs):
    half = rows // 2
    left = []

    def make(h):
        totals = RowTotals(slot, half)

        def body():
            yield ("flag", "reduced%d" % h)
            if h == 0:
                left[:] = [0, 1]
                slot.need(*needs)
                begin()
            for i in range(2):
                tiled_at(h * half + i * (half // 2), half // 2, 32, lambda part, here: first(totals, part, here), i * (half // 2))
                yield ("did", 0.5)
            yield from totals.exchange()
            tiled_at(h * half, half, 32, lambda part, here: second(totals, part, here), 0)
            slot.flush_half(h, *flushed)
            left.remove(h)
            if not left:
                slot.flush(*ended)
            yield ("did", 1.5)

        slot.add(body)

    make(0)
    make(1)


def tiled_at(row, count, tile, body, local):
    @pl.loop(0, count // tile)
    def _(i):
        body(
            pl.ds(pl.multiple_of(row + i * tile, tile), tile),
            pl.ds(pl.multiple_of(local + i * tile, tile), tile),
        )


def fold_rows(value):
    total = value[0:8]
    for i in range(1, value.shape[0] // 8):
        total = total + value[8 * i : 8 * i + 8]
    return total


def attn_finish(slot, line, rows, width, x, gain):
    x, gain = slot.load(x), slot.load(gain.reshape(1, width))
    raw, resid = slot.store((rows, width), F32), slot.store((rows, width), F32)
    resid_b, factor = slot.store((rows, width), BF), slot.store((rows, 128), F32)

    def first(totals, part, here):
        value = line.total(part)
        raw.ref[part] = value
        totals.put(here, jnp.sum(value * value, axis=1, keepdims=True))

    def second(totals, part, here):
        scale = lax.rsqrt(totals.column(here, 0) / D + EPS)
        value = x.ref[part].astype(F32) + raw.ref[part] * scale * gain.ref[...]
        resid.ref[part] = value
        resid_b.ref[part] = value.astype(BF)
        factor.ref[part] = jnp.broadcast_to(scale, (32, 128))

    finish(slot, line, rows, lambda: None, first, second, (resid_b, raw, resid, factor), (), (x, gain))
    return [raw.target, resid.target, resid_b.target, factor.target]


def mlp_finish(slot, line, rows, width, resid, cot, gain):
    resid, cot, gain = slot.load(resid), slot.load(cot), slot.load(gain.reshape(1, width))
    raw = slot.vmem((rows, width), F32)
    out, grad = slot.store((rows, width), BF), slot.store((rows, width), BF)
    gain_grad = slot.store((8, width), F32)

    def begin():
        gain_grad.ref[...] = jnp.zeros((8, width), F32)

    def first(totals, part, here):
        value = line.total(part)
        raw.ref[part] = value
        scaled = cot.ref[part].astype(F32) * gain.ref[...]
        totals.put(here, jnp.sum(value * value, axis=1, keepdims=True), jnp.sum(scaled * value, axis=1, keepdims=True))

    def second(totals, part, here):
        scale = lax.rsqrt(totals.column(here, 0) / D + EPS)
        inner = totals.column(here, 1)
        value = raw.ref[part]
        given = cot.ref[part].astype(F32)
        normed = value * scale
        grad.ref[part] = (scale * (given * gain.ref[...]) - value * (scale * scale * scale * inner / D)).astype(BF)
        out.ref[part] = (resid.ref[part] + normed * gain.ref[...]).astype(BF)
        gain_grad.ref[...] += fold_rows(given * normed)

    finish(slot, line, rows, begin, first, second, (grad, out), (gain_grad,), (resid, cot, gain))
    return [out.target, grad.target, gain_grad.target]


def resid_finish(slot, line, rows, width, cot, attn, factor, gain):
    cot, attn, factor, gain = slot.load(cot), slot.load(attn), slot.load(factor), slot.load(gain.reshape(1, width))
    resid, grad = slot.store((rows, width), F32), slot.store((rows, width), BF)
    gain_grad = slot.store((8, width), F32)

    def begin():
        gain_grad.ref[...] = jnp.zeros((8, width), F32)

    def first(totals, part, here):
        value = line.total(part) + cot.ref[part].astype(F32)
        resid.ref[part] = value
        totals.put(here, jnp.sum(value * gain.ref[...] * attn.ref[part], axis=1, keepdims=True))

    def second(totals, part, here):
        scale = factor.ref[part, 0:1]
        inner = totals.column(here, 0)
        value, given = attn.ref[part], resid.ref[part]
        grad.ref[part] = (scale * (given * gain.ref[...]) - value * (scale * scale * scale * inner / D)).astype(BF)
        gain_grad.ref[...] += fold_rows(given * value * scale)

    finish(slot, line, rows, begin, first, second, (grad, resid), (gain_grad,), (cot, attn, factor, gain))
    return [resid.target, grad.target, gain_grad.target]


def last_finish(slot, line, rows, width, resid):
    resid = slot.load(resid)
    out = slot.store((rows, width), BF)
    half = rows // 2

    def make(h):
        def body():
            yield ("flag", "reduced%d" % h)
            slot.need(resid)

            def only(part, here):
                out.ref[part] = (line.total(part) + resid.ref[part]).astype(BF)

            tiled_at(h * half, half, 32, only, 0)
            slot.flush_half(h, out)
            yield ("did", 0.7)

        slot.add(body)

    make(0)
    make(1)
    return [out.target]


def gate_up(slot, line, rows, w_gate, w_up):
    ff = len(w_gate) * w_gate[0].shape[1]
    acc = slot.vmem((2, rows, ff), F32)
    gate, up, act = (slot.store((rows, ff), BF) for _ in range(3))
    wide = ff // 2

    def multiply(first, left, block, j, part):
        cols = pl.ds(part * wide, wide)
        value = dot_nn(left[...], block[:, cols])
        acc.ref[j, :, cols] = value if first else acc.ref[j, :, cols] + value

    def last():
        piece = rows // 4
        for h in range(4):

            @pl.loop(0, piece // 16)
            def _(i):
                part = pl.ds(pl.multiple_of(h * piece + i * 16, 16), 16)
                g, u = acc.ref[0, part], acc.ref[1, part]
                gate.ref[part] = g.astype(BF)
                up.ref[part] = u.astype(BF)
                act.ref[part] = (g * jax.nn.sigmoid(g) * u).astype(BF)

            if h % 2:
                slot.flush_half(h // 2, act, gate, up)
            yield ("did", 1.0)

    consume(slot, line, (w_gate, w_up), (512, ff), row_block, last, multiply, 2, 1.1)
    return [gate.target, up.target, act.target]


def act_back(slot, line, rows, w_down, gate, up):
    ff = w_down.shape[0]
    acc = slot.vmem((rows, ff), F32)
    gate, up = slot.load(gate), slot.load(up)
    g_gate, g_up = slot.store((rows, ff), BF), slot.store((rows, ff), BF)
    wide = ff // 2

    def multiply(first, left, block, j, part):
        cols = pl.ds(part * wide, wide)
        value = dot_nt(left[...], block[cols])
        acc.ref[:, cols] = value if first else acc.ref[:, cols] + value

    def last():
        slot.need(gate, up)
        piece = rows // 4
        for h in range(4):

            @pl.loop(0, piece // 16)
            def _(i):
                part = pl.ds(pl.multiple_of(h * piece + i * 16, 16), 16)
                grad, g, u = acc.ref[part], gate.ref[part].astype(F32), up.ref[part].astype(F32)
                sigma = jax.nn.sigmoid(g)
                g_gate.ref[part] = (grad * u * sigma * (1.0 + g * (1.0 - sigma))).astype(BF)
                g_up.ref[part] = (grad * g * sigma).astype(BF)

            if h % 2:
                slot.flush_half(h // 2, g_gate, g_up)
            yield ("did", 1.2)

    consume(slot, line, ((w_down,),), (ff, 512), col_block, last, multiply, 2, 1.2)
    return [g_gate.target, g_up.target]


def half_turn(value):
    return pltpu.roll(value, HEAD_DIM // 2, axis=1)


def tables(slot, positions, freqs, sign):
    count = positions.shape[0]
    positions, freqs, sign = slot.load(positions), slot.load(freqs), slot.load(sign)
    cosine, sine = slot.store((count, HEAD_DIM), F32), slot.store((count, HEAD_DIM), F32)

    def body():
        slot.need(positions, freqs, sign)

        def first(part):
            angle = positions.ref[part].astype(F32) * freqs.ref[...]
            cosine.ref[part] = jnp.cos(angle)
            sine.ref[part] = jnp.sin(angle) * sign.ref[...]

        tiled(count, 32, first)
        slot.flush(cosine, sine)
        yield ("did", 6.0)
        slot.mark("tables")

    slot.add(body)
    return cosine, sine


def head_cols(h):
    return pl.ds(h * HEAD_DIM, HEAD_DIM)


def project(slot, line, rows, width, weights, flags, gains, cosine, sine, first_row):
    stages = [slot.late(w) for w in weights]
    gains = [slot.load(g.reshape(1, width)) for g in gains]
    raws = [slot.store((rows, width), F32) for _ in (0, 1)]
    query, kv = slot.store((rows, width), BF), slot.store((rows, 2 * width), BF)
    factor = slot.store((rows, 128), F32)
    half = rows // 2

    def make(h):
        totals = RowTotals(slot, half)

        def body():
            part = pl.ds(h * half, half)
            if h == 0:
                for j in range(3):
                    if flags is not None:
                        yield ("flag", flags[j])
                    slot.fetch(stages[j])
                yield ("flag", "chunk3")
            else:
                yield ("flag", "stages")
            wide = line.wide.ref
            for j in range(3):
                slot.need(stages[j])
                weight = stages[j].ref
                value = dot_nn(wide[0, part], weight[0:width])
                for c in (1, 2, 3):
                    value = value + dot_nn(wide[c, part], weight[c * width : (c + 1) * width])
                if j < 2:
                    raws[j].ref[part] = value
                else:
                    kv.ref[part, width : 2 * width] = value.astype(BF)
                yield ("did", 1.1)

            def first(part, here):
                q, k = raws[0].ref[part], raws[1].ref[part]
                totals.put(here, jnp.sum(q * q, axis=1, keepdims=True), jnp.sum(k * k, axis=1, keepdims=True))

            tiled_at(h * half, half, 32, first, 0)
            slot.flush_half(h, *raws)
            if h == 0:
                slot.mark("stages")
            yield from totals.exchange()
            yield ("flag", "tables")
            slot.need(*gains)
            slot.need(*[t for t in (cosine, sine) if hasattr(t, "source")])

            def second(part, here):
                trig = pl.ds(pl.multiple_of(first_row + h * half + here.start, 32), 32)
                lane = lax.broadcasted_iota(jnp.int32, (32, 128), 1)
                scales = [lax.rsqrt(totals.column(here, j) / D + EPS) for j in (0, 1)]
                factor.ref[part] = jnp.where(lane == 0, scales[0], scales[1])
                co, si = cosine.ref[trig], sine.ref[trig]
                for j, target in ((0, query), (1, kv)):
                    for n in range(width // HEAD_DIM):
                        value = raws[j].ref[part, head_cols(n)] * scales[j] * gains[j].ref[:, head_cols(n)]
                        target.ref[part, head_cols(n)] = (value * co + half_turn(value) * si).astype(BF)

            tiled_at(h * half, half, 32, second, 0)
            slot.flush_half(h, kv, query, factor)
            yield ("did", 1.5)

        slot.add(body)

    make(0)
    make(1)
    return [raws[0].target, raws[1].target, query.target, kv.target, factor.target]


class Mask:
    def __init__(self, slot, seg_all, seg_cols, first, count, turned=False):
        self.slot, self.first, self.count, self.turned = slot, first, count, turned
        self.keys, self.mine = slot.load(seg_all), slot.load(seg_cols)
        self.mask = slot.vmem((4 * count, count) if turned else (count, 4 * count), F32)

    def fill(self, s):
        self.slot.need(self.keys, self.mine)
        count = self.count
        ctx = self.slot.place.ctx
        mine = self.mine.ref[(self.first + s) * count : (self.first + s + 1) * count]
        for c in range(4):
            keys = self.keys.ref[8 * c + self.first + s : 8 * c + self.first + s + 1, :]
            row = ctx * count + lax.broadcasted_iota(jnp.int32, (count, count), 0)
            col = c * count + lax.broadcasted_iota(jnp.int32, (count, count), 1)
            fine = jnp.logical_and(mine[:, 0:1] == keys, row >= col)
            block = jnp.where(fine, 0.0, NEG)
            if self.turned:
                self.mask.ref[c * count : (c + 1) * count] = jnp.transpose(block)
            else:
                self.mask.ref[:, c * count : (c + 1) * count] = block


def attend(slot, flag, kv, query, mask, rows, width):
    kv, query = slot.late(kv), slot.load(query)
    count = mask.count
    heads, heads_b = slot.store((rows, width), F32), slot.store((rows, width), BF)
    logsum = slot.store((rows, 128), F32)
    logits = slot.vmem((count, 4 * count), F32)
    scale = 1.0 / math.sqrt(HEAD_DIM)

    def body():
        yield ("flag", flag)
        slot.fetch(kv)
        mask.fill(0)
        yield ("did", 1.5)
        slot.need(kv, query)
        logsum.ref[...] = jnp.zeros((rows, 128), F32)
        for s in range(rows // count):
            mine = pl.ds(s * count, count)
            if s:
                mask.fill(s)
                yield ("did", 1.0)
            for pair in range(width // HEAD_DIM // 2):
                heads_pair(s, mine, pair)
                yield ("did", 2.2)
        slot.flush(heads_b, heads, logsum)

    def heads_pair(s, mine, pair):
        @pl.loop(2 * pair, 2 * pair + 2)
        def _(h):
            cols = pl.ds(pl.multiple_of(h * HEAD_DIM, HEAD_DIM), HEAD_DIM)
            vcols = pl.ds(pl.multiple_of(width + h * HEAD_DIM, HEAD_DIM), HEAD_DIM)
            q = query.ref[mine, cols]
            peak = jnp.full((count, 1), NEG, F32)
            for c in range(4):
                keys = kv.ref[pl.ds(c * rows + s * count, count), cols]
                block = pl.ds(c * count, count)
                value = dot_nt(q, keys) * scale + mask.mask.ref[:, block]
                logits.ref[:, block] = value
                peak = jnp.maximum(peak, jnp.max(value, axis=1, keepdims=True))
            total = jnp.zeros((count, 1), F32)
            acc = jnp.zeros((count, HEAD_DIM), F32)
            for c in range(4):
                vals = kv.ref[pl.ds(c * rows + s * count, count), vcols]
                weight = jnp.exp(logits.ref[:, pl.ds(c * count, count)] - peak)
                total = total + jnp.sum(weight, axis=1, keepdims=True)
                acc = acc + dot_nn(weight.astype(BF), vals)
            out = acc / total
            heads.ref[mine, cols] = out
            heads_b.ref[mine, cols] = out.astype(BF)
            lane = lax.broadcasted_iota(jnp.int32, (count, 128), 1)
            logsum.ref[mine] = jnp.where(lane == h, peak + jnp.log(total), logsum.ref[mine])

    slot.add(body)
    return [heads.target, heads_b.target, logsum.target]


def attend_back(slot, line, kv, query, heads, logsum, mask, rows, width, w_out):
    kv, query, heads, logsum = slot.load(kv), slot.load(query), slot.load(heads), slot.load(logsum)
    count = mask.count
    grad = slot.vmem((rows, width), BF)
    g_query, g_kv = slot.store((rows, width), F32), slot.store((4 * rows, 2 * width), BF)
    acc = g_query
    rows_of = slot.vmem((2, 128, count), F32)
    scale = 1.0 / math.sqrt(HEAD_DIM)

    def multiply(first, left, block, j, part):
        value = dot_nt(left[...], block[...])
        acc.ref[...] = value if first else acc.ref[...] + value

    def last():
        grad.ref[...] = acc.ref[...].astype(BF)
        slot.need(kv, query, heads, logsum)
        for s in range(rows // count):
            mine = pl.ds(s * count, count)
            mask.fill(s)
            lane = lax.broadcasted_iota(jnp.int32, (count, 128), 1)
            deltas = jnp.zeros((count, 128), F32)
            for h in range(width // HEAD_DIM):
                cols = head_cols(h)
                delta = jnp.sum(grad.ref[mine, cols].astype(F32) * heads.ref[mine, cols], axis=1, keepdims=True)
                deltas = jnp.where(lane == h, delta, deltas)
            rows_of.ref[0] = jnp.transpose(logsum.ref[mine])
            rows_of.ref[1] = jnp.transpose(deltas)
            yield ("did", 1.5)
            for pair in range(width // HEAD_DIM // 2):
                heads_pair(s, mine, pair)
                yield ("did", 3.0)
        slot.flush(g_kv, g_query)

    def heads_pair(s, mine, pair):
        @pl.loop(2 * pair, 2 * pair + 2)
        def _(h):
            cols = pl.ds(pl.multiple_of(h * HEAD_DIM, HEAD_DIM), HEAD_DIM)
            vcols = pl.ds(pl.multiple_of(width + h * HEAD_DIM, HEAD_DIM), HEAD_DIM)
            q, g = query.ref[mine, cols], grad.ref[mine, cols]
            logs, delta = rows_of.ref[0, pl.ds(h, 1)], rows_of.ref[1, pl.ds(h, 1)]
            total = jnp.zeros((count, HEAD_DIM), F32)
            for c in range(4):
                there = pl.ds(c * rows + s * count, count)
                keys, vals = kv.ref[there, cols], kv.ref[there, vcols]
                value = dot_nt(keys, q) * scale + mask.mask.ref[pl.ds(c * count, count)]
                probs = jnp.exp(value - logs)
                slopes = (probs * (dot_nt(vals, g) - delta)).astype(BF)
                total = total + dot_tn(slopes, keys)
                g_kv.ref[there, cols] = (dot_nn(slopes, q) * scale).astype(BF)
                g_kv.ref[there, vcols] = dot_nn(probs.astype(BF), g).astype(BF)
            g_query.ref[mine, cols] = total * scale

    consume(slot, line, ((w_out,),), (width, width), col_block, last, multiply, 1, 0.7)
    return [g_query.target, g_kv.target]


def dot_tn(left, right):
    return lax.dot_general(left, right, (((0,), (0,)), ((), ())), preferred_element_type=F32)


def project_back(slot, flag, g_query, g_kv, raws, factor, gains, cosine, sine, first_row, rows, width):
    g_kv = slot.late(g_kv)
    g_query, factor = slot.load(g_query), slot.load(factor)
    raws = [slot.load(r) for r in raws]
    gains = [slot.load(g.reshape(1, width)) for g in gains]
    cosine, sine = slot.load(cosine), slot.load(sine)
    outs = [slot.store((rows, width), BF) for _ in range(3)]
    gain_grads = [slot.store((8, width), F32) for _ in range(2)]
    half = rows // 2
    left = []

    def make(h):
        totals = RowTotals(slot, half)

        def body():
            yield ("flag", flag)
            if h == 0:
                left[:] = [0, 1]
                slot.fetch(g_kv)
                for g in gain_grads:
                    g.ref[...] = jnp.zeros((8, width), F32)
                slot.need(g_query, factor, cosine, sine, *raws, *gains)
                slot.need(g_kv)
                slot.mark("grads")
            else:
                yield ("flag", "grads")

            def first(part, here):
                trig = pl.ds(pl.multiple_of(first_row + h * half + here.start, 32), 32)
                co, si = cosine.ref[trig], sine.ref[trig]
                sums = []
                for j, source in ((0, g_query), (1, g_kv)):
                    scale = factor.ref[part, j : j + 1]
                    total = jnp.zeros((32, HEAD_DIM), F32)
                    for n in range(width // HEAD_DIM):
                        cols = head_cols(n)
                        value = source.ref[part, cols]
                        value = value * co - half_turn(value) * si
                        source.ref[part, cols] = value
                        term = value * raws[j].ref[part, cols]
                        total = total + term * gains[j].ref[:, cols]
                        gain_grads[j].ref[:, cols] += fold_rows(term * scale)
                    sums.append(jnp.sum(total, axis=1, keepdims=True))
                totals.put(here, *sums)

            tiled_at(h * half, half, 32, first, 0)
            left.remove(h)
            if not left:
                slot.flush(*gain_grads)
            yield ("did", 1.5)
            yield from totals.exchange()

            def second(part, here):
                for j, source in ((0, g_query), (1, g_kv)):
                    scale = factor.ref[part, j : j + 1]
                    inner = totals.column(here, j)
                    value = source.ref[part, 0:width] * gains[j].ref[...]
                    outs[j].ref[part] = (scale * value - raws[j].ref[part] * (scale * scale * scale * inner / D)).astype(BF)
                outs[2].ref[part] = g_kv.ref[part, width : 2 * width].astype(BF)

            tiled_at(h * half, half, 32, second, 0)
            slot.flush_half(h, *outs)
            yield ("did", 1.5)

        slot.add(body)

    make(0)
    make(1)
    return [h.target for h in outs + gain_grads]


def gain_sums(slot, arrays):
    loads = [slot.load(a) for a in arrays]
    width = arrays[0].shape[1]
    mine = [slot.vmem((8, width), F32) for _ in range(3)]
    came = [slot.vmem((8, width), F32) for _ in range(3)]
    out = slot.store((8, width), F32)
    base = slot.sems(6)
    slot.axes |= {"ctx", "dp"}

    def body():
        place = slot.place
        yield ("at", 2.0)
        slot.need(*loads)
        rows = []
        for k in range(0, len(loads), 2):
            rows.append(jnp.sum(loads[k].ref[...] + loads[k + 1].ref[...], axis=0, keepdims=True))
        value = jnp.concatenate(rows + [jnp.zeros((8 - len(rows), width), F32)], axis=0)
        for k, device in enumerate(({"ctx": place.ctx ^ 1}, {"ctx": place.ctx ^ 2}, {"dp": place.dp ^ 1})):
            mine[k].ref[...] = value
            copy = remote(mine[k].ref, came[k].ref, slot, base + 2 * k, base + 2 * k + 1, device)
            copy.start()
            yield ("at", 9.0 + 4.0 * k)
            copy.wait()
            value = mine[k].ref[...] + came[k].ref[...]
        out.ref[...] = value
        slot.flush(out)

    slot.add(body, True)
    return out.target


def grad_blocks(left, right, tall):
    rows, cols = left.shape[1], right.shape[1]
    if tall:
        return (rows, 512), [(0, 512 * k) for k in range(cols // 512)]
    return (512, cols), [(512 * k, 0) for k in range(rows // 512)]


def full_grad(slot, plane, left, right, tall, out, starts, prefix, chosen=None, gates=None):
    shape, where = grad_blocks(left, right, tall)
    chosen = range(len(where)) if chosen is None else chosen
    flags = [prefix + str(k) for k in chosen]
    blocks = [slot.hbm_out(shape, BF) for _ in chosen]
    base = where[chosen[0]]
    weight_grad(slot, left, right, (blocks, shape), [where[k] for k in chosen], flags, 3.6, gates)
    for i, k in enumerate(chosen):
        plane.scatter(blocks[i], 0 if tall else 1, True, 1, starts[i], flags[i], None, (out, (where[k][0] - base[0], where[k][1] - base[1])))


def general_row_total(value):
    return lax.psum(value, "tp")


def general_widen(value):
    return lax.all_gather(value, "tp", axis=1, tiled=True)


def general_narrow(value):
    return lax.psum_scatter(
        value.astype(jnp.bfloat16), "tp", scatter_dimension=1, tiled=True
    ).astype(jnp.float32)


def general_contract_last(left, right):
    return lax.dot_general(
        left, right, (((1,), (1,)), ((), ())), preferred_element_type=jnp.float32
    )


def general_contract_first(left, right):
    return lax.dot_general(
        left, right, (((0,), (0,)), ((), ())), preferred_element_type=jnp.float32
    )


def general_rotary(positions, depth):
    half = depth // 2
    freqs = THETA ** (-(jnp.arange(half, dtype=jnp.float32) * 2.0) / depth)
    angles = positions.astype(jnp.float32)[..., None] * freqs
    return (jnp.cos(angles)[..., None, :], jnp.sin(angles)[..., None, :])


def general_turn(value, cosine, sine):
    half = value.shape[-1] // 2
    first = value[..., :half]
    second = value[..., half:]
    return jnp.concatenate(
        [first * cosine - second * sine, second * cosine + first * sine], axis=-1
    )


def general_turn_back(grad, cosine, sine):
    half = grad.shape[-1] // 2
    first = grad[..., :half]
    second = grad[..., half:]
    return jnp.concatenate(
        [first * cosine + second * sine, second * cosine - first * sine], axis=-1
    )


def general_norm_grad(scaled, value, factor, inner):
    return factor[:, None] * scaled - value * (factor**3 * inner / D)[:, None]


def general(
    hidden,
    cotangent,
    segments,
    positions,
    w_query,
    w_key,
    w_value,
    w_out,
    w_gate,
    w_up,
    w_down,
    q_gain,
    k_gain,
    attn_gain,
    mlp_gain,
):
    local_seqs, slice_len, local_width = hidden.shape
    per_batch = local_seqs // 2
    rows = per_batch * slice_len
    heads_here = q_gain.shape[0] // HEAD_DIM
    scale = 1.0 / math.sqrt(HEAD_DIM)
    query_index = lax.axis_index("ctx") * slice_len + jnp.arange(slice_len, dtype=jnp.int32)
    outputs = []
    input_grads = []
    weight_grads = None
    q_gain_grad = jnp.zeros(q_gain.shape, jnp.float32)
    k_gain_grad = jnp.zeros(k_gain.shape, jnp.float32)
    attn_gain_grad = jnp.zeros(attn_gain.shape, jnp.float32)
    mlp_gain_grad = jnp.zeros(mlp_gain.shape, jnp.float32)
    for batch in range(2):
        lower = batch * per_batch
        tokens_in = hidden[lower : lower + per_batch].reshape(rows, local_width)
        seg_here = segments[lower : lower + per_batch]
        pos_here = positions[lower : lower + per_batch].reshape(rows)
        gathered = (
            lax.all_gather(w_query, ("dp", "ctx"), axis=0, tiled=True),
            lax.all_gather(w_key, ("dp", "ctx"), axis=0, tiled=True),
            lax.all_gather(w_value, ("dp", "ctx"), axis=0, tiled=True),
            lax.all_gather(w_out, ("dp", "ctx"), axis=1, tiled=True),
            lax.all_gather(w_gate, ("dp", "ctx"), axis=0, tiled=True),
            lax.all_gather(w_up, ("dp", "ctx"), axis=0, tiled=True),
            lax.all_gather(w_down, ("dp", "ctx"), axis=1, tiled=True),
        )
        query_full, key_full, value_full, out_full, gate_full, up_full, down_full = gathered
        if weight_grads is None:
            weight_grads = tuple((jnp.zeros(tensor.shape, jnp.float32) for tensor in gathered))
        wide_in = general_widen(tokens_in)
        query_raw = jnp.dot(wide_in, query_full, preferred_element_type=jnp.float32)
        key_raw = jnp.dot(wide_in, key_full, preferred_element_type=jnp.float32)
        value_raw = jnp.dot(wide_in, value_full, preferred_element_type=jnp.float32)
        query_sq, key_sq = general_row_total(
            (jnp.sum(query_raw * query_raw, axis=1), jnp.sum(key_raw * key_raw, axis=1))
        )
        query_scale = lax.rsqrt(query_sq / D + EPS)
        key_scale = lax.rsqrt(key_sq / D + EPS)
        cosine, sine = general_rotary(pos_here, HEAD_DIM)
        query_rot = general_turn(
            (query_raw * query_scale[:, None] * q_gain).reshape(rows, heads_here, HEAD_DIM),
            cosine,
            sine,
        )
        key_rot = general_turn(
            (key_raw * key_scale[:, None] * k_gain).reshape(rows, heads_here, HEAD_DIM),
            cosine,
            sine,
        )
        query_b = query_rot.astype(jnp.bfloat16).reshape(per_batch, slice_len, heads_here, HEAD_DIM)
        key_b = key_rot.astype(jnp.bfloat16).reshape(per_batch, slice_len, heads_here * HEAD_DIM)
        value_b = value_raw.astype(jnp.bfloat16).reshape(
            per_batch, slice_len, heads_here * HEAD_DIM
        )

        def allowed_pairs(seg_piece, count):
            key_index = jnp.arange(count, dtype=jnp.int32)
            causal = query_index[:, None] >= key_index[None, :]
            same = seg_here[:, None, :, None] == seg_piece[:, None, None, :]
            return jnp.logical_and(same, causal[None, None])

        start_peak = jnp.full((per_batch, heads_here, slice_len), NEG, jnp.float32)
        peak = start_peak
        key_piece = lax.all_gather(key_b, "ctx", axis=1, tiled=True)
        value_piece = lax.all_gather(value_b, "ctx", axis=1, tiled=True)
        attend_seg_piece = lax.all_gather(seg_here, "ctx", axis=1, tiled=True)
        attend_count = key_piece.shape[1]
        key_four = key_piece.reshape(per_batch, attend_count, heads_here, HEAD_DIM)
        value_four = value_piece.reshape(per_batch, attend_count, heads_here, HEAD_DIM)
        allowed = allowed_pairs(attend_seg_piece, attend_count)
        logits = scale * jnp.einsum(
            "sqhd,skhd->shqk", query_b, key_four, preferred_element_type=jnp.float32
        )
        logits = jnp.where(allowed, logits, NEG)
        fresh = jnp.maximum(peak, jnp.max(logits, axis=-1))
        weights = jnp.where(allowed, jnp.exp(logits - fresh[..., None]), 0.0)
        total = jnp.sum(weights, axis=-1)
        accum = jnp.einsum(
            "shqk,skhd->shqd",
            weights.astype(jnp.bfloat16),
            value_four,
            preferred_element_type=jnp.float32,
        )
        peak, total, accum = (fresh, total, accum)
        logsum = peak + jnp.log(total)
        out_heads = (
            (accum / total[..., None]).transpose(0, 2, 1, 3).reshape(rows, heads_here * HEAD_DIM)
        )
        out_b = out_heads.astype(jnp.bfloat16)
        attn_raw = general_narrow(jnp.dot(out_b, out_full, preferred_element_type=jnp.float32))
        attn_scale = lax.rsqrt(general_row_total(jnp.sum(attn_raw * attn_raw, axis=1)) / D + EPS)
        resid = tokens_in.astype(jnp.float32) + attn_raw * attn_scale[:, None] * attn_gain
        wide_mid = general_widen(resid.astype(jnp.bfloat16))
        gate = jnp.dot(wide_mid, gate_full, preferred_element_type=jnp.float32)
        up_val = jnp.dot(wide_mid, up_full, preferred_element_type=jnp.float32)
        sigma = jax.nn.sigmoid(gate)
        swish = gate * sigma
        act_b = (swish * up_val).astype(jnp.bfloat16)
        mlp_raw = general_narrow(jnp.dot(act_b, down_full, preferred_element_type=jnp.float32))
        mlp_scale = lax.rsqrt(general_row_total(jnp.sum(mlp_raw * mlp_raw, axis=1)) / D + EPS)
        result = resid + mlp_raw * mlp_scale[:, None] * mlp_gain
        outputs.append(result.astype(jnp.bfloat16).reshape(per_batch, slice_len, local_width))
        again = (
            lax.all_gather(w_query, ("dp", "ctx"), axis=0, tiled=True),
            lax.all_gather(w_key, ("dp", "ctx"), axis=0, tiled=True),
            lax.all_gather(w_value, ("dp", "ctx"), axis=0, tiled=True),
            lax.all_gather(w_out, ("dp", "ctx"), axis=1, tiled=True),
            lax.all_gather(w_gate, ("dp", "ctx"), axis=0, tiled=True),
            lax.all_gather(w_up, ("dp", "ctx"), axis=0, tiled=True),
            lax.all_gather(w_down, ("dp", "ctx"), axis=1, tiled=True),
        )
        query_back, key_back, value_back, out_back, gate_back, up_back, down_back = again
        grad_out = (
            cotangent[lower : lower + per_batch].reshape(rows, local_width).astype(jnp.float32)
        )
        mlp_gain_grad = mlp_gain_grad + jnp.sum(grad_out * mlp_raw * mlp_scale[:, None], axis=0)
        scaled = grad_out * mlp_gain
        grad_mlp = general_norm_grad(
            scaled, mlp_raw, mlp_scale, general_row_total(jnp.sum(scaled * mlp_raw, axis=1))
        )
        wide_grad_mlp = general_widen(grad_mlp.astype(jnp.bfloat16))
        grad_act = general_contract_last(wide_grad_mlp, down_back)
        grad_gate = (grad_act * up_val * sigma * (1.0 + gate * (1.0 - sigma))).astype(jnp.bfloat16)
        grad_up = (grad_act * swish).astype(jnp.bfloat16)
        grad_resid = grad_out + general_narrow(
            general_contract_last(grad_gate, gate_back) + general_contract_last(grad_up, up_back)
        )
        attn_gain_grad = attn_gain_grad + jnp.sum(
            grad_resid * attn_raw * attn_scale[:, None], axis=0
        )
        scaled = grad_resid * attn_gain
        grad_attn = general_norm_grad(
            scaled, attn_raw, attn_scale, general_row_total(jnp.sum(scaled * attn_raw, axis=1))
        )
        wide_grad_attn = general_widen(grad_attn.astype(jnp.bfloat16))
        grad_heads = general_contract_last(wide_grad_attn, out_back).astype(jnp.bfloat16)
        dout_four = grad_heads.reshape(per_batch, slice_len, heads_here, HEAD_DIM)
        delta = jnp.sum(
            (grad_heads.astype(jnp.float32) * out_heads).reshape(
                per_batch, slice_len, heads_here, HEAD_DIM
            ),
            axis=-1,
        ).transpose(0, 2, 1)

        def attend_back(piece):
            key_piece, value_piece, seg_piece = piece
            count = key_piece.shape[1]
            key_four = key_piece.reshape(per_batch, count, heads_here, HEAD_DIM)
            value_four = value_piece.reshape(per_batch, count, heads_here, HEAD_DIM)
            allowed = allowed_pairs(seg_piece, count)
            logits = scale * jnp.einsum(
                "sqhd,skhd->shqk", query_b, key_four, preferred_element_type=jnp.float32
            )
            probs = jnp.where(allowed, jnp.exp(logits - logsum[..., None]), 0.0)
            grad_probs = jnp.einsum(
                "sqhd,skhd->shqk", dout_four, value_four, preferred_element_type=jnp.float32
            )
            grad_logits = (probs * (grad_probs - delta[..., None])).astype(jnp.bfloat16)
            grad_query = scale * jnp.einsum(
                "shqk,skhd->sqhd", grad_logits, key_four, preferred_element_type=jnp.float32
            )
            key_grad = scale * jnp.einsum(
                "shqk,sqhd->skhd", grad_logits, query_b, preferred_element_type=jnp.float32
            )
            value_grad = jnp.einsum(
                "shqk,sqhd->skhd",
                probs.astype(jnp.bfloat16),
                dout_four,
                preferred_element_type=jnp.float32,
            )
            grad_keys = key_grad.reshape(per_batch, count, heads_here * HEAD_DIM)
            grad_values = value_grad.reshape(per_batch, count, heads_here * HEAD_DIM)
            return (grad_query, grad_keys, grad_values)

        grad_query, grad_keys, grad_values = attend_back(
            (
                lax.all_gather(key_b, "ctx", axis=1, tiled=True),
                lax.all_gather(value_b, "ctx", axis=1, tiled=True),
                lax.all_gather(seg_here, "ctx", axis=1, tiled=True),
            )
        )
        key_grad_mine, value_grad_mine = (
            lax.psum_scatter(
                grad_keys.astype(jnp.bfloat16), "ctx", scatter_dimension=1, tiled=True
            ).astype(jnp.float32),
            lax.psum_scatter(
                grad_values.astype(jnp.bfloat16), "ctx", scatter_dimension=1, tiled=True
            ).astype(jnp.float32),
        )
        grad_qnorm = general_turn_back(
            grad_query.reshape(rows, heads_here, HEAD_DIM), cosine, sine
        ).reshape(rows, heads_here * HEAD_DIM)
        grad_knorm = general_turn_back(
            key_grad_mine.reshape(rows, heads_here, HEAD_DIM), cosine, sine
        ).reshape(rows, heads_here * HEAD_DIM)
        q_gain_grad = q_gain_grad + jnp.sum(grad_qnorm * query_raw * query_scale[:, None], axis=0)
        k_gain_grad = k_gain_grad + jnp.sum(grad_knorm * key_raw * key_scale[:, None], axis=0)
        q_scaled = grad_qnorm * q_gain
        k_scaled = grad_knorm * k_gain
        q_inner, k_inner = general_row_total(
            (jnp.sum(q_scaled * query_raw, axis=1), jnp.sum(k_scaled * key_raw, axis=1))
        )
        grad_query_raw = general_norm_grad(q_scaled, query_raw, query_scale, q_inner).astype(jnp.bfloat16)
        grad_key_raw = general_norm_grad(k_scaled, key_raw, key_scale, k_inner).astype(jnp.bfloat16)
        grad_value_raw = value_grad_mine.reshape(rows, heads_here * HEAD_DIM).astype(jnp.bfloat16)
        back_terms = (
            general_contract_last(grad_query_raw, query_back)
            + general_contract_last(grad_key_raw, key_back)
            + general_contract_last(grad_value_raw, value_back)
        )
        grad_in = grad_resid + general_narrow(back_terms)
        input_grads.append(grad_in.astype(jnp.bfloat16).reshape(per_batch, slice_len, local_width))
        fresh_grads = (
            general_contract_first(wide_in, grad_query_raw),
            general_contract_first(wide_in, grad_key_raw),
            general_contract_first(wide_in, grad_value_raw),
            general_contract_first(out_b, wide_grad_attn),
            general_contract_first(wide_mid, grad_gate),
            general_contract_first(wide_mid, grad_up),
            general_contract_first(act_b, wide_grad_mlp),
        )
        weight_grads = tuple((left + right for left, right in zip(weight_grads, fresh_grads)))
    finals = (
        lax.psum_scatter(
            weight_grads[0].astype(jnp.bfloat16), ("dp", "ctx"), scatter_dimension=0, tiled=True
        ).astype(jnp.float32),
        lax.psum_scatter(
            weight_grads[1].astype(jnp.bfloat16), ("dp", "ctx"), scatter_dimension=0, tiled=True
        ).astype(jnp.float32),
        lax.psum_scatter(
            weight_grads[2].astype(jnp.bfloat16), ("dp", "ctx"), scatter_dimension=0, tiled=True
        ).astype(jnp.float32),
        lax.psum_scatter(
            weight_grads[3].astype(jnp.bfloat16), ("dp", "ctx"), scatter_dimension=1, tiled=True
        ).astype(jnp.float32),
        lax.psum_scatter(
            weight_grads[4].astype(jnp.bfloat16), ("dp", "ctx"), scatter_dimension=0, tiled=True
        ).astype(jnp.float32),
        lax.psum_scatter(
            weight_grads[5].astype(jnp.bfloat16), ("dp", "ctx"), scatter_dimension=0, tiled=True
        ).astype(jnp.float32),
        lax.psum_scatter(
            weight_grads[6].astype(jnp.bfloat16), ("dp", "ctx"), scatter_dimension=1, tiled=True
        ).astype(jnp.float32),
    )
    gains = lax.psum((q_gain_grad, k_gain_grad, attn_gain_grad, mlp_gain_grad), ("dp", "ctx"))
    return (
        jnp.concatenate(outputs, axis=0),
        jnp.concatenate(input_grads, axis=0),
        finals[0],
        finals[1],
        finals[2],
        finals[3],
        finals[4],
        finals[5],
        finals[6],
        gains[0],
        gains[1],
        gains[2],
        gains[3],
    )


class Batch:
    pass


def planned(
    hidden, cotangent, segments, positions, w_query, w_key, w_value, w_out, w_gate, w_up, w_down,
    q_gain, k_gain, attn_gain, mlp_gain,
):
    seqs, count, width = hidden.shape
    per = seqs // 2
    rows = per * count
    ff = w_gate.shape[1]
    batches = (Batch(), Batch())
    one, two = batches
    for b, batch in enumerate(batches):
        batch.x = hidden[b * per : (b + 1) * per].reshape(rows, width)
        batch.cot = cotangent[b * per : (b + 1) * per].reshape(rows, width)
    seg_cols = jnp.broadcast_to(segments.reshape(seqs * count, 1), (seqs * count, 128))
    pos_cols = jnp.broadcast_to(positions.reshape(seqs * count, 1), (seqs * count, 128))
    half = HEAD_DIM // 2
    freqs = THETA ** (-(jnp.arange(half, dtype=F32) * 2.0) / HEAD_DIM)
    freqs = jnp.concatenate([freqs, freqs]).reshape(1, HEAD_DIM)
    sign = jnp.concatenate([-jnp.ones(half, F32), jnp.ones(half, F32)]).reshape(1, HEAD_DIM)
    seg_pad = jnp.concatenate([segments, jnp.zeros((8 - seqs, count), segments.dtype)], axis=0)
    norms = (q_gain, k_gain)

    quarters = [(512 * k, 512) for k in range(ff // 512)]
    wg, wu = [], []

    s = Slot("slot0", 0)
    line = Line(s, rows, width, gather=one.x)
    plane = Plane(s)
    seg_h = plane.gather(seg_pad, 0, False)
    full = [plane.gather(w, 0, True, done="w%d" % i) for i, w in enumerate((w_query, w_key, w_value))]
    w_out_h = plane.gather(w_out, 1, True, 1, 12.0)
    some = [plane.gather(w_gate, 0, True, 1, t, cols=c) for t, c in zip((18.0, 26.0), quarters)]
    cosine, sine = tables(s, pos_cols, freqs, sign)
    made = project(s, line, rows, width, full, ("w0", "w1", "w2"), norms, cosine, sine, 0)
    s.run()
    wq, wk, wv = (h.value for h in full)
    wg += [h.value for h in some]
    wo, seg_all, cosine, sine = w_out_h.value, seg_h.value, cosine.target.value, sine.target.value
    one.q_raw, one.k_raw, one.q, one.kv, one.qk_factor = (h.value for h in made)
    one.wide = line.out.value

    s = Slot("slot1", 1)
    line = Line(s, rows, width, gather=two.x)
    plane = Plane(s)
    kvs = plane.gather(one.kv, 0, False, 4, done="kv")
    some = [plane.gather(w_gate, 0, True, cols=c) for c in quarters[2:]]
    more = plane.gather(w_up, 0, True, cols=quarters[0])
    s.mark_early("tables")
    mask = Mask(s, seg_all, seg_cols, 0, count)
    felt = attend(s, "kv", kvs, one.q, mask, rows, width)
    made = project(s, line, rows, width, (wq, wk, wv), None, norms, s.load(cosine), s.load(sine), rows)
    s.run()
    wg += [h.value for h in some]
    wu.append(more.value)
    one.kvs = kvs.value
    two.q_raw, two.k_raw, two.q, two.kv, two.qk_factor = (h.value for h in made)
    one.heads, one.heads_b, one.logsum = (h.value for h in felt)
    two.wide = line.out.value

    s = Slot("slot2", 2, 160.0, 80.0)
    line = Line(s, rows, width, scatter=True)
    plane = Plane(s)
    kvs = plane.gather(two.kv, 0, False, 4, done="kv")
    some = [plane.gather(w_up, 0, True, cols=c) for c in quarters[1:]]
    ends = attn_finish(s, line, rows, width, one.x, attn_gain)
    produce(s, line, [s.load(one.heads_b)], [[wo]], (width, width), col_block, dot_nn, 0.6)
    mask = Mask(s, seg_all, seg_cols, per, count)
    felt = attend(s, "kv", kvs, two.q, mask, rows, width)
    s.run()
    wu += [h.value for h in some]
    two.kvs = kvs.value
    one.attn, one.resid, one.resid_b, one.factor = (h.value for h in ends)
    two.heads, two.heads_b, two.logsum = (h.value for h in felt)

    s = Slot("slot3", 3, 200.0, 80.0)
    line = Line(s, rows, width, gather=one.resid_b, scatter=True)
    w_down_h = Plane(s).gather(w_down, 1, True, 4)
    ends = attn_finish(s, line, rows, width, two.x, attn_gain)
    produce(s, line, [s.load(two.heads_b)], [[wo]], (width, width), col_block, dot_nn, 0.6)
    inner = gate_up(s, line, rows, wg, wu)
    s.run()
    wd, one.mid = w_down_h.value, line.out.value
    two.attn, two.resid, two.resid_b, two.factor = (h.value for h in ends)
    one.gate, one.up, one.act = (h.value for h in inner)

    s = Slot("slot4", 4, 160.0, 80.0)
    line = Line(s, rows, width, gather=two.resid_b, scatter=True)
    ends = mlp_finish(s, line, rows, width, one.resid, one.cot, mlp_gain)
    produce(s, line, [s.load(one.act)], [[wd]], (ff, 512), col_block, dot_nn, 1.8)
    inner = gate_up(s, line, rows, wg, wu)
    s.run()
    two.mid = line.out.value
    one.out, one.g_mlp_b, one.g_mlp_gain = (h.value for h in ends)
    two.gate, two.up, two.act = (h.value for h in inner)

    s = Slot("slot5", 5, 250.0, 80.0)
    line = Line(s, rows, width, gather=one.g_mlp_b, scatter=True)
    ends = mlp_finish(s, line, rows, width, two.resid, two.cot, mlp_gain)
    produce(s, line, [s.load(two.act)], [[wd]], (ff, 512), col_block, dot_nn, 1.8)
    inner = act_back(s, line, rows, wd, one.gate, one.up)
    s.run()
    one.g_mlp = line.out.value
    two.out, two.g_mlp_b, two.g_mlp_gain = (h.value for h in ends)
    one.g_gate, one.g_up = (h.value for h in inner)

    s = Slot("slot6", 6)
    line = Line(s, rows, width, gather=two.g_mlp_b, scatter=True)
    ends = resid_finish(s, line, rows, width, one.cot, one.attn, one.factor, attn_gain)
    produce(s, line, [s.load(one.g_gate), s.load(one.g_up)], [wg, wu], (512, ff), row_block, dot_nt, 3.4)
    inner = act_back(s, line, rows, wd, two.gate, two.up)
    s.run()
    two.g_mlp = line.out.value
    one.g_resid, one.g_attn_b, one.g_attn_gain = (h.value for h in ends)
    two.g_gate, two.g_up = (h.value for h in inner)

    s = Slot("slot7", 7)
    line = Line(s, rows, width, gather=one.g_attn_b, scatter=True)
    plane = Plane(s)
    g_down = s.hbm_out((ff - 512, w_down.shape[1]), F32)
    ends = resid_finish(s, line, rows, width, two.cot, two.attn, two.factor, attn_gain)
    acts, g_mlps = joined(s, (one.act, two.act)), joined(s, (one.g_mlp, two.g_mlp))
    full_grad(s, plane, acts, g_mlps, False, g_down, (12.0, 23.0, 28.0), "d", (0, 1, 2), ("part0", "part1", "part1"))
    produce(s, line, [s.load(two.g_gate), s.load(two.g_up)], [wg, wu], (512, ff), row_block, dot_nt, 3.4)
    mask = Mask(s, seg_all, seg_cols, 0, count, True)
    back = attend_back(s, line, one.kvs, one.q, one.heads, one.logsum, mask, rows, width, wo)
    s.run()
    one.g_attn = line.out.value
    two.g_resid, two.g_attn_b, two.g_attn_gain = (h.value for h in ends)
    one.g_q, one.g_kv = (h.value for h in back)

    s = Slot("slot8", 8)
    line = Line(s, rows, width, gather=two.g_attn_b)
    plane = Plane(s)
    g_kv = plane.scatter(one.g_kv, 0, False, 4, done="kv")
    g_gate = s.hbm_out(w_gate.shape, F32)
    raws = project_back(s, "kv", one.g_q, g_kv, (one.q_raw, one.k_raw), one.qk_factor, norms, cosine, sine, 0, rows, width)
    mids, g_gates = joined(s, (one.mid, two.mid)), joined(s, (one.g_gate, two.g_gate))
    full_grad(s, plane, mids, g_gates, True, g_gate, (7.0, 11.0, 15.0, 19.0), "g")
    mask = Mask(s, seg_all, seg_cols, per, count, True)
    back = attend_back(s, line, two.kvs, two.q, two.heads, two.logsum, mask, rows, width, wo)
    s.run()
    two.g_attn = line.out.value
    one.g_qr, one.g_kr, one.g_vr, one.g_q_gain, one.g_k_gain = (h.value for h in raws)
    two.g_q, two.g_kv = (h.value for h in back)

    s = Slot("slot9", 9)
    line = Line(s, rows, width, scatter=True)
    plane = Plane(s)
    g_kv = plane.scatter(two.g_kv, 0, False, 4, done="kv")
    g_up = s.hbm_out(w_up.shape, F32)
    fin_one = last_finish(s, line, rows, width, one.g_resid)[0]
    raws = project_back(s, "kv", two.g_q, g_kv, (two.q_raw, two.k_raw), two.qk_factor, norms, cosine, sine, rows, rows, width)
    produce(s, line, [s.load(g) for g in (one.g_qr, one.g_kr, one.g_vr)], [[wq], [wk], [wv]], (512, width), row_block, dot_nt, 1.6, "u0")
    mids, g_ups = joined(s, (one.mid, two.mid)), joined(s, (one.g_up, two.g_up))
    full_grad(s, plane, mids, g_ups, True, g_up, (7.0, 18.0, 22.0, 26.0), "u")
    s.run()
    two.g_qr, two.g_kr, two.g_vr, two.g_q_gain, two.g_k_gain = (h.value for h in raws)

    s = Slot("slot10", 10)
    line = Line(s, rows, width, scatter=True)
    plane = Plane(s)
    fin_two = last_finish(s, line, rows, width, two.g_resid)[0]
    produce(s, line, [s.load(g) for g in (two.g_qr, two.g_kr, two.g_vr)], [[wq], [wk], [wv]], (512, width), row_block, dot_nt, 1.6, "d3")
    sums = gain_sums(
        s,
        (one.g_q_gain, two.g_q_gain, one.g_k_gain, two.g_k_gain)
        + (one.g_attn_gain, two.g_attn_gain, one.g_mlp_gain, two.g_mlp_gain),
    )
    g_q, g_k, g_v = (s.hbm_out(w_query.shape, F32) for _ in range(3))
    g_out, g_last = s.hbm_out(w_out.shape, F32), s.hbm_out((512, w_down.shape[1]), F32)
    acts, g_mlps = joined(s, (one.act, two.act)), joined(s, (one.g_mlp, two.g_mlp))
    full_grad(s, plane, acts, g_mlps, False, g_last, (7.0,), "d", (3,))
    wides = joined(s, (one.wide, two.wide))
    full_grad(s, plane, wides, joined(s, (one.g_qr, two.g_qr)), True, g_q, (18.0,), "q")
    full_grad(s, plane, wides, joined(s, (one.g_kr, two.g_kr)), True, g_k, (22.0,), "k")
    full_grad(s, plane, wides, joined(s, (one.g_vr, two.g_vr)), True, g_v, (26.0,), "v")
    heads_b, g_attns = joined(s, (one.heads_b, two.heads_b)), joined(s, (one.g_attn, two.g_attn))
    full_grad(s, plane, heads_b, g_attns, False, g_out, (30.0,), "o")
    s.run()
    gains = [sums.value[k] for k in range(4)]
    shape = (per, count, width)
    return (
        jnp.concatenate([one.out.reshape(shape), two.out.reshape(shape)], axis=0),
        jnp.concatenate([fin_one.value.reshape(shape), fin_two.value.reshape(shape)], axis=0),
        *(g.value for g in (g_q, g_k, g_v, g_out, g_gate, g_up)),
        jnp.concatenate([g_down.value, g_last.value], axis=0),
        *gains,
    )


def solution(mesh):
    rows, cols = P(("dp", "ctx"), "tp"), P("tp", ("dp", "ctx"))
    act, gain = P("dp", "ctx", "tp"), P("tp")
    size = dict(mesh.shape)
    body = planned if (size["dp"], size["ctx"], size["tp"]) == (2, 4, 4) else general
    return jax.shard_map(
        body,
        mesh=mesh,
        in_specs=(act, act, P("dp", "ctx"), P("dp", "ctx"), rows, rows, rows, cols, rows, rows, cols, gain, gain, gain, gain),
        out_specs=(act, act, rows, rows, rows, cols, rows, rows, cols, gain, gain, gain, gain),
        check_vma=False,
    )
```

```python
import functools
import math

import jax
import jax.numpy as jnp
from jax import lax
from jax.experimental import pallas as pl
from jax.experimental.pallas import tpu as pltpu
from jax.sharding import PartitionSpec as P

D = 2048
HEAD_DIM = 128
EPS = 1e-06
THETA = 500000.0
NEG = -1e30
BF = jnp.bfloat16
F32 = jnp.float32
MESH = pl.DeviceIdType.MESH
HBM = pl.BlockSpec(memory_space=pltpu.HBM)


class Place:
    def __init__(self, tp_size):
        self.n = tp_size
        self.tp = lax.axis_index("tp")
        self.dp = lax.axis_index("dp")
        self.ctx = lax.axis_index("ctx")
        self.slot = self.dp * 4 + self.ctx


def remote(src, dst, sem, send, recv, device):
    return pltpu.make_async_remote_copy(
        src_ref=src, dst_ref=dst, send_sem=sem.at(send), recv_sem=sem.at(recv), device_id=device, device_id_type=MESH
    )


class Step:
    def __init__(self, job, name, link, time, deps, rank, issue=None, arrive=None):
        self.job, self.name, self.link, self.time, self.deps, self.rank = job, name, link, time, deps, rank
        self.issue, self.arrive = issue, arrive


class Plane:
    def __init__(self, slot):
        self.slot = slot
        self.jobs = []
        slot.plane = self
        slot.axes.add("ctx")

    def gather(self, array, dim, with_dp, pieces=1, start=0.0, after=None, done=None, cols=None):
        return self.append(Gather(self.slot, array, dim, with_dp, pieces, start, after, done, cols))

    def scatter(self, array, dim, with_dp, pieces=1, start=0.0, after=None, done=None, out=None):
        return self.append(Scatter(self.slot, array, dim, with_dp, pieces, start, after, done, out))

    def append(self, job):
        job.number = len(self.jobs)
        self.jobs.append(job)
        if job.with_dp:
            self.slot.axes.add("dp")
        self.slot.add(lambda: job.body(self), True)
        return job.out

    def plan(self):
        pieces = [(job, p) for job in self.jobs for p in range(job.pieces)]
        choice, load = {}, [0.0, 0.0]
        for job, p in pieces:
            load[0] += job.unit
            load[1] += job.unit if job.with_dp else 0.0
        for job, p in pieces:
            via = 0 if load[0] < load[1] else 1
            choice[job, p] = via
            if job.with_dp:
                load[via] += job.unit
        best = self.lay(choice)
        for _ in range(2):
            for key in pieces:
                if key[0].with_dp:
                    trial = dict(choice)
                    trial[key] = 1 - trial[key]
                    result = self.lay(trial)
                    if result[0] < best[0] - 0.01:
                        choice, best = trial, result
        self.actions = best[1]

    def lay(self, choice):
        steps = [step for job in self.jobs for p in range(job.pieces) for step in job.steps(p, choice[job, p])]
        times, free, actions = {}, [0.0, 0.0], []
        pending = list(steps)
        while pending:
            best = None
            for step in pending:
                if any((step.job, d) not in times for d in step.deps):
                    continue
                ready = max([step.job.start] + [times[step.job, d] for d in step.deps])
                key = (ready, step.job.number, step.rank)
                if best is None or key < best[0]:
                    best = (key, step)
            (ready, _, _), step = best
            pending.remove(step)
            if step.link is None:
                arrive_at = ready + step.time
            else:
                begin = max(ready, free[step.link])
                free[step.link] = begin + step.time
                actions.append((ready, 1, len(actions), step.job, step.issue))
                arrive_at = begin + step.time + 0.7
            actions.append((arrive_at, 0, len(actions), step.job, step.arrive))
            times[step.job, step.name] = arrive_at
        actions.sort(key=lambda a: a[:3])
        return sum(times.values()) / len(times) / 10 + max(times.values()), actions


class Job:
    def body(self, plane):
        slot = self.slot
        if not plane.planned:
            plane.plan()
            plane.planned = True
        if self.after is not None:
            yield ("flag", self.after)
        shift = max(0.0, slot.now - self.start) if self.after is not None else 0.0
        yield ("at", self.start)
        self.begin()
        yield ("at", self.start + shift + 1.0)
        self.settle()
        for time, _, _, job, emit in plane.actions:
            if job is self:
                yield ("at", time + shift)
                emit()
        yield ("at", slot.now + 1.0)
        self.finish()
        if self.done is not None:
            slot.mark(self.done)

    def send(self, index, origin, target, device):
        copy = remote(origin, target, self.slot, self.base + 2 * index, self.base + 2 * index + 1, device)
        copy.start()
        self.sent.append(copy)

    def got(self, index, target):
        remote(target, target, self.slot, self.base + 2 * index, self.base + 2 * index + 1, self.cdev).wait_recv()

    def settle(self):
        pass

    def coordinates(self):
        self.dp, self.ctx = self.slot.place.dp, self.slot.place.ctx
        self.xdev, self.ydev, self.cdev = {"ctx": self.ctx ^ 2}, {"dp": self.dp ^ 1}, {"ctx": self.ctx ^ 1}
        self.sent = []


class Gather(Job):
    def __init__(self, slot, array, dim, with_dp, pieces, start, after, done, cols):
        self.slot, self.dim, self.with_dp, self.pieces = slot, dim, with_dp, pieces
        self.start, self.after, self.done = start, after, done
        self.handle = slot.hbm_in(array)
        shape = list(array.shape)
        self.cols = pl.ds(0, shape[1]) if cols is None else pl.ds(*cols)
        if cols is not None:
            shape[1] = cols[1]
        self.size, self.rows = shape[dim], shape[0]
        self.unit = math.prod(shape) * 2 / (slot.rates[1] * 1e3) / pieces
        self.hold = slot.vmem(tuple(shape), array.dtype)
        shape[dim] *= 8 if with_dp else 4
        self.out = slot.hbm_out(tuple(shape), array.dtype)
        self.own = slot.sems(2)
        self.base = slot.sems(2 * pieces * 7)

    def spot(self, d, c, p):
        out = self.out.ref
        block = d * 4 + c if self.with_dp else c
        step = self.rows // self.pieces
        if self.dim == 1:
            return out.at[pl.ds(p * step, step), pl.ds(pl.multiple_of(block * self.size, self.size), self.size)]
        return out.at[pl.ds(pl.multiple_of(block * self.size + p * step, step), step)]

    def begin(self):
        self.coordinates()
        self.source = src = self.handle.ref.at[:, self.cols]
        step = self.rows // self.pieces
        for p in range(self.pieces):
            part = pl.ds(p * step, step)
            self.send(7 * p, src.at[part], self.spot(self.dp, self.ctx, p), self.cdev)
        if self.dim == 1:
            mine = self.out.ref.at[:, pl.ds(pl.multiple_of((self.dp * 4 + self.ctx) * self.size, self.size), self.size)]
        else:
            block = self.dp * 4 + self.ctx if self.with_dp else self.ctx
            mine = self.out.ref.at[pl.ds(pl.multiple_of(block * self.size, self.size), self.size)]
        self.held = pltpu.make_async_copy(src, self.hold.ref, self.slot.sem(self.own))
        self.kept = pltpu.make_async_copy(self.hold.ref, mine, self.slot.sem(self.own + 1))
        self.held.start()

    def settle(self):
        self.held.wait()
        self.kept.start()

    def steps(self, p, via):
        def direct(k, device):
            def issue():
                step = self.rows // self.pieces
                part = pl.ds(p * step, step)
                self.send(7 * p + 1 + k, self.source.at[part], self.spot(self.dp, self.ctx, p), device())

            return issue

        def forward(k, place):
            def arrive():
                here = self.spot(*place(), p)
                self.got(7 * p + 1 + k, here)
                self.send(7 * p + 4 + k, here, here, self.cdev)

            return arrive

        from_x = lambda: (self.dp, self.ctx ^ 2)
        from_y = lambda: (self.dp ^ 1, self.ctx)
        corner = lambda: (self.dp ^ 1, self.ctx ^ 2)
        xdev, ydev = (lambda: self.xdev), (lambda: self.ydev)
        out = [Step(self, (p, 0), 0, self.unit, [], 2 * p, direct(0, xdev), forward(0, from_x))]
        if self.with_dp:
            out.append(Step(self, (p, 1), 1, self.unit, [], 2 * p, direct(1, ydev), forward(1, from_y)))

            def hop():
                here = self.spot(*(from_y() if via == 0 else from_x()), p)
                self.send(7 * p + 3, here, here, self.xdev if via == 0 else self.ydev)

            out.append(Step(self, (p, 2), via, self.unit, [(p, 1 - via)], 2 * p + 1, hop, forward(2, corner)))
        return out

    def finish(self):
        for p in range(self.pieces):
            self.got(7 * p, self.spot(self.dp, self.ctx ^ 1, p))
            self.got(7 * p + 4, self.spot(self.dp, self.ctx ^ 3, p))
            if self.with_dp:
                self.got(7 * p + 5, self.spot(self.dp ^ 1, self.ctx ^ 1, p))
                self.got(7 * p + 6, self.spot(self.dp ^ 1, self.ctx ^ 3, p))
        for copy in self.sent:
            copy.wait_send()
        self.kept.wait()


class Scatter(Job):
    def __init__(self, slot, array, dim, with_dp, pieces, start, after, done, out):
        self.slot, self.dim, self.with_dp, self.pieces = slot, dim, with_dp, pieces
        self.start, self.after, self.done = start, after, done
        self.source = slot.hbm_in(array)
        shape = list(array.shape)
        self.chips = chips = 4 if with_dp else 2
        shape[dim] //= 2 * chips
        self.size = shape[dim]
        self.rows, self.width = shape
        self.unit = math.prod(shape) * 2 / (slot.rates[1] * 1e3) / pieces
        if out is None:
            self.out, self.where = slot.hbm_out(tuple(shape), F32), None
        else:
            self.out, self.where = out
        block = tuple(shape)
        self.mine, self.came = slot.vmem((chips,) + block, BF), slot.vmem((chips,) + block, BF)
        self.chip_in = slot.vmem((chips // 2,) + block, BF)
        self.diag = slot.vmem(block, BF) if with_dp else None
        self.total = slot.vmem(block, F32)
        self.loads = slot.sems(chips * pieces)
        self.outs = slot.sems(pieces)
        self.base = slot.sems(2 * pieces * (chips + 3))

    def spot(self, q, c, p):
        x = (self.ctx >> 1) ^ (q & 1)
        d = self.dp ^ (q >> 1)
        block = d * 4 + x * 2 + c if self.with_dp else x * 2 + c
        step = self.rows // self.pieces
        if self.dim == 1:
            return self.source.ref.at[pl.ds(p * step, step), pl.ds(pl.multiple_of(block * self.size, self.size), self.size)]
        return self.source.ref.at[pl.ds(pl.multiple_of(block * self.size + p * step, step), step)]

    def part(self, p):
        step = self.rows // self.pieces
        return pl.ds(p * step, step)

    def load(self, q, p):
        core = self.ctx & 1
        return pltpu.make_async_copy(
            self.spot(q, core, p), self.mine.ref.at[q, self.part(p)], self.slot.sem(self.loads + q * self.pieces + p)
        )

    def begin(self):
        self.coordinates()
        core = self.ctx & 1
        self.order = (3, 1, 2, 0) if self.with_dp else (1, 0)
        self.per = self.chips + 3
        for p in range(self.pieces):
            for q in self.order:
                self.send(self.per * p + q, self.spot(q, core ^ 1, p), self.came.ref.at[q, self.part(p)], self.cdev)
                self.load(q, p).start()

    def add(self, into, other, p):
        step = self.rows // self.pieces
        tile = min(32, step)

        @pl.loop(0, step // tile)
        def _(i):
            part = pl.ds(pl.multiple_of(p * step + i * tile, tile), tile)
            into[part] = (into[part].astype(F32) + other[part].astype(F32)).astype(BF)

    def steps(self, p, via):
        mine, came = self.mine, self.came

        def cores():
            for q in self.order:
                self.load(q, p).wait()
                self.got(self.per * p + q, came.ref.at[q, self.part(p)])
                self.add(mine.ref.at[q], came.ref.at[q], p)

        def out(k, q, target, device):
            def issue():
                self.send(self.per * p + self.chips + k, mine.ref.at[q, self.part(p)], target(), device())

            return issue

        xdev, ydev = (lambda: self.xdev), (lambda: self.ydev)
        into = lambda j: (lambda: self.chip_in.ref.at[j, self.part(p)])
        done = {}

        def last(k, j):
            def arrive():
                self.got(self.per * p + self.chips + k, self.chip_in.ref.at[j, self.part(p)])
                done[j] = True
                if len(done) == self.chips // 2:
                    done.clear()
                    self.close(p)

            return arrive

        steps = [Step(self, (p, "c"), None, 2.0 + self.unit * 0.5, [], 3 * p, None, cores)]
        if not self.with_dp:
            steps.append(Step(self, (p, 0), 0, self.unit, [(p, "c")], 3 * p + 1, out(0, 1, into(0), xdev), last(0, 0)))
            return steps
        corner = lambda: self.diag.ref.at[self.part(p)]

        def fold():
            self.got(self.per * p + self.chips + 2, corner())
            self.add(mine.ref.at[2 if via == 0 else 1], self.diag.ref, p)

        steps.append(
            Step(self, (p, 2), via, self.unit, [(p, "c")], 3 * p, out(2, 3, corner, xdev if via == 0 else ydev), fold)
        )
        for k, device in ((0, xdev), (1, ydev)):
            deps = [(p, "c")] if k == via else [(p, 2)]
            steps.append(Step(self, (p, k), k, self.unit, deps, 3 * p + 1, out(k, 1 + k, into(k), device), last(k, k)))
        return steps

    def result(self, p):
        target = self.out.ref
        step = self.rows // self.pieces
        if self.where is None:
            target = target.at[pl.ds(p * step, step)]
        else:
            row, col = self.where
            target = target.at[pl.ds(row + p * step, step), pl.ds(col, self.width)]
        return pltpu.make_async_copy(self.total.ref.at[self.part(p)], target, self.slot.sem(self.outs + p))

    def close(self, p):
        step = self.rows // self.pieces
        tile = min(32, step)
        mine, chip_in, total = self.mine.ref, self.chip_in.ref, self.total.ref

        @pl.loop(0, step // tile)
        def _(i):
            part = pl.ds(pl.multiple_of(p * step + i * tile, tile), tile)
            value = mine[0, part].astype(F32) + chip_in[0, part].astype(F32)
            if self.with_dp:
                value = value + chip_in[1, part].astype(F32)
            total[part] = value

        self.result(p).start()

    def finish(self):
        for copy in self.sent:
            copy.wait_send()
        for p in range(self.pieces):
            self.result(p).wait()


class Handle:
    ref = None
    sem = None
    waited = False
    lazy = False
    halves = False
    cut = None
    value = None

    def __init__(self, shape=None, dtype=None):
        self.shape, self.dtype = shape, dtype


class Rows:
    def __init__(self, array, first, count):
        self.array, self.first = array, first
        self.shape, self.dtype = (count,) + array.shape[1:], array.dtype


class Slot:
    def __init__(self, name, ident, line_rate=97.0, plane_rate=48.0):
        self.name, self.ident = name, ident
        self.rates = (line_rate, plane_rate)
        self.inputs, self.outputs, self.scratch = [], [], []
        self.sem_count = 0
        self.tasks = []
        self.axes = set()
        self.early = []
        self.prologue = []
        self.plane = None
        self.loads, self.stores = [], []
        self.flags = {}
        self.now = 0.0

    def sems(self, number):
        first = self.sem_count
        self.sem_count += number
        return first

    def hbm_in(self, array):
        if isinstance(array, Handle):
            return array
        handle = Handle(array.shape, array.dtype)
        if isinstance(array, Rows):
            handle.cut = pl.ds(array.first, array.shape[0])
            array = array.array
        self.inputs.append((array, handle))
        return handle

    def hbm_out(self, shape, dtype):
        handle = Handle(shape, dtype)
        self.outputs.append((jax.ShapeDtypeStruct(shape, dtype), handle))
        return handle

    def vmem(self, shape, dtype):
        handle = Handle(shape, dtype)
        self.scratch.append((pltpu.VMEM(shape, dtype), handle))
        return handle

    def load(self, array):
        handle = self.vmem(array.shape, array.dtype)
        handle.source = self.hbm_in(array)
        handle.sem = self.sems(1)
        self.loads.append(handle)
        return handle

    def store(self, shape, dtype):
        handle = self.vmem(shape, dtype)
        handle.target = self.hbm_out(shape, dtype)
        handle.sem = self.sems(2)
        self.stores.append(handle)
        return handle

    def late(self, array):
        handle = self.vmem(array.shape, array.dtype)
        handle.source = self.hbm_in(array)
        handle.sem = self.sems(1)
        handle.lazy = True
        self.loads.append(handle)
        return handle

    def fetch(self, *handles):
        for handle in handles:
            pltpu.make_async_copy(handle.source.ref, handle.ref, self.sem(handle.sem)).start()

    def need(self, *handles):
        for handle in handles:
            if not handle.waited:
                handle.waited = True
                pltpu.make_async_copy(handle.source.ref, handle.ref, self.sem(handle.sem)).wait()

    def flush(self, *handles):
        for handle in handles:
            pltpu.make_async_copy(handle.ref, handle.target.ref, self.sem(handle.sem)).start()

    def flush_half(self, h, *handles):
        for handle in handles:
            half = handle.shape[0] // 2
            part = pl.ds(h * half, half)
            handle.halves = True
            pltpu.make_async_copy(handle.ref.at[part], handle.target.ref.at[part], self.sem(handle.sem + h)).start()

    def sem(self, index):
        return self.sem_ref.at[index]

    def at(self, index):
        return self.sem_ref.at[index]

    def add(self, body, transfers=False):
        self.tasks.append((body, transfers))

    def mark(self, flag):
        self.flags[flag] = True

    def mark_early(self, flag):
        self.early.append(flag)

    def kernel(self, *refs):
        refs = list(refs)
        for group in (self.inputs, self.outputs, self.scratch):
            for _, handle in group:
                handle.ref = refs.pop(0)
                if handle.cut is not None:
                    handle.ref = handle.ref.at[handle.cut]
        self.sem_ref = refs.pop(0)
        self.flags, self.now = {flag: True for flag in self.early}, 0.0
        for handle in self.loads:
            handle.waited = False
            if not handle.lazy:
                pltpu.make_async_copy(handle.source.ref, handle.ref, self.sem(handle.sem)).start()
        for begin in self.prologue:
            begin()
        self.place = place = Place(4)
        barrier = pltpu.get_barrier_semaphore()
        peers = []
        if "ctx" in self.axes:
            peers += [{"ctx": place.ctx ^ 1}, {"ctx": place.ctx ^ 2}]
        if "dp" in self.axes:
            peers += [{"dp": place.dp ^ 1}]
        if "tp" in self.axes:
            peers += [{"tp": place.tp ^ k} for k in (1, 2, 3)]
        for device in peers:
            pl.semaphore_signal(barrier, inc=1, device_id=device, device_id_type=MESH)
        pl.semaphore_wait(barrier, len(peers))
        if self.plane is not None:
            self.plane.planned = False
        running = [[("at", 0.0), task(), 0 if transfers else 1, i] for i, (task, transfers) in enumerate(self.tasks)]
        while running:
            ready = None
            for entry in running:
                kind, value = entry[0]
                if (kind == "at" and value <= self.now) or (kind == "flag" and value in self.flags):
                    key = (entry[2], value if kind == "at" and entry[2] == 0 else 0.0, entry[3])
                    if ready is None or key < ready[0]:
                        ready = (key, entry)
            if ready is None:
                self.now = min(entry[0][1] for entry in running if entry[0][0] == "at")
                continue
            entry = ready[1]
            try:
                got = next(entry[1])
            except StopIteration:
                running.remove(entry)
                continue
            if got[0] == "did":
                self.now += got[1]
                got = ("at", self.now)
            entry[0] = got
        for handle in self.stores:
            if not handle.halves:
                pltpu.make_async_copy(handle.ref, handle.target.ref, self.sem(handle.sem)).wait()
                continue
            half = handle.shape[0] // 2
            for h in (0, 1):
                part = pl.ds(h * half, half)
                pltpu.make_async_copy(handle.ref.at[part], handle.target.ref.at[part], self.sem(handle.sem + h)).wait()

    def run(self):
        values = pl.pallas_call(
            self.kernel,
            out_shape=tuple(o for o, _ in self.outputs),
            in_specs=[HBM] * len(self.inputs),
            out_specs=tuple([HBM] * len(self.outputs)),
            scratch_shapes=[s for s, _ in self.scratch] + [pltpu.SemaphoreType.DMA((self.sem_count,))],
            compiler_params=pltpu.CompilerParams(
                collective_id=self.ident, has_side_effects=True, vmem_limit_bytes=62 * 1024 * 1024
            ),
            name=self.name,
        )(*[a for a, _ in self.inputs])
        for (_, handle), value in zip(self.outputs, values):
            handle.value = value


def any_of(me, values):
    values = sorted(values)
    cond = me == values[0]
    for v in values[1:]:
        cond = jnp.logical_or(cond, me == v)
    return cond


def pick(me, table):
    items = sorted(table.items())
    out = jnp.int32(items[0][1])
    for key, value in items[1:]:
        out = jnp.where(me == key, jnp.int32(value), out)
    return out


PAIR = {0: ["A0", "R3", "R2", "R1"], 1: ["A1", "A0", "R3", "R2"], 2: ["A2", "A1", "A0", "R3"]}
ONLY_A = {0: ["A0", "", ""], 1: ["A1", "A0", ""], 2: ["A2", "A1", "A0"]}
ONLY_R = {0: ["R3", "R2", "R1"], 1: ["", "R3", "R2"], 2: ["", "", "R3"]}


class Line:
    def __init__(self, slot, rows, width, gather=None, scatter=False, pieces=2, keep=True):
        self.slot, self.rows, self.width, self.pieces = slot, rows, width, pieces
        self.gather, self.scatter = gather is not None, scatter
        slot.axes.add("tp")
        right = PAIR if self.gather and scatter else (ONLY_A if self.gather else ONLY_R)
        flip = lambda m: m if not m else m[0] + str(3 - int(m[1]))
        self.tables = (right, {3 - d: [flip(m) for m in row] for d, row in right.items()})
        self.steps = len(right[0])
        self.keep = keep
        if self.gather:
            self.source = slot.hbm_in(gather)
            self.wide = slot.vmem((4, rows, width), BF)
            self.own_sem = slot.sems(1)
            if keep:
                self.out = slot.hbm_out((rows, 4 * width), BF)
                self.out_sem = slot.sems(4)
        if scatter:
            self.mine = slot.vmem((4, rows, width), BF)
            self.skip = self.steps - 3
            self.came = slot.vmem((2, 3, rows, width), BF)
        self.base = slot.sems(4 * self.steps * pieces)
        self.unit = rows * width * 4 / (slot.rates[0] * 1e3)
        slot.add(self.body, True)

    def chunk(self, k):
        me = self.slot.place.tp
        return (me, pick(me, {0: 1, 1: 2, 2: 1, 3: 2}), pick(me, {0: 2, 1: 0, 2: 3, 3: 1}), pick(me, {0: 3, 1: 3, 2: 0, 3: 0}))[k]

    def index(self, way, t, p):
        return self.base + 2 * ((way * self.steps + t) * self.pieces + p)

    def part(self, p):
        step = self.rows // self.pieces
        return pl.ds(p * step, step)

    def sends(self, t, p):
        me = self.slot.place.tp
        rows = self.part(p)
        for way in (0, 1):
            for kind in "AR":
                table = {d: int(row[t][1]) for d, row in self.tables[way].items() if row[t][:1] == kind}
                if not table:
                    continue
                block = pick(me, table)
                if kind == "A":
                    target = self.wide.ref.at[block, rows]
                    origin = self.source.ref.at[rows] if t == 0 else target
                else:
                    target = self.came.ref.at[way, t - self.skip, rows]
                    origin = self.mine.ref.at[block, rows]
                index = self.index(way, t, p)
                to = me + 1 if way == 0 else me - 1
                yield kind, any_of(me, table), remote(origin, target, self.slot, index, index + 1, {"tp": to})

    def arrivals(self, t, p):
        me = self.slot.place.tp
        rows = self.part(p)
        step = self.rows // self.pieces
        tile = 64
        for way in (0, 1):
            off = 1 if way == 0 else -1
            froms = {d + off: row[t] for d, row in self.tables[way].items() if row[t]}
            sample = self.wide.ref.at[0, rows] if self.gather else self.came.ref.at[0, 0, rows]
            index = self.index(way, t, p)
            pl.when(any_of(me, froms))(remote(sample, sample, self.slot, index, index + 1, {"tp": me}).wait_recv)
            adds = {d: int(m[1]) for d, m in froms.items() if m[0] == "R" and int(m[1]) != d}
            if adds:
                block = pick(me, adds)
                mine, came = self.mine.ref, self.came.ref

                @pl.when(any_of(me, adds))
                def _():
                    @pl.loop(0, step // tile)
                    def _(i):
                        part = pl.ds(pl.multiple_of(p * step + i * tile, tile), tile)
                        mine[block, part] = (mine[block, part].astype(F32) + came[way, t - self.skip, part].astype(F32)).astype(BF)

    def body(self):
        slot = self.slot
        me = slot.place.tp
        if self.gather:
            own = pltpu.make_async_copy(self.source.ref, self.wide.ref.at[me], slot.sem(self.own_sem))
            own.start()
        start = 0.0
        for t in range(self.steps):
            for p in range(self.pieces):
                if t > 0:
                    yield ("at", start + (t - 1 + (p + 1) / self.pieces) * self.unit + 0.5)
                    self.arrivals(t - 1, p)
                    if p == self.pieces - 1 and self.gather and t <= 3:
                        slot.mark("chunk%d" % t)
                messages = list(self.sends(t, p))
                for kind, cond, copy in messages:
                    if kind == "A":
                        pl.when(cond)(copy.start)
                if any(kind == "R" for kind, _, _ in messages):
                    first = t == (1 if self.gather else 0)
                    if p == 0:
                        for c in ((3, 0) if first else (2, 1)):
                            yield ("flag", "part%d" % c)
                        start = max(start, slot.now - t * self.unit)
                    for kind, cond, copy in messages:
                        if kind == "R":
                            pl.when(cond)(copy.start)
                if t == 0 and p == 0 and self.gather:
                    yield ("at", 1.0)
                    own.wait()
                    slot.mark("chunk0")
        for p in range(self.pieces):
            yield ("at", start + (self.steps - 1 + (p + 1) / self.pieces) * self.unit + 0.5)
            self.arrivals(self.steps - 1, p)
            if self.scatter and (2 * p + 2) % self.pieces == 0:
                slot.mark("reduced%d" % (2 * (p + 1) // self.pieces - 1))
        if self.gather and self.steps == 3:
            slot.mark("chunk3")
        outs = []
        if self.gather and self.keep:
            for c in range(4):
                where = self.out.ref.at[:, pl.ds(c * self.width, self.width)]
                outs.append(pltpu.make_async_copy(self.wide.ref.at[c], where, slot.sem(self.out_sem + c)))
                outs[-1].start()
        yield ("at", start + self.steps * self.unit + 1.0)
        for t in range(self.steps):
            for p in range(self.pieces):
                for _, cond, copy in self.sends(t, p):
                    pl.when(cond)(copy.wait_send)
        for copy in outs:
            copy.wait()

    def total(self, part):
        me = self.slot.place.tp
        last = 2
        left = jnp.where(me > 0, self.came.ref[0, last, part].astype(F32), 0.0)
        right = jnp.where(me < 3, self.came.ref[1, last, part].astype(F32), 0.0)
        return self.mine.ref[me, part].astype(F32) + left + right


def tiled(count, tile, body):
    @pl.loop(0, count // tile)
    def _(i):
        body(pl.ds(pl.multiple_of(i * tile, tile), tile))


class Weights:
    def __init__(self, slot, groups, shape, order, where):
        self.slot, self.order, self.where = slot, order, where
        self.groups = [[slot.hbm_in(a) for a in group] for group in groups]
        self.wide = shape[1] // len(groups[0])
        self.buffer = slot.vmem((2, len(groups)) + shape, BF)
        self.base = slot.sems(2 * sum(len(g) for g in groups))

    def copies(self, step):
        block = self.order[step] if not callable(self.order) else self.order(step)
        index = self.base + step % 2
        for j, group in enumerate(self.groups):
            for k, array in enumerate(group):
                target = self.buffer.ref.at[step % 2, j]
                if len(group) > 1:
                    target = target.at[:, pl.ds(k * self.wide, self.wide)]
                yield pltpu.make_async_copy(self.where(array.ref, block), target, self.slot.sem(index))
                index += 2

    def start(self, step):
        for copy in self.copies(step):
            copy.start()

    def take(self, step):
        for copy in self.copies(step):
            copy.wait()
        return [self.buffer.ref.at[step % 2, j] for j in range(len(self.groups))]


def row_block(ref, c):
    return ref.at[pl.ds(pl.multiple_of(c * 512, 512), 512)]


def col_block(ref, c):
    return ref.at[:, pl.ds(pl.multiple_of(c * 512, 512), 512)]


def consume(slot, line, groups, shape, where, last, multiply, parts, cost):
    weights = Weights(slot, groups, shape, line.chunk, where)

    def body():
        weights.start(0)
        for k in range(4):
            if k < 3:
                weights.start(k + 1)
            yield ("flag", "chunk%d" % k)
            blocks = weights.take(k)
            chunk = line.chunk(k)
            for j, block in enumerate(blocks):
                for part in range(parts):
                    multiply(k == 0, line.wide.ref.at[chunk], block, j, part)
                    yield ("did", cost)
        yield from last()

    slot.add(body)


def dot_nn(left, right):
    return jnp.dot(left, right, preferred_element_type=F32)


def dot_nt(left, right):
    return lax.dot_general(left, right, (((1,), (1,)), ((), ())), preferred_element_type=F32)


def produce(slot, line, lefts, groups, shape, where, dot, cost, gate=None):
    order = (3, 0, 2, 1)
    weights = Weights(slot, groups, shape, order, where)
    lefts = [h.held if hasattr(h, "held") else h for h in lefts]

    def body():
        weights.start(0)
        if gate is not None:
            yield ("flag", gate)
        slot.need(*[h for h in lefts if hasattr(h, "source")])
        half = line.rows // 2
        for k, c in enumerate(order):
            if k < 3:
                weights.start(k + 1)
            blocks = weights.take(k)
            for h in (0, 1):
                part = pl.ds(h * half, half)
                value = None
                for left, block in zip(lefts, blocks):
                    term = dot(left.ref[part], block[...])
                    value = term if value is None else value + term
                line.mine.ref[c, part] = value.astype(BF)
                yield ("did", cost / 2)
            slot.mark("part%d" % c)

    slot.add(body)


def joined(slot, arrays):
    rows = arrays[0].shape[0]
    handle = slot.vmem((len(arrays) * rows, arrays[0].shape[1]), arrays[0].dtype)
    sources = [slot.hbm_in(a) for a in arrays]
    base = slot.sems(len(arrays))

    def copies():
        return [
            pltpu.make_async_copy(a.ref, handle.ref.at[pl.ds(b * rows, rows)], slot.sem(base + b)) for b, a in enumerate(sources)
        ]

    def begin():
        handle.waited = False
        for copy in copies():
            copy.start()

    def ready():
        if not handle.waited:
            handle.waited = True
            for copy in copies():
                copy.wait()

    slot.prologue.append(begin)
    handle.ready = ready
    return handle


def weight_grad(slot, left, right, out, where, flags, cost, gates):
    buffer = slot.vmem(out[1], BF)
    base = slot.sems(1)

    def body():
        yield ("at", 2.5)
        tall, wide = out[1]
        target = buffer.ref
        for k, (rows, cols) in enumerate(where):
            if gates is not None:
                yield ("flag", gates[k])
            left.ready()
            right.ready()
            for i in range((tall // 512) * (wide // 512)):
                r, c = (512 * i, 0) if wide == 512 else (0, 512 * i)
                value = dot_tn(left.ref[:, pl.ds(rows + r, 512)], right.ref[:, pl.ds(cols + c, 512)])
                target[pl.ds(r, 512), pl.ds(c, 512)] = value.astype(BF)
                yield ("did", cost / 4)
            copy = pltpu.make_async_copy(target, out[0][k].ref, slot.sem(base))
            copy.start()
            yield ("at", slot.now + 0.7)
            copy.wait()
            slot.mark(flags[k])

    slot.add(body)


class RowTotals:
    def __init__(self, slot, rows):
        self.slot, self.rows = slot, rows
        self.stat = slot.vmem((rows, 128), F32)
        self.send = slot.vmem((8, rows), F32)
        self.came = slot.vmem((3, 8, rows), F32)
        self.total = slot.vmem((rows, 128), F32)
        self.base = slot.sems(6)

    def put(self, part, *columns):
        lane = lax.broadcasted_iota(jnp.int32, (columns[0].shape[0], 128), 1)
        value = jnp.zeros((columns[0].shape[0], 128), F32)
        for k, column in enumerate(columns):
            value = jnp.where(lane == k, column, value)
        self.stat.ref[part] = value

    def exchange(self):
        slot, me = self.slot, self.slot.place.tp
        send = self.send.ref
        send[...] = jnp.transpose(self.stat.ref[...])[0:8]
        copies = []
        for k in (1, 2, 3):
            copies.append(
                remote(send, self.came.ref.at[k - 1], slot, self.base + 2 * (k - 1), self.base + 2 * (k - 1) + 1, {"tp": me ^ k})
            )
            copies[-1].start()
        yield ("at", slot.now + 2.5)
        for copy in copies:
            copy.wait()
        total = send[...] + self.came.ref[0] + self.came.ref[1] + self.came.ref[2]
        wide = jnp.concatenate([total, jnp.zeros((120, self.rows), F32)], axis=0)
        self.total.ref[...] = jnp.transpose(wide)

    def column(self, part, k):
        return self.total.ref[part, k : k + 1]


def finish(slot, line, rows, begin, first, second, flushed, ended, needs):
    half = rows // 2
    left = []

    def make(h):
        totals = RowTotals(slot, half)

        def body():
            yield ("flag", "reduced%d" % h)
            if h == 0:
                left[:] = [0, 1]
                slot.need(*needs)
                begin()
            for i in range(2):
                tiled_at(h * half + i * (half // 2), half // 2, 32, lambda part, here: first(totals, part, here), i * (half // 2))
                yield ("did", 0.5)
            yield from totals.exchange()
            tiled_at(h * half, half, 32, lambda part, here: second(totals, part, here), 0)
            slot.flush_half(h, *flushed)
            left.remove(h)
            if not left:
                slot.flush(*ended)
            yield ("did", 1.5)

        slot.add(body)

    make(0)
    make(1)


def tiled_at(row, count, tile, body, local):
    @pl.loop(0, count // tile)
    def _(i):
        body(
            pl.ds(pl.multiple_of(row + i * tile, tile), tile),
            pl.ds(pl.multiple_of(local + i * tile, tile), tile),
        )


def fold_rows(value):
    total = value[0:8]
    for i in range(1, value.shape[0] // 8):
        total = total + value[8 * i : 8 * i + 8]
    return total


def attn_finish(slot, line, rows, width, x, gain):
    x, gain = slot.load(x), slot.load(gain.reshape(1, width))
    raw, resid = slot.store((rows, width), F32), slot.store((rows, width), F32)
    resid_b, factor = slot.store((rows, width), BF), slot.store((rows, 128), F32)

    def first(totals, part, here):
        value = line.total(part)
        raw.ref[part] = value
        totals.put(here, jnp.sum(value * value, axis=1, keepdims=True))

    def second(totals, part, here):
        scale = lax.rsqrt(totals.column(here, 0) / D + EPS)
        value = x.ref[part].astype(F32) + raw.ref[part] * scale * gain.ref[...]
        resid.ref[part] = value
        resid_b.ref[part] = value.astype(BF)
        factor.ref[part] = jnp.broadcast_to(scale, (32, 128))

    finish(slot, line, rows, lambda: None, first, second, (resid_b, raw, resid, factor), (), (x, gain))
    return [raw.target, resid.target, resid_b.target, factor.target]


def mlp_finish(slot, line, rows, width, resid, cot, gain):
    resid, cot, gain = slot.load(resid), slot.load(cot), slot.load(gain.reshape(1, width))
    raw = slot.vmem((rows, width), F32)
    out, grad = slot.store((rows, width), BF), slot.store((rows, width), BF)
    gain_grad = slot.store((8, width), F32)

    def begin():
        gain_grad.ref[...] = jnp.zeros((8, width), F32)

    def first(totals, part, here):
        value = line.total(part)
        raw.ref[part] = value
        scaled = cot.ref[part].astype(F32) * gain.ref[...]
        totals.put(here, jnp.sum(value * value, axis=1, keepdims=True), jnp.sum(scaled * value, axis=1, keepdims=True))

    def second(totals, part, here):
        scale = lax.rsqrt(totals.column(here, 0) / D + EPS)
        inner = totals.column(here, 1)
        value = raw.ref[part]
        given = cot.ref[part].astype(F32)
        normed = value * scale
        grad.ref[part] = (scale * (given * gain.ref[...]) - value * (scale * scale * scale * inner / D)).astype(BF)
        out.ref[part] = (resid.ref[part] + normed * gain.ref[...]).astype(BF)
        gain_grad.ref[...] += fold_rows(given * normed)

    finish(slot, line, rows, begin, first, second, (grad, out), (gain_grad,), (resid, cot, gain))
    return [out.target, grad.target, gain_grad.target]


def resid_finish(slot, line, rows, width, cot, attn, factor, gain):
    cot, attn, factor, gain = slot.load(cot), slot.load(attn), slot.load(factor), slot.load(gain.reshape(1, width))
    resid, grad = slot.store((rows, width), F32), slot.store((rows, width), BF)
    gain_grad = slot.store((8, width), F32)

    def begin():
        gain_grad.ref[...] = jnp.zeros((8, width), F32)

    def first(totals, part, here):
        value = line.total(part) + cot.ref[part].astype(F32)
        resid.ref[part] = value
        totals.put(here, jnp.sum(value * gain.ref[...] * attn.ref[part], axis=1, keepdims=True))

    def second(totals, part, here):
        scale = factor.ref[part, 0:1]
        inner = totals.column(here, 0)
        value, given = attn.ref[part], resid.ref[part]
        grad.ref[part] = (scale * (given * gain.ref[...]) - value * (scale * scale * scale * inner / D)).astype(BF)
        gain_grad.ref[...] += fold_rows(given * value * scale)

    finish(slot, line, rows, begin, first, second, (grad, resid), (gain_grad,), (cot, attn, factor, gain))
    return [resid.target, grad.target, gain_grad.target]


def last_finish(slot, line, rows, width, resid):
    resid = slot.load(resid)
    out = slot.store((rows, width), BF)
    half = rows // 2

    def make(h):
        def body():
            yield ("flag", "reduced%d" % h)
            slot.need(resid)

            def only(part, here):
                out.ref[part] = (line.total(part) + resid.ref[part]).astype(BF)

            tiled_at(h * half, half, 32, only, 0)
            slot.flush_half(h, out)
            yield ("did", 0.7)

        slot.add(body)

    make(0)
    make(1)
    return [out.target]


def gate_up(slot, line, rows, w_gate, w_up):
    ff = len(w_gate) * w_gate[0].shape[1]
    acc = slot.vmem((2, rows, ff), F32)
    gate, up, act = (slot.store((rows, ff), BF) for _ in range(3))
    wide = ff // 2

    def multiply(first, left, block, j, part):
        cols = pl.ds(part * wide, wide)
        value = dot_nn(left[...], block[:, cols])
        acc.ref[j, :, cols] = value if first else acc.ref[j, :, cols] + value

    def last():
        piece = rows // 4
        for h in range(4):

            @pl.loop(0, piece // 16)
            def _(i):
                part = pl.ds(pl.multiple_of(h * piece + i * 16, 16), 16)
                g, u = acc.ref[0, part], acc.ref[1, part]
                gate.ref[part] = g.astype(BF)
                up.ref[part] = u.astype(BF)
                act.ref[part] = (g * jax.nn.sigmoid(g) * u).astype(BF)

            if h % 2:
                slot.flush_half(h // 2, act, gate, up)
            yield ("did", 1.0)

    consume(slot, line, (w_gate, w_up), (512, ff), row_block, last, multiply, 2, 1.1)
    return [gate.target, up.target, act.target]


def act_back(slot, line, rows, w_down, gate, up):
    ff = w_down.shape[0]
    acc = slot.vmem((rows, ff), F32)
    gate, up = slot.load(gate), slot.load(up)
    g_gate, g_up = slot.store((rows, ff), BF), slot.store((rows, ff), BF)
    wide = ff // 2

    def multiply(first, left, block, j, part):
        cols = pl.ds(part * wide, wide)
        value = dot_nt(left[...], block[cols])
        acc.ref[:, cols] = value if first else acc.ref[:, cols] + value

    def last():
        slot.need(gate, up)
        piece = rows // 4
        for h in range(4):

            @pl.loop(0, piece // 16)
            def _(i):
                part = pl.ds(pl.multiple_of(h * piece + i * 16, 16), 16)
                grad, g, u = acc.ref[part], gate.ref[part].astype(F32), up.ref[part].astype(F32)
                sigma = jax.nn.sigmoid(g)
                g_gate.ref[part] = (grad * u * sigma * (1.0 + g * (1.0 - sigma))).astype(BF)
                g_up.ref[part] = (grad * g * sigma).astype(BF)

            if h % 2:
                slot.flush_half(h // 2, g_gate, g_up)
            yield ("did", 1.2)

    consume(slot, line, ((w_down,),), (ff, 512), col_block, last, multiply, 2, 1.2)
    return [g_gate.target, g_up.target]


def half_turn(value):
    return pltpu.roll(value, HEAD_DIM // 2, axis=1)


def tables(slot, positions, freqs, sign):
    count = positions.shape[0]
    positions, freqs, sign = slot.load(positions), slot.load(freqs), slot.load(sign)
    cosine, sine = slot.store((count, HEAD_DIM), F32), slot.store((count, HEAD_DIM), F32)

    def body():
        slot.need(positions, freqs, sign)

        def first(part):
            angle = positions.ref[part].astype(F32) * freqs.ref[...]
            cosine.ref[part] = jnp.cos(angle)
            sine.ref[part] = jnp.sin(angle) * sign.ref[...]

        tiled(count, 32, first)
        slot.flush(cosine, sine)
        yield ("did", 6.0)
        slot.mark("tables")

    slot.add(body)
    return cosine, sine


def head_cols(h):
    return pl.ds(h * HEAD_DIM, HEAD_DIM)


def project(slot, line, rows, width, weights, flags, gains, cosine, sine, first_row):
    stages = [slot.late(w) for w in weights]
    gains = [slot.load(g.reshape(1, width)) for g in gains]
    raws = [slot.store((rows, width), F32) for _ in (0, 1)]
    query, kv = slot.store((rows, width), BF), slot.store((rows, 2 * width), BF)
    factor = slot.store((rows, 128), F32)
    value = slot.vmem((rows, width), F32)
    half = rows // 2

    def products():
        for j in range(3):
            if flags is not None:
                yield ("flag", flags[j])
            slot.fetch(stages[j])
        for k in range(4):
            yield ("flag", "chunk%d" % k)
            slot.need(*stages)
            chunk = line.chunk(k)
            block = pl.ds(pl.multiple_of(chunk * width, width), width)
            for j, acc in enumerate((raws[0], raws[1], value)):
                term = dot_nn(line.wide.ref[chunk], stages[j].ref[block])
                acc.ref[...] = term if k == 0 else acc.ref[...] + term
                yield ("did", 0.6)
        slot.mark("products")

    slot.add(products)

    def make(h):
        totals = RowTotals(slot, half)

        def body():
            yield ("flag", "products")

            def first(part, here):
                q, k = raws[0].ref[part], raws[1].ref[part]
                totals.put(here, jnp.sum(q * q, axis=1, keepdims=True), jnp.sum(k * k, axis=1, keepdims=True))

            tiled_at(h * half, half, 32, first, 0)
            slot.flush_half(h, *raws)
            yield ("did", 0.7)
            yield from totals.exchange()
            yield ("flag", "tables")
            slot.need(*gains)
            slot.need(*[t for t in (cosine, sine) if hasattr(t, "source")])

            def second(part, here):
                trig = pl.ds(pl.multiple_of(first_row + h * half + here.start, 32), 32)
                lane = lax.broadcasted_iota(jnp.int32, (32, 128), 1)
                scales = [lax.rsqrt(totals.column(here, j) / D + EPS) for j in (0, 1)]
                factor.ref[part] = jnp.where(lane == 0, scales[0], scales[1])
                co, si = cosine.ref[trig], sine.ref[trig]
                for j, target in ((0, query), (1, kv)):
                    for n in range(width // HEAD_DIM):
                        turned = raws[j].ref[part, head_cols(n)] * scales[j] * gains[j].ref[:, head_cols(n)]
                        target.ref[part, head_cols(n)] = (turned * co + half_turn(turned) * si).astype(BF)
                kv.ref[part, width : 2 * width] = value.ref[part].astype(BF)

            tiled_at(h * half, half, 32, second, 0)
            slot.flush_half(h, kv, query, factor)
            yield ("did", 1.5)

        slot.add(body)

    make(0)
    make(1)
    return [raws[0].target, raws[1].target, query.target, kv.target, factor.target]


class Mask:
    def __init__(self, slot, seg_all, seg_cols, first, count, turned=False):
        self.slot, self.first, self.count, self.turned = slot, first, count, turned
        self.keys, self.mine = slot.load(seg_all), slot.load(seg_cols)
        self.mask = slot.vmem((4 * count, count) if turned else (count, 4 * count), F32)

    def fill(self, s):
        self.slot.need(self.keys, self.mine)
        count = self.count
        ctx = self.slot.place.ctx
        mine = self.mine.ref[(self.first + s) * count : (self.first + s + 1) * count]
        for c in range(4):
            keys = self.keys.ref[8 * c + self.first + s : 8 * c + self.first + s + 1, :]
            row = ctx * count + lax.broadcasted_iota(jnp.int32, (count, count), 0)
            col = c * count + lax.broadcasted_iota(jnp.int32, (count, count), 1)
            fine = jnp.logical_and(mine[:, 0:1] == keys, row >= col)
            block = jnp.where(fine, 0.0, NEG)
            if self.turned:
                self.mask.ref[c * count : (c + 1) * count] = jnp.transpose(block)
            else:
                self.mask.ref[:, c * count : (c + 1) * count] = block


def attend(slot, flag, kv, query, mask, rows, width):
    kv, query = slot.late(kv), slot.load(query)
    count = mask.count
    heads, heads_b = slot.store((rows, width), F32), slot.store((rows, width), BF)
    logsum = slot.store((rows, 128), F32)
    logits = slot.vmem((count, 4 * count), F32)
    scale = 1.0 / math.sqrt(HEAD_DIM)

    def body():
        yield ("flag", flag)
        slot.fetch(kv)
        mask.fill(0)
        yield ("did", 1.5)
        slot.need(kv, query)
        logsum.ref[...] = jnp.zeros((rows, 128), F32)
        for s in range(rows // count):
            mine = pl.ds(s * count, count)
            if s:
                mask.fill(s)
                yield ("did", 1.0)
            for pair in range(width // HEAD_DIM // 2):
                heads_pair(s, mine, pair)
                yield ("did", 2.2)
        slot.flush(heads_b, heads, logsum)

    def heads_pair(s, mine, pair):
        @pl.loop(2 * pair, 2 * pair + 2)
        def _(h):
            cols = pl.ds(pl.multiple_of(h * HEAD_DIM, HEAD_DIM), HEAD_DIM)
            vcols = pl.ds(pl.multiple_of(width + h * HEAD_DIM, HEAD_DIM), HEAD_DIM)
            q = query.ref[mine, cols]
            peak = jnp.full((count, 1), NEG, F32)
            for c in range(4):
                keys = kv.ref[pl.ds(c * rows + s * count, count), cols]
                block = pl.ds(c * count, count)
                value = dot_nt(q, keys) * scale + mask.mask.ref[:, block]
                logits.ref[:, block] = value
                peak = jnp.maximum(peak, jnp.max(value, axis=1, keepdims=True))
            total = jnp.zeros((count, 1), F32)
            acc = jnp.zeros((count, HEAD_DIM), F32)
            for c in range(4):
                vals = kv.ref[pl.ds(c * rows + s * count, count), vcols]
                weight = jnp.exp(logits.ref[:, pl.ds(c * count, count)] - peak)
                total = total + jnp.sum(weight, axis=1, keepdims=True)
                acc = acc + dot_nn(weight.astype(BF), vals)
            out = acc / total
            heads.ref[mine, cols] = out
            heads_b.ref[mine, cols] = out.astype(BF)
            lane = lax.broadcasted_iota(jnp.int32, (count, 128), 1)
            logsum.ref[mine] = jnp.where(lane == h, peak + jnp.log(total), logsum.ref[mine])

    slot.add(body)
    return [heads.target, heads_b.target, logsum.target]


def attend_back(slot, line, kv, query, heads, logsum, mask, rows, width, w_out):
    kv, query, heads, logsum = slot.load(kv), slot.load(query), slot.load(heads), slot.load(logsum)
    count = mask.count
    grad = slot.vmem((rows, width), BF)
    g_query, g_kv = slot.store((rows, width), F32), slot.store((4 * rows, 2 * width), BF)
    acc = g_query
    rows_of = slot.vmem((2, 128, count), F32)
    scale = 1.0 / math.sqrt(HEAD_DIM)

    def multiply(first, left, block, j, part):
        value = dot_nt(left[...], block[...])
        acc.ref[...] = value if first else acc.ref[...] + value

    def last():
        grad.ref[...] = acc.ref[...].astype(BF)
        slot.need(kv, query, heads, logsum)
        for s in range(rows // count):
            mine = pl.ds(s * count, count)
            mask.fill(s)
            lane = lax.broadcasted_iota(jnp.int32, (count, 128), 1)
            deltas = jnp.zeros((count, 128), F32)
            for h in range(width // HEAD_DIM):
                cols = head_cols(h)
                delta = jnp.sum(grad.ref[mine, cols].astype(F32) * heads.ref[mine, cols], axis=1, keepdims=True)
                deltas = jnp.where(lane == h, delta, deltas)
            rows_of.ref[0] = jnp.transpose(logsum.ref[mine])
            rows_of.ref[1] = jnp.transpose(deltas)
            yield ("did", 1.5)
            for pair in range(width // HEAD_DIM // 2):
                heads_pair(s, mine, pair)
                yield ("did", 3.0)
        slot.flush(g_kv, g_query)

    def heads_pair(s, mine, pair):
        @pl.loop(2 * pair, 2 * pair + 2)
        def _(h):
            cols = pl.ds(pl.multiple_of(h * HEAD_DIM, HEAD_DIM), HEAD_DIM)
            vcols = pl.ds(pl.multiple_of(width + h * HEAD_DIM, HEAD_DIM), HEAD_DIM)
            q, g = query.ref[mine, cols], grad.ref[mine, cols]
            logs, delta = rows_of.ref[0, pl.ds(h, 1)], rows_of.ref[1, pl.ds(h, 1)]
            there = [pl.ds(c * rows + s * count, count) for c in range(4)]
            values = [dot_nt(kv.ref[t, cols], q) for t in there]
            slopes = [dot_nt(kv.ref[t, vcols], g) for t in there]
            probs = [
                jnp.exp(v * scale + mask.mask.ref[pl.ds(c * count, count)] - logs) for c, v in enumerate(values)
            ]
            slopes = [(p * (v - delta)).astype(BF) for p, v in zip(probs, slopes)]
            total = jnp.zeros((count, HEAD_DIM), F32)
            for t, p, v in zip(there, probs, slopes):
                total = total + dot_tn(v, kv.ref[t, cols])
                g_kv.ref[t, cols] = (dot_nn(v, q) * scale).astype(BF)
                g_kv.ref[t, vcols] = dot_nn(p.astype(BF), g).astype(BF)
            g_query.ref[mine, cols] = total * scale

    consume(slot, line, ((w_out,),), (width, width), col_block, last, multiply, 1, 0.7)
    return [g_query.target, g_kv.target]


def dot_tn(left, right):
    return lax.dot_general(left, right, (((0,), (0,)), ((), ())), preferred_element_type=F32)


def project_back(slot, flag, g_query, g_kv, raws, factor, gains, cosine, sine, first_row, rows, width):
    g_kv = slot.late(g_kv)
    g_query, factor = slot.load(g_query), slot.load(factor)
    raws = [slot.load(r) for r in raws]
    gains = [slot.load(g.reshape(1, width)) for g in gains]
    cosine, sine = slot.load(cosine), slot.load(sine)
    outs = [slot.store((rows, width), BF) for _ in range(3)]
    ended = []
    gain_grads = [slot.store((8, width), F32) for _ in range(2)]
    half = rows // 2
    left = []

    def make(h):
        totals = RowTotals(slot, half)

        def body():
            yield ("flag", flag)
            if h == 0:
                left[:] = [0, 1]
                ended[:] = [0, 1]
                slot.fetch(g_kv)
                for g in gain_grads:
                    g.ref[...] = jnp.zeros((8, width), F32)
                slot.need(g_query, factor, cosine, sine, *raws, *gains)
                slot.need(g_kv)
                slot.mark(flag + "_in")
            else:
                yield ("flag", flag + "_in")

            def first(part, here):
                trig = pl.ds(pl.multiple_of(first_row + h * half + here.start, 32), 32)
                co, si = cosine.ref[trig], sine.ref[trig]
                sums = []
                for j, source in ((0, g_query), (1, g_kv)):
                    scale = factor.ref[part, j : j + 1]
                    total = jnp.zeros((32, HEAD_DIM), F32)
                    for n in range(width // HEAD_DIM):
                        cols = head_cols(n)
                        value = source.ref[part, cols]
                        value = value * co - half_turn(value) * si
                        source.ref[part, cols] = value
                        term = value * raws[j].ref[part, cols]
                        total = total + term * gains[j].ref[:, cols]
                        gain_grads[j].ref[:, cols] += fold_rows(term * scale)
                    sums.append(jnp.sum(total, axis=1, keepdims=True))
                totals.put(here, *sums)

            tiled_at(h * half, half, 32, first, 0)
            left.remove(h)
            if not left:
                slot.flush(*gain_grads)
            yield ("did", 1.5)
            yield from totals.exchange()

            def second(part, here):
                for j, source in ((0, g_query), (1, g_kv)):
                    scale = factor.ref[part, j : j + 1]
                    inner = totals.column(here, j)
                    value = source.ref[part, 0:width] * gains[j].ref[...]
                    outs[j].ref[part] = (scale * value - raws[j].ref[part] * (scale * scale * scale * inner / D)).astype(BF)
                outs[2].ref[part] = g_kv.ref[part, width : 2 * width].astype(BF)

            tiled_at(h * half, half, 32, second, 0)
            slot.flush_half(h, *outs)
            ended.remove(h)
            if not ended:
                slot.mark(flag + "_done")
            yield ("did", 1.5)

        slot.add(body)

    make(0)
    make(1)
    for out in outs:
        out.target.held = out
    return [h.target for h in outs + gain_grads]


def gain_sums(slot, arrays):
    loads = [slot.load(a) for a in arrays]
    width = arrays[0].shape[1]
    mine = [slot.vmem((8, width), F32) for _ in range(3)]
    came = [slot.vmem((8, width), F32) for _ in range(3)]
    out = slot.store((8, width), F32)
    base = slot.sems(6)
    slot.axes |= {"ctx", "dp"}

    def body():
        place = slot.place
        yield ("at", 2.0)
        slot.need(*loads)
        rows = []
        for k in range(0, len(loads), 2):
            rows.append(jnp.sum(loads[k].ref[...] + loads[k + 1].ref[...], axis=0, keepdims=True))
        value = jnp.concatenate(rows + [jnp.zeros((8 - len(rows), width), F32)], axis=0)
        for k, device in enumerate(({"ctx": place.ctx ^ 1}, {"ctx": place.ctx ^ 2}, {"dp": place.dp ^ 1})):
            mine[k].ref[...] = value
            copy = remote(mine[k].ref, came[k].ref, slot, base + 2 * k, base + 2 * k + 1, device)
            copy.start()
            yield ("at", 9.0 + 4.0 * k)
            copy.wait()
            value = mine[k].ref[...] + came[k].ref[...]
        out.ref[...] = value
        slot.flush(out)

    slot.add(body, True)
    return out.target


def grad_blocks(left, right, tall):
    rows, cols = left.shape[1], right.shape[1]
    if tall:
        return (rows, 512), [(0, 512 * k) for k in range(cols // 512)]
    return (512, cols), [(512 * k, 0) for k in range(rows // 512)]


def full_grad(slot, plane, left, right, tall, out, starts, prefix, chosen=None, gates=None):
    shape, where = grad_blocks(left, right, tall)
    chosen = range(len(where)) if chosen is None else chosen
    flags = [prefix + str(k) for k in chosen]
    blocks = [slot.hbm_out(shape, BF) for _ in chosen]
    base = where[chosen[0]]
    weight_grad(slot, left, right, (blocks, shape), [where[k] for k in chosen], flags, 3.6, gates)
    for i, k in enumerate(chosen):
        plane.scatter(blocks[i], 0 if tall else 1, True, 1, starts[i], flags[i], None, (out, (where[k][0] - base[0], where[k][1] - base[1])))


def general_row_total(value):
    return lax.psum(value, "tp")


def general_widen(value):
    return lax.all_gather(value, "tp", axis=1, tiled=True)


def general_narrow(value):
    return lax.psum_scatter(
        value.astype(jnp.bfloat16), "tp", scatter_dimension=1, tiled=True
    ).astype(jnp.float32)


def general_contract_last(left, right):
    return lax.dot_general(
        left, right, (((1,), (1,)), ((), ())), preferred_element_type=jnp.float32
    )


def general_contract_first(left, right):
    return lax.dot_general(
        left, right, (((0,), (0,)), ((), ())), preferred_element_type=jnp.float32
    )


def general_rotary(positions, depth):
    half = depth // 2
    freqs = THETA ** (-(jnp.arange(half, dtype=jnp.float32) * 2.0) / depth)
    angles = positions.astype(jnp.float32)[..., None] * freqs
    return (jnp.cos(angles)[..., None, :], jnp.sin(angles)[..., None, :])


def general_turn(value, cosine, sine):
    half = value.shape[-1] // 2
    first = value[..., :half]
    second = value[..., half:]
    return jnp.concatenate(
        [first * cosine - second * sine, second * cosine + first * sine], axis=-1
    )


def general_turn_back(grad, cosine, sine):
    half = grad.shape[-1] // 2
    first = grad[..., :half]
    second = grad[..., half:]
    return jnp.concatenate(
        [first * cosine + second * sine, second * cosine - first * sine], axis=-1
    )


def general_norm_grad(scaled, value, factor, inner):
    return factor[:, None] * scaled - value * (factor**3 * inner / D)[:, None]


def general(
    hidden,
    cotangent,
    segments,
    positions,
    w_query,
    w_key,
    w_value,
    w_out,
    w_gate,
    w_up,
    w_down,
    q_gain,
    k_gain,
    attn_gain,
    mlp_gain,
):
    local_seqs, slice_len, local_width = hidden.shape
    per_batch = local_seqs // 2
    rows = per_batch * slice_len
    heads_here = q_gain.shape[0] // HEAD_DIM
    scale = 1.0 / math.sqrt(HEAD_DIM)
    query_index = lax.axis_index("ctx") * slice_len + jnp.arange(slice_len, dtype=jnp.int32)
    outputs = []
    input_grads = []
    weight_grads = None
    q_gain_grad = jnp.zeros(q_gain.shape, jnp.float32)
    k_gain_grad = jnp.zeros(k_gain.shape, jnp.float32)
    attn_gain_grad = jnp.zeros(attn_gain.shape, jnp.float32)
    mlp_gain_grad = jnp.zeros(mlp_gain.shape, jnp.float32)
    for batch in range(2):
        lower = batch * per_batch
        tokens_in = hidden[lower : lower + per_batch].reshape(rows, local_width)
        seg_here = segments[lower : lower + per_batch]
        pos_here = positions[lower : lower + per_batch].reshape(rows)
        gathered = (
            lax.all_gather(w_query, ("dp", "ctx"), axis=0, tiled=True),
            lax.all_gather(w_key, ("dp", "ctx"), axis=0, tiled=True),
            lax.all_gather(w_value, ("dp", "ctx"), axis=0, tiled=True),
            lax.all_gather(w_out, ("dp", "ctx"), axis=1, tiled=True),
            lax.all_gather(w_gate, ("dp", "ctx"), axis=0, tiled=True),
            lax.all_gather(w_up, ("dp", "ctx"), axis=0, tiled=True),
            lax.all_gather(w_down, ("dp", "ctx"), axis=1, tiled=True),
        )
        query_full, key_full, value_full, out_full, gate_full, up_full, down_full = gathered
        if weight_grads is None:
            weight_grads = tuple((jnp.zeros(tensor.shape, jnp.float32) for tensor in gathered))
        wide_in = general_widen(tokens_in)
        query_raw = jnp.dot(wide_in, query_full, preferred_element_type=jnp.float32)
        key_raw = jnp.dot(wide_in, key_full, preferred_element_type=jnp.float32)
        value_raw = jnp.dot(wide_in, value_full, preferred_element_type=jnp.float32)
        query_sq, key_sq = general_row_total(
            (jnp.sum(query_raw * query_raw, axis=1), jnp.sum(key_raw * key_raw, axis=1))
        )
        query_scale = lax.rsqrt(query_sq / D + EPS)
        key_scale = lax.rsqrt(key_sq / D + EPS)
        cosine, sine = general_rotary(pos_here, HEAD_DIM)
        query_rot = general_turn(
            (query_raw * query_scale[:, None] * q_gain).reshape(rows, heads_here, HEAD_DIM),
            cosine,
            sine,
        )
        key_rot = general_turn(
            (key_raw * key_scale[:, None] * k_gain).reshape(rows, heads_here, HEAD_DIM),
            cosine,
            sine,
        )
        query_b = query_rot.astype(jnp.bfloat16).reshape(per_batch, slice_len, heads_here, HEAD_DIM)
        key_b = key_rot.astype(jnp.bfloat16).reshape(per_batch, slice_len, heads_here * HEAD_DIM)
        value_b = value_raw.astype(jnp.bfloat16).reshape(
            per_batch, slice_len, heads_here * HEAD_DIM
        )

        def allowed_pairs(seg_piece, count):
            key_index = jnp.arange(count, dtype=jnp.int32)
            causal = query_index[:, None] >= key_index[None, :]
            same = seg_here[:, None, :, None] == seg_piece[:, None, None, :]
            return jnp.logical_and(same, causal[None, None])

        start_peak = jnp.full((per_batch, heads_here, slice_len), NEG, jnp.float32)
        peak = start_peak
        key_piece = lax.all_gather(key_b, "ctx", axis=1, tiled=True)
        value_piece = lax.all_gather(value_b, "ctx", axis=1, tiled=True)
        attend_seg_piece = lax.all_gather(seg_here, "ctx", axis=1, tiled=True)
        attend_count = key_piece.shape[1]
        key_four = key_piece.reshape(per_batch, attend_count, heads_here, HEAD_DIM)
        value_four = value_piece.reshape(per_batch, attend_count, heads_here, HEAD_DIM)
        allowed = allowed_pairs(attend_seg_piece, attend_count)
        logits = scale * jnp.einsum(
            "sqhd,skhd->shqk", query_b, key_four, preferred_element_type=jnp.float32
        )
        logits = jnp.where(allowed, logits, NEG)
        fresh = jnp.maximum(peak, jnp.max(logits, axis=-1))
        weights = jnp.where(allowed, jnp.exp(logits - fresh[..., None]), 0.0)
        total = jnp.sum(weights, axis=-1)
        accum = jnp.einsum(
            "shqk,skhd->shqd",
            weights.astype(jnp.bfloat16),
            value_four,
            preferred_element_type=jnp.float32,
        )
        peak, total, accum = (fresh, total, accum)
        logsum = peak + jnp.log(total)
        out_heads = (
            (accum / total[..., None]).transpose(0, 2, 1, 3).reshape(rows, heads_here * HEAD_DIM)
        )
        out_b = out_heads.astype(jnp.bfloat16)
        attn_raw = general_narrow(jnp.dot(out_b, out_full, preferred_element_type=jnp.float32))
        attn_scale = lax.rsqrt(general_row_total(jnp.sum(attn_raw * attn_raw, axis=1)) / D + EPS)
        resid = tokens_in.astype(jnp.float32) + attn_raw * attn_scale[:, None] * attn_gain
        wide_mid = general_widen(resid.astype(jnp.bfloat16))
        gate = jnp.dot(wide_mid, gate_full, preferred_element_type=jnp.float32)
        up_val = jnp.dot(wide_mid, up_full, preferred_element_type=jnp.float32)
        sigma = jax.nn.sigmoid(gate)
        swish = gate * sigma
        act_b = (swish * up_val).astype(jnp.bfloat16)
        mlp_raw = general_narrow(jnp.dot(act_b, down_full, preferred_element_type=jnp.float32))
        mlp_scale = lax.rsqrt(general_row_total(jnp.sum(mlp_raw * mlp_raw, axis=1)) / D + EPS)
        result = resid + mlp_raw * mlp_scale[:, None] * mlp_gain
        outputs.append(result.astype(jnp.bfloat16).reshape(per_batch, slice_len, local_width))
        again = (
            lax.all_gather(w_query, ("dp", "ctx"), axis=0, tiled=True),
            lax.all_gather(w_key, ("dp", "ctx"), axis=0, tiled=True),
            lax.all_gather(w_value, ("dp", "ctx"), axis=0, tiled=True),
            lax.all_gather(w_out, ("dp", "ctx"), axis=1, tiled=True),
            lax.all_gather(w_gate, ("dp", "ctx"), axis=0, tiled=True),
            lax.all_gather(w_up, ("dp", "ctx"), axis=0, tiled=True),
            lax.all_gather(w_down, ("dp", "ctx"), axis=1, tiled=True),
        )
        query_back, key_back, value_back, out_back, gate_back, up_back, down_back = again
        grad_out = (
            cotangent[lower : lower + per_batch].reshape(rows, local_width).astype(jnp.float32)
        )
        mlp_gain_grad = mlp_gain_grad + jnp.sum(grad_out * mlp_raw * mlp_scale[:, None], axis=0)
        scaled = grad_out * mlp_gain
        grad_mlp = general_norm_grad(
            scaled, mlp_raw, mlp_scale, general_row_total(jnp.sum(scaled * mlp_raw, axis=1))
        )
        wide_grad_mlp = general_widen(grad_mlp.astype(jnp.bfloat16))
        grad_act = general_contract_last(wide_grad_mlp, down_back)
        grad_gate = (grad_act * up_val * sigma * (1.0 + gate * (1.0 - sigma))).astype(jnp.bfloat16)
        grad_up = (grad_act * swish).astype(jnp.bfloat16)
        grad_resid = grad_out + general_narrow(
            general_contract_last(grad_gate, gate_back) + general_contract_last(grad_up, up_back)
        )
        attn_gain_grad = attn_gain_grad + jnp.sum(
            grad_resid * attn_raw * attn_scale[:, None], axis=0
        )
        scaled = grad_resid * attn_gain
        grad_attn = general_norm_grad(
            scaled, attn_raw, attn_scale, general_row_total(jnp.sum(scaled * attn_raw, axis=1))
        )
        wide_grad_attn = general_widen(grad_attn.astype(jnp.bfloat16))
        grad_heads = general_contract_last(wide_grad_attn, out_back).astype(jnp.bfloat16)
        dout_four = grad_heads.reshape(per_batch, slice_len, heads_here, HEAD_DIM)
        delta = jnp.sum(
            (grad_heads.astype(jnp.float32) * out_heads).reshape(
                per_batch, slice_len, heads_here, HEAD_DIM
            ),
            axis=-1,
        ).transpose(0, 2, 1)

        def attend_back(piece):
            key_piece, value_piece, seg_piece = piece
            count = key_piece.shape[1]
            key_four = key_piece.reshape(per_batch, count, heads_here, HEAD_DIM)
            value_four = value_piece.reshape(per_batch, count, heads_here, HEAD_DIM)
            allowed = allowed_pairs(seg_piece, count)
            logits = scale * jnp.einsum(
                "sqhd,skhd->shqk", query_b, key_four, preferred_element_type=jnp.float32
            )
            probs = jnp.where(allowed, jnp.exp(logits - logsum[..., None]), 0.0)
            grad_probs = jnp.einsum(
                "sqhd,skhd->shqk", dout_four, value_four, preferred_element_type=jnp.float32
            )
            grad_logits = (probs * (grad_probs - delta[..., None])).astype(jnp.bfloat16)
            grad_query = scale * jnp.einsum(
                "shqk,skhd->sqhd", grad_logits, key_four, preferred_element_type=jnp.float32
            )
            key_grad = scale * jnp.einsum(
                "shqk,sqhd->skhd", grad_logits, query_b, preferred_element_type=jnp.float32
            )
            value_grad = jnp.einsum(
                "shqk,sqhd->skhd",
                probs.astype(jnp.bfloat16),
                dout_four,
                preferred_element_type=jnp.float32,
            )
            grad_keys = key_grad.reshape(per_batch, count, heads_here * HEAD_DIM)
            grad_values = value_grad.reshape(per_batch, count, heads_here * HEAD_DIM)
            return (grad_query, grad_keys, grad_values)

        grad_query, grad_keys, grad_values = attend_back(
            (
                lax.all_gather(key_b, "ctx", axis=1, tiled=True),
                lax.all_gather(value_b, "ctx", axis=1, tiled=True),
                lax.all_gather(seg_here, "ctx", axis=1, tiled=True),
            )
        )
        key_grad_mine, value_grad_mine = (
            lax.psum_scatter(
                grad_keys.astype(jnp.bfloat16), "ctx", scatter_dimension=1, tiled=True
            ).astype(jnp.float32),
            lax.psum_scatter(
                grad_values.astype(jnp.bfloat16), "ctx", scatter_dimension=1, tiled=True
            ).astype(jnp.float32),
        )
        grad_qnorm = general_turn_back(
            grad_query.reshape(rows, heads_here, HEAD_DIM), cosine, sine
        ).reshape(rows, heads_here * HEAD_DIM)
        grad_knorm = general_turn_back(
            key_grad_mine.reshape(rows, heads_here, HEAD_DIM), cosine, sine
        ).reshape(rows, heads_here * HEAD_DIM)
        q_gain_grad = q_gain_grad + jnp.sum(grad_qnorm * query_raw * query_scale[:, None], axis=0)
        k_gain_grad = k_gain_grad + jnp.sum(grad_knorm * key_raw * key_scale[:, None], axis=0)
        q_scaled = grad_qnorm * q_gain
        k_scaled = grad_knorm * k_gain
        q_inner, k_inner = general_row_total(
            (jnp.sum(q_scaled * query_raw, axis=1), jnp.sum(k_scaled * key_raw, axis=1))
        )
        grad_query_raw = general_norm_grad(q_scaled, query_raw, query_scale, q_inner).astype(jnp.bfloat16)
        grad_key_raw = general_norm_grad(k_scaled, key_raw, key_scale, k_inner).astype(jnp.bfloat16)
        grad_value_raw = value_grad_mine.reshape(rows, heads_here * HEAD_DIM).astype(jnp.bfloat16)
        back_terms = (
            general_contract_last(grad_query_raw, query_back)
            + general_contract_last(grad_key_raw, key_back)
            + general_contract_last(grad_value_raw, value_back)
        )
        grad_in = grad_resid + general_narrow(back_terms)
        input_grads.append(grad_in.astype(jnp.bfloat16).reshape(per_batch, slice_len, local_width))
        fresh_grads = (
            general_contract_first(wide_in, grad_query_raw),
            general_contract_first(wide_in, grad_key_raw),
            general_contract_first(wide_in, grad_value_raw),
            general_contract_first(out_b, wide_grad_attn),
            general_contract_first(wide_mid, grad_gate),
            general_contract_first(wide_mid, grad_up),
            general_contract_first(act_b, wide_grad_mlp),
        )
        weight_grads = tuple((left + right for left, right in zip(weight_grads, fresh_grads)))
    finals = (
        lax.psum_scatter(
            weight_grads[0].astype(jnp.bfloat16), ("dp", "ctx"), scatter_dimension=0, tiled=True
        ).astype(jnp.float32),
        lax.psum_scatter(
            weight_grads[1].astype(jnp.bfloat16), ("dp", "ctx"), scatter_dimension=0, tiled=True
        ).astype(jnp.float32),
        lax.psum_scatter(
            weight_grads[2].astype(jnp.bfloat16), ("dp", "ctx"), scatter_dimension=0, tiled=True
        ).astype(jnp.float32),
        lax.psum_scatter(
            weight_grads[3].astype(jnp.bfloat16), ("dp", "ctx"), scatter_dimension=1, tiled=True
        ).astype(jnp.float32),
        lax.psum_scatter(
            weight_grads[4].astype(jnp.bfloat16), ("dp", "ctx"), scatter_dimension=0, tiled=True
        ).astype(jnp.float32),
        lax.psum_scatter(
            weight_grads[5].astype(jnp.bfloat16), ("dp", "ctx"), scatter_dimension=0, tiled=True
        ).astype(jnp.float32),
        lax.psum_scatter(
            weight_grads[6].astype(jnp.bfloat16), ("dp", "ctx"), scatter_dimension=1, tiled=True
        ).astype(jnp.float32),
    )
    gains = lax.psum((q_gain_grad, k_gain_grad, attn_gain_grad, mlp_gain_grad), ("dp", "ctx"))
    return (
        jnp.concatenate(outputs, axis=0),
        jnp.concatenate(input_grads, axis=0),
        finals[0],
        finals[1],
        finals[2],
        finals[3],
        finals[4],
        finals[5],
        finals[6],
        gains[0],
        gains[1],
        gains[2],
        gains[3],
    )


class Batch:
    pass


def planned(
    hidden, cotangent, segments, positions, w_query, w_key, w_value, w_out, w_gate, w_up, w_down,
    q_gain, k_gain, attn_gain, mlp_gain,
):
    seqs, count, width = hidden.shape
    per = seqs // 2
    rows = per * count
    ff = w_gate.shape[1]
    batches = (Batch(), Batch())
    one, two = batches
    for b, batch in enumerate(batches):
        batch.x = Rows(hidden.reshape(seqs * count, width), b * rows, rows)
        batch.cot = Rows(cotangent.reshape(seqs * count, width), b * rows, rows)
    seg_cols = jnp.broadcast_to(segments.reshape(seqs * count, 1), (seqs * count, 128))
    pos_cols = jnp.broadcast_to(positions.reshape(seqs * count, 1), (seqs * count, 128))
    half = HEAD_DIM // 2
    freqs = THETA ** (-(jnp.arange(half, dtype=F32) * 2.0) / HEAD_DIM)
    freqs = jnp.concatenate([freqs, freqs]).reshape(1, HEAD_DIM)
    sign = jnp.concatenate([-jnp.ones(half, F32), jnp.ones(half, F32)]).reshape(1, HEAD_DIM)
    seg_pad = jnp.concatenate([segments, jnp.zeros((8 - seqs, count), segments.dtype)], axis=0)
    norms = (q_gain, k_gain)

    quarters = [(512 * k, 512) for k in range(ff // 512)]
    wg, wu = [], []

    s = Slot("slot0", 0, 97.0, 48.0)
    line = Line(s, rows, width, gather=one.x)
    plane = Plane(s)
    seg_h = plane.gather(seg_pad, 0, False)
    full = [plane.gather(w, 0, True, done="w%d" % i) for i, w in enumerate((w_query, w_key, w_value))]
    w_out_h = plane.gather(w_out, 1, True, 1, 12.0)
    some = [plane.gather(w_gate, 0, True, 1, t, cols=c) for t, c in zip((18.0, 26.0), quarters)]
    cosine, sine = tables(s, pos_cols, freqs, sign)
    made = project(s, line, rows, width, full, ("w0", "w1", "w2"), norms, cosine, sine, 0)
    s.run()
    wq, wk, wv = (h.value for h in full)
    wg += [h.value for h in some]
    wo, seg_all, cosine, sine = w_out_h.value, seg_h.value, cosine.target.value, sine.target.value
    one.q_raw, one.k_raw, one.q, one.kv, one.qk_factor = (h.value for h in made)
    one.wide = line.out.value

    s = Slot("slot1", 1, 85.0, 42.0)
    line = Line(s, rows, width, gather=two.x)
    plane = Plane(s)
    kvs = plane.gather(one.kv, 0, False, 4, done="kv")
    some = [plane.gather(w_gate, 0, True, cols=c) for c in quarters[2:]]
    more = plane.gather(w_up, 0, True, cols=quarters[0])
    s.mark_early("tables")
    mask = Mask(s, seg_all, seg_cols, 0, count)
    felt = attend(s, "kv", kvs, one.q, mask, rows, width)
    made = project(s, line, rows, width, (wq, wk, wv), None, norms, s.load(cosine), s.load(sine), rows)
    s.run()
    wg += [h.value for h in some]
    wu.append(more.value)
    one.kvs = kvs.value
    two.q_raw, two.k_raw, two.q, two.kv, two.qk_factor = (h.value for h in made)
    one.heads, one.heads_b, one.logsum = (h.value for h in felt)
    two.wide = line.out.value

    s = Slot("slot2", 2, 130.0, 60.0)
    line = Line(s, rows, width, scatter=True)
    plane = Plane(s)
    kvs = plane.gather(two.kv, 0, False, 4, done="kv")
    some = [plane.gather(w_up, 0, True, cols=c) for c in quarters[1:]]
    ends = attn_finish(s, line, rows, width, one.x, attn_gain)
    produce(s, line, [s.load(one.heads_b)], [[wo]], (width, width), col_block, dot_nn, 0.6)
    mask = Mask(s, seg_all, seg_cols, per, count)
    felt = attend(s, "kv", kvs, two.q, mask, rows, width)
    s.run()
    wu += [h.value for h in some]
    two.kvs = kvs.value
    one.attn, one.resid, one.resid_b, one.factor = (h.value for h in ends)
    two.heads, two.heads_b, two.logsum = (h.value for h in felt)

    s = Slot("slot3", 3, 200.0, 80.0)
    line = Line(s, rows, width, gather=one.resid_b, scatter=True)
    w_down_h = Plane(s).gather(w_down, 1, True, 4)
    ends = attn_finish(s, line, rows, width, two.x, attn_gain)
    produce(s, line, [s.load(two.heads_b)], [[wo]], (width, width), col_block, dot_nn, 0.6)
    inner = gate_up(s, line, rows, wg, wu)
    s.run()
    wd, one.mid = w_down_h.value, line.out.value
    two.attn, two.resid, two.resid_b, two.factor = (h.value for h in ends)
    one.gate, one.up, one.act = (h.value for h in inner)

    s = Slot("slot4", 4, 130.0, 60.0)
    line = Line(s, rows, width, gather=two.resid_b, scatter=True)
    ends = mlp_finish(s, line, rows, width, one.resid, one.cot, mlp_gain)
    produce(s, line, [s.load(one.act)], [[wd]], (ff, 512), col_block, dot_nn, 1.8)
    inner = gate_up(s, line, rows, wg, wu)
    s.run()
    two.mid = line.out.value
    one.out, one.g_mlp_b, one.g_mlp_gain = (h.value for h in ends)
    two.gate, two.up, two.act = (h.value for h in inner)

    s = Slot("slot5", 5, 130.0, 60.0)
    line = Line(s, rows, width, gather=one.g_mlp_b, scatter=True)
    ends = mlp_finish(s, line, rows, width, two.resid, two.cot, mlp_gain)
    produce(s, line, [s.load(two.act)], [[wd]], (ff, 512), col_block, dot_nn, 1.8)
    inner = act_back(s, line, rows, wd, one.gate, one.up)
    s.run()
    one.g_mlp = line.out.value
    two.out, two.g_mlp_b, two.g_mlp_gain = (h.value for h in ends)
    one.g_gate, one.g_up = (h.value for h in inner)

    s = Slot("slot6", 6, 130.0, 60.0)
    line = Line(s, rows, width, gather=two.g_mlp_b, scatter=True)
    ends = resid_finish(s, line, rows, width, one.cot, one.attn, one.factor, attn_gain)
    produce(s, line, [s.load(one.g_gate), s.load(one.g_up)], [wg, wu], (512, ff), row_block, dot_nt, 3.4)
    inner = act_back(s, line, rows, wd, two.gate, two.up)
    s.run()
    two.g_mlp = line.out.value
    one.g_resid, one.g_attn_b, one.g_attn_gain = (h.value for h in ends)
    two.g_gate, two.g_up = (h.value for h in inner)

    s = Slot("slot7", 7, 97.0, 48.0)
    line = Line(s, rows, width, gather=one.g_attn_b, scatter=True)
    plane = Plane(s)
    g_down = s.hbm_out((ff - 512, w_down.shape[1]), F32)
    ends = resid_finish(s, line, rows, width, two.cot, two.attn, two.factor, attn_gain)
    acts, g_mlps = joined(s, (one.act, two.act)), joined(s, (one.g_mlp, two.g_mlp))
    full_grad(s, plane, acts, g_mlps, False, g_down, (12.0, 23.0, 28.0), "d", (0, 1, 2), ("part0", "part1", "part1"))
    produce(s, line, [s.load(two.g_gate), s.load(two.g_up)], [wg, wu], (512, ff), row_block, dot_nt, 3.4)
    mask = Mask(s, seg_all, seg_cols, 0, count, True)
    back = attend_back(s, line, one.kvs, one.q, one.heads, one.logsum, mask, rows, width, wo)
    s.run()
    one.g_attn = line.out.value
    two.g_resid, two.g_attn_b, two.g_attn_gain = (h.value for h in ends)
    one.g_q, one.g_kv = (h.value for h in back)

    s = Slot("slot8", 8, 92.0, 46.0)
    line = Line(s, rows, width, gather=two.g_attn_b)
    plane = Plane(s)
    g_kv = plane.scatter(one.g_kv, 0, False, 4, done="kv")
    g_gate = s.hbm_out(w_gate.shape, F32)
    raws = project_back(s, "kv", one.g_q, g_kv, (one.q_raw, one.k_raw), one.qk_factor, norms, cosine, sine, 0, rows, width)
    mids, g_gates = joined(s, (one.mid, two.mid)), joined(s, (one.g_gate, two.g_gate))
    full_grad(s, plane, mids, g_gates, True, g_gate, (7.0, 11.0, 15.0, 19.0), "g")
    mask = Mask(s, seg_all, seg_cols, per, count, True)
    back = attend_back(s, line, two.kvs, two.q, two.heads, two.logsum, mask, rows, width, wo)
    s.run()
    two.g_attn = line.out.value
    one.g_qr, one.g_kr, one.g_vr, one.g_q_gain, one.g_k_gain = (h.value for h in raws)
    two.g_q, two.g_kv = (h.value for h in back)

    s = Slot("slot9", 9, 75.0, 38.0)
    line = Line(s, rows, width, scatter=True)
    plane = Plane(s)
    g_kv = plane.scatter(two.g_kv, 0, False, 4, done="kv")
    g_up = s.hbm_out(w_up.shape, F32)
    fin_one = last_finish(s, line, rows, width, one.g_resid)[0]
    raws = project_back(s, "kv", two.g_q, g_kv, (two.q_raw, two.k_raw), two.qk_factor, norms, cosine, sine, rows, rows, width)
    produce(s, line, [s.load(g) for g in (one.g_qr, one.g_kr, one.g_vr)], [[wq], [wk], [wv]], (512, width), row_block, dot_nt, 1.6, "u0")
    mids, g_ups = joined(s, (one.mid, two.mid)), joined(s, (one.g_up, two.g_up))
    full_grad(s, plane, mids, g_ups, True, g_up, (7.0, 18.0, 22.0, 26.0), "u")
    s.run()
    two.g_qr, two.g_kr, two.g_vr, two.g_q_gain, two.g_k_gain = (h.value for h in raws)

    s = Slot("slot10", 10, 75.0, 38.0)
    line = Line(s, rows, width, scatter=True)
    plane = Plane(s)
    fin_two = last_finish(s, line, rows, width, two.g_resid)[0]
    produce(s, line, [s.load(g) for g in (two.g_qr, two.g_kr, two.g_vr)], [[wq], [wk], [wv]], (512, width), row_block, dot_nt, 1.6, "d3")
    sums = gain_sums(
        s,
        (one.g_q_gain, two.g_q_gain, one.g_k_gain, two.g_k_gain)
        + (one.g_attn_gain, two.g_attn_gain, one.g_mlp_gain, two.g_mlp_gain),
    )
    g_q, g_k, g_v = (s.hbm_out(w_query.shape, F32) for _ in range(3))
    g_out, g_last = s.hbm_out(w_out.shape, F32), s.hbm_out((512, w_down.shape[1]), F32)
    acts, g_mlps = joined(s, (one.act, two.act)), joined(s, (one.g_mlp, two.g_mlp))
    full_grad(s, plane, acts, g_mlps, False, g_last, (7.0,), "d", (3,))
    wides = joined(s, (one.wide, two.wide))
    full_grad(s, plane, wides, joined(s, (one.g_qr, two.g_qr)), True, g_q, (18.0,), "q")
    full_grad(s, plane, wides, joined(s, (one.g_kr, two.g_kr)), True, g_k, (22.0,), "k")
    full_grad(s, plane, wides, joined(s, (one.g_vr, two.g_vr)), True, g_v, (26.0,), "v")
    heads_b, g_attns = joined(s, (one.heads_b, two.heads_b)), joined(s, (one.g_attn, two.g_attn))
    full_grad(s, plane, heads_b, g_attns, False, g_out, (30.0,), "o")
    s.run()
    gains = [sums.value[k] for k in range(4)]
    shape = (per, count, width)
    return (
        jnp.concatenate([one.out.reshape(shape), two.out.reshape(shape)], axis=0),
        jnp.concatenate([fin_one.value.reshape(shape), fin_two.value.reshape(shape)], axis=0),
        *(g.value for g in (g_q, g_k, g_v, g_out, g_gate, g_up)),
        jnp.concatenate([g_down.value, g_last.value], axis=0),
        *gains,
    )


def solution(mesh):
    rows, cols = P(("dp", "ctx"), "tp"), P("tp", ("dp", "ctx"))
    act, gain = P("dp", "ctx", "tp"), P("tp")
    size = dict(mesh.shape)
    body = planned if (size["dp"], size["ctx"], size["tp"]) == (2, 4, 4) else general
    return jax.shard_map(
        body,
        mesh=mesh,
        in_specs=(act, act, P("dp", "ctx"), P("dp", "ctx"), rows, rows, rows, cols, rows, rows, cols, gain, gain, gain, gain),
        out_specs=(act, act, rows, rows, rows, cols, rows, rows, cols, gain, gain, gain, gain),
        check_vma=False,
    )
```

```python
import functools
import math

import jax
import jax.numpy as jnp
from jax import lax
from jax.experimental import pallas as pl
from jax.experimental.pallas import tpu as pltpu
from jax.sharding import PartitionSpec as P

D = 2048
HEAD_DIM = 128
EPS = 1e-06
THETA = 500000.0
NEG = -1e30
BF = jnp.bfloat16
F32 = jnp.float32
MESH = pl.DeviceIdType.MESH
HBM = pl.BlockSpec(memory_space=pltpu.HBM)


class Place:
    def __init__(self, tp_size):
        self.n = tp_size
        self.tp = lax.axis_index("tp")
        self.dp = lax.axis_index("dp")
        self.ctx = lax.axis_index("ctx")
        self.slot = self.dp * 4 + self.ctx


def remote(src, dst, sem, send, recv, device):
    return pltpu.make_async_remote_copy(
        src_ref=src, dst_ref=dst, send_sem=sem.at(send), recv_sem=sem.at(recv), device_id=device, device_id_type=MESH
    )


class Step:
    def __init__(self, job, name, link, time, deps, rank, issue=None, arrive=None):
        self.job, self.name, self.link, self.time, self.deps, self.rank = job, name, link, time, deps, rank
        self.issue, self.arrive = issue, arrive


class Plane:
    def __init__(self, slot):
        self.slot = slot
        self.jobs = []
        slot.plane = self
        slot.axes.add("ctx")

    def gather(self, array, dim, with_dp, pieces=1, start=0.0, after=None, done=None, cols=None):
        return self.append(Gather(self.slot, array, dim, with_dp, pieces, start, after, done, cols))

    def scatter(self, array, dim, with_dp, pieces=1, start=0.0, after=None, done=None, out=None):
        return self.append(Scatter(self.slot, array, dim, with_dp, pieces, start, after, done, out))

    def append(self, job):
        job.number = len(self.jobs)
        self.jobs.append(job)
        if job.with_dp:
            self.slot.axes.add("dp")
        self.slot.add(lambda: job.body(self), True)
        return job.out

    def plan(self):
        pieces = [(job, p) for job in self.jobs for p in range(job.pieces)]
        choice, load = {}, [0.0, 0.0]
        for job, p in pieces:
            load[0] += job.unit
            load[1] += job.unit if job.with_dp else 0.0
        for job, p in pieces:
            via = 0 if load[0] < load[1] else 1
            choice[job, p] = via
            if job.with_dp:
                load[via] += job.unit
        best = self.lay(choice)
        for _ in range(2):
            for key in pieces:
                if key[0].with_dp:
                    trial = dict(choice)
                    trial[key] = 1 - trial[key]
                    result = self.lay(trial)
                    if result[0] < best[0] - 0.01:
                        choice, best = trial, result
        self.actions = best[1]

    def lay(self, choice):
        steps = [step for job in self.jobs for p in range(job.pieces) for step in job.steps(p, choice[job, p])]
        times, free, actions = {}, [0.0, 0.0], []
        pending = list(steps)
        while pending:
            best = None
            for step in pending:
                if any((step.job, d) not in times for d in step.deps):
                    continue
                ready = max([step.job.start] + [times[step.job, d] for d in step.deps])
                key = (ready, step.job.number, step.rank)
                if best is None or key < best[0]:
                    best = (key, step)
            (ready, _, _), step = best
            pending.remove(step)
            if step.link is None:
                arrive_at = ready + step.time
            else:
                begin = max(ready, free[step.link])
                free[step.link] = begin + step.time
                actions.append((ready, 1, len(actions), step.job, step.issue))
                arrive_at = begin + step.time + 0.7
            actions.append((arrive_at, 0, len(actions), step.job, step.arrive))
            times[step.job, step.name] = arrive_at
        actions.sort(key=lambda a: a[:3])
        return sum(times.values()) / len(times) / 10 + max(times.values()), actions


class Job:
    def body(self, plane):
        slot = self.slot
        if not plane.planned:
            plane.plan()
            plane.planned = True
        if self.after is not None:
            yield ("flag", self.after)
        shift = max(0.0, slot.now - self.start) if self.after is not None else 0.0
        yield ("at", self.start)
        self.begin()
        yield ("at", self.start + shift + 1.0)
        self.settle()
        for time, _, _, job, emit in plane.actions:
            if job is self:
                yield ("at", time + shift)
                emit()
        yield ("at", slot.now + 1.0)
        self.finish()
        if self.done is not None:
            slot.mark(self.done)

    def send(self, index, origin, target, device):
        copy = remote(origin, target, self.slot, self.base + 2 * index, self.base + 2 * index + 1, device)
        copy.start()
        self.sent.append(copy)

    def got(self, index, target):
        remote(target, target, self.slot, self.base + 2 * index, self.base + 2 * index + 1, self.cdev).wait_recv()

    def settle(self):
        pass

    def coordinates(self):
        self.dp, self.ctx = self.slot.place.dp, self.slot.place.ctx
        self.xdev, self.ydev, self.cdev = {"ctx": self.ctx ^ 2}, {"dp": self.dp ^ 1}, {"ctx": self.ctx ^ 1}
        self.sent = []


class Gather(Job):
    def __init__(self, slot, array, dim, with_dp, pieces, start, after, done, cols):
        self.slot, self.dim, self.with_dp, self.pieces = slot, dim, with_dp, pieces
        self.start, self.after, self.done = start, after, done
        self.handle = slot.hbm_in(array)
        shape = list(array.shape)
        self.cols = pl.ds(0, shape[1]) if cols is None else pl.ds(*cols)
        if cols is not None:
            shape[1] = cols[1]
        self.size, self.rows = shape[dim], shape[0]
        self.unit = math.prod(shape) * 2 / (slot.rates[1] * 1e3) / pieces
        self.hold = slot.vmem(tuple(shape), array.dtype)
        shape[dim] *= 8 if with_dp else 4
        self.out = slot.hbm_out(tuple(shape), array.dtype)
        self.own = slot.sems(2)
        self.base = slot.sems(2 * pieces * 7)

    def spot(self, d, c, p):
        out = self.out.ref
        block = d * 4 + c if self.with_dp else c
        step = self.rows // self.pieces
        if self.dim == 1:
            return out.at[pl.ds(p * step, step), pl.ds(pl.multiple_of(block * self.size, self.size), self.size)]
        return out.at[pl.ds(pl.multiple_of(block * self.size + p * step, step), step)]

    def begin(self):
        self.coordinates()
        self.source = src = self.handle.ref.at[:, self.cols]
        step = self.rows // self.pieces
        for p in range(self.pieces):
            part = pl.ds(p * step, step)
            self.send(7 * p, src.at[part], self.spot(self.dp, self.ctx, p), self.cdev)
        if self.dim == 1:
            mine = self.out.ref.at[:, pl.ds(pl.multiple_of((self.dp * 4 + self.ctx) * self.size, self.size), self.size)]
        else:
            block = self.dp * 4 + self.ctx if self.with_dp else self.ctx
            mine = self.out.ref.at[pl.ds(pl.multiple_of(block * self.size, self.size), self.size)]
        self.held = pltpu.make_async_copy(src, self.hold.ref, self.slot.sem(self.own))
        self.kept = pltpu.make_async_copy(self.hold.ref, mine, self.slot.sem(self.own + 1))
        self.held.start()

    def settle(self):
        self.held.wait()
        self.kept.start()

    def steps(self, p, via):
        def direct(k, device):
            def issue():
                step = self.rows // self.pieces
                part = pl.ds(p * step, step)
                self.send(7 * p + 1 + k, self.source.at[part], self.spot(self.dp, self.ctx, p), device())

            return issue

        def forward(k, place):
            def arrive():
                here = self.spot(*place(), p)
                self.got(7 * p + 1 + k, here)
                self.send(7 * p + 4 + k, here, here, self.cdev)

            return arrive

        from_x = lambda: (self.dp, self.ctx ^ 2)
        from_y = lambda: (self.dp ^ 1, self.ctx)
        corner = lambda: (self.dp ^ 1, self.ctx ^ 2)
        xdev, ydev = (lambda: self.xdev), (lambda: self.ydev)
        out = [Step(self, (p, 0), 0, self.unit, [], 2 * p, direct(0, xdev), forward(0, from_x))]
        if self.with_dp:
            out.append(Step(self, (p, 1), 1, self.unit, [], 2 * p, direct(1, ydev), forward(1, from_y)))

            def hop():
                here = self.spot(*(from_y() if via == 0 else from_x()), p)
                self.send(7 * p + 3, here, here, self.xdev if via == 0 else self.ydev)

            out.append(Step(self, (p, 2), via, self.unit, [(p, 1 - via)], 2 * p + 1, hop, forward(2, corner)))
        return out

    def finish(self):
        for p in range(self.pieces):
            self.got(7 * p, self.spot(self.dp, self.ctx ^ 1, p))
            self.got(7 * p + 4, self.spot(self.dp, self.ctx ^ 3, p))
            if self.with_dp:
                self.got(7 * p + 5, self.spot(self.dp ^ 1, self.ctx ^ 1, p))
                self.got(7 * p + 6, self.spot(self.dp ^ 1, self.ctx ^ 3, p))
        for copy in self.sent:
            copy.wait_send()
        self.kept.wait()


class Scatter(Job):
    def __init__(self, slot, array, dim, with_dp, pieces, start, after, done, out):
        self.slot, self.dim, self.with_dp, self.pieces = slot, dim, with_dp, pieces
        self.start, self.after, self.done = start, after, done
        self.source = slot.hbm_in(array)
        shape = list(array.shape)
        self.chips = chips = 4 if with_dp else 2
        shape[dim] //= 2 * chips
        self.size = shape[dim]
        self.rows, self.width = shape
        self.unit = math.prod(shape) * 2 / (slot.rates[1] * 1e3) / pieces
        if out is None:
            self.out, self.where = slot.hbm_out(tuple(shape), F32), None
        else:
            self.out, self.where = out
        block = tuple(shape)
        self.mine, self.came = slot.vmem((chips,) + block, BF), slot.vmem((chips,) + block, BF)
        self.chip_in = slot.vmem((chips // 2,) + block, BF)
        self.diag = slot.vmem(block, BF) if with_dp else None
        self.total = slot.vmem(block, F32)
        self.loads = slot.sems(chips * pieces)
        self.outs = slot.sems(pieces)
        self.base = slot.sems(2 * pieces * (chips + 3))

    def spot(self, q, c, p):
        x = (self.ctx >> 1) ^ (q & 1)
        d = self.dp ^ (q >> 1)
        block = d * 4 + x * 2 + c if self.with_dp else x * 2 + c
        step = self.rows // self.pieces
        if self.dim == 1:
            return self.source.ref.at[pl.ds(p * step, step), pl.ds(pl.multiple_of(block * self.size, self.size), self.size)]
        return self.source.ref.at[pl.ds(pl.multiple_of(block * self.size + p * step, step), step)]

    def part(self, p):
        step = self.rows // self.pieces
        return pl.ds(p * step, step)

    def load(self, q, p):
        core = self.ctx & 1
        return pltpu.make_async_copy(
            self.spot(q, core, p), self.mine.ref.at[q, self.part(p)], self.slot.sem(self.loads + q * self.pieces + p)
        )

    def begin(self):
        self.coordinates()
        core = self.ctx & 1
        self.order = (3, 1, 2, 0) if self.with_dp else (1, 0)
        self.per = self.chips + 3
        for p in range(self.pieces):
            for q in self.order:
                self.send(self.per * p + q, self.spot(q, core ^ 1, p), self.came.ref.at[q, self.part(p)], self.cdev)
                self.load(q, p).start()

    def add(self, into, other, p):
        step = self.rows // self.pieces
        tile = min(32, step)

        @pl.loop(0, step // tile)
        def _(i):
            part = pl.ds(pl.multiple_of(p * step + i * tile, tile), tile)
            into[part] = (into[part].astype(F32) + other[part].astype(F32)).astype(BF)

    def steps(self, p, via):
        mine, came = self.mine, self.came

        def cores():
            for q in self.order:
                self.load(q, p).wait()
                self.got(self.per * p + q, came.ref.at[q, self.part(p)])
                self.add(mine.ref.at[q], came.ref.at[q], p)

        def out(k, q, target, device):
            def issue():
                self.send(self.per * p + self.chips + k, mine.ref.at[q, self.part(p)], target(), device())

            return issue

        xdev, ydev = (lambda: self.xdev), (lambda: self.ydev)
        into = lambda j: (lambda: self.chip_in.ref.at[j, self.part(p)])
        done = {}

        def last(k, j):
            def arrive():
                self.got(self.per * p + self.chips + k, self.chip_in.ref.at[j, self.part(p)])
                done[j] = True
                if len(done) == self.chips // 2:
                    done.clear()
                    self.close(p)

            return arrive

        steps = [Step(self, (p, "c"), None, 2.0 + self.unit * 0.5, [], 3 * p, None, cores)]
        if not self.with_dp:
            steps.append(Step(self, (p, 0), 0, self.unit, [(p, "c")], 3 * p + 1, out(0, 1, into(0), xdev), last(0, 0)))
            return steps
        corner = lambda: self.diag.ref.at[self.part(p)]

        def fold():
            self.got(self.per * p + self.chips + 2, corner())
            self.add(mine.ref.at[2 if via == 0 else 1], self.diag.ref, p)

        steps.append(
            Step(self, (p, 2), via, self.unit, [(p, "c")], 3 * p, out(2, 3, corner, xdev if via == 0 else ydev), fold)
        )
        for k, device in ((0, xdev), (1, ydev)):
            deps = [(p, "c")] if k == via else [(p, 2)]
            steps.append(Step(self, (p, k), k, self.unit, deps, 3 * p + 1, out(k, 1 + k, into(k), device), last(k, k)))
        return steps

    def result(self, p):
        target = self.out.ref
        step = self.rows // self.pieces
        if self.where is None:
            target = target.at[pl.ds(p * step, step)]
        else:
            row, col = self.where
            target = target.at[pl.ds(row + p * step, step), pl.ds(col, self.width)]
        return pltpu.make_async_copy(self.total.ref.at[self.part(p)], target, self.slot.sem(self.outs + p))

    def close(self, p):
        step = self.rows // self.pieces
        tile = min(32, step)
        mine, chip_in, total = self.mine.ref, self.chip_in.ref, self.total.ref

        @pl.loop(0, step // tile)
        def _(i):
            part = pl.ds(pl.multiple_of(p * step + i * tile, tile), tile)
            value = mine[0, part].astype(F32) + chip_in[0, part].astype(F32)
            if self.with_dp:
                value = value + chip_in[1, part].astype(F32)
            total[part] = value

        self.result(p).start()

    def finish(self):
        for copy in self.sent:
            copy.wait_send()
        for p in range(self.pieces):
            self.result(p).wait()


class Handle:
    ref = None
    sem = None
    waited = False
    lazy = False
    halves = False
    cut = None
    value = None

    def __init__(self, shape=None, dtype=None):
        self.shape, self.dtype = shape, dtype


class Rows:
    def __init__(self, array, first, count):
        self.array, self.first = array, first
        self.shape, self.dtype = (count,) + array.shape[1:], array.dtype


class Slot:
    def __init__(self, name, ident, line_rate=97.0, plane_rate=48.0):
        self.name, self.ident = name, ident
        self.rates = (line_rate, plane_rate)
        self.inputs, self.outputs, self.scratch = [], [], []
        self.sem_count = 0
        self.tasks = []
        self.axes = set()
        self.early = []
        self.prologue = []
        self.plane = None
        self.loads, self.stores = [], []
        self.flags = {}
        self.now = 0.0

    def sems(self, number):
        first = self.sem_count
        self.sem_count += number
        return first

    def hbm_in(self, array):
        if isinstance(array, Handle):
            return array
        handle = Handle(array.shape, array.dtype)
        if isinstance(array, Rows):
            handle.cut = pl.ds(array.first, array.shape[0])
            array = array.array
        self.inputs.append((array, handle))
        return handle

    def hbm_out(self, shape, dtype):
        handle = Handle(shape, dtype)
        self.outputs.append((jax.ShapeDtypeStruct(shape, dtype), handle))
        return handle

    def vmem(self, shape, dtype):
        handle = Handle(shape, dtype)
        self.scratch.append((pltpu.VMEM(shape, dtype), handle))
        return handle

    def load(self, array):
        handle = self.vmem(array.shape, array.dtype)
        handle.source = self.hbm_in(array)
        handle.sem = self.sems(1)
        self.loads.append(handle)
        return handle

    def store(self, shape, dtype):
        handle = self.vmem(shape, dtype)
        handle.target = self.hbm_out(shape, dtype)
        handle.sem = self.sems(2)
        self.stores.append(handle)
        return handle

    def late(self, array):
        handle = self.vmem(array.shape, array.dtype)
        handle.source = self.hbm_in(array)
        handle.sem = self.sems(1)
        handle.lazy = True
        self.loads.append(handle)
        return handle

    def fetch(self, *handles):
        for handle in handles:
            pltpu.make_async_copy(handle.source.ref, handle.ref, self.sem(handle.sem)).start()

    def need(self, *handles):
        for handle in handles:
            if not handle.waited:
                handle.waited = True
                pltpu.make_async_copy(handle.source.ref, handle.ref, self.sem(handle.sem)).wait()

    def flush(self, *handles):
        for handle in handles:
            pltpu.make_async_copy(handle.ref, handle.target.ref, self.sem(handle.sem)).start()

    def flush_half(self, h, *handles):
        for handle in handles:
            half = handle.shape[0] // 2
            part = pl.ds(h * half, half)
            handle.halves = True
            pltpu.make_async_copy(handle.ref.at[part], handle.target.ref.at[part], self.sem(handle.sem + h)).start()

    def sem(self, index):
        return self.sem_ref.at[index]

    def at(self, index):
        return self.sem_ref.at[index]

    def add(self, body, transfers=False):
        self.tasks.append((body, transfers))

    def mark(self, flag):
        self.flags[flag] = True

    def mark_early(self, flag):
        self.early.append(flag)

    def kernel(self, *refs):
        refs = list(refs)
        for group in (self.inputs, self.outputs, self.scratch):
            for _, handle in group:
                handle.ref = refs.pop(0)
                if handle.cut is not None:
                    handle.ref = handle.ref.at[handle.cut]
        self.sem_ref = refs.pop(0)
        self.flags, self.now = {flag: True for flag in self.early}, 0.0
        for handle in self.loads:
            handle.waited = False
            if not handle.lazy:
                pltpu.make_async_copy(handle.source.ref, handle.ref, self.sem(handle.sem)).start()
        for begin in self.prologue:
            begin()
        self.place = place = Place(4)
        barrier = pltpu.get_barrier_semaphore()
        peers = []
        if "ctx" in self.axes:
            peers += [{"ctx": place.ctx ^ 1}, {"ctx": place.ctx ^ 2}]
        if "dp" in self.axes:
            peers += [{"dp": place.dp ^ 1}]
        if "tp" in self.axes:
            peers += [{"tp": place.tp ^ k} for k in (1, 2, 3)]
        for device in peers:
            pl.semaphore_signal(barrier, inc=1, device_id=device, device_id_type=MESH)
        pl.semaphore_wait(barrier, len(peers))
        if self.plane is not None:
            self.plane.planned = False
        running = [[("at", 0.0), task(), 0 if transfers else 1, i] for i, (task, transfers) in enumerate(self.tasks)]
        while running:
            ready = None
            for entry in running:
                kind, value = entry[0]
                if (kind == "at" and value <= self.now) or (kind == "flag" and value in self.flags):
                    key = (entry[2], value if kind == "at" and entry[2] == 0 else 0.0, entry[3])
                    if ready is None or key < ready[0]:
                        ready = (key, entry)
            if ready is None:
                self.now = min(entry[0][1] for entry in running if entry[0][0] == "at")
                continue
            entry = ready[1]
            try:
                got = next(entry[1])
            except StopIteration:
                running.remove(entry)
                continue
            if got[0] == "did":
                self.now += got[1]
                got = ("at", self.now)
            entry[0] = got
        for handle in self.stores:
            if not handle.halves:
                pltpu.make_async_copy(handle.ref, handle.target.ref, self.sem(handle.sem)).wait()
                continue
            half = handle.shape[0] // 2
            for h in (0, 1):
                part = pl.ds(h * half, half)
                pltpu.make_async_copy(handle.ref.at[part], handle.target.ref.at[part], self.sem(handle.sem + h)).wait()

    def run(self):
        values = pl.pallas_call(
            self.kernel,
            out_shape=tuple(o for o, _ in self.outputs),
            in_specs=[HBM] * len(self.inputs),
            out_specs=tuple([HBM] * len(self.outputs)),
            scratch_shapes=[s for s, _ in self.scratch] + [pltpu.SemaphoreType.DMA((self.sem_count,))],
            compiler_params=pltpu.CompilerParams(
                collective_id=self.ident, has_side_effects=True, vmem_limit_bytes=62 * 1024 * 1024
            ),
            name=self.name,
        )(*[a for a, _ in self.inputs])
        for (_, handle), value in zip(self.outputs, values):
            handle.value = value


def any_of(me, values):
    values = sorted(values)
    cond = me == values[0]
    for v in values[1:]:
        cond = jnp.logical_or(cond, me == v)
    return cond


def pick(me, table):
    items = sorted(table.items())
    out = jnp.int32(items[0][1])
    for key, value in items[1:]:
        out = jnp.where(me == key, jnp.int32(value), out)
    return out


PAIR = {0: ["A0", "R3", "R2", "R1"], 1: ["A1", "A0", "R3", "R2"], 2: ["A2", "A1", "A0", "R3"]}
ONLY_A = {0: ["A0", "", ""], 1: ["A1", "A0", ""], 2: ["A2", "A1", "A0"]}
ONLY_R = {0: ["R3", "R2", "R1"], 1: ["", "R3", "R2"], 2: ["", "", "R3"]}


class Line:
    def __init__(self, slot, rows, width, gather=None, scatter=False, pieces=2, keep=True):
        self.slot, self.rows, self.width, self.pieces = slot, rows, width, pieces
        self.gather, self.scatter = gather is not None, scatter
        slot.axes.add("tp")
        right = PAIR if self.gather and scatter else (ONLY_A if self.gather else ONLY_R)
        flip = lambda m: m if not m else m[0] + str(3 - int(m[1]))
        self.tables = (right, {3 - d: [flip(m) for m in row] for d, row in right.items()})
        self.steps = len(right[0])
        self.keep = keep
        if self.gather:
            self.source = slot.hbm_in(gather)
            self.wide = slot.vmem((4, rows, width), BF)
            self.own_sem = slot.sems(1)
            if keep:
                self.out = slot.hbm_out((rows, 4 * width), BF)
                self.out_sem = slot.sems(4)
        if scatter:
            self.mine = slot.vmem((4, rows, width), BF)
            self.skip = self.steps - 3
            self.came = slot.vmem((2, 3, rows, width), BF)
        self.base = slot.sems(4 * self.steps * pieces)
        self.unit = rows * width * 4 / (slot.rates[0] * 1e3)
        slot.add(self.body, True)

    def chunk(self, k):
        me = self.slot.place.tp
        return (me, pick(me, {0: 1, 1: 2, 2: 1, 3: 2}), pick(me, {0: 2, 1: 0, 2: 3, 3: 1}), pick(me, {0: 3, 1: 3, 2: 0, 3: 0}))[k]

    def index(self, way, t, p):
        return self.base + 2 * ((way * self.steps + t) * self.pieces + p)

    def part(self, p):
        step = self.rows // self.pieces
        return pl.ds(p * step, step)

    def sends(self, t, p):
        me = self.slot.place.tp
        rows = self.part(p)
        for way in (0, 1):
            for kind in "AR":
                table = {d: int(row[t][1]) for d, row in self.tables[way].items() if row[t][:1] == kind}
                if not table:
                    continue
                block = pick(me, table)
                if kind == "A":
                    target = self.wide.ref.at[block, rows]
                    origin = self.source.ref.at[rows] if t == 0 else target
                else:
                    target = self.came.ref.at[way, t - self.skip, rows]
                    origin = self.mine.ref.at[block, rows]
                index = self.index(way, t, p)
                to = me + 1 if way == 0 else me - 1
                yield kind, any_of(me, table), remote(origin, target, self.slot, index, index + 1, {"tp": to})

    def arrivals(self, t, p):
        me = self.slot.place.tp
        rows = self.part(p)
        step = self.rows // self.pieces
        tile = 64
        for way in (0, 1):
            off = 1 if way == 0 else -1
            froms = {d + off: row[t] for d, row in self.tables[way].items() if row[t]}
            sample = self.wide.ref.at[0, rows] if self.gather else self.came.ref.at[0, 0, rows]
            index = self.index(way, t, p)
            pl.when(any_of(me, froms))(remote(sample, sample, self.slot, index, index + 1, {"tp": me}).wait_recv)
            adds = {d: int(m[1]) for d, m in froms.items() if m[0] == "R" and int(m[1]) != d}
            if adds:
                block = pick(me, adds)
                mine, came = self.mine.ref, self.came.ref

                @pl.when(any_of(me, adds))
                def _():
                    @pl.loop(0, step // tile)
                    def _(i):
                        part = pl.ds(pl.multiple_of(p * step + i * tile, tile), tile)
                        mine[block, part] = (mine[block, part].astype(F32) + came[way, t - self.skip, part].astype(F32)).astype(BF)

    def body(self):
        slot = self.slot
        me = slot.place.tp
        if self.gather:
            own = pltpu.make_async_copy(self.source.ref, self.wide.ref.at[me], slot.sem(self.own_sem))
            own.start()
        start = 0.0
        for t in range(self.steps):
            for p in range(self.pieces):
                if t > 0:
                    yield ("at", start + (t - 1 + (p + 1) / self.pieces) * self.unit + 0.5)
                    self.arrivals(t - 1, p)
                    if p == self.pieces - 1 and self.gather and t <= 3:
                        slot.mark("chunk%d" % t)
                messages = list(self.sends(t, p))
                for kind, cond, copy in messages:
                    if kind == "A":
                        pl.when(cond)(copy.start)
                if any(kind == "R" for kind, _, _ in messages):
                    first = t == (1 if self.gather else 0)
                    if p == 0:
                        for c in ((3, 0) if first else (2, 1)):
                            yield ("flag", "part%d" % c)
                        start = max(start, slot.now - t * self.unit)
                    for kind, cond, copy in messages:
                        if kind == "R":
                            pl.when(cond)(copy.start)
                if t == 0 and p == 0 and self.gather:
                    yield ("at", 1.0)
                    own.wait()
                    slot.mark("chunk0")
        for p in range(self.pieces):
            yield ("at", start + (self.steps - 1 + (p + 1) / self.pieces) * self.unit + 0.5)
            self.arrivals(self.steps - 1, p)
            if self.scatter and (2 * p + 2) % self.pieces == 0:
                slot.mark("reduced%d" % (2 * (p + 1) // self.pieces - 1))
        if self.gather and self.steps == 3:
            slot.mark("chunk3")
        outs = []
        if self.gather and self.keep:
            for c in range(4):
                where = self.out.ref.at[:, pl.ds(c * self.width, self.width)]
                outs.append(pltpu.make_async_copy(self.wide.ref.at[c], where, slot.sem(self.out_sem + c)))
                outs[-1].start()
        yield ("at", start + self.steps * self.unit + 1.0)
        for t in range(self.steps):
            for p in range(self.pieces):
                for _, cond, copy in self.sends(t, p):
                    pl.when(cond)(copy.wait_send)
        for copy in outs:
            copy.wait()

    def total(self, part):
        me = self.slot.place.tp
        last = 2
        left = jnp.where(me > 0, self.came.ref[0, last, part].astype(F32), 0.0)
        right = jnp.where(me < 3, self.came.ref[1, last, part].astype(F32), 0.0)
        return self.mine.ref[me, part].astype(F32) + left + right


def tiled(count, tile, body):
    @pl.loop(0, count // tile)
    def _(i):
        body(pl.ds(pl.multiple_of(i * tile, tile), tile))


class Weights:
    def __init__(self, slot, groups, shape, order, where):
        self.slot, self.order, self.where = slot, order, where
        self.groups = [[slot.hbm_in(a) for a in group] for group in groups]
        self.wide = shape[1] // len(groups[0])
        self.buffer = slot.vmem((2, len(groups)) + shape, BF)
        self.base = slot.sems(2 * sum(len(g) for g in groups))

    def copies(self, step):
        block = self.order[step] if not callable(self.order) else self.order(step)
        index = self.base + step % 2
        for j, group in enumerate(self.groups):
            for k, array in enumerate(group):
                target = self.buffer.ref.at[step % 2, j]
                if len(group) > 1:
                    target = target.at[:, pl.ds(k * self.wide, self.wide)]
                yield pltpu.make_async_copy(self.where(array.ref, block), target, self.slot.sem(index))
                index += 2

    def start(self, step):
        for copy in self.copies(step):
            copy.start()

    def take(self, step):
        for copy in self.copies(step):
            copy.wait()
        return [self.buffer.ref.at[step % 2, j] for j in range(len(self.groups))]


def row_block(ref, c):
    return ref.at[pl.ds(pl.multiple_of(c * 512, 512), 512)]


def col_block(ref, c):
    return ref.at[:, pl.ds(pl.multiple_of(c * 512, 512), 512)]


def consume(slot, line, groups, shape, where, last, multiply, parts, cost):
    weights = Weights(slot, groups, shape, line.chunk, where)

    def body():
        weights.start(0)
        for k in range(4):
            if k < 3:
                weights.start(k + 1)
            yield ("flag", "chunk%d" % k)
            blocks = weights.take(k)
            chunk = line.chunk(k)
            for j, block in enumerate(blocks):
                for part in range(parts):
                    multiply(k == 0, line.wide.ref.at[chunk], block, j, part)
                    yield ("did", cost)
        yield from last()

    slot.add(body)


def dot_nn(left, right):
    return jnp.dot(left, right, preferred_element_type=F32)


def dot_nt(left, right):
    return lax.dot_general(left, right, (((1,), (1,)), ((), ())), preferred_element_type=F32)


def produce(slot, line, lefts, groups, shape, where, dot, cost, gate=None):
    order = (3, 0, 2, 1)
    weights = Weights(slot, groups, shape, order, where)
    lefts = [h.held if hasattr(h, "held") else h for h in lefts]

    def body():
        weights.start(0)
        if gate is not None:
            yield ("flag", gate)
        slot.need(*[h for h in lefts if hasattr(h, "source")])
        half = line.rows // 2
        for k, c in enumerate(order):
            if k < 3:
                weights.start(k + 1)
            blocks = weights.take(k)
            for h in (0, 1):
                part = pl.ds(h * half, half)
                value = None
                for left, block in zip(lefts, blocks):
                    term = dot(left.ref[part], block[...])
                    value = term if value is None else value + term
                line.mine.ref[c, part] = value.astype(BF)
                yield ("did", cost / 2)
            slot.mark("part%d" % c)

    slot.add(body)


def joined(slot, arrays):
    rows = arrays[0].shape[0]
    handle = slot.vmem((len(arrays) * rows, arrays[0].shape[1]), arrays[0].dtype)
    sources = [slot.hbm_in(a) for a in arrays]
    base = slot.sems(len(arrays))

    def copies():
        return [
            pltpu.make_async_copy(a.ref, handle.ref.at[pl.ds(b * rows, rows)], slot.sem(base + b)) for b, a in enumerate(sources)
        ]

    def begin():
        handle.waited = False
        for copy in copies():
            copy.start()

    def ready():
        if not handle.waited:
            handle.waited = True
            for copy in copies():
                copy.wait()

    slot.prologue.append(begin)
    handle.ready = ready
    return handle


def weight_grad(slot, left, right, out, where, flags, cost, gates):
    buffer = slot.vmem(out[1], BF)
    base = slot.sems(1)

    def body():
        yield ("at", 2.5)
        tall, wide = out[1]
        target = buffer.ref
        for k, (rows, cols) in enumerate(where):
            if gates is not None:
                yield ("flag", gates[k])
            left.ready()
            right.ready()
            for i in range((tall // 512) * (wide // 512)):
                r, c = (512 * i, 0) if wide == 512 else (0, 512 * i)
                value = dot_tn(left.ref[:, pl.ds(rows + r, 512)], right.ref[:, pl.ds(cols + c, 512)])
                target[pl.ds(r, 512), pl.ds(c, 512)] = value.astype(BF)
                yield ("did", cost / 4)
            copy = pltpu.make_async_copy(target, out[0][k].ref, slot.sem(base))
            copy.start()
            yield ("at", slot.now + 0.7)
            copy.wait()
            slot.mark(flags[k])

    slot.add(body)


class RowTotals:
    def __init__(self, slot, rows):
        self.slot, self.rows = slot, rows
        self.stat = slot.vmem((rows, 128), F32)
        self.send = slot.vmem((8, rows), F32)
        self.came = slot.vmem((3, 8, rows), F32)
        self.total = slot.vmem((rows, 128), F32)
        self.base = slot.sems(6)

    def put(self, part, *columns):
        lane = lax.broadcasted_iota(jnp.int32, (columns[0].shape[0], 128), 1)
        value = jnp.zeros((columns[0].shape[0], 128), F32)
        for k, column in enumerate(columns):
            value = jnp.where(lane == k, column, value)
        self.stat.ref[part] = value

    def exchange(self):
        slot, me = self.slot, self.slot.place.tp
        send = self.send.ref
        send[...] = jnp.transpose(self.stat.ref[...])[0:8]
        copies = []
        for k in (1, 2, 3):
            copies.append(
                remote(send, self.came.ref.at[k - 1], slot, self.base + 2 * (k - 1), self.base + 2 * (k - 1) + 1, {"tp": me ^ k})
            )
            copies[-1].start()
        yield ("at", slot.now + 2.5)
        for copy in copies:
            copy.wait()
        total = send[...] + self.came.ref[0] + self.came.ref[1] + self.came.ref[2]
        wide = jnp.concatenate([total, jnp.zeros((120, self.rows), F32)], axis=0)
        self.total.ref[...] = jnp.transpose(wide)

    def column(self, part, k):
        return self.total.ref[part, k : k + 1]


def finish(slot, line, rows, begin, first, second, flushed, ended, needs):
    half = rows // 2
    left = []

    def make(h):
        totals = RowTotals(slot, half)

        def body():
            yield ("flag", "reduced%d" % h)
            if h == 0:
                left[:] = [0, 1]
                slot.need(*needs)
                begin()
            for i in range(2):
                tiled_at(h * half + i * (half // 2), half // 2, 32, lambda part, here: first(totals, part, here), i * (half // 2))
                yield ("did", 0.5)
            yield from totals.exchange()
            tiled_at(h * half, half, 32, lambda part, here: second(totals, part, here), 0)
            slot.flush_half(h, *flushed)
            left.remove(h)
            if not left:
                slot.flush(*ended)
            yield ("did", 1.5)

        slot.add(body)

    make(0)
    make(1)


def tiled_at(row, count, tile, body, local):
    @pl.loop(0, count // tile)
    def _(i):
        body(
            pl.ds(pl.multiple_of(row + i * tile, tile), tile),
            pl.ds(pl.multiple_of(local + i * tile, tile), tile),
        )


def fold_rows(value):
    total = value[0:8]
    for i in range(1, value.shape[0] // 8):
        total = total + value[8 * i : 8 * i + 8]
    return total


def attn_finish(slot, line, rows, width, x, gain):
    x, gain = slot.load(x), slot.load(gain.reshape(1, width))
    raw, resid = slot.store((rows, width), F32), slot.store((rows, width), F32)
    resid_b, factor = slot.store((rows, width), BF), slot.store((rows, 128), F32)

    def first(totals, part, here):
        value = line.total(part)
        raw.ref[part] = value
        totals.put(here, jnp.sum(value * value, axis=1, keepdims=True))

    def second(totals, part, here):
        scale = lax.rsqrt(totals.column(here, 0) / D + EPS)
        value = x.ref[part].astype(F32) + raw.ref[part] * scale * gain.ref[...]
        resid.ref[part] = value
        resid_b.ref[part] = value.astype(BF)
        factor.ref[part] = jnp.broadcast_to(scale, (32, 128))

    finish(slot, line, rows, lambda: None, first, second, (resid_b, raw, resid, factor), (), (x, gain))
    return [raw.target, resid.target, resid_b.target, factor.target]


def mlp_finish(slot, line, rows, width, resid, cot, gain):
    resid, cot, gain = slot.load(resid), slot.load(cot), slot.load(gain.reshape(1, width))
    raw = slot.vmem((rows, width), F32)
    out, grad = slot.store((rows, width), BF), slot.store((rows, width), BF)
    gain_grad = slot.store((8, width), F32)

    def begin():
        gain_grad.ref[...] = jnp.zeros((8, width), F32)

    def first(totals, part, here):
        value = line.total(part)
        raw.ref[part] = value
        scaled = cot.ref[part].astype(F32) * gain.ref[...]
        totals.put(here, jnp.sum(value * value, axis=1, keepdims=True), jnp.sum(scaled * value, axis=1, keepdims=True))

    def second(totals, part, here):
        scale = lax.rsqrt(totals.column(here, 0) / D + EPS)
        inner = totals.column(here, 1)
        value = raw.ref[part]
        given = cot.ref[part].astype(F32)
        normed = value * scale
        grad.ref[part] = (scale * (given * gain.ref[...]) - value * (scale * scale * scale * inner / D)).astype(BF)
        out.ref[part] = (resid.ref[part] + normed * gain.ref[...]).astype(BF)
        gain_grad.ref[...] += fold_rows(given * normed)

    finish(slot, line, rows, begin, first, second, (grad, out), (gain_grad,), (resid, cot, gain))
    return [out.target, grad.target, gain_grad.target]


def resid_finish(slot, line, rows, width, cot, attn, factor, gain):
    cot, attn, factor, gain = slot.load(cot), slot.load(attn), slot.load(factor), slot.load(gain.reshape(1, width))
    resid, grad = slot.store((rows, width), F32), slot.store((rows, width), BF)
    gain_grad = slot.store((8, width), F32)

    def begin():
        gain_grad.ref[...] = jnp.zeros((8, width), F32)

    def first(totals, part, here):
        value = line.total(part) + cot.ref[part].astype(F32)
        resid.ref[part] = value
        totals.put(here, jnp.sum(value * gain.ref[...] * attn.ref[part], axis=1, keepdims=True))

    def second(totals, part, here):
        scale = factor.ref[part, 0:1]
        inner = totals.column(here, 0)
        value, given = attn.ref[part], resid.ref[part]
        grad.ref[part] = (scale * (given * gain.ref[...]) - value * (scale * scale * scale * inner / D)).astype(BF)
        gain_grad.ref[...] += fold_rows(given * value * scale)

    finish(slot, line, rows, begin, first, second, (grad, resid), (gain_grad,), (cot, attn, factor, gain))
    return [resid.target, grad.target, gain_grad.target]


def last_finish(slot, line, rows, width, resid):
    resid = slot.load(resid)
    out = slot.store((rows, width), BF)
    half = rows // 2

    def make(h):
        def body():
            yield ("flag", "reduced%d" % h)
            slot.need(resid)

            def only(part, here):
                out.ref[part] = (line.total(part) + resid.ref[part]).astype(BF)

            tiled_at(h * half, half, 32, only, 0)
            slot.flush_half(h, out)
            yield ("did", 0.7)

        slot.add(body)

    make(0)
    make(1)
    return [out.target]


def gate_up(slot, line, rows, w_gate, w_up):
    ff = len(w_gate) * w_gate[0].shape[1]
    acc = slot.vmem((2, rows, ff), F32)
    gate, up, act = (slot.store((rows, ff), BF) for _ in range(3))
    wide = ff // 2

    def multiply(first, left, block, j, part):
        cols = pl.ds(part * wide, wide)
        value = dot_nn(left[...], block[:, cols])
        acc.ref[j, :, cols] = value if first else acc.ref[j, :, cols] + value

    def last():
        piece = rows // 4
        for h in range(4):

            @pl.loop(0, piece // 16)
            def _(i):
                part = pl.ds(pl.multiple_of(h * piece + i * 16, 16), 16)
                g, u = acc.ref[0, part], acc.ref[1, part]
                gate.ref[part] = g.astype(BF)
                up.ref[part] = u.astype(BF)
                act.ref[part] = (g * jax.nn.sigmoid(g) * u).astype(BF)

            if h % 2:
                slot.flush_half(h // 2, act, gate, up)
            yield ("did", 1.0)

    consume(slot, line, (w_gate, w_up), (512, ff), row_block, last, multiply, 2, 1.1)
    return [gate.target, up.target, act.target]


def act_back(slot, line, rows, w_down, gate, up):
    ff = w_down.shape[0]
    acc = slot.vmem((rows, ff), F32)
    gate, up = slot.load(gate), slot.load(up)
    g_gate, g_up = slot.store((rows, ff), BF), slot.store((rows, ff), BF)
    wide = ff // 2

    def multiply(first, left, block, j, part):
        cols = pl.ds(part * wide, wide)
        value = dot_nt(left[...], block[cols])
        acc.ref[:, cols] = value if first else acc.ref[:, cols] + value

    def last():
        slot.need(gate, up)
        piece = rows // 4
        for h in range(4):

            @pl.loop(0, piece // 16)
            def _(i):
                part = pl.ds(pl.multiple_of(h * piece + i * 16, 16), 16)
                grad, g, u = acc.ref[part], gate.ref[part].astype(F32), up.ref[part].astype(F32)
                sigma = jax.nn.sigmoid(g)
                g_gate.ref[part] = (grad * u * sigma * (1.0 + g * (1.0 - sigma))).astype(BF)
                g_up.ref[part] = (grad * g * sigma).astype(BF)

            if h % 2:
                slot.flush_half(h // 2, g_gate, g_up)
            yield ("did", 1.2)

    consume(slot, line, ((w_down,),), (ff, 512), col_block, last, multiply, 2, 1.2)
    return [g_gate.target, g_up.target]


def half_turn(value):
    return pltpu.roll(value, HEAD_DIM // 2, axis=1)


def tables(slot, positions, freqs, sign):
    count = positions.shape[0]
    positions, freqs, sign = slot.load(positions), slot.load(freqs), slot.load(sign)
    cosine, sine = slot.store((count, HEAD_DIM), F32), slot.store((count, HEAD_DIM), F32)

    def body():
        slot.need(positions, freqs, sign)

        def first(part):
            angle = positions.ref[part].astype(F32) * freqs.ref[...]
            cosine.ref[part] = jnp.cos(angle)
            sine.ref[part] = jnp.sin(angle) * sign.ref[...]

        tiled(count, 32, first)
        slot.flush(cosine, sine)
        yield ("did", 6.0)
        slot.mark("tables")

    slot.add(body)
    return cosine, sine


def head_cols(h):
    return pl.ds(h * HEAD_DIM, HEAD_DIM)


def project(slot, line, rows, width, weights, flags, gains, cosine, sine, first_row):
    stages = [slot.late(w) for w in weights]
    gains = [slot.load(g.reshape(1, width)) for g in gains]
    raws = [slot.store((rows, width), F32) for _ in (0, 1)]
    query, kv = slot.store((rows, width), BF), slot.store((rows, 2 * width), BF)
    factor = slot.store((rows, 128), F32)
    value = slot.vmem((rows, width), F32)
    half = rows // 2

    def products():
        for j in range(3):
            if flags is not None:
                yield ("flag", flags[j])
            slot.fetch(stages[j])
        for k in range(4):
            yield ("flag", "chunk%d" % k)
            slot.need(*stages)
            chunk = line.chunk(k)
            block = pl.ds(pl.multiple_of(chunk * width, width), width)
            for j, acc in enumerate((raws[0], raws[1], value)):
                term = dot_nn(line.wide.ref[chunk], stages[j].ref[block])
                acc.ref[...] = term if k == 0 else acc.ref[...] + term
                yield ("did", 0.6)
        slot.mark("products")

    slot.add(products)

    def make(h):
        totals = RowTotals(slot, half)

        def body():
            yield ("flag", "products")

            def first(part, here):
                q, k = raws[0].ref[part], raws[1].ref[part]
                totals.put(here, jnp.sum(q * q, axis=1, keepdims=True), jnp.sum(k * k, axis=1, keepdims=True))

            tiled_at(h * half, half, 32, first, 0)
            slot.flush_half(h, *raws)
            yield ("did", 0.7)
            yield from totals.exchange()
            yield ("flag", "tables")
            slot.need(*gains)
            slot.need(*[t for t in (cosine, sine) if hasattr(t, "source")])

            def second(part, here):
                trig = pl.ds(pl.multiple_of(first_row + h * half + here.start, 32), 32)
                lane = lax.broadcasted_iota(jnp.int32, (32, 128), 1)
                scales = [lax.rsqrt(totals.column(here, j) / D + EPS) for j in (0, 1)]
                factor.ref[part] = jnp.where(lane == 0, scales[0], scales[1])
                co, si = cosine.ref[trig], sine.ref[trig]
                for j, target in ((0, query), (1, kv)):
                    for n in range(width // HEAD_DIM):
                        turned = raws[j].ref[part, head_cols(n)] * scales[j] * gains[j].ref[:, head_cols(n)]
                        target.ref[part, head_cols(n)] = (turned * co + half_turn(turned) * si).astype(BF)
                kv.ref[part, width : 2 * width] = value.ref[part].astype(BF)

            tiled_at(h * half, half, 32, second, 0)
            slot.flush_half(h, kv, query, factor)
            yield ("did", 1.5)

        slot.add(body)

    make(0)
    make(1)
    return [raws[0].target, raws[1].target, query.target, kv.target, factor.target]


class Mask:
    def __init__(self, slot, seg_all, seg_cols, first, count, turned=False):
        self.slot, self.first, self.count, self.turned = slot, first, count, turned
        self.keys, self.mine = slot.load(seg_all), slot.load(seg_cols)
        self.mask = slot.vmem((4 * count, count) if turned else (count, 4 * count), F32)

    def fill(self, s):
        self.slot.need(self.keys, self.mine)
        count = self.count
        ctx = self.slot.place.ctx
        mine = self.mine.ref[(self.first + s) * count : (self.first + s + 1) * count]
        for c in range(4):
            keys = self.keys.ref[8 * c + self.first + s : 8 * c + self.first + s + 1, :]
            row = ctx * count + lax.broadcasted_iota(jnp.int32, (count, count), 0)
            col = c * count + lax.broadcasted_iota(jnp.int32, (count, count), 1)
            fine = jnp.logical_and(mine[:, 0:1] == keys, row >= col)
            block = jnp.where(fine, 0.0, NEG)
            if self.turned:
                self.mask.ref[c * count : (c + 1) * count] = jnp.transpose(block)
            else:
                self.mask.ref[:, c * count : (c + 1) * count] = block


def attend(slot, flag, kv, query, mask, rows, width):
    kv, query = slot.late(kv), slot.load(query)
    count = mask.count
    heads, heads_b = slot.store((rows, width), F32), slot.store((rows, width), BF)
    logsum = slot.store((rows, 128), F32)
    logits = slot.vmem((count, 4 * count), F32)
    scale = 1.0 / math.sqrt(HEAD_DIM)

    def body():
        yield ("flag", flag)
        slot.fetch(kv)
        mask.fill(0)
        yield ("did", 1.5)
        slot.need(kv, query)
        logsum.ref[...] = jnp.zeros((rows, 128), F32)
        for s in range(rows // count):
            mine = pl.ds(s * count, count)
            if s:
                mask.fill(s)
                yield ("did", 1.0)
            for pair in range(width // HEAD_DIM // 2):
                heads_pair(s, mine, pair)
                yield ("did", 2.2)
        slot.flush(heads_b, heads, logsum)

    def heads_pair(s, mine, pair):
        @pl.loop(2 * pair, 2 * pair + 2)
        def _(h):
            cols = pl.ds(pl.multiple_of(h * HEAD_DIM, HEAD_DIM), HEAD_DIM)
            vcols = pl.ds(pl.multiple_of(width + h * HEAD_DIM, HEAD_DIM), HEAD_DIM)
            q = query.ref[mine, cols]
            peak = jnp.full((count, 1), NEG, F32)
            for c in range(4):
                keys = kv.ref[pl.ds(c * rows + s * count, count), cols]
                block = pl.ds(c * count, count)
                value = dot_nt(q, keys) * scale + mask.mask.ref[:, block]
                logits.ref[:, block] = value
                peak = jnp.maximum(peak, jnp.max(value, axis=1, keepdims=True))
            total = jnp.zeros((count, 1), F32)
            acc = jnp.zeros((count, HEAD_DIM), F32)
            for c in range(4):
                vals = kv.ref[pl.ds(c * rows + s * count, count), vcols]
                weight = jnp.exp(logits.ref[:, pl.ds(c * count, count)] - peak)
                total = total + jnp.sum(weight, axis=1, keepdims=True)
                acc = acc + dot_nn(weight.astype(BF), vals)
            out = acc / total
            heads.ref[mine, cols] = out
            heads_b.ref[mine, cols] = out.astype(BF)
            lane = lax.broadcasted_iota(jnp.int32, (count, 128), 1)
            logsum.ref[mine] = jnp.where(lane == h, peak + jnp.log(total), logsum.ref[mine])

    slot.add(body)
    return [heads.target, heads_b.target, logsum.target]


def attend_back(slot, line, kv, query, heads, logsum, mask, rows, width, w_out):
    kv, query, heads, logsum = slot.load(kv), slot.load(query), slot.load(heads), slot.load(logsum)
    count = mask.count
    grad = slot.vmem((rows, width), BF)
    g_query, g_kv = slot.store((rows, width), F32), slot.store((4 * rows, 2 * width), BF)
    acc = g_query
    rows_of = slot.vmem((2, 128, count), F32)
    scale = 1.0 / math.sqrt(HEAD_DIM)

    def multiply(first, left, block, j, part):
        value = dot_nt(left[...], block[...])
        acc.ref[...] = value if first else acc.ref[...] + value

    def last():
        grad.ref[...] = acc.ref[...].astype(BF)
        slot.need(kv, query, heads, logsum)
        for s in range(rows // count):
            mine = pl.ds(s * count, count)
            mask.fill(s)
            lane = lax.broadcasted_iota(jnp.int32, (count, 128), 1)
            deltas = jnp.zeros((count, 128), F32)
            for h in range(width // HEAD_DIM):
                cols = head_cols(h)
                delta = jnp.sum(grad.ref[mine, cols].astype(F32) * heads.ref[mine, cols], axis=1, keepdims=True)
                deltas = jnp.where(lane == h, delta, deltas)
            rows_of.ref[0] = jnp.transpose(logsum.ref[mine])
            rows_of.ref[1] = jnp.transpose(deltas)
            yield ("did", 1.5)
            for pair in range(width // HEAD_DIM // 2):
                heads_pair(s, mine, pair)
                yield ("did", 3.0)
        slot.flush(g_kv, g_query)

    def heads_pair(s, mine, pair):
        @pl.loop(2 * pair, 2 * pair + 2)
        def _(h):
            cols = pl.ds(pl.multiple_of(h * HEAD_DIM, HEAD_DIM), HEAD_DIM)
            vcols = pl.ds(pl.multiple_of(width + h * HEAD_DIM, HEAD_DIM), HEAD_DIM)
            q, g = query.ref[mine, cols], grad.ref[mine, cols]
            logs, delta = rows_of.ref[0, pl.ds(h, 1)], rows_of.ref[1, pl.ds(h, 1)]
            there = [pl.ds(c * rows + s * count, count) for c in range(4)]
            values = [dot_nt(kv.ref[t, cols], q) for t in there]
            slopes = [dot_nt(kv.ref[t, vcols], g) for t in there]
            probs = [
                jnp.exp(v * scale + mask.mask.ref[pl.ds(c * count, count)] - logs) for c, v in enumerate(values)
            ]
            slopes = [(p * (v - delta)).astype(BF) for p, v in zip(probs, slopes)]
            total = jnp.zeros((count, HEAD_DIM), F32)
            for t, p, v in zip(there, probs, slopes):
                total = total + dot_tn(v, kv.ref[t, cols])
                g_kv.ref[t, cols] = (dot_nn(v, q) * scale).astype(BF)
                g_kv.ref[t, vcols] = dot_nn(p.astype(BF), g).astype(BF)
            g_query.ref[mine, cols] = total * scale

    consume(slot, line, ((w_out,),), (width, width), col_block, last, multiply, 1, 0.7)
    return [g_query.target, g_kv.target]


def dot_tn(left, right):
    return lax.dot_general(left, right, (((0,), (0,)), ((), ())), preferred_element_type=F32)


def project_back(slot, flag, g_query, g_kv, raws, factor, gains, cosine, sine, first_row, rows, width):
    g_kv = slot.late(g_kv)
    g_query, factor = slot.load(g_query), slot.load(factor)
    raws = [slot.load(r) for r in raws]
    gains = [slot.load(g.reshape(1, width)) for g in gains]
    cosine, sine = slot.load(cosine), slot.load(sine)
    outs = [slot.store((rows, width), BF) for _ in range(3)]
    ended = []
    gain_grads = [slot.store((8, width), F32) for _ in range(2)]
    half = rows // 2
    left = []

    def make(h):
        totals = RowTotals(slot, half)

        def body():
            yield ("flag", flag)
            if h == 0:
                left[:] = [0, 1]
                ended[:] = [0, 1]
                slot.fetch(g_kv)
                for g in gain_grads:
                    g.ref[...] = jnp.zeros((8, width), F32)
                slot.need(g_query, factor, cosine, sine, *raws, *gains)
                slot.need(g_kv)
                slot.mark(flag + "_in")
            else:
                yield ("flag", flag + "_in")

            def first(part, here):
                trig = pl.ds(pl.multiple_of(first_row + h * half + here.start, 32), 32)
                co, si = cosine.ref[trig], sine.ref[trig]
                sums = []
                for j, source in ((0, g_query), (1, g_kv)):
                    scale = factor.ref[part, j : j + 1]
                    total = jnp.zeros((32, HEAD_DIM), F32)
                    for n in range(width // HEAD_DIM):
                        cols = head_cols(n)
                        value = source.ref[part, cols]
                        value = value * co - half_turn(value) * si
                        source.ref[part, cols] = value
                        term = value * raws[j].ref[part, cols]
                        total = total + term * gains[j].ref[:, cols]
                        gain_grads[j].ref[:, cols] += fold_rows(term * scale)
                    sums.append(jnp.sum(total, axis=1, keepdims=True))
                totals.put(here, *sums)

            tiled_at(h * half, half, 32, first, 0)
            left.remove(h)
            if not left:
                slot.flush(*gain_grads)
            yield ("did", 1.5)
            yield from totals.exchange()

            def second(part, here):
                for j, source in ((0, g_query), (1, g_kv)):
                    scale = factor.ref[part, j : j + 1]
                    inner = totals.column(here, j)
                    value = source.ref[part, 0:width] * gains[j].ref[...]
                    outs[j].ref[part] = (scale * value - raws[j].ref[part] * (scale * scale * scale * inner / D)).astype(BF)
                outs[2].ref[part] = g_kv.ref[part, width : 2 * width].astype(BF)

            tiled_at(h * half, half, 32, second, 0)
            slot.flush_half(h, *outs)
            ended.remove(h)
            if not ended:
                slot.mark(flag + "_done")
            yield ("did", 1.5)

        slot.add(body)

    make(0)
    make(1)
    for out in outs:
        out.target.held = out
    return [h.target for h in outs + gain_grads]


def gain_sums(slot, arrays):
    loads = [slot.load(a) for a in arrays]
    width = arrays[0].shape[1]
    mine = [slot.vmem((8, width), F32) for _ in range(3)]
    came = [slot.vmem((8, width), F32) for _ in range(3)]
    out = slot.store((8, width), F32)
    base = slot.sems(6)
    slot.axes |= {"ctx", "dp"}

    def body():
        place = slot.place
        yield ("at", 2.0)
        slot.need(*loads)
        rows = []
        for k in range(0, len(loads), 2):
            rows.append(jnp.sum(loads[k].ref[...] + loads[k + 1].ref[...], axis=0, keepdims=True))
        value = jnp.concatenate(rows + [jnp.zeros((8 - len(rows), width), F32)], axis=0)
        for k, device in enumerate(({"ctx": place.ctx ^ 1}, {"ctx": place.ctx ^ 2}, {"dp": place.dp ^ 1})):
            mine[k].ref[...] = value
            copy = remote(mine[k].ref, came[k].ref, slot, base + 2 * k, base + 2 * k + 1, device)
            copy.start()
            yield ("at", 9.0 + 4.0 * k)
            copy.wait()
            value = mine[k].ref[...] + came[k].ref[...]
        out.ref[...] = value
        slot.flush(out)

    slot.add(body, True)
    return out.target


def grad_blocks(left, right, tall):
    rows, cols = left.shape[1], right.shape[1]
    if tall:
        return (rows, 512), [(0, 512 * k) for k in range(cols // 512)]
    return (512, cols), [(512 * k, 0) for k in range(rows // 512)]


def full_grad(slot, plane, left, right, tall, out, starts, prefix, chosen=None, gates=None):
    shape, where = grad_blocks(left, right, tall)
    chosen = range(len(where)) if chosen is None else chosen
    flags = [prefix + str(k) for k in chosen]
    blocks = [slot.hbm_out(shape, BF) for _ in chosen]
    base = where[chosen[0]]
    weight_grad(slot, left, right, (blocks, shape), [where[k] for k in chosen], flags, 3.6, gates)
    for i, k in enumerate(chosen):
        plane.scatter(blocks[i], 0 if tall else 1, True, 1, starts[i], flags[i], None, (out, (where[k][0] - base[0], where[k][1] - base[1])))


def general_row_total(value):
    return lax.psum(value, "tp")


def general_widen(value):
    return lax.all_gather(value, "tp", axis=1, tiled=True)


def general_narrow(value):
    return lax.psum_scatter(
        value.astype(jnp.bfloat16), "tp", scatter_dimension=1, tiled=True
    ).astype(jnp.float32)


def general_contract_last(left, right):
    return lax.dot_general(
        left, right, (((1,), (1,)), ((), ())), preferred_element_type=jnp.float32
    )


def general_contract_first(left, right):
    return lax.dot_general(
        left, right, (((0,), (0,)), ((), ())), preferred_element_type=jnp.float32
    )


def general_rotary(positions, depth):
    half = depth // 2
    freqs = THETA ** (-(jnp.arange(half, dtype=jnp.float32) * 2.0) / depth)
    angles = positions.astype(jnp.float32)[..., None] * freqs
    return (jnp.cos(angles)[..., None, :], jnp.sin(angles)[..., None, :])


def general_turn(value, cosine, sine):
    half = value.shape[-1] // 2
    first = value[..., :half]
    second = value[..., half:]
    return jnp.concatenate(
        [first * cosine - second * sine, second * cosine + first * sine], axis=-1
    )


def general_turn_back(grad, cosine, sine):
    half = grad.shape[-1] // 2
    first = grad[..., :half]
    second = grad[..., half:]
    return jnp.concatenate(
        [first * cosine + second * sine, second * cosine - first * sine], axis=-1
    )


def general_norm_grad(scaled, value, factor, inner):
    return factor[:, None] * scaled - value * (factor**3 * inner / D)[:, None]


def general(
    hidden,
    cotangent,
    segments,
    positions,
    w_query,
    w_key,
    w_value,
    w_out,
    w_gate,
    w_up,
    w_down,
    q_gain,
    k_gain,
    attn_gain,
    mlp_gain,
):
    local_seqs, slice_len, local_width = hidden.shape
    per_batch = local_seqs // 2
    rows = per_batch * slice_len
    heads_here = q_gain.shape[0] // HEAD_DIM
    scale = 1.0 / math.sqrt(HEAD_DIM)
    query_index = lax.axis_index("ctx") * slice_len + jnp.arange(slice_len, dtype=jnp.int32)
    outputs = []
    input_grads = []
    weight_grads = None
    q_gain_grad = jnp.zeros(q_gain.shape, jnp.float32)
    k_gain_grad = jnp.zeros(k_gain.shape, jnp.float32)
    attn_gain_grad = jnp.zeros(attn_gain.shape, jnp.float32)
    mlp_gain_grad = jnp.zeros(mlp_gain.shape, jnp.float32)
    for batch in range(2):
        lower = batch * per_batch
        tokens_in = hidden[lower : lower + per_batch].reshape(rows, local_width)
        seg_here = segments[lower : lower + per_batch]
        pos_here = positions[lower : lower + per_batch].reshape(rows)
        gathered = (
            lax.all_gather(w_query, ("dp", "ctx"), axis=0, tiled=True),
            lax.all_gather(w_key, ("dp", "ctx"), axis=0, tiled=True),
            lax.all_gather(w_value, ("dp", "ctx"), axis=0, tiled=True),
            lax.all_gather(w_out, ("dp", "ctx"), axis=1, tiled=True),
            lax.all_gather(w_gate, ("dp", "ctx"), axis=0, tiled=True),
            lax.all_gather(w_up, ("dp", "ctx"), axis=0, tiled=True),
            lax.all_gather(w_down, ("dp", "ctx"), axis=1, tiled=True),
        )
        query_full, key_full, value_full, out_full, gate_full, up_full, down_full = gathered
        if weight_grads is None:
            weight_grads = tuple((jnp.zeros(tensor.shape, jnp.float32) for tensor in gathered))
        wide_in = general_widen(tokens_in)
        query_raw = jnp.dot(wide_in, query_full, preferred_element_type=jnp.float32)
        key_raw = jnp.dot(wide_in, key_full, preferred_element_type=jnp.float32)
        value_raw = jnp.dot(wide_in, value_full, preferred_element_type=jnp.float32)
        query_sq, key_sq = general_row_total(
            (jnp.sum(query_raw * query_raw, axis=1), jnp.sum(key_raw * key_raw, axis=1))
        )
        query_scale = lax.rsqrt(query_sq / D + EPS)
        key_scale = lax.rsqrt(key_sq / D + EPS)
        cosine, sine = general_rotary(pos_here, HEAD_DIM)
        query_rot = general_turn(
            (query_raw * query_scale[:, None] * q_gain).reshape(rows, heads_here, HEAD_DIM),
            cosine,
            sine,
        )
        key_rot = general_turn(
            (key_raw * key_scale[:, None] * k_gain).reshape(rows, heads_here, HEAD_DIM),
            cosine,
            sine,
        )
        query_b = query_rot.astype(jnp.bfloat16).reshape(per_batch, slice_len, heads_here, HEAD_DIM)
        key_b = key_rot.astype(jnp.bfloat16).reshape(per_batch, slice_len, heads_here * HEAD_DIM)
        value_b = value_raw.astype(jnp.bfloat16).reshape(
            per_batch, slice_len, heads_here * HEAD_DIM
        )

        def allowed_pairs(seg_piece, count):
            key_index = jnp.arange(count, dtype=jnp.int32)
            causal = query_index[:, None] >= key_index[None, :]
            same = seg_here[:, None, :, None] == seg_piece[:, None, None, :]
            return jnp.logical_and(same, causal[None, None])

        start_peak = jnp.full((per_batch, heads_here, slice_len), NEG, jnp.float32)
        peak = start_peak
        key_piece = lax.all_gather(key_b, "ctx", axis=1, tiled=True)
        value_piece = lax.all_gather(value_b, "ctx", axis=1, tiled=True)
        attend_seg_piece = lax.all_gather(seg_here, "ctx", axis=1, tiled=True)
        attend_count = key_piece.shape[1]
        key_four = key_piece.reshape(per_batch, attend_count, heads_here, HEAD_DIM)
        value_four = value_piece.reshape(per_batch, attend_count, heads_here, HEAD_DIM)
        allowed = allowed_pairs(attend_seg_piece, attend_count)
        logits = scale * jnp.einsum(
            "sqhd,skhd->shqk", query_b, key_four, preferred_element_type=jnp.float32
        )
        logits = jnp.where(allowed, logits, NEG)
        fresh = jnp.maximum(peak, jnp.max(logits, axis=-1))
        weights = jnp.where(allowed, jnp.exp(logits - fresh[..., None]), 0.0)
        total = jnp.sum(weights, axis=-1)
        accum = jnp.einsum(
            "shqk,skhd->shqd",
            weights.astype(jnp.bfloat16),
            value_four,
            preferred_element_type=jnp.float32,
        )
        peak, total, accum = (fresh, total, accum)
        logsum = peak + jnp.log(total)
        out_heads = (
            (accum / total[..., None]).transpose(0, 2, 1, 3).reshape(rows, heads_here * HEAD_DIM)
        )
        out_b = out_heads.astype(jnp.bfloat16)
        attn_raw = general_narrow(jnp.dot(out_b, out_full, preferred_element_type=jnp.float32))
        attn_scale = lax.rsqrt(general_row_total(jnp.sum(attn_raw * attn_raw, axis=1)) / D + EPS)
        resid = tokens_in.astype(jnp.float32) + attn_raw * attn_scale[:, None] * attn_gain
        wide_mid = general_widen(resid.astype(jnp.bfloat16))
        gate = jnp.dot(wide_mid, gate_full, preferred_element_type=jnp.float32)
        up_val = jnp.dot(wide_mid, up_full, preferred_element_type=jnp.float32)
        sigma = jax.nn.sigmoid(gate)
        swish = gate * sigma
        act_b = (swish * up_val).astype(jnp.bfloat16)
        mlp_raw = general_narrow(jnp.dot(act_b, down_full, preferred_element_type=jnp.float32))
        mlp_scale = lax.rsqrt(general_row_total(jnp.sum(mlp_raw * mlp_raw, axis=1)) / D + EPS)
        result = resid + mlp_raw * mlp_scale[:, None] * mlp_gain
        outputs.append(result.astype(jnp.bfloat16).reshape(per_batch, slice_len, local_width))
        again = (
            lax.all_gather(w_query, ("dp", "ctx"), axis=0, tiled=True),
            lax.all_gather(w_key, ("dp", "ctx"), axis=0, tiled=True),
            lax.all_gather(w_value, ("dp", "ctx"), axis=0, tiled=True),
            lax.all_gather(w_out, ("dp", "ctx"), axis=1, tiled=True),
            lax.all_gather(w_gate, ("dp", "ctx"), axis=0, tiled=True),
            lax.all_gather(w_up, ("dp", "ctx"), axis=0, tiled=True),
            lax.all_gather(w_down, ("dp", "ctx"), axis=1, tiled=True),
        )
        query_back, key_back, value_back, out_back, gate_back, up_back, down_back = again
        grad_out = (
            cotangent[lower : lower + per_batch].reshape(rows, local_width).astype(jnp.float32)
        )
        mlp_gain_grad = mlp_gain_grad + jnp.sum(grad_out * mlp_raw * mlp_scale[:, None], axis=0)
        scaled = grad_out * mlp_gain
        grad_mlp = general_norm_grad(
            scaled, mlp_raw, mlp_scale, general_row_total(jnp.sum(scaled * mlp_raw, axis=1))
        )
        wide_grad_mlp = general_widen(grad_mlp.astype(jnp.bfloat16))
        grad_act = general_contract_last(wide_grad_mlp, down_back)
        grad_gate = (grad_act * up_val * sigma * (1.0 + gate * (1.0 - sigma))).astype(jnp.bfloat16)
        grad_up = (grad_act * swish).astype(jnp.bfloat16)
        grad_resid = grad_out + general_narrow(
            general_contract_last(grad_gate, gate_back) + general_contract_last(grad_up, up_back)
        )
        attn_gain_grad = attn_gain_grad + jnp.sum(
            grad_resid * attn_raw * attn_scale[:, None], axis=0
        )
        scaled = grad_resid * attn_gain
        grad_attn = general_norm_grad(
            scaled, attn_raw, attn_scale, general_row_total(jnp.sum(scaled * attn_raw, axis=1))
        )
        wide_grad_attn = general_widen(grad_attn.astype(jnp.bfloat16))
        grad_heads = general_contract_last(wide_grad_attn, out_back).astype(jnp.bfloat16)
        dout_four = grad_heads.reshape(per_batch, slice_len, heads_here, HEAD_DIM)
        delta = jnp.sum(
            (grad_heads.astype(jnp.float32) * out_heads).reshape(
                per_batch, slice_len, heads_here, HEAD_DIM
            ),
            axis=-1,
        ).transpose(0, 2, 1)

        def attend_back(piece):
            key_piece, value_piece, seg_piece = piece
            count = key_piece.shape[1]
            key_four = key_piece.reshape(per_batch, count, heads_here, HEAD_DIM)
            value_four = value_piece.reshape(per_batch, count, heads_here, HEAD_DIM)
            allowed = allowed_pairs(seg_piece, count)
            logits = scale * jnp.einsum(
                "sqhd,skhd->shqk", query_b, key_four, preferred_element_type=jnp.float32
            )
            probs = jnp.where(allowed, jnp.exp(logits - logsum[..., None]), 0.0)
            grad_probs = jnp.einsum(
                "sqhd,skhd->shqk", dout_four, value_four, preferred_element_type=jnp.float32
            )
            grad_logits = (probs * (grad_probs - delta[..., None])).astype(jnp.bfloat16)
            grad_query = scale * jnp.einsum(
                "shqk,skhd->sqhd", grad_logits, key_four, preferred_element_type=jnp.float32
            )
            key_grad = scale * jnp.einsum(
                "shqk,sqhd->skhd", grad_logits, query_b, preferred_element_type=jnp.float32
            )
            value_grad = jnp.einsum(
                "shqk,sqhd->skhd",
                probs.astype(jnp.bfloat16),
                dout_four,
                preferred_element_type=jnp.float32,
            )
            grad_keys = key_grad.reshape(per_batch, count, heads_here * HEAD_DIM)
            grad_values = value_grad.reshape(per_batch, count, heads_here * HEAD_DIM)
            return (grad_query, grad_keys, grad_values)

        grad_query, grad_keys, grad_values = attend_back(
            (
                lax.all_gather(key_b, "ctx", axis=1, tiled=True),
                lax.all_gather(value_b, "ctx", axis=1, tiled=True),
                lax.all_gather(seg_here, "ctx", axis=1, tiled=True),
            )
        )
        key_grad_mine, value_grad_mine = (
            lax.psum_scatter(
                grad_keys.astype(jnp.bfloat16), "ctx", scatter_dimension=1, tiled=True
            ).astype(jnp.float32),
            lax.psum_scatter(
                grad_values.astype(jnp.bfloat16), "ctx", scatter_dimension=1, tiled=True
            ).astype(jnp.float32),
        )
        grad_qnorm = general_turn_back(
            grad_query.reshape(rows, heads_here, HEAD_DIM), cosine, sine
        ).reshape(rows, heads_here * HEAD_DIM)
        grad_knorm = general_turn_back(
            key_grad_mine.reshape(rows, heads_here, HEAD_DIM), cosine, sine
        ).reshape(rows, heads_here * HEAD_DIM)
        q_gain_grad = q_gain_grad + jnp.sum(grad_qnorm * query_raw * query_scale[:, None], axis=0)
        k_gain_grad = k_gain_grad + jnp.sum(grad_knorm * key_raw * key_scale[:, None], axis=0)
        q_scaled = grad_qnorm * q_gain
        k_scaled = grad_knorm * k_gain
        q_inner, k_inner = general_row_total(
            (jnp.sum(q_scaled * query_raw, axis=1), jnp.sum(k_scaled * key_raw, axis=1))
        )
        grad_query_raw = general_norm_grad(q_scaled, query_raw, query_scale, q_inner).astype(jnp.bfloat16)
        grad_key_raw = general_norm_grad(k_scaled, key_raw, key_scale, k_inner).astype(jnp.bfloat16)
        grad_value_raw = value_grad_mine.reshape(rows, heads_here * HEAD_DIM).astype(jnp.bfloat16)
        back_terms = (
            general_contract_last(grad_query_raw, query_back)
            + general_contract_last(grad_key_raw, key_back)
            + general_contract_last(grad_value_raw, value_back)
        )
        grad_in = grad_resid + general_narrow(back_terms)
        input_grads.append(grad_in.astype(jnp.bfloat16).reshape(per_batch, slice_len, local_width))
        fresh_grads = (
            general_contract_first(wide_in, grad_query_raw),
            general_contract_first(wide_in, grad_key_raw),
            general_contract_first(wide_in, grad_value_raw),
            general_contract_first(out_b, wide_grad_attn),
            general_contract_first(wide_mid, grad_gate),
            general_contract_first(wide_mid, grad_up),
            general_contract_first(act_b, wide_grad_mlp),
        )
        weight_grads = tuple((left + right for left, right in zip(weight_grads, fresh_grads)))
    finals = (
        lax.psum_scatter(
            weight_grads[0].astype(jnp.bfloat16), ("dp", "ctx"), scatter_dimension=0, tiled=True
        ).astype(jnp.float32),
        lax.psum_scatter(
            weight_grads[1].astype(jnp.bfloat16), ("dp", "ctx"), scatter_dimension=0, tiled=True
        ).astype(jnp.float32),
        lax.psum_scatter(
            weight_grads[2].astype(jnp.bfloat16), ("dp", "ctx"), scatter_dimension=0, tiled=True
        ).astype(jnp.float32),
        lax.psum_scatter(
            weight_grads[3].astype(jnp.bfloat16), ("dp", "ctx"), scatter_dimension=1, tiled=True
        ).astype(jnp.float32),
        lax.psum_scatter(
            weight_grads[4].astype(jnp.bfloat16), ("dp", "ctx"), scatter_dimension=0, tiled=True
        ).astype(jnp.float32),
        lax.psum_scatter(
            weight_grads[5].astype(jnp.bfloat16), ("dp", "ctx"), scatter_dimension=0, tiled=True
        ).astype(jnp.float32),
        lax.psum_scatter(
            weight_grads[6].astype(jnp.bfloat16), ("dp", "ctx"), scatter_dimension=1, tiled=True
        ).astype(jnp.float32),
    )
    gains = lax.psum((q_gain_grad, k_gain_grad, attn_gain_grad, mlp_gain_grad), ("dp", "ctx"))
    return (
        jnp.concatenate(outputs, axis=0),
        jnp.concatenate(input_grads, axis=0),
        finals[0],
        finals[1],
        finals[2],
        finals[3],
        finals[4],
        finals[5],
        finals[6],
        gains[0],
        gains[1],
        gains[2],
        gains[3],
    )


class Batch:
    pass


def planned(
    hidden, cotangent, segments, positions, w_query, w_key, w_value, w_out, w_gate, w_up, w_down,
    q_gain, k_gain, attn_gain, mlp_gain,
):
    seqs, count, width = hidden.shape
    per = seqs // 2
    rows = per * count
    ff = w_gate.shape[1]
    batches = (Batch(), Batch())
    one, two = batches
    for b, batch in enumerate(batches):
        batch.x = Rows(hidden.reshape(seqs * count, width), b * rows, rows)
        batch.cot = Rows(cotangent.reshape(seqs * count, width), b * rows, rows)
    seg_cols = jnp.broadcast_to(segments.reshape(seqs * count, 1), (seqs * count, 128))
    pos_cols = jnp.broadcast_to(positions.reshape(seqs * count, 1), (seqs * count, 128))
    half = HEAD_DIM // 2
    freqs = THETA ** (-(jnp.arange(half, dtype=F32) * 2.0) / HEAD_DIM)
    freqs = jnp.concatenate([freqs, freqs]).reshape(1, HEAD_DIM)
    sign = jnp.concatenate([-jnp.ones(half, F32), jnp.ones(half, F32)]).reshape(1, HEAD_DIM)
    seg_pad = jnp.concatenate([segments, jnp.zeros((8 - seqs, count), segments.dtype)], axis=0)
    norms = (q_gain, k_gain)

    quarters = [(512 * k, 512) for k in range(ff // 512)]
    wg, wu = [], []

    s = Slot("slot0", 0, 97.0, 48.0)
    line = Line(s, rows, width, gather=one.x)
    plane = Plane(s)
    full = [plane.gather(w, 0, True, done="w%d" % i) for i, w in enumerate((w_query, w_key, w_value))]
    w_out_h = plane.gather(w_out, 1, True, 1, 12.0)
    some = [plane.gather(w_gate, 0, True, 1, t, cols=c) for t, c in zip((18.0, 26.0), quarters)]
    seg_h = plane.gather(seg_pad, 0, False, 1, 20.0)
    cosine, sine = tables(s, pos_cols, freqs, sign)
    made = project(s, line, rows, width, full, ("w0", "w1", "w2"), norms, cosine, sine, 0)
    s.run()
    wq, wk, wv = (h.value for h in full)
    wg += [h.value for h in some]
    wo, seg_all, cosine, sine = w_out_h.value, seg_h.value, cosine.target.value, sine.target.value
    one.q_raw, one.k_raw, one.q, one.kv, one.qk_factor = (h.value for h in made)
    one.wide = line.out.value

    s = Slot("slot1", 1, 92.0, 44.0)
    line = Line(s, rows, width, gather=two.x)
    plane = Plane(s)
    kvs = plane.gather(one.kv, 0, False, 4, done="kv")
    some = [plane.gather(w_gate, 0, True, cols=c) for c in quarters[2:]]
    more = plane.gather(w_up, 0, True, cols=quarters[0])
    s.mark_early("tables")
    mask = Mask(s, seg_all, seg_cols, 0, count)
    felt = attend(s, "kv", kvs, one.q, mask, rows, width)
    made = project(s, line, rows, width, (wq, wk, wv), None, norms, s.load(cosine), s.load(sine), rows)
    s.run()
    wg += [h.value for h in some]
    wu.append(more.value)
    one.kvs = kvs.value
    two.q_raw, two.k_raw, two.q, two.kv, two.qk_factor = (h.value for h in made)
    one.heads, one.heads_b, one.logsum = (h.value for h in felt)
    two.wide = line.out.value

    s = Slot("slot2", 2, 130.0, 60.0)
    line = Line(s, rows, width, scatter=True)
    plane = Plane(s)
    kvs = plane.gather(two.kv, 0, False, 4, done="kv")
    some = [plane.gather(w_up, 0, True, cols=c) for c in quarters[1:]]
    ends = attn_finish(s, line, rows, width, one.x, attn_gain)
    produce(s, line, [s.load(one.heads_b)], [[wo]], (width, width), col_block, dot_nn, 0.6)
    mask = Mask(s, seg_all, seg_cols, per, count)
    felt = attend(s, "kv", kvs, two.q, mask, rows, width)
    s.run()
    wu += [h.value for h in some]
    two.kvs = kvs.value
    one.attn, one.resid, one.resid_b, one.factor = (h.value for h in ends)
    two.heads, two.heads_b, two.logsum = (h.value for h in felt)

    s = Slot("slot3", 3, 160.0, 70.0)
    line = Line(s, rows, width, gather=one.resid_b, scatter=True)
    w_down_h = Plane(s).gather(w_down, 1, True, 4)
    ends = attn_finish(s, line, rows, width, two.x, attn_gain)
    produce(s, line, [s.load(two.heads_b)], [[wo]], (width, width), col_block, dot_nn, 0.6)
    inner = gate_up(s, line, rows, wg, wu)
    s.run()
    wd, one.mid = w_down_h.value, line.out.value
    two.attn, two.resid, two.resid_b, two.factor = (h.value for h in ends)
    one.gate, one.up, one.act = (h.value for h in inner)

    s = Slot("slot4", 4, 160.0, 80.0)
    line = Line(s, rows, width, gather=two.resid_b, scatter=True)
    ends = mlp_finish(s, line, rows, width, one.resid, one.cot, mlp_gain)
    produce(s, line, [s.load(one.act)], [[wd]], (ff, 512), col_block, dot_nn, 1.8)
    inner = gate_up(s, line, rows, wg, wu)
    s.run()
    two.mid = line.out.value
    one.out, one.g_mlp_b, one.g_mlp_gain = (h.value for h in ends)
    two.gate, two.up, two.act = (h.value for h in inner)

    s = Slot("slot5", 5, 130.0, 60.0)
    line = Line(s, rows, width, gather=one.g_mlp_b, scatter=True)
    ends = mlp_finish(s, line, rows, width, two.resid, two.cot, mlp_gain)
    produce(s, line, [s.load(two.act)], [[wd]], (ff, 512), col_block, dot_nn, 1.8)
    inner = act_back(s, line, rows, wd, one.gate, one.up)
    s.run()
    one.g_mlp = line.out.value
    two.out, two.g_mlp_b, two.g_mlp_gain = (h.value for h in ends)
    one.g_gate, one.g_up = (h.value for h in inner)

    s = Slot("slot6", 6, 130.0, 60.0)
    line = Line(s, rows, width, gather=two.g_mlp_b, scatter=True)
    ends = resid_finish(s, line, rows, width, one.cot, one.attn, one.factor, attn_gain)
    produce(s, line, [s.load(one.g_gate), s.load(one.g_up)], [wg, wu], (512, ff), row_block, dot_nt, 3.4)
    inner = act_back(s, line, rows, wd, two.gate, two.up)
    s.run()
    two.g_mlp = line.out.value
    one.g_resid, one.g_attn_b, one.g_attn_gain = (h.value for h in ends)
    two.g_gate, two.g_up = (h.value for h in inner)

    s = Slot("slot7", 7, 97.0, 48.0)
    line = Line(s, rows, width, gather=one.g_attn_b, scatter=True)
    plane = Plane(s)
    g_down = s.hbm_out((ff - 512, w_down.shape[1]), F32)
    ends = resid_finish(s, line, rows, width, two.cot, two.attn, two.factor, attn_gain)
    acts, g_mlps = joined(s, (one.act, two.act)), joined(s, (one.g_mlp, two.g_mlp))
    full_grad(s, plane, acts, g_mlps, False, g_down, (12.0, 23.0, 28.0), "d", (0, 1, 2), ("part0", "part1", "part1"))
    produce(s, line, [s.load(two.g_gate), s.load(two.g_up)], [wg, wu], (512, ff), row_block, dot_nt, 3.4)
    mask = Mask(s, seg_all, seg_cols, 0, count, True)
    back = attend_back(s, line, one.kvs, one.q, one.heads, one.logsum, mask, rows, width, wo)
    s.run()
    one.g_attn = line.out.value
    two.g_resid, two.g_attn_b, two.g_attn_gain = (h.value for h in ends)
    one.g_q, one.g_kv = (h.value for h in back)

    s = Slot("slot8", 8, 92.0, 46.0)
    line = Line(s, rows, width, gather=two.g_attn_b)
    plane = Plane(s)
    g_kv = plane.scatter(one.g_kv, 0, False, 4, done="kv")
    g_gate = s.hbm_out(w_gate.shape, F32)
    raws = project_back(s, "kv", one.g_q, g_kv, (one.q_raw, one.k_raw), one.qk_factor, norms, cosine, sine, 0, rows, width)
    mids, g_gates = joined(s, (one.mid, two.mid)), joined(s, (one.g_gate, two.g_gate))
    full_grad(s, plane, mids, g_gates, True, g_gate, (7.0, 11.0, 15.0, 19.0), "g")
    mask = Mask(s, seg_all, seg_cols, per, count, True)
    back = attend_back(s, line, two.kvs, two.q, two.heads, two.logsum, mask, rows, width, wo)
    s.run()
    two.g_attn = line.out.value
    one.g_qr, one.g_kr, one.g_vr, one.g_q_gain, one.g_k_gain = (h.value for h in raws)
    two.g_q, two.g_kv = (h.value for h in back)

    s = Slot("slot9", 9, 80.0, 40.0)
    line = Line(s, rows, width, scatter=True)
    plane = Plane(s)
    g_kv = plane.scatter(two.g_kv, 0, False, 4, done="kv")
    g_up = s.hbm_out(w_up.shape, F32)
    fin_one = last_finish(s, line, rows, width, one.g_resid)[0]
    raws = project_back(s, "kv", two.g_q, g_kv, (two.q_raw, two.k_raw), two.qk_factor, norms, cosine, sine, rows, rows, width)
    produce(s, line, [s.load(g) for g in (one.g_qr, one.g_kr, one.g_vr)], [[wq], [wk], [wv]], (512, width), row_block, dot_nt, 1.6, "u1")
    mids, g_ups = joined(s, (one.mid, two.mid)), joined(s, (one.g_up, two.g_up))
    full_grad(s, plane, mids, g_ups, True, g_up, (7.0, 11.0, 22.0, 26.0), "u")
    s.run()
    two.g_qr, two.g_kr, two.g_vr, two.g_q_gain, two.g_k_gain = (h.value for h in raws)

    s = Slot("slot10", 10, 75.0, 38.0)
    line = Line(s, rows, width, scatter=True)
    plane = Plane(s)
    fin_two = last_finish(s, line, rows, width, two.g_resid)[0]
    produce(s, line, [s.load(g) for g in (two.g_qr, two.g_kr, two.g_vr)], [[wq], [wk], [wv]], (512, width), row_block, dot_nt, 1.6, "d3")
    sums = gain_sums(
        s,
        (one.g_q_gain, two.g_q_gain, one.g_k_gain, two.g_k_gain)
        + (one.g_attn_gain, two.g_attn_gain, one.g_mlp_gain, two.g_mlp_gain),
    )
    g_q, g_k, g_v = (s.hbm_out(w_query.shape, F32) for _ in range(3))
    g_out, g_last = s.hbm_out(w_out.shape, F32), s.hbm_out((512, w_down.shape[1]), F32)
    acts, g_mlps = joined(s, (one.act, two.act)), joined(s, (one.g_mlp, two.g_mlp))
    full_grad(s, plane, acts, g_mlps, False, g_last, (7.0,), "d", (3,))
    wides = joined(s, (one.wide, two.wide))
    full_grad(s, plane, wides, joined(s, (one.g_qr, two.g_qr)), True, g_q, (18.0,), "q")
    full_grad(s, plane, wides, joined(s, (one.g_kr, two.g_kr)), True, g_k, (22.0,), "k")
    full_grad(s, plane, wides, joined(s, (one.g_vr, two.g_vr)), True, g_v, (26.0,), "v")
    heads_b, g_attns = joined(s, (one.heads_b, two.heads_b)), joined(s, (one.g_attn, two.g_attn))
    full_grad(s, plane, heads_b, g_attns, False, g_out, (30.0,), "o")
    s.run()
    gains = [sums.value[k] for k in range(4)]
    shape = (per, count, width)
    return (
        jnp.concatenate([one.out.reshape(shape), two.out.reshape(shape)], axis=0),
        jnp.concatenate([fin_one.value.reshape(shape), fin_two.value.reshape(shape)], axis=0),
        *(g.value for g in (g_q, g_k, g_v, g_out, g_gate, g_up)),
        jnp.concatenate([g_down.value, g_last.value], axis=0),
        *gains,
    )


def solution(mesh):
    rows, cols = P(("dp", "ctx"), "tp"), P("tp", ("dp", "ctx"))
    act, gain = P("dp", "ctx", "tp"), P("tp")
    size = dict(mesh.shape)
    body = planned if (size["dp"], size["ctx"], size["tp"]) == (2, 4, 4) else general
    return jax.shard_map(
        body,
        mesh=mesh,
        in_specs=(act, act, P("dp", "ctx"), P("dp", "ctx"), rows, rows, rows, cols, rows, rows, cols, gain, gain, gain, gain),
        out_specs=(act, act, rows, rows, rows, cols, rows, rows, cols, gain, gain, gain, gain),
        check_vma=False,
    )
```
